32 devices in a mesh: dp: 8 (over y, x, core), tensor: 4 (over z).
Axes of the slice: x: 2, y: 2, z: 4, core: 2. Of those that a mesh axis runs over, the one named last changes fastest.
Arguments:
- tokens: bfloat16 [8192, 1024], P(('dp', 'tensor')), may hold values from -6 to 6
- lengths: int32 [32], replicated, may hold values from 64 to 832, as said below
- seq_order: int32 [32], replicated, may hold values from 0 to 31, as said below
- gain_attn: bfloat16 [1024], P('dp'), may hold values from 0.5 to 1.5
- w_qkv: bfloat16 [3, 1024, 1024], P(None, 'dp', 'tensor'), may hold values from -0.25 to 0.25
- w_attn_out: bfloat16 [1024, 1024], P('tensor', 'dp'), may hold values from -0.375 to 0.375
- gain_mlp: bfloat16 [1024], P('dp'), may hold values from 0.5 to 1.5
- w_in: bfloat16 [1024, 2, 2624], P('dp', None, 'tensor'), may hold values from -0.1875 to 0.1875
- w_mlp_out: bfloat16 [2624, 1024], P('tensor', 'dp'), may hold values from -0.15625 to 0.15625
- cotangent: bfloat16 [8192, 1024], P(('dp', 'tensor')), may hold values from -6 to 6
Outputs:
- output: bfloat16 [8192, 1024], P(('dp', 'tensor'))
- d_tokens: float32 [8192, 1024], P(('dp', 'tensor'))
- d_gain_attn: float32 [1024], P('dp')
- d_w_qkv: float32 [3, 1024, 1024], P(None, 'dp', 'tensor')
- d_w_attn_out: float32 [1024, 1024], P('tensor', 'dp')
- d_gain_mlp: float32 [1024], P('dp')
- d_w_in: float32 [1024, 2, 2624], P('dp', None, 'tensor')
- d_w_mlp_out: float32 [2624, 1024], P('tensor', 'dp')
The draws below stay inside these ranges and needn't reach their ends.
Inputs may be any that keep to these rules, and one draw needn't show every extreme that they name: For every g the lengths of the sequences seq_order[g * 4] to seq_order[g * 4 + 3] add up to 1024; in every draw some g holds one sequence of the greatest length and 3 of the least. `seq_order`: each sequence number stands once.
All inputs are finite; a program needn't handle non-finite values.
Results may differ from the reference program's by a relative error of at most 0.017.
Values may be sent and summed in bfloat16 or wider, within the bound.
A program may use at most 128 MiB of HBM per device.

```python
import jax
import jax.numpy as jnp
from jax import lax

D = 1024
HEADS = 16
HEAD_DIM = 64
FF = 2624
SEQ_GRP = 4
MINLEN = 64
TOK_GRP = 1024
NSEQ = 32
TOKENS = 8192


def dealt_layout(key):
    base_key = jax.random.fold_in(key, 7)
    cut_key, busy_key, slot_key, order_key = jax.random.split(base_key, 4)
    group_count = NSEQ // SEQ_GRP
    spare_tokens = TOK_GRP - SEQ_GRP * MINLEN
    cut_points = jnp.sort(jax.random.randint(cut_key, (group_count, SEQ_GRP - 1), 0, spare_tokens + 1).astype(jnp.int32), axis=1)
    edge_points = jnp.concatenate([jnp.zeros((group_count, 1), jnp.int32), cut_points, jnp.full((group_count, 1), spare_tokens, jnp.int32)], axis=1)
    dealt_lengths = edge_points[:, 1:] - edge_points[:, :-1] + MINLEN
    busy_group = jax.random.randint(busy_key, (), 0, group_count).astype(jnp.int32)
    long_slot = jax.random.randint(slot_key, (), 0, SEQ_GRP).astype(jnp.int32)
    pattern = jnp.where(jnp.arange(SEQ_GRP, dtype=jnp.int32) == long_slot, TOK_GRP - (SEQ_GRP - 1) * MINLEN, MINLEN).astype(jnp.int32)
    is_busy = jnp.arange(group_count, dtype=jnp.int32) == busy_group
    dealt_lengths = jnp.where(is_busy[:, None], pattern[None, :], dealt_lengths).astype(jnp.int32)
    order_list = jax.random.permutation(order_key, NSEQ).astype(jnp.int32)
    lengths = jnp.zeros((NSEQ,), jnp.int32).at[order_list].set(dealt_lengths.reshape(-1))
    return (lengths, order_list)


def draw_lengths(key, part):
    return dealt_layout(key)[0]


def draw_seq_order(key, part):
    return dealt_layout(key)[1]


def block_levels(stream_key, shape, cuts, least, top_value):
    def one(dim, parts):
        steps = jax.random.uniform(jax.random.fold_in(jax.random.fold_in(stream_key, 6), dim), (parts,), jnp.float32, least / len(cuts), top_value / len(cuts))
        return jnp.repeat(jnp.exp(steps), shape[dim] // parts).reshape((-1,) + (1,) * (len(shape) - dim - 1))

    factor_of = one(*cuts[0])
    for cut in cuts[1:]:
        factor_of = factor_of * one(*cut)
    return factor_of


def bell_draw(stream_key, dims, scale, bound, cuts=(), kind=jnp.bfloat16):
    factor_of = block_levels(stream_key, dims, cuts, -0.22, 0.18) if cuts else 1.0
    entries = jax.random.normal(stream_key, dims, jnp.float32) * scale * factor_of
    return jnp.minimum(jnp.maximum(entries, -bound), bound).astype(kind)


def setup_inputs(seed: int = 0) -> dict:
    splits = jax.random.split(jax.random.key(seed), 11)
    return {
        "tokens": bell_draw(splits[0], (TOKENS, D), 1.0, 6.0, ((0, 32),)),
        "lengths": draw_lengths(jax.random.fold_in(splits[10], 71), 0),
        "seq_order": draw_seq_order(jax.random.fold_in(splits[10], 71), 0),
        "gain_attn": jnp.clip(1.0 + 0.1 * jax.random.normal(splits[3], (D,), jnp.float32), 0.5, 1.5).astype(jnp.bfloat16),
        "w_qkv": bell_draw(splits[4], (3, D, D), (D // 2) ** -0.5, 0.25, ((1, 8), (2, 4))),
        "w_attn_out": bell_draw(splits[5], (D, D), (D // 4) ** -0.5, 0.375, ((0, 4), (1, 8))),
        "gain_mlp": jnp.clip(1.0 + 0.1 * jax.random.normal(splits[6], (D,), jnp.float32), 0.5, 1.5).astype(jnp.bfloat16),
        "w_in": bell_draw(splits[7], (D, 2, FF), D ** -0.5, 0.1875, ((0, 8), (2, 4))),
        "w_mlp_out": bell_draw(splits[8], (FF, D), (FF // 2) ** -0.5, 0.15625, ((0, 4), (1, 8))),
        "cotangent": bell_draw(splits[9], (TOKENS, D), 1.0, 6.0, ((0, 32),)),
    }


rope_base = 160000.0
norm_eps = 1e-05
masked_fill = -1e+30
highest = lax.Precision.HIGHEST

@jax.custom_vjp
def low(v):
    return lax.optimization_barrier(v.astype(jnp.bfloat16)).astype(jnp.float32)

@jax.custom_vjp
def low_back(v):
    return v

def low_keep(v):
    return (low(v), None)

def low_pass(kept, grad):
    return (grad,)

def back_keep(v):
    return (v, None)

def back_low(kept, grad):
    return (low(grad),)
low.defvjp(low_keep, low_pass)
low_back.defvjp(back_keep, back_low)

def layer_norm(field_in, norm_gain):
    row_mean = lax.optimization_barrier(jnp.mean(field_in, axis=-1, keepdims=True))
    centered = field_in - row_mean
    variance = lax.optimization_barrier(jnp.mean(centered * centered, axis=-1, keepdims=True))
    return centered * lax.rsqrt(variance + norm_eps) * norm_gain

def rotate(field_in, position):
    half_size = field_in.shape[-1] // 2
    index_range = jnp.arange(half_size, dtype=jnp.float32)
    frequency = rope_base ** (-2.0 * index_range / field_in.shape[-1])
    angles = position[:, None] * frequency[None, :]
    cosine = jnp.cos(angles)[:, None, :]
    sine_part = jnp.sin(angles)[:, None, :]
    first_half = field_in[..., :half_size]
    second_half = field_in[..., half_size:]
    return jnp.concatenate([first_half * cosine - second_half * sine_part, second_half * cosine + first_half * sine_part], axis=-1)

def geglu(act_part, up_part):
    return jax.nn.gelu(act_part, approximate=False) * up_part

def attend_block(query_block, key_group, value_group, segment_block, segment_group):
    raw_scores = jnp.einsum('qhd,khd->hqk', query_block, key_group, precision=highest)
    scores = low_back(raw_scores * query_block.shape[-1] ** (-0.5))
    allowed = segment_block[:, None] == segment_group[None, :]
    scores = jnp.where(allowed[None], scores, masked_fill)
    probs_low = low(jax.nn.softmax(scores, axis=-1))
    return jnp.einsum('hqk,khd->qhd', probs_low, value_group, precision=highest)

def block_pass(query_block, segment_block, key_group, value_group, segment_group):
    return attend_block(query_block, key_group, value_group, segment_block, segment_group)

def attend_group(packed):
    query_group, key_group, value_group, segment_group = packed
    group_rows = query_group.shape[0]
    block_rows = min(512, group_rows)
    block_count = group_rows // block_rows
    query_blocks = query_group.reshape((block_count, block_rows) + query_group.shape[1:])
    segment_blocks = segment_group.reshape(block_count, block_rows)
    saved_pass = jax.checkpoint(block_pass)

    def one_block(paired):
        return saved_pass(paired[0], paired[1], key_group, value_group, segment_group)
    results = lax.map(one_block, (query_blocks, segment_blocks))
    return results.reshape(query_group.shape)

def forward(tokens_in, gain_one, qkv_weight, out_weight, gain_two, in_weight, down_weight, segment, position):
    row_total = tokens_in.shape[0]
    normed_one = low(layer_norm(tokens_in, gain_one))
    qkv = low_back(jnp.einsum('rd,pdc->prc', normed_one, qkv_weight, precision=highest))
    shaped = qkv.reshape(3, row_total, HEADS, HEAD_DIM)
    query_rot = low(rotate(shaped[0], position))
    key_rot = low(rotate(shaped[1], position))
    value_low = low(shaped[2])
    group_shape = (row_total // TOK_GRP, TOK_GRP, HEADS, HEAD_DIM)
    attended = lax.map(jax.checkpoint(attend_group), (query_rot.reshape(group_shape), key_rot.reshape(group_shape), value_low.reshape(group_shape), segment.reshape(-1, TOK_GRP)))
    attn_low = low(low_back(attended.reshape(row_total, HEADS * HEAD_DIM)))
    resid_mid = tokens_in + low_back(jnp.dot(attn_low, out_weight, precision=highest))
    normed_two = low(layer_norm(resid_mid, gain_two))
    gate_up = low_back(jnp.einsum('rd,dpc->prc', normed_two, in_weight, precision=highest))
    hidden = low(geglu(gate_up[0], gate_up[1]))
    return resid_mid + low_back(jnp.dot(hidden, down_weight, precision=highest))

def reference(tokens, lengths, seq_order, gain_attn, w_qkv, w_attn_out, gain_mlp, w_in, w_mlp_out, cotangent):
    group_count = seq_order.shape[0] // SEQ_GRP
    dealt_lengths = lengths[seq_order.reshape(group_count, SEQ_GRP)].astype(jnp.int32)
    seq_ends = jnp.cumsum(dealt_lengths, axis=1).astype(jnp.int32)
    row_index = jnp.arange(TOK_GRP, dtype=jnp.int32)
    passed = row_index[None, :, None] >= seq_ends[:, None, :]
    segment = lax.optimization_barrier(jnp.sum(passed.astype(jnp.int32), axis=2)).astype(jnp.int32).reshape(-1)
    row_start = lax.optimization_barrier(jnp.sum(jnp.where(passed, dealt_lengths[:, None, :], 0), axis=2)).astype(jnp.int32)
    position = (row_index[None, :] - row_start).reshape(-1).astype(jnp.float32)

    def layer(tokens_in, gain_one, qkv_weight, out_weight, gain_two, in_weight, down_weight):
        return forward(tokens_in, gain_one, qkv_weight, out_weight, gain_two, in_weight, down_weight, segment, position)
    primals = (tokens.astype(jnp.float32), gain_attn.astype(jnp.float32), w_qkv.astype(jnp.float32), w_attn_out.astype(jnp.float32), gain_mlp.astype(jnp.float32), w_in.astype(jnp.float32), w_mlp_out.astype(jnp.float32))
    layer_out, pull_back = jax.vjp(layer, *primals)
    gradients = pull_back(cotangent.astype(jnp.float32))
    return (layer_out.astype(jnp.bfloat16), gradients[0], gradients[1], gradients[2], gradients[3], gradients[4], gradients[5], gradients[6])
```

```python
import functools

import jax
import jax.numpy as jnp
from jax import lax
from jax.experimental import pallas as pl
from jax.experimental.pallas import tpu as pltpu
from jax.sharding import PartitionSpec as P

HEAD_DIM = 64
SEQ_GRP = 4
rope_base = 160000.0
norm_eps = 1e-05
masked_fill = -1e30
MESH = pl.DeviceIdType.MESH
BF = jnp.bfloat16
F32 = jnp.float32

NT = (((1,), (1,)), ((), ()))
TN = (((0,), (0,)), ((), ()))


def place():
    dp = lax.axis_index("dp")
    z = lax.axis_index("tensor")
    c = lax.rem(dp, 2)
    x = lax.rem(lax.div(dp, 2), 2)
    y = lax.div(dp, 4)
    return dp, z, c, x, y


def flip(dp, bits, distance):
    out = dp
    for b, bit in enumerate(bits):
        if (distance >> b) & 1:
            out = out + (1 << b) - (2 << b) * bit
    return out


def remote(src, dst, send, recv, dev):
    return pltpu.make_async_remote_copy(
        src_ref=src, dst_ref=dst, send_sem=send, recv_sem=recv, device_id=dev, device_id_type=MESH
    )


def cols(start, size):
    return pl.ds(pl.multiple_of(start, size), size)


def greet(dp, z, bits):
    c = bits[0]
    barrier = pltpu.get_barrier_semaphore()
    peers = [(flip(dp, bits, d), z) for d in range(1, 8)]
    core = flip(dp, bits, 1)
    for k in range(1, 4):
        peers.append((dp, lax.rem(z + k, 4)))
        peers.append((core, lax.rem(z + k, 4)))
    for p in peers:
        pl.semaphore_signal(barrier, inc=1, device_id=p, device_id_type=MESH)
    pl.semaphore_wait(barrier, len(peers))


def norm_rows(v):
    mean = jnp.mean(v, axis=-1, keepdims=True)
    centered = v - mean
    var = jnp.mean(centered * centered, axis=-1, keepdims=True)
    rstd = lax.rsqrt(var + norm_eps)
    return centered * rstd, rstd


def turn(v, cs, sn):
    lane = lax.broadcasted_iota(jnp.int32, cs.shape, 1)
    low_half = lax.rem(lane, HEAD_DIM) < HEAD_DIM // 2
    parts = []
    for t in range(v.shape[1] // 128):
        piece = v[:, t * 128 : (t + 1) * 128]
        swapped = jnp.where(low_half, pltpu.roll(piece, 96, 1), pltpu.roll(piece, 32, 1))
        parts.append(piece * cs + swapped * sn)
    return jnp.concatenate(parts, axis=1)


def gain_row(gains, row):
    return jnp.concatenate([gains[p, row : row + 1, :] for p in range(8)], axis=1)


HID = 656
PACK = 3 * HID + 256
CUTS = ((0, 560), (560, 560), (1120, 560), (1680, 544))


def forward_kernel(
    tok, wqkv, w4, gains, cs, sn, segc, segr, cot,
    q_o, k_o, v_o, lse_o, att_o, attn2_o, h1_o, wq_o, G_o, gains_o, cot2_o,
    tall, km, vT, S, Pm, oT,
    us, ds, rb, ra, wr_s, wr_r, wc_s, wc_r, g_s, g_r, co_s, co_r, hop_s, hop_r,
    zu_s, zd_s, zr, pa_s, pb_s, pf_s, pa_r, pb_r, at_s, at_r, lc,
):
    dp, z, c, x, y = place()
    bits = (c, x, y)
    core = flip(dp, bits, 1)
    px, py = flip(dp, bits, 2), flip(dp, bits, 4)
    a = (1 - c) * px + c * py
    b = (1 - c) * py + c * px
    chip, chip_a, chip_b = lax.div(dp, 2), lax.div(a, 2), lax.div(b, 2)
    chip_d = 3 - chip
    home = lax.div(z, 2)
    org = c == home
    zq = lax.rem(z, 2)
    greet(dp, z, bits)

    def tok_up(k, h):
        ref = tall.at[z - k, pl.ds(h * 128, 128)]
        src = tok.at[pl.ds(h * 128, 128)] if k == 0 else ref
        return remote(src, ref, us.at[k, h], rb.at[k + 1, h], (dp, z + 1))

    def tok_down(k, h):
        ref = tall.at[z + k, pl.ds(h * 128, 128)]
        src = tok.at[pl.ds(h * 128, 128)] if k == 0 else ref
        return remote(src, ref, ds.at[k, h], ra.at[k + 1, h], (dp, z - 1))

    def up_ok(k):
        return (z >= k) & (z < 3)

    def down_ok(k):
        return (z + k <= 3) & (z > 0)

    for h in range(2):
        pl.when(up_ok(0))(lambda h=h: tok_up(0, h).start())
        pl.when(down_ok(0))(lambda h=h: tok_down(0, h).start())

    for d in range(1, 8):
        remote(gains, gains_o.at[dp], g_s.at[d], g_r.at[d], (flip(dp, bits, d), z)).start()
    own_rows = cols(dp * 128, 128)
    for j, d in enumerate((2, 4, 6)):
        remote(wqkv, wq_o.at[:, own_rows], wr_s.at[j], wr_r.at[j], (flip(dp, bits, d), z)).start()
    remote(wqkv, wq_o.at[:, own_rows], wc_s.at[3], wc_r.at[3], (core, z)).start()
    mine = G_o.at[zq, :, cols(dp * 128, 128)]
    local_pack = pltpu.make_async_copy(w4, mine, lc.at[0])
    hop = remote(w4, mine, hop_s, hop_r, (core, z))
    pl.when(org)(lambda: local_pack.start())
    pl.when(jnp.logical_not(org))(lambda: hop.start())
    cot_copy = remote(cot, cot2_o.at[cols(c * 256, 256)], co_s, co_r, (core, z))
    cot_copy.start()

    gains_o[dp] = gains[...]
    wq_o[:, own_rows, :] = wqkv[...]
    tall[z] = tok[...]
    cot2_o[cols(c * 256, 256), :] = cot[...]

    def piece(q, u, where):
        r0, n = CUTS[u]
        return G_o.at[q, pl.ds(r0, n), cols(where * 256, 256)]

    def send_up(q, u):
        return remote(piece(q, u, chip), piece(q, u, chip), zu_s.at[q, u], zr.at[q, u], (dp, z + 1))

    def send_down(q, u):
        return remote(piece(q, u, chip), piece(q, u, chip), zd_s.at[q, u], zr.at[q, u], (dp, z - 1))

    def plane_a(q, u):
        return remote(piece(q, u, chip), piece(q, u, chip), pa_s.at[q, u], pa_r.at[q, u], (a, z))

    def plane_b(q, u):
        return remote(piece(q, u, chip), piece(q, u, chip), pb_s.at[q, u], pb_r.at[q, 0, u], (b, z))

    def plane_f(q, u):
        return remote(piece(q, u, chip_a), piece(q, u, chip_a), pf_s.at[q, u], pb_r.at[q, 1, u], (b, z))

    def goes_up(q):
        return (z >= 2 * c + q) & (z < 3)

    def goes_down(q):
        return (z <= 2 * c + q) & (z > 0)

    def spread(q, u):
        plane_a(q, u).start()
        plane_b(q, u).start()

    def arrive(q, u):
        remote(piece(q, u, chip), piece(q, u, chip), zu_s.at[q, u], zr.at[q, u], (core, z)).wait_recv()

    def onward(q, u):
        pl.when(goes_up(q))(lambda: send_up(q, u).start())
        pl.when(goes_down(q))(lambda: send_down(q, u).start())

    def across(q, u):
        remote(piece(q, u, chip_a), piece(q, u, chip_a), pa_s.at[q, u], pa_r.at[q, u], (a, z)).wait_recv()
        plane_f(q, u).start()

    near = (1 - c) * lax.div(z + 2, 3) + c * lax.div(z, 3)
    far = 1 - near

    for d in range(1, 8):
        p = flip(dp, bits, d)
        remote(gains, gains_o.at[p], g_s.at[d], g_r.at[d], (p, z)).wait_recv()

    @pl.when(org)
    def _():
        local_pack.wait()
        remote(w4, G_o.at[zq, :, cols(core * 128, 128)], hop_s, hop_r, (core, z)).wait_recv()
        for u in range(4):
            spread(near, u)

    for j, d in enumerate((2, 4, 6)):
        p = flip(dp, bits, d)
        rows = wq_o.at[:, cols(p * 128, 128)]
        remote(wqkv, rows, wr_s.at[j], wr_r.at[j], (p, z)).wait_recv()
        remote(rows, rows, wc_s.at[j], wc_r.at[j], (core, z)).start()
    for j, d in enumerate((3, 5, 7, 1)):
        p = flip(dp, bits, d)
        remote(wqkv, wq_o.at[:, cols(p * 128, 128)], wc_s.at[j], wc_r.at[j], (core, z)).wait_recv()

    gain = gain_row(gains_o, 0)

    def project(s):
        base = s * 256

        @pl.loop(0, 8)
        def _(r):
            xhat, _r = norm_rows(tall[s, pl.ds(pl.multiple_of(r * 32, 32), 32), :].astype(F32))
            h1_o[pl.ds(pl.multiple_of(base + r * 32, 32), 32), :] = (xhat * gain).astype(BF)

        rows = pl.ds(pl.multiple_of(base, 256), 256)
        hb = h1_o[rows, :]
        cb, sb = cs[rows, :], sn[rows, :]
        for p, out in enumerate((q_o, k_o, v_o)):
            r = jnp.dot(hb, wq_o[p], preferred_element_type=F32)
            if p < 2:
                r = turn(r, cb, sb)
            if p == 0:
                r = r * (HEAD_DIM**-0.5)
            out[rows, :] = r.astype(BF)

    project(z)
    for k in range(1, 4):
        below, above = z - k >= 0, z + k <= 3
        for h in range(2):

            @pl.when(below)
            def _(k=k, h=h):
                ref = tall.at[z - k, pl.ds(h * 128, 128)]
                remote(ref, ref, us.at[k, h], rb.at[k, h], (core, z)).wait_recv()
                if k < 3:
                    pl.when(up_ok(k))(lambda: tok_up(k, h).start())

            @pl.when(above)
            def _(k=k, h=h):
                ref = tall.at[z + k, pl.ds(h * 128, 128)]
                remote(ref, ref, ds.at[k, h], ra.at[k, h], (core, z)).wait_recv()
                if k < 3:
                    pl.when(down_ok(k))(lambda: tok_down(k, h).start())

        @pl.when(org & (z + 1 == k))
        def _():
            for u in range(4):
                send_up(near, u).start()

        @pl.when(org & (4 - z == k))
        def _():
            for u in range(4):
                send_down(near, u).start()

        if k == 1:

            @pl.when(org)
            def _():
                for u in range(4):
                    across(near, u)

        @pl.loop(0, 2)
        def _(t, k=k):
            s = z - k + 2 * k * t
            pl.when((s >= 0) & (s <= 3))(lambda: project(s))

    lane = lax.broadcasted_iota(jnp.int32, (1024, 256), 1)
    for h in range(4):
        km[h] = jnp.where(lax.div(lane, HEAD_DIM) == h, k_o[...], jnp.zeros((), BF))
    for s in range(4):
        vT[:, s * 256 : (s + 1) * 256] = v_o[s * 256 : (s + 1) * 256, :].T

    def attend(i):
        rows = pl.ds(pl.multiple_of(i * 256, 256), 256)
        qb = q_o[rows, :]
        seg_q = segr[0:1, rows]

        @pl.loop(0, 4)
        def _(h):
            top = jnp.full((8, 256), -jnp.inf, F32)
            for kc in range(4):
                keys = pl.ds(kc * 256, 256)
                s = lax.dot_general(km[h, keys, :], qb, NT, preferred_element_type=F32)
                seg_k = segc[keys, :]
                same = jnp.concatenate([seg_k, seg_k], axis=1) == seg_q
                s = jnp.where(same, s, masked_fill)
                S[keys, :] = s
                top = jnp.maximum(top, jnp.max(s.reshape(32, 8, 256), axis=0))
            row_top = jnp.max(top, axis=0, keepdims=True)
            total = jnp.zeros((8, 256), F32)
            for kc in range(4):
                keys = pl.ds(kc * 256, 256)
                p = jnp.exp(S[keys, :] - row_top)
                total = total + jnp.sum(p.reshape(32, 8, 256), axis=0)
                Pm[keys, :] = p.astype(BF)
            row_total = jnp.sum(total, axis=0, keepdims=True)
            hr = pl.ds(pl.multiple_of(h * HEAD_DIM, HEAD_DIM), HEAD_DIM)
            o = jnp.dot(vT[hr, :], Pm[...], preferred_element_type=F32)
            oT[hr, :] = o * (1.0 / row_total)
            lse_o[h, i] = jnp.broadcast_to(row_top + jnp.log(row_total), (8, 256))

        att_o[rows, :] = oT[...].T.astype(BF)

    def att_slot(src_core, q):
        return attn2_o.at[cols(src_core * 256, 256), cols(q * 256, 256)]

    def att_copy(n, i):
        rows = pl.ds(pl.multiple_of(i * 256, 256), 256)
        return remote(
            att_o.at[rows, :], att_slot(c, zq), at_s.at[n], at_r.at[c, zq], (2 * chip + home, i)
        )

    late1 = jnp.where(org, far, near)

    def stage(q, u):
        arrive(q, u)
        onward(q, u)
        spread(q, u)

    order = [lax.rem(z + 1 + n, 4) for n in range(4)]
    for n in range(4):
        i = order[n]
        attend(i)
        if n < 3:
            att_copy(n, i).start()
        else:
            pl.when(jnp.logical_not(org))(lambda: att_copy(3, i).start())

            @pl.when(org)
            def _():
                attn2_o[cols(c * 256, 256), cols(zq * 256, 256)] = att_o[
                    pl.ds(pl.multiple_of(z * 256, 256), 256), :
                ]

        if n == 1:
            stage(late1, 0)
            stage(late1, 1)
        if n == 2:
            stage(late1, 2)
            across(late1, 0)
    stage(late1, 3)
    for u in range(1, 4):
        across(late1, u)

    @pl.when(jnp.logical_not(org))
    def _():
        for u in range(4):
            stage(far, u)
        for u in range(4):
            across(far, u)

    for src in range(2):
        for q in range(2):
            mine_too = (c == src) & (z == 2 * c + q)

            @pl.when(jnp.logical_not(mine_too))
            def _(src=src, q=q):
                slot = att_slot(src, q)
                remote(slot, slot, at_s.at[0], at_r.at[src, q], (core, z)).wait_recv()

    remote(cot, cot2_o.at[cols((1 - c) * 256, 256)], co_s, co_r, (core, z)).wait_recv()
    for q in range(2):
        for u in range(4):
            for w, where in enumerate((chip_b, chip_d)):
                ref = piece(q, u, where)
                remote(ref, ref, pb_s.at[q, u], pb_r.at[q, w, u], (b, z)).wait_recv()
    for k in range(3):
        for h in range(2):
            pl.when(up_ok(k))(lambda k=k, h=h: tok_up(k, h).wait_send())
            pl.when(down_ok(k))(lambda k=k, h=h: tok_down(k, h).wait_send())
    for d in range(1, 8):
        remote(gains, gains_o.at[dp], g_s.at[d], g_r.at[d], (core, z)).wait_send()
    for j in range(3):
        remote(wqkv, wq_o.at[:, own_rows], wr_s.at[j], wr_r.at[j], (core, z)).wait_send()
    for j in range(4):
        remote(wqkv, wq_o.at[:, own_rows], wc_s.at[j], wc_r.at[j], (core, z)).wait_send()
    pl.when(jnp.logical_not(org))(lambda: hop.wait_send())
    cot_copy.wait_send()
    for q in range(2):
        for u in range(4):
            pl.when(goes_up(q))(lambda q=q, u=u: send_up(q, u).wait_send())
            pl.when(goes_down(q))(lambda q=q, u=u: send_down(q, u).wait_send())
            plane_a(q, u).wait_send()
            plane_b(q, u).wait_send()
            plane_f(q, u).wait_send()
    for n in range(3):
        att_copy(n, order[n]).wait_send()
    pl.when(jnp.logical_not(org))(lambda: att_copy(3, order[3]).wait_send())


def run_forward(tok, wqkv, w4, gains, cs, sn, segc, segr, cot):
    V = pl.BlockSpec(memory_space=pltpu.VMEM)
    A = pl.BlockSpec(memory_space=pl.ANY)
    dma = pltpu.SemaphoreType.DMA
    s = jax.ShapeDtypeStruct
    return pl.pallas_call(
        forward_kernel,
        out_shape=(
            s((1024, 256), BF), s((1024, 256), BF), s((1024, 256), BF), s((4, 4, 8, 256), F32),
            s((1024, 256), BF), s((512, 512), BF), s((1024, 1024), BF), s((3, 1024, 256), BF),
            s((2, PACK, 1024), BF), s((8, 8, 128), F32), s((512, 1024), BF),
        ),
        in_specs=[V, V, A, V, V, V, V, V, V],
        out_specs=[V] * 8 + [A, V, V],
        scratch_shapes=[
            pltpu.VMEM((4, 256, 1024), BF), pltpu.VMEM((4, 1024, 256), BF), pltpu.VMEM((256, 1024), BF),
            pltpu.VMEM((1024, 256), F32), pltpu.VMEM((1024, 256), BF), pltpu.VMEM((256, 256), F32),
            dma((4, 2)), dma((4, 2)), dma((4, 2)), dma((4, 2)),
            dma((3,)), dma((3,)), dma((4,)), dma((4,)), dma((8,)), dma((8,)), dma, dma, dma, dma,
            dma((2, 4)), dma((2, 4)), dma((2, 4)), dma((2, 4)), dma((2, 4)), dma((2, 4)),
            dma((2, 4)), dma((2, 2, 4)), dma((4,)), dma((2, 2)), dma((1,)),
        ],
        compiler_params=pltpu.CompilerParams(
            collective_id=1, has_side_effects=True, vmem_limit_bytes=56 << 20
        ),
        name="forward_attention",
    )(tok, wqkv, w4, gains, cs, sn, segc, segr, cot)


def layout(lengths, seq_order, group_rows):
    seq_total = seq_order.shape[0]
    first_seq = lax.axis_index("dp") * SEQ_GRP
    chosen = lax.dynamic_slice_in_dim(seq_order, first_seq, SEQ_GRP)
    matched = chosen[:, None] == jnp.arange(seq_total, dtype=jnp.int32)[None, :]
    dealt_lengths = jnp.sum(jnp.where(matched, lengths[None, :], 0), axis=1)
    seq_ends = jnp.cumsum(dealt_lengths)
    row_index = jnp.arange(group_rows, dtype=jnp.int32)
    passed = row_index[:, None] >= seq_ends[None, :]
    segment = jnp.sum(passed.astype(jnp.int32), axis=1)
    row_start = jnp.sum(jnp.where(passed, dealt_lengths[None, :], 0), axis=1)
    return (segment, (row_index - row_start).astype(jnp.float32))


def prepare(lengths, seq_order, gain_attn, w_attn_out, gain_mlp, w_in, w_mlp_out):
    segment, position = layout(lengths, seq_order, 1024)
    half = HEAD_DIM // 2
    index_range = jnp.arange(half, dtype=F32)
    frequency = rope_base ** (-2.0 * index_range / HEAD_DIM)
    angles = position[:, None] * frequency[None, :]
    cosine, sine = jnp.cos(angles), jnp.sin(angles)
    cs = jnp.concatenate([cosine] * 4, axis=1)
    sn = jnp.concatenate([-sine, sine, -sine, sine], axis=1)
    seg = segment.astype(F32)
    segc = jnp.broadcast_to(seg[:, None], (1024, 128))
    segr = jnp.broadcast_to(seg[None, :], (8, 1024))
    w4 = jnp.concatenate(
        [w_in.transpose(1, 2, 0).reshape(2 * HID, 128), w_mlp_out, w_attn_out], axis=0
    )
    gains = jnp.concatenate(
        [gain_attn[None, :].astype(F32), gain_mlp[None, :].astype(F32), jnp.zeros((6, 128), F32)], axis=0
    )
    return w4, gains, cs, sn, segc, segr


ROWS = ((0, HID), (HID, HID), (2 * HID, HID), (3 * HID, 256))
UNITS = ((0, 2), (0, 0), (0, 1), (1, 2), (1, 0), (1, 1), (0, 3), (1, 3))
INV_SQRT2 = 0.7071067811865476
INV_SQRT_2PI = 0.3989422804014327


def backward_kernel(
    q, k, v, lse, att, attn2, h1, wq, G_in, gains, cot2, tok, cs, sn, segc, segr, wqkv, w4,
    out_o, dtok_o, dwq_o, dw4_o, dg_o,
    G, X1, h2a, yr, dr, ur, acc, hidT, daT, duT, dya, dX1, dxo, dsend, datt, delta,
    dq, dk, dv, dqkvT, Hs, Hi, Hx, Rb, Ra, Z, give, Wp, Wc, Wb, Wa, gz,
    ld, y_s, y_r, h_s, h_r, d_s, d_r, u_s, u_r, e_s, e_r, t_s, t_r,
    b_s, b_r, a_s, a_r, zu_s, zd_s, z_r, fin_s, fin_r,
    hu_s, hd_s, hi_r, hx_r, wc_s, wc_r, wb_s, wb_r, wa_s, wa_r, gz_s, gz_r,
):
    dp, z, c, x, y = place()
    bits = (c, x, y)
    core = flip(dp, bits, 1)
    px, py = flip(dp, bits, 2), flip(dp, bits, 4)
    a = (1 - c) * px + c * py
    b = (1 - c) * py + c * px
    chip, chip_a, chip_b = lax.div(dp, 2), lax.div(a, 2), lax.div(b, 2)
    chip_d = 3 - chip
    home = lax.div(z, 2)
    org = c == home
    zq = lax.rem(z, 2)
    loads = []
    for qi in range(2):
        for n, (r0, m) in enumerate(ROWS):
            cp = pltpu.make_async_copy(G_in.at[qi, pl.ds(r0, m)], G.at[qi, pl.ds(r0, m)], ld.at[qi, n])
            cp.start()
            loads.append(cp)
    greet(dp, z, bits)
    own = cols(c * 256, 256)
    other = cols((1 - c) * 256, 256)
    gain1, gain2 = gain_row(gains, 0), gain_row(gains, 1)

    def w_rows(qi, m):
        r0, n = ROWS[m]
        return pl.ds(r0, n)

    loads[3].wait()
    loads[7].wait()

    def out_proj(rows):
        return sum(
            jnp.dot(
                attn2[rows, qi * 256 : (qi + 1) * 256], G[qi, w_rows(qi, 3), :], preferred_element_type=F32
            )
            for qi in range(2)
        )

    acc[...] = out_proj(other)
    y_copy = remote(acc, yr, y_s, y_r, (core, z))
    y_copy.start()
    X1[...] = tok[...].astype(F32) + out_proj(own)
    y_copy.wait()

    def chunk(r):
        return pl.ds(pl.multiple_of(r * 32, 32), 32)

    def own_chunk(r):
        return pl.ds(pl.multiple_of(c * 256 + r * 32, 32), 32)

    @pl.loop(0, 8)
    def _(r):
        x1 = X1[chunk(r), :] + yr[chunk(r), :]
        X1[chunk(r), :] = x1
        xhat, _r = norm_rows(x1)
        h2a[own_chunk(r), :] = (xhat * gain2).astype(BF)

    h_copy = remote(h2a.at[own], h2a.at[own], h_s, h_r, (core, z))
    h_copy.start()
    for n in (0, 1, 2, 4, 5, 6):
        loads[n].wait()
    h_copy.wait()

    TILES = ((0, 224), (224, 224), (448, 208))
    for r0, n in TILES:

        @pl.loop(0, 2)
        def _(qi, r0=r0, n=n):
            h2 = h2a[...]
            act = lax.dot_general(G[qi, pl.ds(r0, n), :], h2, NT, preferred_element_type=F32)
            up = lax.dot_general(G[qi, pl.ds(HID + r0, n), :], h2, NT, preferred_element_type=F32)
            dh = lax.dot_general(G[qi, pl.ds(2 * HID + r0, n), :], cot2[...], NT, preferred_element_type=F32)
            Phi = 0.5 + 0.5 * lax.erf(act * INV_SQRT2)
            phi = jnp.exp(-0.5 * act * act) * INV_SQRT_2PI
            gel = act * Phi
            rr = pl.ds(r0, n)
            hidT[qi, rr, :] = (gel * up).astype(BF)
            daT[qi, rr, :] = (dh * up * (Phi + act * phi)).astype(BF)
            duT[qi, rr, :] = (dh * gel).astype(BF)

    def tn(lhs, rhs):
        return lax.dot_general(lhs, rhs, TN, preferred_element_type=F32)

    def d_norm(dst, rows):
        for half in range(2):
            hc = slice(half * 512, half * 512 + 512)
            dst[:, hc] = sum(
                tn(daT[qi, :, rows], G[qi, w_rows(qi, 0), hc]) + tn(duT[qi, :, rows], G[qi, w_rows(qi, 1), hc])
                for qi in range(2)
            )

    def mlp_out(dst, rows, plus=None):
        for half in range(2):
            hc = slice(half * 512, half * 512 + 512)
            r = sum(tn(hidT[qi, :, rows], G[qi, w_rows(qi, 2), hc]) for qi in range(2))
            dst[:, hc] = r if plus is None else r + plus[:, hc]

    def grads(qi, m):
        lhs, rhs = ((daT, h2a), (duT, h2a), (hidT, cot2))[m]

        @pl.loop(0, 4)
        def _(t):
            tc = cols(t * 256, 256)
            G[qi, w_rows(qi, m), tc] = jnp.dot(lhs[qi], rhs[:, tc], preferred_element_type=F32).astype(BF)

    def part(qi, m, where):
        return G.at[qi, w_rows(qi, m), cols(where * 256, 256)]

    def unit_b(e, slot):
        qi, m = UNITS[e]
        where = chip_b if slot == 0 else chip_d
        return remote(part(qi, m, where), Rb.at[slot, qi, w_rows(qi, m)], b_s.at[slot, e], b_r.at[slot, e], (b, z))

    def unit_a(e):
        qi, m = UNITS[e]
        return remote(part(qi, m, chip_a), Ra.at[qi, w_rows(qi, m)], a_s.at[e], a_r.at[e], (a, z))

    def send_b(e):
        unit_b(e, 1).start()
        unit_b(e, 0).start()

    def stage1(e):
        qi, m = UNITS[e]
        unit_b(e, 1).wait_recv()
        ref = part(qi, m, chip_a)
        ref[...] = (ref[...].astype(F32) + Rb[1, qi, w_rows(qi, m), :].astype(F32)).astype(BF)
        unit_a(e).start()

    def line_up(e, slot):
        qi, m = UNITS[e]
        return remote(part(qi, m, chip), Z.at[slot, w_rows(qi, m)], zu_s.at[e], z_r.at[slot, e], (dp, z + 1))

    def line_down(e):
        qi, m = UNITS[e]
        return remote(part(qi, m, chip), Z.at[qi, w_rows(qi, m)], zd_s.at[e], z_r.at[qi, e], (dp, z - 1))

    def target(e):
        return 2 * c + UNITS[e][0]

    def inward(e):
        qi = UNITS[e][0]
        t = target(e)
        pl.when(z > t)(lambda: line_down(e).start())
        pl.when(z + 1 == t)(lambda: line_up(e, 2).start())
        pl.when(z + 1 < t)(lambda: line_up(e, qi).start())

    def stage2(e):
        qi, m = UNITS[e]
        unit_b(e, 0).wait_recv()
        unit_a(e).wait_recv()
        rows = w_rows(qi, m)
        ref = part(qi, m, chip)
        ref[...] = (ref[...].astype(F32) + Rb[0, qi, rows, :].astype(F32) + Ra[qi, rows, :].astype(F32)).astype(BF)
        t = target(e)
        pl.when(((z == 3) & (z > t)) | ((z == 0) & (z < t)))(lambda: inward(e))

    def line_wait(e, slot):
        qi, m = UNITS[e]
        ref = Z.at[slot, w_rows(qi, m)]
        remote(ref, ref, zu_s.at[e], z_r.at[slot, e], (core, z)).wait_recv()

    def stage3(e, depth):
        qi, m = UNITS[e]
        t = target(e)
        mid = ((z > t) & (z == 3 - depth)) | ((z < t) & (z == depth))

        @pl.when(mid)
        def _():
            line_wait(e, qi)
            ref = part(qi, m, chip)
            ref[...] = (ref[...].astype(F32) + Z[qi, w_rows(qi, m), :].astype(F32)).astype(BF)
            inward(e)


    def stage4(e):
        qi, m = UNITS[e]
        t = target(e)
        rows = w_rows(qi, m)

        @pl.when(z == t)
        def _():
            dst = dw4_o.at[rows]
            gift = give.at[rows]
            dst[...] = G[qi, rows, cols(dp * 128, 128)].astype(F32)
            gift[...] = G[qi, rows, cols(core * 128, 128)].astype(F32)

            def take(slot):
                line_wait(e, slot)
                for who, ref in ((c, dst), (1 - c, gift)):
                    ref[...] = ref[...] + Z[slot, rows, cols(who * 128, 128)].astype(F32)

            pl.when(z < 3)(lambda: take(qi))
            pl.when(z > 0)(lambda: take(2))
            remote(gift, dst, fin_s.at[m], fin_r.at[m], (core, z)).start()

    d_norm(acc, other)
    d_copy = remote(acc, dr, d_s, d_r, (core, z))
    d_copy.start()
    mlp_out(dxo, other)
    u_copy = remote(dxo, ur, u_s, u_r, (core, z))
    u_copy.start()
    d_norm(dX1, own)
    mlp_out(dtok_o, own, X1)
    for e in range(2):
        grads(*UNITS[e])
        send_b(e)
    d_copy.wait()

    @pl.loop(0, 8)
    def _(r):
        dh2 = dX1[chunk(r), :] + dr[chunk(r), :]
        xhat, rstd = norm_rows(X1[chunk(r), :])
        e2 = dh2 * gain2
        m1 = jnp.mean(e2, axis=-1, keepdims=True)
        m2 = jnp.mean(e2 * xhat, axis=-1, keepdims=True)
        dx = cot2[own_chunk(r), :].astype(F32) + rstd * (e2 - m1 - xhat * m2)
        dX1[chunk(r), :] = dx
        dya[own_chunk(r), :] = dx.astype(BF)

    e_copy = remote(dya.at[own], dya.at[own], e_s, e_r, (core, z))
    e_copy.start()
    grads(*UNITS[2])
    send_b(2)
    e_copy.wait()
    for qi in range(2):
        dsend[qi] = lax.dot_general(dya[...], G[qi, w_rows(qi, 3), :], NT, preferred_element_type=F32).astype(BF)

    def att_back(c0, qi):
        dst = datt.at[cols(z * 256, 256)]
        return remote(
            dsend.at[qi, pl.ds(c0 * 256, 256)], dst, t_s.at[c0, qi], t_r.at[z], (2 * chip + c0, 2 * c + qi)
        )

    def is_self(c0, qi):
        return (c == c0) & (z == 2 * c + qi)

    for c0 in range(2):
        for qi in range(2):
            pl.when(jnp.logical_not(is_self(c0, qi)))(lambda c0=c0, qi=qi: att_back(c0, qi).start())

            @pl.when(is_self(c0, qi))
            def _(c0=c0, qi=qi):
                datt[cols(z * 256, 256), :] = dsend[qi, c0 * 256 : (c0 + 1) * 256, :]

    for e in range(3, 6):
        grads(*UNITS[e])
        send_b(e)
    for e in (6, 7):
        qi = UNITS[e][0]

        @pl.loop(0, 4)
        def _(t, qi=qi):
            tc = cols(t * 256, 256)
            G[qi, w_rows(qi, 3), tc] = tn(attn2[:, qi * 256 : (qi + 1) * 256], dya[:, tc]).astype(BF)

        send_b(e)
    u_copy.wait()
    out_o[...] = (dtok_o[...] + ur[...]).astype(BF)
    dq[...] = jnp.zeros_like(dq)
    dk[...] = jnp.zeros_like(dk)
    dv[...] = jnp.zeros_like(dv)
    for i in range(4):

        @pl.when(jnp.logical_not(org & (z == i)))
        def _(i=i):
            ref = datt.at[pl.ds(i * 256, 256)]
            remote(ref, ref, t_s.at[0, 0], t_r.at[i], (core, z)).wait_recv()

    @pl.loop(0, 4)
    def _(i):
        rows = pl.ds(pl.multiple_of(i * 256, 256), 256)
        t = (datt[rows, :].astype(F32) * att[rows, :].astype(F32)).T
        for h in range(4):
            s = jnp.sum(t[h * 64 : (h + 1) * 64, :], axis=0, keepdims=True)
            delta[h, i] = jnp.broadcast_to(s, (8, 256))

    head_of = lax.div(lax.broadcasted_iota(jnp.int32, (256, 256), 1), HEAD_DIM)

    def block_order(l):
        return jnp.minimum(l, 1) * (lax.rem(l + 1, 3) + 1)

    def pair(i, j):
        ri = pl.ds(pl.multiple_of(i * 256, 256), 256)
        rj = pl.ds(pl.multiple_of(j * 256, 256), 256)

        @pl.loop(0, 4)
        def _(h):
            mine = head_of == h
            kj, vj = k[rj, :], v[rj, :]
            qh = jnp.where(mine, q[ri, :], jnp.zeros((), BF))
            dah = jnp.where(mine, datt[ri, :], jnp.zeros((), BF))
            s = lax.dot_general(kj, qh, NT, preferred_element_type=F32)
            seg_k = segc[rj, :]
            same = jnp.concatenate([seg_k, seg_k], axis=1) == segr[0:1, ri]
            p = jnp.exp(jnp.where(same, s, masked_fill) - lse[h, i, 0:1, :])
            dp_ = lax.dot_general(vj, dah, NT, preferred_element_type=F32)
            dsc = (p * (dp_ - delta[h, i, 0:1, :])).astype(BF)
            dv[rj, :] = dv[rj, :] + jnp.dot(p.astype(BF), dah, preferred_element_type=F32)
            dk[rj, :] = dk[rj, :] + jnp.dot(dsc, qh, preferred_element_type=F32)
            dq[ri, :] = dq[ri, :] + jnp.where(mine, tn(dsc, kj), 0.0)

    def h_up(i, last):
        if last:
            return remote(Hs.at[i], Hx, hu_s.at[i], hx_r, (dp, z + 1))
        return remote(Hs.at[i], Hi.at[i], hu_s.at[i], hi_r.at[i], (dp, z + 1))

    def h_down(i):
        return remote(Hs.at[i], Hi.at[i], hd_s.at[i], hi_r.at[i], (dp, z - 1))

    def h_inward(i, act):
        pl.when(z > i)(lambda: act(h_down(i)))
        pl.when(z + 1 == i)(lambda: act(h_up(i, True)))
        pl.when(z + 1 < i)(lambda: act(h_up(i, False)))

    def begin(cp):
        cp.start()

    def h_wait(i):
        remote(Hi.at[i], Hi.at[i], hd_s.at[i], hi_r.at[i], (core, z)).wait_recv()

    def h_mid(i, depth):
        mid = ((z > i) & (z == 3 - depth)) | ((z < i) & (z == depth))

        @pl.when(mid)
        def _():
            h_wait(i)
            Hs[i] = (Hs[i].astype(F32) + Hi[i].astype(F32)).astype(BF)
            h_inward(i, begin)

    def finish(i):
        rows = pl.ds(pl.multiple_of(i * 256, 256), 256)
        cb, sb = cs[rows, :], -sn[rows, :]
        low = (
            turn(dq[rows, :] * (HEAD_DIM**-0.5), cb, sb).astype(BF),
            turn(dk[rows, :], cb, sb).astype(BF),
            dv[rows, :].astype(BF),
        )
        for p in range(3):
            dqkvT[p * 256 : (p + 1) * 256, rows] = low[p].T
        for half in range(2):
            hc = slice(half * 512, half * 512 + 512)
            dh = sum(
                lax.dot_general(low[p], wq[p, hc, :], NT, preferred_element_type=F32) for p in range(3)
            )
            Hs[i, :, hc] = dh.astype(BF)

            @pl.when(z == i)
            def _(dh=dh, hc=hc):
                acc[:, hc] = dh

        pl.when(((z == 3) & (z > i)) | ((z == 0) & (z < i)))(lambda: h_inward(i, begin))

    def tick(t):
        if t < 8:
            stage1(t)
        if 0 <= t - 1 < 8:
            stage2(t - 1)
        if 0 <= t - 2 < 8:
            stage3(t - 2, 1)
        if 0 <= t - 3 < 8:
            stage3(t - 3, 2)
        if 0 <= t - 4 < 8:
            stage4(t - 4)

    slots = {2: [lambda: tick(0)], 6: [lambda: tick(1)], 9: [lambda: tick(2)], 13: [lambda: tick(3)],
             11: [lambda: h_mid(0, 1)], 14: [lambda: h_mid(0, 2), lambda: h_mid(3, 1)]}

    @pl.loop(0, 16)
    def _(n):
        def past(v):
            return lax.div(n + 16 - v, 16)

        ph = past(7) + past(12) + past(15)
        t = n - 7 * past(7) - 5 * past(12) - 3 * past(15)
        left = 4 - ph
        over = lax.div(t, left)
        li = ph + over * (t - left + 1)
        lj = ph + (1 - over) * t
        pair(block_order(li), block_order(lj))
        pl.when((n == 6) | (n == 11) | (n == 14) | (n == 15))(lambda: finish(block_order(ph)))
        for s, ops in slots.items():

            @pl.when(n == s)
            def _(ops=ops):
                for op in ops:
                    op()

    @pl.loop(0, 4)
    def _(t):
        tc = cols(t * 256, 256)
        Wp[:, tc] = jnp.dot(dqkvT[...], h1[:, tc], preferred_element_type=F32).astype(BF)

    def core_copy(w):
        return remote(
            Wp.at[:, cols(w * 256 + (1 - c) * 128, 128)], Wc.at[w], wc_s.at[w], wc_r.at[w], (core, z)
        )

    for w in range(4):
        core_copy(w).start()
    h_mid(3, 2)
    h_mid(1, 1)
    h_mid(2, 1)

    def both(w):
        Wc[w] = (Wc[w].astype(F32) + Wp[:, cols(w * 256 + c * 128, 128)].astype(F32)).astype(BF)

    for w in range(4):
        core_copy(w).wait_recv()
    both(chip_d)
    both(chip_b)
    wb_copy = [
        remote(Wc.at[where], Wb.at[slot], wb_s.at[slot], wb_r.at[slot], (b, z))
        for slot, where in ((0, chip_b), (1, chip_d))
    ]
    wb_copy[1].start()
    wb_copy[0].start()
    both(chip_a)
    both(chip)
    wa_copy = remote(Wc.at[chip_a], Wa, wa_s, wa_r, (a, z))
    tick(4)
    wb_copy[1].wait_recv()
    Wc[chip_a] = (Wc[chip_a].astype(F32) + Wb[1].astype(F32)).astype(BF)
    wa_copy.start()
    tick(5)

    pl.when(z < 3)(lambda: h_wait(z))
    pl.when(z > 0)(lambda: remote(Hx, Hx, hu_s.at[0], hx_r, (core, z)).wait_recv())
    has_above, has_below = z < 3, z > 0

    @pl.when(has_above)
    def _():
        acc[...] = acc[...] + Hi[z].astype(F32)

    @pl.when(has_below)
    def _():
        acc[...] = acc[...] + Hx[...].astype(F32)

    @pl.loop(0, 8)
    def _(r):
        xhat, rstd = norm_rows(tok[chunk(r), :].astype(F32))
        e1 = acc[chunk(r), :] * gain1
        m1 = jnp.mean(e1, axis=-1, keepdims=True)
        m2 = jnp.mean(e1 * xhat, axis=-1, keepdims=True)
        dtok_o[chunk(r), :] = dX1[chunk(r), :] + rstd * (e1 - m1 - xhat * m2)

    wb_copy[0].wait_recv()
    wa_copy.wait_recv()
    total = Wc[chip].astype(F32) + Wb[0].astype(F32) + Wa[...].astype(F32)
    dot_one = jnp.zeros((1, 128), F32)
    for p in range(3):
        piece = total[p * 256 : (p + 1) * 256, :]
        dwq_o[p] = piece.T
        dot_one = dot_one + jnp.sum(piece * wqkv[p].T.astype(F32), axis=0, keepdims=True)
    for t in range(6, 12):
        tick(t)
    for m in range(4):

        @pl.when(jnp.logical_not(org))
        def _(m=m):
            ref = dw4_o.at[w_rows(0, m)]
            remote(ref, ref, fin_s.at[m], fin_r.at[m], (core, z)).wait_recv()

    part_two = jnp.sum(dw4_o[0 : 2 * HID, :] * w4[0 : 2 * HID, :].astype(F32), axis=0, keepdims=True)
    gz[z, 0:1, :] = dot_one / gains[dp, 0:1, :]
    gz[z, 1:2, :] = part_two / gains[dp, 1:2, :]
    gz[z, 2:8, :] = jnp.zeros((6, 128), F32)
    gain_copy = [
        remote(gz.at[z], gz.at[z], gz_s.at[n], gz_r.at[z], (dp, lax.rem(z + n, 4))) for n in range(1, 4)
    ]
    for cp in gain_copy:
        cp.start()
    for n in range(1, 4):
        o = lax.rem(z + n, 4)
        remote(gz.at[o], gz.at[o], gz_s.at[n], gz_r.at[o], (core, z)).wait_recv()
    dg_o[...] = gz[0] + gz[1] + gz[2] + gz[3]

    for cp in gain_copy:
        cp.wait_send()
    for w in range(4):
        core_copy(w).wait_send()
    wb_copy[0].wait_send()
    wb_copy[1].wait_send()
    wa_copy.wait_send()
    for i in range(4):
        h_inward(i, lambda cp: cp.wait_send())
    for c0 in range(2):
        for qi in range(2):
            pl.when(jnp.logical_not(is_self(c0, qi)))(lambda c0=c0, qi=qi: att_back(c0, qi).wait_send())
    for e in range(8):
        qi, m = UNITS[e]
        unit_b(e, 0).wait_send()
        unit_b(e, 1).wait_send()
        unit_a(e).wait_send()
        t = target(e)
        pl.when(z > t)(lambda e=e: line_down(e).wait_send())
        pl.when(z + 1 == t)(lambda e=e: line_up(e, 2).wait_send())
        pl.when(z + 1 < t)(lambda e=e, qi=qi: line_up(e, qi).wait_send())

        @pl.when(z == t)
        def _(m=m):
            rows = w_rows(0, m)
            remote(give.at[rows], dw4_o.at[rows], fin_s.at[m], fin_r.at[m], (core, z)).wait_send()


def run_backward(*args):
    V = pl.BlockSpec(memory_space=pltpu.VMEM)
    A = pl.BlockSpec(memory_space=pl.ANY)
    dma = pltpu.SemaphoreType.DMA
    s = jax.ShapeDtypeStruct
    vm = pltpu.VMEM
    return pl.pallas_call(
        backward_kernel,
        out_shape=(
            s((256, 1024), BF), s((256, 1024), F32), s((3, 128, 256), F32), s((PACK, 128), F32), s((8, 128), F32),
        ),
        in_specs=[V] * 8 + [A] + [V] * 9,
        out_specs=[V] * 5,
        scratch_shapes=[
            vm((2, PACK, 1024), BF), vm((256, 1024), F32), vm((512, 1024), BF), vm((256, 1024), F32),
            vm((256, 1024), F32), vm((256, 1024), F32), vm((256, 1024), F32), vm((2, HID, 512), BF),
            vm((2, HID, 512), BF), vm((2, HID, 512), BF), vm((512, 1024), BF), vm((256, 1024), F32),
            vm((256, 1024), F32), vm((2, 512, 256), BF), vm((1024, 256), BF), vm((4, 4, 8, 256), F32),
            vm((1024, 256), F32), vm((1024, 256), F32), vm((1024, 256), F32), vm((768, 1024), BF),
            vm((4, 256, 1024), BF), vm((4, 256, 1024), BF), vm((256, 1024), BF), vm((2, 2, PACK, 256), BF),
            vm((2, PACK, 256), BF), vm((3, PACK, 256), BF), vm((PACK, 128), F32), vm((768, 1024), BF),
            vm((4, 768, 128), BF), vm((2, 768, 128), BF), vm((768, 128), BF), vm((4, 8, 128), F32),
            dma((2, 4)), dma, dma, dma, dma, dma, dma, dma, dma, dma, dma, dma((2, 2)), dma((4,)),
            dma((2, 8)), dma((2, 8)), dma((8,)), dma((8,)), dma((8,)), dma((8,)), dma((3, 8)),
            dma((4,)), dma((4,)), dma((4,)), dma((4,)), dma((4,)), dma,
            dma((4,)), dma((4,)), dma((2,)), dma((2,)), dma, dma, dma((4,)), dma((4,)),
        ],
        compiler_params=pltpu.CompilerParams(
            collective_id=2, has_side_effects=True, vmem_limit_bytes=62 << 20
        ),
        name="feed_forward_backward",
    )(*args)


def local_fast(
    tokens, lengths, seq_order, gain_attn, w_qkv, w_attn_out, gain_mlp, w_in, w_mlp_out, cotangent
):
    w4, gains, cs, sn, segc, segr = prepare(
        lengths, seq_order, gain_attn, w_attn_out, gain_mlp, w_in, w_mlp_out
    )
    q, k, v, lse, att, attn2, h1, wq, packed, all_gains, cot2 = run_forward(
        tokens, w_qkv, w4, gains, cs, sn, segc, segr, cotangent
    )
    out, d_tok, d_qkv, d_pack, d_gain = run_backward(
        q, k, v, lse, att, attn2, h1, wq, packed, all_gains, cot2, tokens, cs, sn, segc, segr, w_qkv, w4
    )
    d_in = d_pack[: 2 * HID].reshape(2, HID, 128).transpose(2, 0, 1)
    return (
        out, d_tok, d_gain[0], d_qkv, d_pack[3 * HID :], d_gain[1], d_in, d_pack[2 * HID : 3 * HID],
    )


def layer_norm(field_in, norm_gain):
    row_mean = jnp.mean(field_in, axis=-1, keepdims=True)
    centered = field_in - row_mean
    variance = jnp.mean(centered * centered, axis=-1, keepdims=True)
    return centered * lax.rsqrt(variance + norm_eps) * norm_gain


def rotate(field_in, position):
    half_size = field_in.shape[-1] // 2
    index_range = jnp.arange(half_size, dtype=jnp.float32)
    frequency = rope_base ** (-2.0 * index_range / field_in.shape[-1])
    angles = position[:, None] * frequency[None, :]
    cosine = jnp.cos(angles)[:, None, :]
    sine_part = jnp.sin(angles)[:, None, :]
    first_half = field_in[..., :half_size]
    second_half = field_in[..., half_size:]
    return jnp.concatenate(
        [
            first_half * cosine - second_half * sine_part,
            second_half * cosine + first_half * sine_part,
        ],
        axis=-1,
    )


def geglu(act_part, up_part):
    return jax.nn.gelu(act_part, approximate=False) * up_part


def item_layout(array_in, block_rows):
    group_rows, head_count, head_size = array_in.shape
    block_count = group_rows // block_rows
    shaped = array_in.reshape(block_count, block_rows, head_count, head_size)
    return shaped.transpose(2, 0, 1, 3).reshape(head_count * block_count, block_rows, head_size)


def from_items(items, group_rows):
    item_count, block_rows, head_size = items.shape
    block_count = group_rows // block_rows
    head_count = item_count // block_count
    shaped = items.reshape(head_count, block_count, block_rows, head_size)
    return shaped.transpose(1, 2, 0, 3).reshape(group_rows, head_count, head_size)


def masked_scores(query_block, key_head, segment_block, segment):
    score_scale = query_block.shape[-1] ** (-0.5)
    raw_scores = lax.dot_general(
        query_block, key_head, (((1,), (1,)), ((), ())), preferred_element_type=jnp.float32
    )
    allowed = segment_block[:, None] == segment[None, :]
    return jnp.where(allowed, raw_scores * score_scale, masked_fill)


def attend_forward(query_rot, key_rot, value_low, segment, block_rows):
    group_rows, head_count, head_size = query_rot.shape
    block_count = group_rows // block_rows
    query_items = item_layout(query_rot, block_rows)
    key_heads = key_rot.transpose(1, 0, 2)
    value_heads = value_low.transpose(1, 0, 2)
    segment_blocks = segment.reshape(block_count, block_rows)

    def one_item(item_index):
        head_index = item_index // block_count
        block_index = item_index % block_count
        query_block = lax.dynamic_index_in_dim(query_items, item_index, 0, False)
        key_head = lax.dynamic_index_in_dim(key_heads, head_index, 0, False)
        value_head = lax.dynamic_index_in_dim(value_heads, head_index, 0, False)
        segment_block = lax.dynamic_index_in_dim(segment_blocks, block_index, 0, False)
        scores = masked_scores(query_block, key_head, segment_block, segment)
        row_top = jnp.max(scores, axis=1, keepdims=True)
        weights = jnp.exp(scores - row_top)
        row_total = jnp.sum(weights, axis=1, keepdims=True)
        probs_low = (weights / row_total).astype(jnp.bfloat16)
        result = jnp.dot(probs_low, value_head, preferred_element_type=jnp.float32)
        return (result, row_top[:, 0] + jnp.log(row_total[:, 0]))

    results, log_totals = lax.map(one_item, jnp.arange(head_count * block_count, dtype=jnp.int32))
    return (from_items(results, group_rows), log_totals)


def attend_backward(query_rot, key_rot, value_low, grad_out, log_totals, segment, block_rows):
    group_rows, head_count, head_size = query_rot.shape
    block_count = group_rows // block_rows
    score_scale = head_size ** (-0.5)
    query_items = item_layout(query_rot, block_rows)
    grad_items = item_layout(grad_out, block_rows)
    key_heads = key_rot.transpose(1, 0, 2)
    value_heads = value_low.transpose(1, 0, 2)
    segment_blocks = segment.reshape(block_count, block_rows)

    def one_item(carried, item_index):
        key_grads, value_grads = carried
        head_index = item_index // block_count
        block_index = item_index % block_count
        query_block = lax.dynamic_index_in_dim(query_items, item_index, 0, False)
        grad_block = lax.dynamic_index_in_dim(grad_items, item_index, 0, False)
        log_row = lax.dynamic_index_in_dim(log_totals, item_index, 0, False)
        key_head = lax.dynamic_index_in_dim(key_heads, head_index, 0, False)
        value_head = lax.dynamic_index_in_dim(value_heads, head_index, 0, False)
        segment_block = lax.dynamic_index_in_dim(segment_blocks, block_index, 0, False)
        scores = masked_scores(query_block, key_head, segment_block, segment)
        prob_full = jnp.exp(scores - log_row[:, None])
        probs_low = prob_full.astype(jnp.bfloat16)
        grad_probs = lax.dot_general(
            grad_block, value_head, (((1,), (1,)), ((), ())), preferred_element_type=jnp.float32
        )
        row_delta = jnp.sum(prob_full * grad_probs, axis=1, keepdims=True)
        grad_scores = (prob_full * (grad_probs - row_delta)).astype(jnp.bfloat16)
        grad_query = (
            jnp.dot(grad_scores, key_head, preferred_element_type=jnp.float32) * score_scale
        )
        grad_key = (
            lax.dot_general(
                grad_scores,
                query_block,
                (((0,), (0,)), ((), ())),
                preferred_element_type=jnp.float32,
            )
            * score_scale
        )
        grad_value = lax.dot_general(
            probs_low, grad_block, (((0,), (0,)), ((), ())), preferred_element_type=jnp.float32
        )
        key_grads = lax.dynamic_update_index_in_dim(
            key_grads,
            lax.dynamic_index_in_dim(key_grads, head_index, 0, False) + grad_key,
            head_index,
            0,
        )
        value_grads = lax.dynamic_update_index_in_dim(
            value_grads,
            lax.dynamic_index_in_dim(value_grads, head_index, 0, False) + grad_value,
            head_index,
            0,
        )
        return ((key_grads, value_grads), grad_query)

    zero_heads = jnp.zeros((head_count, group_rows, head_size), jnp.float32)
    (key_grads, value_grads), query_grads = lax.scan(
        one_item, (zero_heads, zero_heads), jnp.arange(head_count * block_count, dtype=jnp.int32)
    )
    return (
        from_items(query_grads, group_rows),
        key_grads.transpose(1, 0, 2),
        value_grads.transpose(1, 0, 2),
    )


def spread_rows(local_rows):
    return lax.all_gather(local_rows, "tensor", axis=0, tiled=True)


def spread_grads(local_grads):
    return lax.all_gather(local_grads, "tensor", axis=0, tiled=True)


def sum_heads(activations, weight_part, row_count):

    def row_term(first_row, row_number):
        return jnp.dot(activations, weight_part, preferred_element_type=jnp.float32)

    return lax.psum_scatter(
        row_term(jnp.int32(0), row_count * lax.axis_size("tensor")),
        "tensor",
        scatter_dimension=0,
        tiled=True,
    )


def sum_grads(grads_low, weight_full, einsum_form, row_count):

    def row_term(first_row, row_number):
        return jnp.einsum(einsum_form, grads_low, weight_full, preferred_element_type=jnp.float32)

    return lax.psum_scatter(
        row_term(jnp.int32(0), row_count * lax.axis_size("tensor")),
        "tensor",
        scatter_dimension=0,
        tiled=True,
    )


def local_plain(
    tokens, lengths, seq_order, gain_attn, w_qkv, w_attn_out, gain_mlp, w_in, w_mlp_out, cotangent
):
    row_count = tokens.shape[0]
    group_rows = row_count * lax.axis_size("tensor")
    block_rows = min(512, group_rows)
    segment, position = layout(lengths, seq_order, group_rows)
    gain_low_one, qkv_weight, out_weight, gain_low_two, in_weight, down_weight = (
        lax.all_gather(gain_attn, "dp", axis=0, tiled=True),
        lax.all_gather(w_qkv, "dp", axis=1, tiled=True),
        lax.all_gather(w_attn_out, "dp", axis=1, tiled=True),
        lax.all_gather(gain_mlp, "dp", axis=0, tiled=True),
        lax.all_gather(w_in, "dp", axis=0, tiled=True),
        lax.all_gather(w_mlp_out, "dp", axis=1, tiled=True),
    )
    gain_one = gain_low_one.astype(jnp.float32)
    gain_two = gain_low_two.astype(jnp.float32)
    residual = tokens.astype(jnp.float32)
    normed_one = spread_rows(layer_norm(residual, gain_one).astype(jnp.bfloat16))
    qkv = jnp.einsum("rd,pdc->rpc", normed_one, qkv_weight, preferred_element_type=jnp.float32)
    head_count = qkv.shape[2] // HEAD_DIM
    head_shape = (group_rows, head_count, HEAD_DIM)
    query_rot = rotate(qkv[:, 0].reshape(head_shape), position).astype(jnp.bfloat16)
    key_rot = rotate(qkv[:, 1].reshape(head_shape), position).astype(jnp.bfloat16)
    value_low = qkv[:, 2].reshape(head_shape).astype(jnp.bfloat16)
    attended, log_totals = attend_forward(query_rot, key_rot, value_low, segment, block_rows)
    attn_low = attended.reshape(group_rows, head_count * HEAD_DIM).astype(jnp.bfloat16)
    resid_mid = residual + sum_heads(attn_low, out_weight, row_count)
    normed_two = spread_rows(layer_norm(resid_mid, gain_two).astype(jnp.bfloat16))
    gate_up = jnp.einsum("rd,dpc->rpc", normed_two, in_weight, preferred_element_type=jnp.float32)
    hidden = geglu(gate_up[:, 0], gate_up[:, 1]).astype(jnp.bfloat16)
    output = (resid_mid + sum_heads(hidden, down_weight, row_count)).astype(jnp.bfloat16)
    grad_two = spread_grads(cotangent)
    d_hidden = lax.dot_general(
        grad_two, down_weight, (((1,), (1,)), ((), ())), preferred_element_type=jnp.float32
    )
    d_down = lax.dot_general(
        hidden, grad_two, (((0,), (0,)), ((), ())), preferred_element_type=jnp.float32
    )
    geglu_pull = jax.vjp(geglu, gate_up[:, 0], gate_up[:, 1])[1]
    d_act, d_up = geglu_pull(d_hidden)
    d_gate_up = jnp.stack([d_act, d_up], axis=1).astype(jnp.bfloat16)
    d_in = jnp.einsum("rd,rpc->dpc", normed_two, d_gate_up, preferred_element_type=jnp.float32)
    d_normed_two = sum_grads(d_gate_up, in_weight, "rpc,dpc->rd", row_count)
    norm_pull_two = jax.vjp(layer_norm, resid_mid, gain_two)[1]
    d_mid_norm, d_gain_two = norm_pull_two(d_normed_two)
    d_mid = cotangent.astype(jnp.float32) + d_mid_norm
    grad_one = spread_grads(d_mid.astype(jnp.bfloat16))
    d_out = lax.dot_general(
        attn_low, grad_one, (((0,), (0,)), ((), ())), preferred_element_type=jnp.float32
    )
    d_att = lax.dot_general(
        grad_one, out_weight, (((1,), (1,)), ((), ())), preferred_element_type=jnp.float32
    ).astype(jnp.bfloat16)
    d_query_rot, d_key_rot, d_value = attend_backward(
        query_rot, key_rot, value_low, d_att.reshape(head_shape), log_totals, segment, block_rows
    )
    rotate_pull = jax.vjp(lambda field_in: rotate(field_in, position), d_query_rot)[1]
    d_query = rotate_pull(d_query_rot)[0]
    d_key = rotate_pull(d_key_rot)[0]
    flat_shape = (group_rows, head_count * HEAD_DIM)
    d_qkv = jnp.stack(
        [d_query.reshape(flat_shape), d_key.reshape(flat_shape), d_value.reshape(flat_shape)],
        axis=1,
    ).astype(jnp.bfloat16)
    d_qkv_weight = jnp.einsum("rd,rpc->pdc", normed_one, d_qkv, preferred_element_type=jnp.float32)
    d_normed_one = sum_grads(d_qkv, qkv_weight, "rpc,pdc->rd", row_count)
    norm_pull_one = jax.vjp(layer_norm, residual, gain_one)[1]
    d_first, d_gain_one = norm_pull_one(d_normed_one)
    d_tokens = d_mid + d_first
    gain_sums = lax.psum((d_gain_one, d_gain_two), "tensor")
    shares = (
        lax.psum_scatter(gain_sums[0], "dp", scatter_dimension=0, tiled=True),
        lax.psum_scatter(d_qkv_weight, "dp", scatter_dimension=1, tiled=True),
        lax.psum_scatter(d_out, "dp", scatter_dimension=1, tiled=True),
        lax.psum_scatter(gain_sums[1], "dp", scatter_dimension=0, tiled=True),
        lax.psum_scatter(d_in, "dp", scatter_dimension=0, tiled=True),
        lax.psum_scatter(d_down, "dp", scatter_dimension=1, tiled=True),
    )
    return (output, d_tokens, shares[0], shares[1], shares[2], shares[3], shares[4], shares[5])


def solution(mesh):
    fast = mesh.shape["dp"] == 8 and mesh.shape["tensor"] == 4
    return jax.shard_map(
        local_fast if fast else local_plain,
        mesh=mesh,
        in_specs=(
            P(("dp", "tensor"), None),
            P(),
            P(),
            P("dp"),
            P(None, "dp", "tensor"),
            P("tensor", "dp"),
            P("dp"),
            P("dp", None, "tensor"),
            P("tensor", "dp"),
            P(("dp", "tensor"), None),
        ),
        out_specs=(
            P(("dp", "tensor"), None),
            P(("dp", "tensor"), None),
            P("dp"),
            P(None, "dp", "tensor"),
            P("tensor", "dp"),
            P("dp"),
            P("dp", None, "tensor"),
            P("tensor", "dp"),
        ),
        check_vma=False,
    )
```

```python
import functools

import jax
import jax.numpy as jnp
from jax import lax
from jax.experimental import pallas as pl
from jax.experimental.pallas import tpu as pltpu
from jax.sharding import PartitionSpec as P

HEAD_DIM = 64
SEQ_GRP = 4
rope_base = 160000.0
norm_eps = 1e-05
masked_fill = -1e30
MESH = pl.DeviceIdType.MESH
BF = jnp.bfloat16
F32 = jnp.float32

NT = (((1,), (1,)), ((), ()))
TN = (((0,), (0,)), ((), ()))


def place():
    dp = lax.axis_index("dp")
    z = lax.axis_index("tensor")
    c = lax.rem(dp, 2)
    x = lax.rem(lax.div(dp, 2), 2)
    y = lax.div(dp, 4)
    return dp, z, c, x, y


def flip(dp, bits, distance):
    out = dp
    for b, bit in enumerate(bits):
        if (distance >> b) & 1:
            out = out + (1 << b) - (2 << b) * bit
    return out


def remote(src, dst, send, recv, dev):
    return pltpu.make_async_remote_copy(
        src_ref=src, dst_ref=dst, send_sem=send, recv_sem=recv, device_id=dev, device_id_type=MESH
    )


def cols(start, size):
    return pl.ds(pl.multiple_of(start, size), size)


def greet(dp, z, bits):
    c = bits[0]
    barrier = pltpu.get_barrier_semaphore()
    peers = [(flip(dp, bits, d), z) for d in range(1, 8)]
    core = flip(dp, bits, 1)
    for k in range(1, 4):
        peers.append((dp, lax.rem(z + k, 4)))
        peers.append((core, lax.rem(z + k, 4)))
    for p in peers:
        pl.semaphore_signal(barrier, inc=1, device_id=p, device_id_type=MESH)
    pl.semaphore_wait(barrier, len(peers))


def norm_rows(v):
    mean = jnp.mean(v, axis=-1, keepdims=True)
    centered = v - mean
    var = jnp.mean(centered * centered, axis=-1, keepdims=True)
    rstd = lax.rsqrt(var + norm_eps)
    return centered * rstd, rstd


def turn(v, cs, sn):
    lane = lax.broadcasted_iota(jnp.int32, cs.shape, 1)
    low_half = lax.rem(lane, HEAD_DIM) < HEAD_DIM // 2
    parts = []
    for t in range(v.shape[1] // 128):
        piece = v[:, t * 128 : (t + 1) * 128]
        swapped = jnp.where(low_half, pltpu.roll(piece, 96, 1), pltpu.roll(piece, 32, 1))
        parts.append(piece * cs + swapped * sn)
    return jnp.concatenate(parts, axis=1)


def gain_row(gains, row):
    return jnp.concatenate([gains[p, row : row + 1, :] for p in range(8)], axis=1)


HID = 656
PACK = 3 * HID + 256
ROWS = ((256, HID), (256 + HID, HID), (256 + 2 * HID, HID), (0, 256))
CUTS = ((0, 544), (544, 560), (1104, 560), (1664, 560))
HALVES = tuple((m, o, n) for m in (2, 0, 1) for o, n in ((0, 336), (336, 320))) + ((3, 0, 256),)
UNITS = tuple((q, k) for q in range(2) for k in range(6)) + ((0, 6), (1, 6))
NU = len(UNITS)
INV_SQRT2 = 0.7071067811865476
INV_SQRT_2PI = 0.3989422804014327


def layer_kernel(
    lengths, seq_order, tok, wqkv, win, wmlp, wout, gains_in, cot,
    out_o, dtok_o, dwq_o, dwin_o, dwmlp_o, dwout_o, dg_o,
    gains, w4, cs, sn, segc, segr, q, k, v, lse, att, attn2, h1, wq, cot2,
    G, X1, pool, yr, dr, acc, hidT, daT, duT, dX1, dxo, dsend, datt, delta,
    dq, dk, dv, Hs, Hi, Hx, Rb, Ra, Z, give, Wp, Wc, Wb, Wa, gz,
    us, ds, rb, ra, wr_s, wr_r, wx_s, wx_r, g_s, g_r, co_s, co_r, hop_s, hop_r,
    qu_s, qd_s, q_r, pa_s, pb_s, pf_s, pa_r, pb_r, at_s, at_r,
    y_s, y_r, h_s, h_r, d_s, d_r, u_s, u_r, e_s, e_r, t_s, t_r,
    b_s, b_r, a_s, a_r, zu_s, zd_s, z_r, fin_s, fin_r,
    hu_s, hd_s, hi_r, hx_r, wc_s, wc_r, wb_s, wb_r, wa_s, wa_r, gz_s, gz_r, lc,
):
    dp, z, c, x, y = place()
    bits = (c, x, y)
    core = flip(dp, bits, 1)
    px, py = flip(dp, bits, 2), flip(dp, bits, 4)
    a = (1 - c) * px + c * py
    b = (1 - c) * py + c * px
    chip, chip_a, chip_b = lax.div(dp, 2), lax.div(a, 2), lax.div(b, 2)
    chip_d = 3 - chip
    home = lax.div(z, 2)
    org = c == home
    zq = lax.rem(z, 2)
    end = (z == 0) | (z == 3)
    own = cols(c * 256, 256)
    other = cols((1 - c) * 256, 256)
    tall, vT, ur, oT = Hs, Hx, yr, acc.at[:, 0:256]
    h2a, dya, dqkvT = pool.at[0:512], pool.at[512:1024], pool.at[0:768]
    dw4 = (dwin_o.at[0:HID], dwin_o.at[HID : 2 * HID], dwmlp_o, dwout_o)
    greet(dp, z, bits)

    def no(cond):
        return jnp.logical_not(cond)

    def tok_up(k_, h):
        ref = tall.at[z - k_, pl.ds(h * 128, 128)]
        src = tok.at[pl.ds(h * 128, 128)] if k_ == 0 else ref
        return remote(src, ref, us.at[k_, h], rb.at[k_ + 1, h], (dp, z + 1))

    def tok_down(k_, h):
        ref = tall.at[z + k_, pl.ds(h * 128, 128)]
        src = tok.at[pl.ds(h * 128, 128)] if k_ == 0 else ref
        return remote(src, ref, ds.at[k_, h], ra.at[k_ + 1, h], (dp, z - 1))

    def up_ok(k_):
        return (z >= k_) & (z < 3)

    def down_ok(k_):
        return (z + k_ <= 3) & (z > 0)

    for h in range(2):
        pl.when(up_ok(0))(lambda h=h: tok_up(0, h).start())
        pl.when(down_ok(0))(lambda h=h: tok_down(0, h).start())

    for d in range(1, 8):
        remote(gains_in, gains.at[dp], g_s.at[d], g_r.at[d], (flip(dp, bits, d), z)).start()
    own_rows = cols(dp * 128, 128)
    for j, d in enumerate((2, 4, 6)):
        remote(wqkv, wq.at[:, own_rows], wr_s.at[j], wr_r.at[j], (flip(dp, bits, d), z)).start()
    remote(wqkv, wq.at[:, own_rows], wx_s.at[3], wx_r.at[3], (core, z)).start()
    cot_copy = remote(cot, cot2.at[own], co_s, co_r, (core, z))
    cot_copy.start()
    cot_local = pltpu.make_async_copy(cot, cot2.at[own], lc)
    cot_local.start()

    w4[0:256, :] = wout[...]
    w4[256 : 256 + 2 * HID, :] = win[...]
    w4[256 + 2 * HID : PACK, :] = wmlp[...]
    mine = G.at[zq, :, cols(dp * 128, 128)]
    hop = remote(w4, mine, hop_s, hop_r, (core, z))
    pl.when(no(org))(lambda: hop.start())

    @pl.when(org)
    def _():
        G[zq, :, cols(dp * 128, 128)] = w4[...]

    gains[dp] = gains_in[...]
    wq[:, own_rows, :] = wqkv[...]
    tall[z] = tok[...]
    cot_local.wait()

    def piece(qi, u, where):
        r0, n = CUTS[u]
        return G.at[qi, pl.ds(r0, n), cols(where * 256, 256)]

    def line_send(qi, u, up, act):
        ref = piece(qi, u, chip)
        if up:
            pl.when((z >= 2 * c + qi) & (z < 3))(
                lambda: act(remote(ref, ref, qu_s.at[qi, u], q_r.at[qi, u], (dp, z + 1)))
            )
        else:
            pl.when((z <= 2 * c + qi) & (z > 0))(
                lambda: act(remote(ref, ref, qd_s.at[qi, u], q_r.at[qi, u], (dp, z - 1)))
            )

    def plane_a(qi, u):
        return remote(piece(qi, u, chip), piece(qi, u, chip), pa_s.at[qi, u], pa_r.at[qi, u], (a, z))

    def plane_b(qi, u):
        return remote(piece(qi, u, chip), piece(qi, u, chip), pb_s.at[qi, u], pb_r.at[qi, 0, u], (b, z))

    def plane_f(qi, u):
        return remote(piece(qi, u, chip_a), piece(qi, u, chip_a), pf_s.at[qi, u], pb_r.at[qi, 1, u], (b, z))

    def spread(qi, u):
        plane_a(qi, u).start()
        plane_b(qi, u).start()

    near = (1 - c) * lax.div(z + 2, 3) + c * lax.div(z, 3)
    far = 1 - near

    def begin(cp):
        cp.start()

    def arrive(qi, u):
        ref = piece(qi, u, chip)
        remote(ref, ref, qu_s.at[qi, u], q_r.at[qi, u], (core, z)).wait_recv()

    def across(qi, u):
        ref = piece(qi, u, chip_a)
        remote(ref, ref, pa_s.at[qi, u], pa_r.at[qi, u], (a, z)).wait_recv()
        plane_f(qi, u).start()

    def stage(qi, u):
        arrive(qi, u)
        line_send(qi, u, True, begin)
        line_send(qi, u, False, begin)
        spread(qi, u)

    def stage_far(u):
        stage(far, u)

    def stage_near(u):
        stage(near, u)

    ends, starts, total = [], [], 0
    for j in range(SEQ_GRP):
        ends.append(total)
        total = total + lengths[seq_order[dp * SEQ_GRP + j]]
    for dst, shape, axis in ((segc, (1024, 128), 0), (segr, (8, 1024), 1)):
        row = lax.broadcasted_iota(jnp.int32, shape, axis)
        seg = jnp.zeros(shape, F32)
        start = jnp.zeros(shape, jnp.int32)
        for j in range(1, SEQ_GRP):
            passed = row >= ends[j]
            seg = jnp.where(passed, float(j), seg)
            start = jnp.where(passed, ends[j], start)
        dst[...] = seg
        if axis == 0:
            angle = (row - start).astype(F32) * gains_in[2:3, :]
            cs[...] = jnp.cos(angle)
            sn[...] = jnp.sin(angle) * gains_in[3:4, :]

    for d in range(1, 8):
        p = flip(dp, bits, d)
        remote(gains_in, gains.at[p], g_s.at[d], g_r.at[d], (p, z)).wait_recv()

    @pl.when(org)
    def _():
        remote(w4, G.at[zq, :, cols(core * 128, 128)], hop_s, hop_r, (core, z)).wait_recv()
        for u in range(4):
            spread(near, u)

    @pl.when(org)
    def _():
        for u in range(4):
            pl.when((z == 0) | (z == 2))(lambda u=u: line_send(near, u, True, begin))
            pl.when((z == 1) | (z == 3))(lambda u=u: line_send(near, u, False, begin))

    for j, d in enumerate((2, 4, 6)):
        p = flip(dp, bits, d)
        rows = wq.at[:, cols(p * 128, 128)]
        remote(wqkv, rows, wr_s.at[j], wr_r.at[j], (p, z)).wait_recv()
        remote(rows, rows, wx_s.at[j], wx_r.at[j], (core, z)).start()
    for j, d in enumerate((3, 5, 7, 1)):
        p = flip(dp, bits, d)
        remote(wqkv, wq.at[:, cols(p * 128, 128)], wx_s.at[j], wx_r.at[j], (core, z)).wait_recv()

    gain1, gain2 = gain_row(gains, 0), gain_row(gains, 1)

    def project(s):
        base = s * 256

        @pl.loop(0, 8)
        def _(r):
            xhat, _r = norm_rows(tall[s, pl.ds(pl.multiple_of(r * 32, 32), 32), :].astype(F32))
            h1[pl.ds(pl.multiple_of(base + r * 32, 32), 32), :] = (xhat * gain1).astype(BF)

        rows = pl.ds(pl.multiple_of(base, 256), 256)
        hb = h1[rows, :]
        cb, sb = cs[rows, :], sn[rows, :]
        for p, dst in enumerate((q, k, v)):
            r = jnp.dot(hb, wq[p], preferred_element_type=F32)
            if p < 2:
                r = turn(r, cb, sb)
            if p == 0:
                r = r * (HEAD_DIM**-0.5)
            dst[rows, :] = r.astype(BF)

    for k_ in range(4):
        if k_ > 0:
            below, above = z - k_ >= 0, z + k_ <= 3
            for h in range(2):

                @pl.when(below)
                def _(k_=k_, h=h):
                    ref = tall.at[z - k_, pl.ds(h * 128, 128)]
                    remote(ref, ref, us.at[k_, h], rb.at[k_, h], (core, z)).wait_recv()
                    if k_ < 3:
                        pl.when(up_ok(k_))(lambda: tok_up(k_, h).start())

                @pl.when(above)
                def _(k_=k_, h=h):
                    ref = tall.at[z + k_, pl.ds(h * 128, 128)]
                    remote(ref, ref, ds.at[k_, h], ra.at[k_, h], (core, z)).wait_recv()
                    if k_ < 3:
                        pl.when(down_ok(k_))(lambda: tok_down(k_, h).start())

        if k_ == 1:

            @pl.when(org & no(end))
            def _():
                for u in range(4):
                    pl.when(z == 1)(lambda u=u: line_send(near, u, True, begin))
                    pl.when(z == 2)(lambda u=u: line_send(near, u, False, begin))

        @pl.loop(0, 2)
        def _(t, k_=k_):
            s = z - k_ + 2 * k_ * t
            pl.when((s >= 0) & (s <= 3) & ((k_ > 0) | (t == 0)))(lambda: project(s))

        if k_ == 1:

            @pl.when(org)
            def _():
                for u in range(4):
                    across(near, u)
                for u in range(3):
                    stage_far(u)

        if k_ == 2:

            @pl.when(org)
            def _():
                stage_far(3)
                across(far, 0)
                across(far, 1)

            @pl.when(no(org) & no(end))
            def _():
                stage_near(0)
                stage_near(1)

        if k_ == 3:

            @pl.when(org)
            def _():
                across(far, 2)
                across(far, 3)

    for s in range(4):
        vT[:, s * 256 : (s + 1) * 256] = v[s * 256 : (s + 1) * 256, :].T
    head_of = lax.div(lax.broadcasted_iota(jnp.int32, (256, 256), 1), HEAD_DIM)

    def attend(i):
        rows = pl.ds(pl.multiple_of(i * 256, 256), 256)
        qb = q[rows, :]
        seg_q = segr[0:1, rows]
        heads = range(4)
        qh = [jnp.where(head_of == h, qb, jnp.zeros((), BF)) for h in heads]
        top = [jnp.full((1, 256), masked_fill, F32) for h in heads]
        tot = [jnp.zeros((1, 256), F32) for h in heads]
        out = [jnp.zeros((HEAD_DIM, 256), F32) for h in heads]
        for kc in range(4):
            keys = slice(kc * 256, kc * 256 + 256)
            kb = k[keys, :]
            seg_k = segc[keys, :]
            same = jnp.concatenate([seg_k, seg_k], axis=1) == seg_q
            for h in heads:
                s = lax.dot_general(kb, qh[h], NT, preferred_element_type=F32)
                s = jnp.where(same, s, masked_fill)
                new = jnp.maximum(top[h], jnp.max(s, axis=0, keepdims=True))
                p = jnp.exp(s - new)
                keep = jnp.exp(top[h] - new)
                tot[h] = tot[h] * keep + jnp.sum(p, axis=0, keepdims=True)
                vh = vT[h * HEAD_DIM : (h + 1) * HEAD_DIM, keys]
                out[h] = out[h] * keep + jnp.dot(vh, p.astype(BF), preferred_element_type=F32)
                top[h] = new
        for h in heads:
            oT[h * HEAD_DIM : (h + 1) * HEAD_DIM, :] = out[h] * (1.0 / tot[h])
            lse[h, i] = jnp.broadcast_to(top[h] + jnp.log(tot[h]), (8, 256))
        att[rows, :] = oT[...].T.astype(BF)

    def att_slot(src_core, q):
        return attn2.at[cols(src_core * 256, 256), cols(q * 256, 256)]

    def att_copy(n, i):
        rows = pl.ds(pl.multiple_of(i * 256, 256), 256)
        return remote(
            att.at[rows, :], att_slot(c, zq), at_s.at[n], at_r.at[c, zq], (2 * chip + home, i)
        )

    @pl.loop(0, 4)
    def _(n):
        i = lax.rem(z + 1 + n, 4)
        attend(i)
        for m in range(4):

            @pl.when((n == m) & ((m < 3) | no(org)))
            def _(m=m):
                att_copy(m, i).start()

        @pl.when((n == 3) & org)
        def _():
            attn2[own, cols(zq * 256, 256)] = att[pl.ds(pl.multiple_of(z * 256, 256), 256), :]

        sf, sn_, af, an = stage_far, stage_near, lambda u: across(far, u), lambda u: across(near, u)
        plans = (
            (no(org) & no(end), (((sn_, 2), (sn_, 3)), ((sf, 0), (sf, 1), (an, 0), (an, 1)),
                                 ((sf, 2), (an, 2), (an, 3)), ((sf, 3), (af, 0), (af, 1)))),
            (no(org) & end, (((sn_, 0),), ((sn_, 1), (sn_, 2)), ((sn_, 3), (an, 0), (an, 1)),
                             ((sf, 0), (an, 2)))),
        )
        for who, plan in plans:
            for m, ops in enumerate(plan):

                @pl.when(who & (n == m))
                def _(ops=ops):
                    for op, u in ops:
                        op(u)

    @pl.when(no(org) & no(end))
    def _():
        across(far, 2)
        across(far, 3)

    @pl.when(no(org) & end)
    def _():
        stage_far(1)
        across(near, 3)
        across(far, 0)
        stage_far(2)
        across(far, 1)
        stage_far(3)
        across(far, 2)
        across(far, 3)

    for k_ in range(3):
        for h in range(2):
            pl.when(up_ok(k_))(lambda k_=k_, h=h: tok_up(k_, h).wait_send())
            pl.when(down_ok(k_))(lambda k_=k_, h=h: tok_down(k_, h).wait_send())
    for src in range(2):
        for qi in range(2):
            mine_too = (c == src) & (z == 2 * c + qi)

            @pl.when(no(mine_too))
            def _(src=src, qi=qi):
                slot = att_slot(src, qi)
                remote(slot, slot, at_s.at[0], at_r.at[src, qi], (core, z)).wait_recv()

    def pack_wait(u):
        for qi in range(2):
            for w, where in enumerate((chip_b, chip_d)):
                ref = piece(qi, u, where)
                remote(ref, ref, pb_s.at[qi, u], pb_r.at[qi, w, u], (b, z)).wait_recv()

    def w_rows(qi, m):
        r0, n = ROWS[m]
        return pl.ds(r0, n)

    pack_wait(0)

    def out_proj(rows):
        return sum(
            jnp.dot(
                attn2[rows, qi * 256 : (qi + 1) * 256], G[qi, w_rows(qi, 3), :], preferred_element_type=F32
            )
            for qi in range(2)
        )

    acc[...] = out_proj(other)
    y_copy = remote(acc, yr, y_s, y_r, (core, z))
    y_copy.start()
    X1[...] = tok[...].astype(F32) + out_proj(own)
    y_copy.wait()

    def chunk(r):
        return pl.ds(pl.multiple_of(r * 32, 32), 32)

    def own_chunk(r):
        return pl.ds(pl.multiple_of(c * 256 + r * 32, 32), 32)

    @pl.loop(0, 8)
    def _(r):
        x1 = X1[chunk(r), :] + yr[chunk(r), :]
        X1[chunk(r), :] = x1
        xhat, _r = norm_rows(x1)
        h2a[own_chunk(r), :] = (xhat * gain2).astype(BF)

    h_copy = remote(h2a.at[own], h2a.at[own], h_s, h_r, (core, z))
    h_copy.start()
    remote(cot, cot2.at[other], co_s, co_r, (core, z)).wait_recv()
    for u in range(1, 4):
        pack_wait(u)
    h_copy.wait()

    TILES = ((0, 224), (224, 224), (448, 208))
    for r0, n in TILES:

        @pl.loop(0, 2)
        def _(qi, r0=r0, n=n):
            h2 = h2a[...]
            act = lax.dot_general(G[qi, pl.ds(ROWS[0][0] + r0, n), :], h2, NT, preferred_element_type=F32)
            up = lax.dot_general(G[qi, pl.ds(ROWS[1][0] + r0, n), :], h2, NT, preferred_element_type=F32)
            dh = lax.dot_general(G[qi, pl.ds(ROWS[2][0] + r0, n), :], cot2[...], NT, preferred_element_type=F32)
            Phi = 0.5 + 0.5 * lax.erf(act * INV_SQRT2)
            phi = jnp.exp(-0.5 * act * act) * INV_SQRT_2PI
            gel = act * Phi
            rr = pl.ds(r0, n)
            hidT[qi, rr, :] = (gel * up).astype(BF)
            daT[qi, rr, :] = (dh * up * (Phi + act * phi)).astype(BF)
            duT[qi, rr, :] = (dh * gel).astype(BF)

    def tn(lhs, rhs):
        return lax.dot_general(lhs, rhs, TN, preferred_element_type=F32)

    def d_norm(dst, rows):
        for half in range(2):
            hc = slice(half * 512, half * 512 + 512)
            dst[:, hc] = sum(
                tn(daT[qi, :, rows], G[qi, w_rows(qi, 0), hc]) + tn(duT[qi, :, rows], G[qi, w_rows(qi, 1), hc])
                for qi in range(2)
            )

    def mlp_out(dst, rows, plus=None):
        for half in range(2):
            hc = slice(half * 512, half * 512 + 512)
            r = sum(tn(hidT[qi, :, rows], G[qi, w_rows(qi, 2), hc]) for qi in range(2))
            dst[:, hc] = r if plus is None else r + plus[:, hc]

    def grads(qi, m):
        lhs, rhs = ((daT, h2a), (duT, h2a), (hidT, cot2))[m]

        @pl.loop(0, 4)
        def _(t):
            tc = cols(t * 256, 256)
            G[qi, w_rows(qi, m), tc] = jnp.dot(lhs[qi], rhs[:, tc], preferred_element_type=F32).astype(BF)

    def unit(e):
        qi, k_ = UNITS[e]
        m, o, n = HALVES[k_]
        return qi, pl.ds(ROWS[m][0] + o, n)

    def part(e, where):
        qi, rows = unit(e)
        return G.at[qi, rows, cols(where * 256, 256)]

    def unit_b(e, slot):
        qi, rows = unit(e)
        src = part(e, chip_b if slot == 0 else chip_d)
        return remote(src, Rb.at[slot, qi, rows], b_s.at[slot, e], b_r.at[slot, e], (b, z))

    def unit_a(e):
        qi, rows = unit(e)
        return remote(part(e, chip_a), Ra.at[qi, rows], a_s.at[e], a_r.at[e], (a, z))

    def send_b(e):
        unit_b(e, 1).start()
        unit_b(e, 0).start()

    def stage1(e):
        qi, rows = unit(e)
        unit_b(e, 1).wait_recv()
        ref = part(e, chip_a)
        ref[...] = (ref[...].astype(F32) + Rb[1, qi, rows, :].astype(F32)).astype(BF)
        unit_a(e).start()

    def line_up(e, slot):
        rows = unit(e)[1]
        return remote(part(e, chip), Z.at[slot, rows], zu_s.at[e], z_r.at[slot, e], (dp, z + 1))

    def line_down(e):
        qi, rows = unit(e)
        return remote(part(e, chip), Z.at[qi, rows], zd_s.at[e], z_r.at[qi, e], (dp, z - 1))

    def target(e):
        return 2 * c + UNITS[e][0]

    def inward(e, act):
        t = target(e)
        pl.when(z > t)(lambda: act(line_down(e)))
        pl.when(z + 1 == t)(lambda: act(line_up(e, 2)))
        pl.when(z + 1 < t)(lambda: act(line_up(e, UNITS[e][0])))

    def stage2(e):
        qi, rows = unit(e)
        unit_b(e, 0).wait_recv()
        unit_a(e).wait_recv()
        ref = part(e, chip)
        ref[...] = (ref[...].astype(F32) + Rb[0, qi, rows, :].astype(F32) + Ra[qi, rows, :].astype(F32)).astype(BF)
        t = target(e)
        pl.when(((z == 3) & (z > t)) | ((z == 0) & (z < t)))(lambda: inward(e, begin))

    def line_wait(e, slot):
        ref = Z.at[slot, unit(e)[1]]
        remote(ref, ref, zu_s.at[e], z_r.at[slot, e], (core, z)).wait_recv()

    def stage3(e, depth):
        qi, rows = unit(e)
        t = target(e)
        mid = ((z > t) & (z == 3 - depth)) | ((z < t) & (z == depth))

        @pl.when(mid)
        def _():
            line_wait(e, qi)
            ref = part(e, chip)
            ref[...] = (ref[...].astype(F32) + Z[qi, rows, :].astype(F32)).astype(BF)
            inward(e, begin)

    def final(k_):
        m, o, n = HALVES[k_]
        return give.at[pl.ds(ROWS[m][0] + o, n)], dw4[m].at[pl.ds(o, n)]

    def stage4(e):
        qi, rows = unit(e)
        k_ = UNITS[e][1]

        @pl.when(z == target(e))
        def _():
            gift, dst = final(k_)
            dst[...] = G[qi, rows, cols(dp * 128, 128)].astype(F32)
            gift[...] = G[qi, rows, cols(core * 128, 128)].astype(F32)

            def take(slot):
                line_wait(e, slot)
                for who, ref in ((c, dst), (1 - c, gift)):
                    ref[...] = ref[...] + Z[slot, rows, cols(who * 128, 128)].astype(F32)

            pl.when(z < 3)(lambda: take(qi))
            pl.when(z > 0)(lambda: take(2))
            remote(gift, dst, fin_s.at[k_], fin_r.at[k_], (core, z)).start()

    def tick(t):
        for lag, step in enumerate(
            (stage1, stage2, lambda e: stage3(e, 1), lambda e: stage3(e, 2), stage4)
        ):
            if 0 <= t - lag < NU:
                step(t - lag)

    d_norm(acc, other)
    d_copy = remote(acc, dr, d_s, d_r, (core, z))
    d_copy.start()
    mlp_out(dxo, other)
    u_copy = remote(dxo, ur, u_s, u_r, (core, z))
    u_copy.start()
    d_norm(dX1, own)
    mlp_out(dtok_o, own, X1)
    for u in range(4):
        for qi in range(2):
            line_send(qi, u, True, lambda cp: cp.wait_send())
            line_send(qi, u, False, lambda cp: cp.wait_send())
        for qi in range(2):
            plane_a(qi, u).wait_send()
            plane_b(qi, u).wait_send()
            plane_f(qi, u).wait_send()
    def ff_grads(qi, m):
        grads(qi, m)
        for e in range(NU):
            if UNITS[e][0] == qi and HALVES[UNITS[e][1]][0] == m:
                send_b(e)

    ff_grads(0, 2)
    ff_grads(0, 0)
    d_copy.wait()

    @pl.loop(0, 8)
    def _(r):
        dh2 = dX1[chunk(r), :] + dr[chunk(r), :]
        xhat, rstd = norm_rows(X1[chunk(r), :])
        e2 = dh2 * gain2
        m1 = jnp.mean(e2, axis=-1, keepdims=True)
        m2 = jnp.mean(e2 * xhat, axis=-1, keepdims=True)
        dx = cot2[own_chunk(r), :].astype(F32) + rstd * (e2 - m1 - xhat * m2)
        dX1[chunk(r), :] = dx
        dya[own_chunk(r), :] = dx.astype(BF)

    e_copy = remote(dya.at[own], dya.at[own], e_s, e_r, (core, z))
    e_copy.start()
    ff_grads(0, 1)
    e_copy.wait()
    for qi in range(2):
        dsend[qi] = lax.dot_general(dya[...], G[qi, w_rows(qi, 3), :], NT, preferred_element_type=F32).astype(BF)

    def att_back(c0, qi):
        dst = datt.at[cols(z * 256, 256)]
        return remote(
            dsend.at[qi, pl.ds(c0 * 256, 256)], dst, t_s.at[c0, qi], t_r.at[z], (2 * chip + c0, 2 * c + qi)
        )

    def is_self(c0, qi):
        return (c == c0) & (z == 2 * c + qi)

    for c0 in range(2):
        for qi in range(2):
            pl.when(no(is_self(c0, qi)))(lambda c0=c0, qi=qi: att_back(c0, qi).start())

            @pl.when(is_self(c0, qi))
            def _(c0=c0, qi=qi):
                datt[cols(z * 256, 256), :] = dsend[qi, c0 * 256 : (c0 + 1) * 256, :]

    for m in (2, 0, 1):
        ff_grads(1, m)
    for qi in range(2):

        @pl.loop(0, 4)
        def _(t, qi=qi):
            tc = cols(t * 256, 256)
            G[qi, w_rows(qi, 3), tc] = tn(attn2[:, qi * 256 : (qi + 1) * 256], dya[:, tc]).astype(BF)

        send_b(12 + qi)
    tick(0)
    u_copy.wait()
    out_o[...] = (dtok_o[...] + ur[...]).astype(BF)
    dq[...] = jnp.zeros_like(dq)
    dk[...] = jnp.zeros_like(dk)
    dv[...] = jnp.zeros_like(dv)
    for i in range(4):

        @pl.when(no(org & (z == i)))
        def _(i=i):
            ref = datt.at[pl.ds(i * 256, 256)]
            remote(ref, ref, t_s.at[0, 0], t_r.at[i], (core, z)).wait_recv()

    @pl.loop(0, 4)
    def _(i):
        rows = pl.ds(pl.multiple_of(i * 256, 256), 256)
        t = (datt[rows, :].astype(F32) * att[rows, :].astype(F32)).T
        for h in range(4):
            s = jnp.sum(t[h * 64 : (h + 1) * 64, :], axis=0, keepdims=True)
            delta[h, i] = jnp.broadcast_to(s, (8, 256))

    def block_order(l):
        return jnp.minimum(l, 1) * (lax.rem(l + 1, 3) + 1)

    def pair(i, j):
        ri = pl.ds(pl.multiple_of(i * 256, 256), 256)
        rj = pl.ds(pl.multiple_of(j * 256, 256), 256)

        kj, vj, qi_, dai = k[rj, :], v[rj, :], q[ri, :], datt[ri, :]
        seg_k = segc[rj, :]
        same = jnp.concatenate([seg_k, seg_k], axis=1) == segr[0:1, ri]
        none = jnp.zeros((), BF)
        dvs, dks, dqs = [], [], []
        for h in range(4):
            mine = head_of == h
            qh, dah = jnp.where(mine, qi_, none), jnp.where(mine, dai, none)
            s = lax.dot_general(kj, qh, NT, preferred_element_type=F32)
            p = jnp.exp(jnp.where(same, s, masked_fill) - lse[h, i, 0:1, :])
            dp_ = lax.dot_general(vj, dah, NT, preferred_element_type=F32)
            dsc = (p * (dp_ - delta[h, i, 0:1, :])).astype(BF)
            dvs.append(jnp.dot(p.astype(BF), dah, preferred_element_type=F32))
            dks.append(jnp.dot(dsc, qh, preferred_element_type=F32))
            dqs.append(tn(dsc, jnp.where(mine, kj, none)))
        dv[rj, :] = dv[rj, :] + (dvs[0] + dvs[1] + dvs[2] + dvs[3])
        dk[rj, :] = dk[rj, :] + (dks[0] + dks[1] + dks[2] + dks[3])
        dq[ri, :] = dq[ri, :] + (dqs[0] + dqs[1] + dqs[2] + dqs[3])

    def h_up(i, last):
        if last:
            return remote(Hs.at[i], Hx, hu_s.at[i], hx_r, (dp, z + 1))
        return remote(Hs.at[i], Hi.at[i], hu_s.at[i], hi_r.at[i], (dp, z + 1))

    def h_down(i):
        return remote(Hs.at[i], Hi.at[i], hd_s.at[i], hi_r.at[i], (dp, z - 1))

    def h_inward(i, act):
        pl.when(z > i)(lambda: act(h_down(i)))
        pl.when(z + 1 == i)(lambda: act(h_up(i, True)))
        pl.when(z + 1 < i)(lambda: act(h_up(i, False)))

    def h_wait(i):
        remote(Hi.at[i], Hi.at[i], hd_s.at[i], hi_r.at[i], (core, z)).wait_recv()

    def h_mid(i, depth):
        mid = ((z > i) & (z == 3 - depth)) | ((z < i) & (z == depth))

        @pl.when(mid)
        def _():
            h_wait(i)
            Hs[i] = (Hs[i].astype(F32) + Hi[i].astype(F32)).astype(BF)
            h_inward(i, begin)

    def finish(i):
        rows = pl.ds(pl.multiple_of(i * 256, 256), 256)
        cb, sb = cs[rows, :], -sn[rows, :]
        low = (
            turn(dq[rows, :] * (HEAD_DIM**-0.5), cb, sb).astype(BF),
            turn(dk[rows, :], cb, sb).astype(BF),
            dv[rows, :].astype(BF),
        )
        for p in range(3):
            dqkvT[p * 256 : (p + 1) * 256, rows] = low[p].T
        for half in range(2):
            hc = slice(half * 512, half * 512 + 512)
            dh = sum(
                lax.dot_general(low[p], wq[p, hc, :], NT, preferred_element_type=F32) for p in range(3)
            )
            Hs[i, :, hc] = dh.astype(BF)

            @pl.when(z == i)
            def _(dh=dh, hc=hc):
                acc[:, hc] = dh

        pl.when(((z == 3) & (z > i)) | ((z == 0) & (z < i)))(lambda: h_inward(i, begin))

    tick(1)
    slots = {1: [2], 4: [3], 7: [4], 9: [5], 11: [6], 13: [7], 15: [8]}
    h_slots = {11: [(0, 1)], 15: [(0, 2), (3, 1)]}

    @pl.loop(0, 16)
    def _(n):
        def past(v):
            return lax.div(n + 16 - v, 16)

        ph = past(7) + past(12) + past(15)
        t = n - 7 * past(7) - 5 * past(12) - 3 * past(15)
        left = 4 - ph
        over = lax.div(t, left)
        li = ph + over * (t - left + 1)
        lj = ph + (1 - over) * t
        pair(block_order(li), block_order(lj))
        pl.when((n == 6) | (n == 11) | (n == 14) | (n == 15))(lambda: finish(block_order(ph)))
        for s in range(16):
            todo = [lambda t=t: tick(t) for t in slots.get(s, ())]
            todo += [lambda i=i, d=d: h_mid(i, d) for i, d in h_slots.get(s, ())]

            @pl.when(n == s)
            def _(todo=todo):
                for op in todo:
                    op()

    @pl.loop(0, 4)
    def _(t):
        tc = cols(t * 256, 256)
        Wp[:, tc] = jnp.dot(dqkvT[...], h1[:, tc], preferred_element_type=F32).astype(BF)

    def core_copy(w):
        return remote(
            Wp.at[:, cols(w * 256 + (1 - c) * 128, 128)], Wc.at[w], wc_s.at[w], wc_r.at[w], (core, z)
        )

    for w in range(4):
        core_copy(w).start()
    tick(9)
    h_mid(3, 2)
    h_mid(1, 1)
    h_mid(2, 1)

    def both(w):
        Wc[w] = (Wc[w].astype(F32) + Wp[:, cols(w * 256 + c * 128, 128)].astype(F32)).astype(BF)

    for w in range(4):
        core_copy(w).wait_recv()
    both(chip_d)
    both(chip_b)
    wb_copy = [
        remote(Wc.at[where], Wb.at[slot], wb_s.at[slot], wb_r.at[slot], (b, z))
        for slot, where in ((0, chip_b), (1, chip_d))
    ]
    wb_copy[1].start()
    wb_copy[0].start()
    both(chip_a)
    both(chip)
    wa_copy = remote(Wc.at[chip_a], Wa, wa_s, wa_r, (a, z))
    for t in range(10, 14):
        tick(t)
    wb_copy[1].wait_recv()
    Wc[chip_a] = (Wc[chip_a].astype(F32) + Wb[1].astype(F32)).astype(BF)
    wa_copy.start()
    tick(14)
    tick(15)

    pl.when(z < 3)(lambda: h_wait(z))
    pl.when(z > 0)(lambda: remote(Hx, Hx, hu_s.at[0], hx_r, (core, z)).wait_recv())
    has_above, has_below = z < 3, z > 0

    @pl.when(has_above)
    def _():
        acc[...] = acc[...] + Hi[z].astype(F32)

    @pl.when(has_below)
    def _():
        acc[...] = acc[...] + Hx[...].astype(F32)

    @pl.loop(0, 8)
    def _(r):
        xhat, rstd = norm_rows(tok[chunk(r), :].astype(F32))
        e1 = acc[chunk(r), :] * gain1
        m1 = jnp.mean(e1, axis=-1, keepdims=True)
        m2 = jnp.mean(e1 * xhat, axis=-1, keepdims=True)
        dtok_o[chunk(r), :] = dX1[chunk(r), :] + rstd * (e1 - m1 - xhat * m2)

    wb_copy[0].wait_recv()
    wa_copy.wait_recv()
    total = Wc[chip].astype(F32) + Wb[0].astype(F32) + Wa[...].astype(F32)
    dot_one = jnp.zeros((1, 128), F32)
    for p in range(3):
        piece = total[p * 256 : (p + 1) * 256, :]
        dwq_o[p] = piece.T
        dot_one = dot_one + jnp.sum(piece * wqkv[p].T.astype(F32), axis=0, keepdims=True)
    for t in range(16, NU + 4):
        tick(t)
    for k_ in range(7):

        @pl.when(no(org))
        def _(k_=k_):
            ref = final(k_)[1]
            remote(ref, ref, fin_s.at[k_], fin_r.at[k_], (core, z)).wait_recv()

    part_two = jnp.sum(dwin_o[...] * w4[256 : 256 + 2 * HID, :].astype(F32), axis=0, keepdims=True)
    gz[z, 0:1, :] = dot_one / gains[dp, 0:1, :]
    gz[z, 1:2, :] = part_two / gains[dp, 1:2, :]
    gz[z, 2:8, :] = jnp.zeros((6, 128), F32)
    gain_copy = [
        remote(gz.at[z], gz.at[z], gz_s.at[n], gz_r.at[z], (dp, lax.rem(z + n, 4))) for n in range(1, 4)
    ]
    for cp in gain_copy:
        cp.start()
    for n in range(1, 4):
        o = lax.rem(z + n, 4)
        remote(gz.at[o], gz.at[o], gz_s.at[n], gz_r.at[o], (core, z)).wait_recv()
    dg_o[...] = gz[0] + gz[1] + gz[2] + gz[3]

    for cp in gain_copy:
        cp.wait_send()
    for w in range(4):
        core_copy(w).wait_send()
    wb_copy[0].wait_send()
    wb_copy[1].wait_send()
    wa_copy.wait_send()
    for i in range(4):
        h_inward(i, lambda cp: cp.wait_send())
    for c0 in range(2):
        for qi in range(2):
            pl.when(no(is_self(c0, qi)))(lambda c0=c0, qi=qi: att_back(c0, qi).wait_send())
    for e in range(NU):
        unit_b(e, 0).wait_send()
        unit_b(e, 1).wait_send()
        unit_a(e).wait_send()
        inward(e, lambda cp: cp.wait_send())

        @pl.when(z == target(e))
        def _(e=e):
            k_ = UNITS[e][1]
            gift, dst = final(k_)
            remote(gift, dst, fin_s.at[k_], fin_r.at[k_], (core, z)).wait_send()

    for d in range(1, 8):
        remote(gains_in, gains.at[dp], g_s.at[d], g_r.at[d], (core, z)).wait_send()
    for j in range(3):
        remote(wqkv, wq.at[:, own_rows], wr_s.at[j], wr_r.at[j], (core, z)).wait_send()
    for j in range(4):
        remote(wqkv, wq.at[:, own_rows], wx_s.at[j], wx_r.at[j], (core, z)).wait_send()
    pl.when(no(org))(lambda: hop.wait_send())
    cot_copy.wait_send()
    for n in range(3):
        att_copy(n, lax.rem(z + 1 + n, 4)).wait_send()
    pl.when(no(org))(lambda: att_copy(3, z).wait_send())


def run_layer(*args):
    V = pl.BlockSpec(memory_space=pltpu.VMEM)
    S = pl.BlockSpec(memory_space=pltpu.SMEM)
    dma = pltpu.SemaphoreType.DMA
    s = jax.ShapeDtypeStruct
    vm = pltpu.VMEM
    return pl.pallas_call(
        layer_kernel,
        out_shape=(
            s((256, 1024), BF), s((256, 1024), F32), s((3, 128, 256), F32), s((2 * HID, 128), F32),
            s((HID, 128), F32), s((256, 128), F32), s((8, 128), F32),
        ),
        in_specs=[S, S] + [V] * 6 + [pl.BlockSpec(memory_space=pl.ANY)],
        out_specs=[V] * 7,
        scratch_shapes=[
            vm((8, 8, 128), F32), vm((PACK, 128), BF), vm((1024, 128), F32), vm((1024, 128), F32),
            vm((1024, 128), F32), vm((8, 1024), F32), vm((1024, 256), BF), vm((1024, 256), BF),
            vm((1024, 256), BF), vm((4, 4, 8, 256), F32), vm((1024, 256), BF), vm((512, 512), BF),
            vm((1024, 1024), BF), vm((3, 1024, 256), BF), vm((512, 1024), BF),
            vm((2, PACK, 1024), BF), vm((256, 1024), F32), vm((1024, 1024), BF), vm((256, 1024), F32),
            vm((256, 1024), F32), vm((256, 1024), F32), vm((2, HID, 512), BF), vm((2, HID, 512), BF),
            vm((2, HID, 512), BF), vm((256, 1024), F32), vm((256, 1024), F32), vm((2, 512, 256), BF),
            vm((1024, 256), BF), vm((4, 4, 8, 256), F32),
            vm((1024, 256), F32), vm((1024, 256), F32), vm((1024, 256), F32),
            vm((4, 256, 1024), BF), vm((4, 256, 1024), BF), vm((256, 1024), BF), vm((2, 2, PACK, 256), BF),
            vm((2, PACK, 256), BF), vm((3, PACK, 256), BF), vm((PACK, 128), F32),
            vm((768, 1024), BF), vm((4, 768, 128), BF), vm((2, 768, 128), BF), vm((768, 128), BF), vm((4, 8, 128), F32),
            dma((4, 2)), dma((4, 2)), dma((4, 2)), dma((4, 2)),
            dma((3,)), dma((3,)), dma((4,)), dma((4,)), dma((8,)), dma((8,)), dma, dma, dma, dma,
            dma((2, 4)), dma((2, 4)), dma((2, 4)), dma((2, 4)), dma((2, 4)), dma((2, 4)),
            dma((2, 4)), dma((2, 2, 4)), dma((4,)), dma((2, 2)),
            dma, dma, dma, dma, dma, dma, dma, dma, dma, dma, dma((2, 2)), dma((4,)),
            dma((2, NU)), dma((2, NU)), dma((NU,)), dma((NU,)), dma((NU,)), dma((NU,)), dma((3, NU)),
            dma((7,)), dma((7,)), dma((4,)), dma((4,)), dma((4,)), dma,
            dma((4,)), dma((4,)), dma((2,)), dma((2,)), dma, dma, dma((4,)), dma((4,)), dma,
        ],
        compiler_params=pltpu.CompilerParams(
            collective_id=1, has_side_effects=True, vmem_limit_bytes=63 << 20
        ),
        name="layer",
    )(*args)


def local_fast(
    tokens, lengths, seq_order, gain_attn, w_qkv, w_attn_out, gain_mlp, w_in, w_mlp_out, cotangent
):
    half = HEAD_DIM // 2
    frequency = jnp.tile(rope_base ** (-2.0 * jnp.arange(half, dtype=F32) / HEAD_DIM), 4)
    sign = jnp.tile(jnp.repeat(jnp.array([-1.0, 1.0], F32), half), 2)
    rows = (gain_attn.astype(F32), gain_mlp.astype(F32), frequency, sign)
    gains = jnp.concatenate([r[None, :] for r in rows] + [jnp.zeros((4, 128), F32)], axis=0)
    out, d_tok, d_qkv, d_in, d_down, d_out, d_gain = run_layer(
        lengths, seq_order, tokens, w_qkv, w_in.transpose(1, 2, 0).reshape(2 * HID, 128), w_mlp_out, w_attn_out, gains, cotangent
    )
    return (out, d_tok, d_gain[0], d_qkv, d_out, d_gain[1], d_in.reshape(2, HID, 128).transpose(2, 0, 1), d_down)


def layer_norm(field_in, norm_gain):
    row_mean = jnp.mean(field_in, axis=-1, keepdims=True)
    centered = field_in - row_mean
    variance = jnp.mean(centered * centered, axis=-1, keepdims=True)
    return centered * lax.rsqrt(variance + norm_eps) * norm_gain


def rotate(field_in, position):
    half_size = field_in.shape[-1] // 2
    index_range = jnp.arange(half_size, dtype=jnp.float32)
    frequency = rope_base ** (-2.0 * index_range / field_in.shape[-1])
    angles = position[:, None] * frequency[None, :]
    cosine = jnp.cos(angles)[:, None, :]
    sine_part = jnp.sin(angles)[:, None, :]
    first_half = field_in[..., :half_size]
    second_half = field_in[..., half_size:]
    return jnp.concatenate(
        [
            first_half * cosine - second_half * sine_part,
            second_half * cosine + first_half * sine_part,
        ],
        axis=-1,
    )


def geglu(act_part, up_part):
    return jax.nn.gelu(act_part, approximate=False) * up_part


def layout(lengths, seq_order, group_rows):
    seq_total = seq_order.shape[0]
    first_seq = lax.axis_index("dp") * SEQ_GRP
    chosen = lax.dynamic_slice_in_dim(seq_order, first_seq, SEQ_GRP)
    matched = chosen[:, None] == jnp.arange(seq_total, dtype=jnp.int32)[None, :]
    dealt_lengths = jnp.sum(jnp.where(matched, lengths[None, :], 0), axis=1)
    seq_ends = jnp.cumsum(dealt_lengths)
    row_index = jnp.arange(group_rows, dtype=jnp.int32)
    passed = row_index[:, None] >= seq_ends[None, :]
    segment = jnp.sum(passed.astype(jnp.int32), axis=1)
    row_start = jnp.sum(jnp.where(passed, dealt_lengths[None, :], 0), axis=1)
    return (segment, (row_index - row_start).astype(jnp.float32))


def item_layout(array_in, block_rows):
    group_rows, head_count, head_size = array_in.shape
    block_count = group_rows // block_rows
    shaped = array_in.reshape(block_count, block_rows, head_count, head_size)
    return shaped.transpose(2, 0, 1, 3).reshape(head_count * block_count, block_rows, head_size)


def from_items(items, group_rows):
    item_count, block_rows, head_size = items.shape
    block_count = group_rows // block_rows
    head_count = item_count // block_count
    shaped = items.reshape(head_count, block_count, block_rows, head_size)
    return shaped.transpose(1, 2, 0, 3).reshape(group_rows, head_count, head_size)


def masked_scores(query_block, key_head, segment_block, segment):
    score_scale = query_block.shape[-1] ** (-0.5)
    raw_scores = lax.dot_general(
        query_block, key_head, (((1,), (1,)), ((), ())), preferred_element_type=jnp.float32
    )
    allowed = segment_block[:, None] == segment[None, :]
    return jnp.where(allowed, raw_scores * score_scale, masked_fill)


def attend_forward(query_rot, key_rot, value_low, segment, block_rows):
    group_rows, head_count, head_size = query_rot.shape
    block_count = group_rows // block_rows
    query_items = item_layout(query_rot, block_rows)
    key_heads = key_rot.transpose(1, 0, 2)
    value_heads = value_low.transpose(1, 0, 2)
    segment_blocks = segment.reshape(block_count, block_rows)

    def one_item(item_index):
        head_index = item_index // block_count
        block_index = item_index % block_count
        query_block = lax.dynamic_index_in_dim(query_items, item_index, 0, False)
        key_head = lax.dynamic_index_in_dim(key_heads, head_index, 0, False)
        value_head = lax.dynamic_index_in_dim(value_heads, head_index, 0, False)
        segment_block = lax.dynamic_index_in_dim(segment_blocks, block_index, 0, False)
        scores = masked_scores(query_block, key_head, segment_block, segment)
        row_top = jnp.max(scores, axis=1, keepdims=True)
        weights = jnp.exp(scores - row_top)
        row_total = jnp.sum(weights, axis=1, keepdims=True)
        probs_low = (weights / row_total).astype(jnp.bfloat16)
        result = jnp.dot(probs_low, value_head, preferred_element_type=jnp.float32)
        return (result, row_top[:, 0] + jnp.log(row_total[:, 0]))

    results, log_totals = lax.map(one_item, jnp.arange(head_count * block_count, dtype=jnp.int32))
    return (from_items(results, group_rows), log_totals)


def attend_backward(query_rot, key_rot, value_low, grad_out, log_totals, segment, block_rows):
    group_rows, head_count, head_size = query_rot.shape
    block_count = group_rows // block_rows
    score_scale = head_size ** (-0.5)
    query_items = item_layout(query_rot, block_rows)
    grad_items = item_layout(grad_out, block_rows)
    key_heads = key_rot.transpose(1, 0, 2)
    value_heads = value_low.transpose(1, 0, 2)
    segment_blocks = segment.reshape(block_count, block_rows)

    def one_item(carried, item_index):
        key_grads, value_grads = carried
        head_index = item_index // block_count
        block_index = item_index % block_count
        query_block = lax.dynamic_index_in_dim(query_items, item_index, 0, False)
        grad_block = lax.dynamic_index_in_dim(grad_items, item_index, 0, False)
        log_row = lax.dynamic_index_in_dim(log_totals, item_index, 0, False)
        key_head = lax.dynamic_index_in_dim(key_heads, head_index, 0, False)
        value_head = lax.dynamic_index_in_dim(value_heads, head_index, 0, False)
        segment_block = lax.dynamic_index_in_dim(segment_blocks, block_index, 0, False)
        scores = masked_scores(query_block, key_head, segment_block, segment)
        prob_full = jnp.exp(scores - log_row[:, None])
        probs_low = prob_full.astype(jnp.bfloat16)
        grad_probs = lax.dot_general(
            grad_block, value_head, (((1,), (1,)), ((), ())), preferred_element_type=jnp.float32
        )
        row_delta = jnp.sum(prob_full * grad_probs, axis=1, keepdims=True)
        grad_scores = (prob_full * (grad_probs - row_delta)).astype(jnp.bfloat16)
        grad_query = (
            jnp.dot(grad_scores, key_head, preferred_element_type=jnp.float32) * score_scale
        )
        grad_key = (
            lax.dot_general(
                grad_scores,
                query_block,
                (((0,), (0,)), ((), ())),
                preferred_element_type=jnp.float32,
            )
            * score_scale
        )
        grad_value = lax.dot_general(
            probs_low, grad_block, (((0,), (0,)), ((), ())), preferred_element_type=jnp.float32
        )
        key_grads = lax.dynamic_update_index_in_dim(
            key_grads,
            lax.dynamic_index_in_dim(key_grads, head_index, 0, False) + grad_key,
            head_index,
            0,
        )
        value_grads = lax.dynamic_update_index_in_dim(
            value_grads,
            lax.dynamic_index_in_dim(value_grads, head_index, 0, False) + grad_value,
            head_index,
            0,
        )
        return ((key_grads, value_grads), grad_query)

    zero_heads = jnp.zeros((head_count, group_rows, head_size), jnp.float32)
    (key_grads, value_grads), query_grads = lax.scan(
        one_item, (zero_heads, zero_heads), jnp.arange(head_count * block_count, dtype=jnp.int32)
    )
    return (
        from_items(query_grads, group_rows),
        key_grads.transpose(1, 0, 2),
        value_grads.transpose(1, 0, 2),
    )


def spread_rows(local_rows):
    return lax.all_gather(local_rows, "tensor", axis=0, tiled=True)


def spread_grads(local_grads):
    return lax.all_gather(local_grads, "tensor", axis=0, tiled=True)


def sum_heads(activations, weight_part, row_count):

    def row_term(first_row, row_number):
        return jnp.dot(activations, weight_part, preferred_element_type=jnp.float32)

    return lax.psum_scatter(
        row_term(jnp.int32(0), row_count * lax.axis_size("tensor")),
        "tensor",
        scatter_dimension=0,
        tiled=True,
    )


def sum_grads(grads_low, weight_full, einsum_form, row_count):

    def row_term(first_row, row_number):
        return jnp.einsum(einsum_form, grads_low, weight_full, preferred_element_type=jnp.float32)

    return lax.psum_scatter(
        row_term(jnp.int32(0), row_count * lax.axis_size("tensor")),
        "tensor",
        scatter_dimension=0,
        tiled=True,
    )


def local_plain(
    tokens, lengths, seq_order, gain_attn, w_qkv, w_attn_out, gain_mlp, w_in, w_mlp_out, cotangent
):
    row_count = tokens.shape[0]
    group_rows = row_count * lax.axis_size("tensor")
    block_rows = min(512, group_rows)
    segment, position = layout(lengths, seq_order, group_rows)
    gain_low_one, qkv_weight, out_weight, gain_low_two, in_weight, down_weight = (
        lax.all_gather(gain_attn, "dp", axis=0, tiled=True),
        lax.all_gather(w_qkv, "dp", axis=1, tiled=True),
        lax.all_gather(w_attn_out, "dp", axis=1, tiled=True),
        lax.all_gather(gain_mlp, "dp", axis=0, tiled=True),
        lax.all_gather(w_in, "dp", axis=0, tiled=True),
        lax.all_gather(w_mlp_out, "dp", axis=1, tiled=True),
    )
    gain_one = gain_low_one.astype(jnp.float32)
    gain_two = gain_low_two.astype(jnp.float32)
    residual = tokens.astype(jnp.float32)
    normed_one = spread_rows(layer_norm(residual, gain_one).astype(jnp.bfloat16))
    qkv = jnp.einsum("rd,pdc->rpc", normed_one, qkv_weight, preferred_element_type=jnp.float32)
    head_count = qkv.shape[2] // HEAD_DIM
    head_shape = (group_rows, head_count, HEAD_DIM)
    query_rot = rotate(qkv[:, 0].reshape(head_shape), position).astype(jnp.bfloat16)
    key_rot = rotate(qkv[:, 1].reshape(head_shape), position).astype(jnp.bfloat16)
    value_low = qkv[:, 2].reshape(head_shape).astype(jnp.bfloat16)
    attended, log_totals = attend_forward(query_rot, key_rot, value_low, segment, block_rows)
    attn_low = attended.reshape(group_rows, head_count * HEAD_DIM).astype(jnp.bfloat16)
    resid_mid = residual + sum_heads(attn_low, out_weight, row_count)
    normed_two = spread_rows(layer_norm(resid_mid, gain_two).astype(jnp.bfloat16))
    gate_up = jnp.einsum("rd,dpc->rpc", normed_two, in_weight, preferred_element_type=jnp.float32)
    hidden = geglu(gate_up[:, 0], gate_up[:, 1]).astype(jnp.bfloat16)
    output = (resid_mid + sum_heads(hidden, down_weight, row_count)).astype(jnp.bfloat16)
    grad_two = spread_grads(cotangent)
    d_hidden = lax.dot_general(
        grad_two, down_weight, (((1,), (1,)), ((), ())), preferred_element_type=jnp.float32
    )
    d_down = lax.dot_general(
        hidden, grad_two, (((0,), (0,)), ((), ())), preferred_element_type=jnp.float32
    )
    geglu_pull = jax.vjp(geglu, gate_up[:, 0], gate_up[:, 1])[1]
    d_act, d_up = geglu_pull(d_hidden)
    d_gate_up = jnp.stack([d_act, d_up], axis=1).astype(jnp.bfloat16)
    d_in = jnp.einsum("rd,rpc->dpc", normed_two, d_gate_up, preferred_element_type=jnp.float32)
    d_normed_two = sum_grads(d_gate_up, in_weight, "rpc,dpc->rd", row_count)
    norm_pull_two = jax.vjp(layer_norm, resid_mid, gain_two)[1]
    d_mid_norm, d_gain_two = norm_pull_two(d_normed_two)
    d_mid = cotangent.astype(jnp.float32) + d_mid_norm
    grad_one = spread_grads(d_mid.astype(jnp.bfloat16))
    d_out = lax.dot_general(
        attn_low, grad_one, (((0,), (0,)), ((), ())), preferred_element_type=jnp.float32
    )
    d_att = lax.dot_general(
        grad_one, out_weight, (((1,), (1,)), ((), ())), preferred_element_type=jnp.float32
    ).astype(jnp.bfloat16)
    d_query_rot, d_key_rot, d_value = attend_backward(
        query_rot, key_rot, value_low, d_att.reshape(head_shape), log_totals, segment, block_rows
    )
    rotate_pull = jax.vjp(lambda field_in: rotate(field_in, position), d_query_rot)[1]
    d_query = rotate_pull(d_query_rot)[0]
    d_key = rotate_pull(d_key_rot)[0]
    flat_shape = (group_rows, head_count * HEAD_DIM)
    d_qkv = jnp.stack(
        [d_query.reshape(flat_shape), d_key.reshape(flat_shape), d_value.reshape(flat_shape)],
        axis=1,
    ).astype(jnp.bfloat16)
    d_qkv_weight = jnp.einsum("rd,rpc->pdc", normed_one, d_qkv, preferred_element_type=jnp.float32)
    d_normed_one = sum_grads(d_qkv, qkv_weight, "rpc,pdc->rd", row_count)
    norm_pull_one = jax.vjp(layer_norm, residual, gain_one)[1]
    d_first, d_gain_one = norm_pull_one(d_normed_one)
    d_tokens = d_mid + d_first
    gain_sums = lax.psum((d_gain_one, d_gain_two), "tensor")
    shares = (
        lax.psum_scatter(gain_sums[0], "dp", scatter_dimension=0, tiled=True),
        lax.psum_scatter(d_qkv_weight, "dp", scatter_dimension=1, tiled=True),
        lax.psum_scatter(d_out, "dp", scatter_dimension=1, tiled=True),
        lax.psum_scatter(gain_sums[1], "dp", scatter_dimension=0, tiled=True),
        lax.psum_scatter(d_in, "dp", scatter_dimension=0, tiled=True),
        lax.psum_scatter(d_down, "dp", scatter_dimension=1, tiled=True),
    )
    return (output, d_tokens, shares[0], shares[1], shares[2], shares[3], shares[4], shares[5])


def solution(mesh):
    fast = mesh.shape["dp"] == 8 and mesh.shape["tensor"] == 4
    return jax.shard_map(
        local_fast if fast else local_plain,
        mesh=mesh,
        in_specs=(
            P(("dp", "tensor"), None),
            P(),
            P(),
            P("dp"),
            P(None, "dp", "tensor"),
            P("tensor", "dp"),
            P("dp"),
            P("dp", None, "tensor"),
            P("tensor", "dp"),
            P(("dp", "tensor"), None),
        ),
        out_specs=(
            P(("dp", "tensor"), None),
            P(("dp", "tensor"), None),
            P("dp"),
            P(None, "dp", "tensor"),
            P("tensor", "dp"),
            P("dp"),
            P("dp", None, "tensor"),
            P("tensor", "dp"),
        ),
        check_vma=False,
    )
```

```python
import functools

import jax
import jax.numpy as jnp
from jax import lax
from jax.experimental import pallas as pl
from jax.experimental.pallas import tpu as pltpu
from jax.sharding import PartitionSpec as P

HEAD_DIM = 64
SEQ_GRP = 4
rope_base = 160000.0
norm_eps = 1e-05
masked_fill = -1e30
MESH = pl.DeviceIdType.MESH
BF = jnp.bfloat16
F32 = jnp.float32

NT = (((1,), (1,)), ((), ()))
TN = (((0,), (0,)), ((), ()))


def place():
    dp = lax.axis_index("dp")
    z = lax.axis_index("tensor")
    c = lax.rem(dp, 2)
    x = lax.rem(lax.div(dp, 2), 2)
    y = lax.div(dp, 4)
    return dp, z, c, x, y


def flip(dp, bits, distance):
    out = dp
    for b, bit in enumerate(bits):
        if (distance >> b) & 1:
            out = out + (1 << b) - (2 << b) * bit
    return out


def remote(src, dst, send, recv, dev):
    return pltpu.make_async_remote_copy(
        src_ref=src, dst_ref=dst, send_sem=send, recv_sem=recv, device_id=dev, device_id_type=MESH
    )


def cols(start, size):
    return pl.ds(pl.multiple_of(start, size), size)


def greet(dp, z, bits):
    c = bits[0]
    barrier = pltpu.get_barrier_semaphore()
    peers = [(flip(dp, bits, d), z) for d in range(1, 8)]
    core = flip(dp, bits, 1)
    for k in range(1, 4):
        peers.append((dp, lax.rem(z + k, 4)))
        peers.append((core, lax.rem(z + k, 4)))
    for p in peers:
        pl.semaphore_signal(barrier, inc=1, device_id=p, device_id_type=MESH)
    pl.semaphore_wait(barrier, len(peers))


def norm_rows(v):
    mean = jnp.mean(v, axis=-1, keepdims=True)
    centered = v - mean
    var = jnp.mean(centered * centered, axis=-1, keepdims=True)
    rstd = lax.rsqrt(var + norm_eps)
    return centered * rstd, rstd


def turn(v, cs, sn):
    lane = lax.broadcasted_iota(jnp.int32, cs.shape, 1)
    low_half = lax.rem(lane, HEAD_DIM) < HEAD_DIM // 2
    parts = []
    for t in range(v.shape[1] // 128):
        piece = v[:, t * 128 : (t + 1) * 128]
        swapped = jnp.where(low_half, pltpu.roll(piece, 96, 1), pltpu.roll(piece, 32, 1))
        parts.append(piece * cs + swapped * sn)
    return jnp.concatenate(parts, axis=1)


def gain_row(gains, row):
    return jnp.concatenate([gains[p, row : row + 1, :] for p in range(8)], axis=1)


HID = 656
FF3 = 3 * HID
FROWS = ((0, HID), (HID, HID), (2 * HID, HID))
CUTS = ((0, 496), (496, 496), (992, 496), (1488, 480))
HALVES = tuple((m, o, n) for m in (2, 0, 1) for o, n in ((0, 336), (336, 320)))
NF = len(HALVES)
NU = NF + 2
INV_SQRT2 = 0.7071067811865476
INV_SQRT_2PI = 0.3989422804014327


def layer_kernel(
    lengths, seq_order, tok, wqkv, win, wmlp, wout, gains_in, cot,
    out_o, dtok_o, dwq_o, dwin_o, dwmlp_o, dwout_o, dg_o,
    gains, w3, cs, sn, segc, segr, q, k, v, lse, att, attn2, h1, wq, cot4,
    G, Wo, X1, h2a, dya, yr, acc, hidT, daT, duT, dX1, dsb, dr, dzs, dzr, usb, ur, uzs, uzr, dsend, datt, delta,
    dq, dk, dv, Hs, Hi, Hx, Rb, Ra, Z, Rbo, Rao, Zo, give, Wp, Wc, Wb, Wa, gz,
    us, ds, rb, ra, wr_s, wr_r, wx_s, wx_r, g_s, g_r, cx_s, cx_r, hop_s, hop_r,
    ou_s, o_r, oa_s, ob_s, of_s, oa_r, ob_r,
    fz_s, fz_r, pa_s, pb_s, pf_s, pa_r, pb_r, at_s, at_r,
    y_s, y_r, n_s, n_r, d_s, d_r, u_s, u_r, e_s, e_r, t_s, t_r,
    b_s, b_r, a_s, a_r, zu_s, z_r, fin_s, fin_r,
    hu_s, hd_s, hi_r, hx_r, wc_s, wc_r, wb_s, wb_r, wa_s, wa_r, gz_s, gz_r, lc,
):
    dp, z, c, x, y = place()
    bits = (c, x, y)
    core = flip(dp, bits, 1)
    px, py = flip(dp, bits, 2), flip(dp, bits, 4)
    a = (1 - c) * px + c * py
    b = (1 - c) * py + c * px
    chip, chip_a, chip_b = lax.div(dp, 2), lax.div(a, 2), lax.div(b, 2)
    chip_d = 3 - chip
    home = lax.div(z, 2)
    org = c == home
    zq = lax.rem(z, 2)
    zp = z + 1 - 2 * zq
    z2 = z + 2 - 4 * home
    end = (z == 0) | (z == 3)
    own = cols(c * 256, 256)
    other = cols((1 - c) * 256, 256)

    def block(core_bit, line_bit):
        return cols((2 * line_bit + core_bit) * 256, 256)

    ob, cb, zb, db = block(c, zq), block(1 - c, zq), block(c, 1 - zq), block(1 - c, 1 - zq)
    tall, vT, oT, dqkvT = Hs, Hx, acc.at[:, 0:256], h2a.at[0:768]
    dw4 = (dwin_o.at[0:HID], dwin_o.at[HID : 2 * HID], dwmlp_o)
    greet(dp, z, bits)

    def no(cond):
        return jnp.logical_not(cond)

    def tok_up(k_, h):
        ref = tall.at[z - k_, pl.ds(h * 128, 128)]
        src = tok.at[pl.ds(h * 128, 128)] if k_ == 0 else ref
        return remote(src, ref, us.at[k_, h], rb.at[k_ + 1, h], (dp, z + 1))

    def tok_down(k_, h):
        ref = tall.at[z + k_, pl.ds(h * 128, 128)]
        src = tok.at[pl.ds(h * 128, 128)] if k_ == 0 else ref
        return remote(src, ref, ds.at[k_, h], ra.at[k_ + 1, h], (dp, z - 1))

    def up_ok(k_):
        return (z >= k_) & (z < 3)

    def down_ok(k_):
        return (z + k_ <= 3) & (z > 0)

    for h in range(2):
        pl.when(up_ok(0))(lambda h=h: tok_up(0, h).start())
        pl.when(down_ok(0))(lambda h=h: tok_down(0, h).start())

    for d in range(1, 8):
        remote(gains_in, gains.at[dp], g_s.at[d], g_r.at[d], (flip(dp, bits, d), z)).start()
    own_rows = cols(dp * 128, 128)
    for j, d in enumerate((2, 4, 6)):
        remote(wqkv, wq.at[:, own_rows], wr_s.at[j], wr_r.at[j], (flip(dp, bits, d), z)).start()
    remote(wqkv, wq.at[:, own_rows], wx_s.at[3], wx_r.at[3], (core, z)).start()
    cot_copy = (
        remote(cot, cot4.at[ob], cx_s.at[0], cx_r.at[0], (core, z)),
        remote(cot, cot4.at[ob], cx_s.at[1], cx_r.at[1], (dp, zp)),
        remote(cot4.at[zb], cot4.at[zb], cx_s.at[2], cx_r.at[2], (core, z)),
    )
    cot_copy[0].start()
    cot_local = pltpu.make_async_copy(cot, cot4.at[ob], lc)
    cot_local.start()

    w3[0 : 2 * HID, :] = win[...]
    w3[2 * HID : FF3, :] = wmlp[...]
    lanes = cols(dp * 128, 128)
    hop = (
        remote(w3, G.at[:, lanes], hop_s.at[0], hop_r.at[0], (core, z)),
        remote(wout, Wo.at[zq, :, lanes], hop_s.at[1], hop_r.at[1], (core, z)),
    )

    @pl.when(no(org))
    def _():
        hop[1].start()
        hop[0].start()

    @pl.when(org)
    def _():
        G[:, lanes] = w3[...]
        Wo[zq, :, lanes] = wout[...]

    gains[dp] = gains_in[...]
    wq[:, own_rows, :] = wqkv[...]
    tall[z] = tok[...]
    cot_local.wait()

    def begin(cp):
        cp.start()

    def done(cp):
        cp.wait_send()

    def piece(u, where):
        r0, n = CUTS[u]
        return G.at[pl.ds(r0, n), cols(where * 256, 256)]

    def plane_a(u):
        return remote(piece(u, chip), piece(u, chip), pa_s.at[u], pa_r.at[u], (a, z))

    def plane_b(u):
        return remote(piece(u, chip), piece(u, chip), pb_s.at[u], pb_r.at[0, u], (b, z))

    def plane_f(u):
        return remote(piece(u, chip_a), piece(u, chip_a), pf_s.at[u], pb_r.at[1, u], (b, z))

    def leap(u):
        return remote(piece(u, chip), piece(u, chip), fz_s.at[u], fz_r.at[u], (dp, z2))

    def spread(u):
        plane_a(u).start()
        plane_b(u).start()

    def across(u):
        ref = piece(u, chip_a)
        remote(ref, ref, pa_s.at[u], pa_r.at[u], (a, z)).wait_recv()
        plane_f(u).start()

    def land(u):
        leap(u).wait_recv()
        spread(u)

    near = (1 - c) * lax.div(z + 2, 3) + c * lax.div(z, 3)
    far = 1 - near

    def opiece(qi, where):
        return Wo.at[qi, :, cols(where * 256, 256)]

    def ofar(k_):
        ref = opiece(zq, chip)
        return remote(ref, ref, ou_s.at[k_], o_r.at[zq], (dp, lax.rem(z + k_, 4)))

    def oplane(qi):
        ref, ref_a = opiece(qi, chip), opiece(qi, chip_a)
        return (
            remote(ref, ref, oa_s.at[qi], oa_r.at[qi], (a, z)),
            remote(ref, ref, ob_s.at[qi], ob_r.at[0, qi], (b, z)),
            remote(ref_a, ref_a, of_s.at[qi], ob_r.at[1, qi], (b, z)),
        )

    def ospread(qi):
        cps = oplane(qi)
        cps[0].start()
        cps[1].start()

    def oland(qi):
        ref = opiece(qi, chip)
        remote(ref, ref, ou_s.at[1], o_r.at[qi], (core, z)).wait_recv()
        ospread(qi)

    def oacross(qi):
        ref = opiece(qi, chip_a)
        remote(ref, ref, oa_s.at[qi], oa_r.at[qi], (a, z)).wait_recv()
        oplane(qi)[2].start()

    ends, starts, total = [], [], 0
    for j in range(SEQ_GRP):
        ends.append(total)
        total = total + lengths[seq_order[dp * SEQ_GRP + j]]
    for dst, shape, axis in ((segc, (1024, 128), 0), (segr, (8, 1024), 1)):
        row = lax.broadcasted_iota(jnp.int32, shape, axis)
        seg = jnp.zeros(shape, F32)
        start = jnp.zeros(shape, jnp.int32)
        for j in range(1, SEQ_GRP):
            passed = row >= ends[j]
            seg = jnp.where(passed, float(j), seg)
            start = jnp.where(passed, ends[j], start)
        dst[...] = seg
        if axis == 0:
            angle = (row - start).astype(F32) * gains_in[2:3, :]
            cs[...] = jnp.cos(angle)
            sn[...] = jnp.sin(angle) * gains_in[3:4, :]

    for d in range(1, 8):
        p = flip(dp, bits, d)
        remote(gains_in, gains.at[p], g_s.at[d], g_r.at[d], (p, z)).wait_recv()

    @pl.when(org)
    def _():
        remote(wout, Wo.at[zq, :, cols(core * 128, 128)], hop_s.at[1], hop_r.at[1], (core, z)).wait_recv()
        ospread(near)
        remote(w3, G.at[:, cols(core * 128, 128)], hop_s.at[0], hop_r.at[0], (core, z)).wait_recv()
        for u in range(4):
            spread(u)

    for j, d in enumerate((2, 4, 6)):
        p = flip(dp, bits, d)
        rows = wq.at[:, cols(p * 128, 128)]
        remote(wqkv, rows, wr_s.at[j], wr_r.at[j], (p, z)).wait_recv()
        remote(rows, rows, wx_s.at[j], wx_r.at[j], (core, z)).start()
    for j, d in enumerate((3, 5, 7, 1)):
        p = flip(dp, bits, d)
        remote(wqkv, wq.at[:, cols(p * 128, 128)], wx_s.at[j], wx_r.at[j], (core, z)).wait_recv()

    gain1, gain2 = gain_row(gains, 0), gain_row(gains, 1)

    def project(s):
        base = s * 256

        @pl.loop(0, 8)
        def _(r):
            xhat, _r = norm_rows(tall[s, pl.ds(pl.multiple_of(r * 32, 32), 32), :].astype(F32))
            h1[pl.ds(pl.multiple_of(base + r * 32, 32), 32), :] = (xhat * gain1).astype(BF)

        rows = pl.ds(pl.multiple_of(base, 256), 256)
        hb = h1[rows, :]
        cb, sb = cs[rows, :], sn[rows, :]
        for p, dst in enumerate((q, k, v)):
            r = jnp.dot(hb, wq[p], preferred_element_type=F32)
            if p < 2:
                r = turn(r, cb, sb)
            if p == 0:
                r = r * (HEAD_DIM**-0.5)
            dst[rows, :] = r.astype(BF)

    for k_ in range(4):
        if k_ > 0:
            below, above = z - k_ >= 0, z + k_ <= 3
            for h in range(2):

                @pl.when(below)
                def _(k_=k_, h=h):
                    ref = tall.at[z - k_, pl.ds(h * 128, 128)]
                    remote(ref, ref, us.at[k_, h], rb.at[k_, h], (core, z)).wait_recv()
                    if k_ < 3:
                        pl.when(up_ok(k_))(lambda: tok_up(k_, h).start())

                @pl.when(above)
                def _(k_=k_, h=h):
                    ref = tall.at[z + k_, pl.ds(h * 128, 128)]
                    remote(ref, ref, ds.at[k_, h], ra.at[k_, h], (core, z)).wait_recv()
                    if k_ < 3:
                        pl.when(down_ok(k_))(lambda: tok_down(k_, h).start())

        @pl.loop(0, 2)
        def _(t, k_=k_):
            s = z - k_ + 2 * k_ * t
            pl.when((s >= 0) & (s <= 3) & ((k_ > 0) | (t == 0)))(lambda: project(s))

        if k_ == 1:

            @pl.when(org)
            def _():
                oacross(near)
                for u in range(4):
                    across(u)

        if k_ == 2:

            @pl.when(org & end)
            def _():
                for n in range(1, 4):
                    ofar(n).start()
                for u in range(4):
                    leap(u).start()

    for s in range(4):
        vT[:, s * 256 : (s + 1) * 256] = v[s * 256 : (s + 1) * 256, :].T
    head_of = lax.div(lax.broadcasted_iota(jnp.int32, (256, 256), 1), HEAD_DIM)

    def attend(i):
        rows = pl.ds(pl.multiple_of(i * 256, 256), 256)
        qb = q[rows, :]
        seg_q = segr[0:1, rows]
        heads = range(4)
        qh = [jnp.where(head_of == h, qb, jnp.zeros((), BF)) for h in heads]
        top = [jnp.full((1, 256), masked_fill, F32) for h in heads]
        tot = [jnp.zeros((1, 256), F32) for h in heads]
        out = [jnp.zeros((HEAD_DIM, 256), F32) for h in heads]
        for kc in range(4):
            keys = slice(kc * 256, kc * 256 + 256)
            kb = k[keys, :]
            seg_k = segc[keys, :]
            same = jnp.concatenate([seg_k, seg_k], axis=1) == seg_q
            for h in heads:
                s = lax.dot_general(kb, qh[h], NT, preferred_element_type=F32)
                s = jnp.where(same, s, masked_fill)
                new = jnp.maximum(top[h], jnp.max(s, axis=0, keepdims=True))
                p = jnp.exp(s - new)
                keep = jnp.exp(top[h] - new)
                tot[h] = tot[h] * keep + jnp.sum(p, axis=0, keepdims=True)
                vh = vT[h * HEAD_DIM : (h + 1) * HEAD_DIM, keys]
                out[h] = out[h] * keep + jnp.dot(vh, p.astype(BF), preferred_element_type=F32)
                top[h] = new
        for h in heads:
            oT[h * HEAD_DIM : (h + 1) * HEAD_DIM, :] = out[h] * (1.0 / tot[h])
            lse[h, i] = jnp.broadcast_to(top[h] + jnp.log(tot[h]), (8, 256))
        att[rows, :] = oT[...].T.astype(BF)

    def att_slot(src_core, q):
        return attn2.at[cols(src_core * 256, 256), cols(q * 256, 256)]

    def att_copy(n, i):
        rows = pl.ds(pl.multiple_of(i * 256, 256), 256)
        return remote(
            att.at[rows, :], att_slot(c, zq), at_s.at[n], at_r.at[c, zq], (2 * chip + home, i)
        )

    @pl.loop(0, 4)
    def _(n):
        i = lax.rem(z + 1 + n, 4)
        attend(i)
        for m in range(4):

            @pl.when((n == m) & ((m < 3) | no(org)))
            def _(m=m):
                att_copy(m, i).start()

        @pl.when((n == 3) & org)
        def _():
            attn2[own, cols(zq * 256, 256)] = att[pl.ds(pl.multiple_of(z * 256, 256), 256), :]

        @pl.when((n == 0) & org & no(end))
        def _():
            for m in range(1, 4):
                ofar(m).start()
            for u in range(4):
                leap(u).start()

        pl.when(n == 1)(lambda: cot_copy[1].start())

    @pl.when(org)
    def _():
        oland(far)
        oacross(far)

    @pl.when(no(org))
    def _():
        land(0)
        oland(near)
        oland(far)
        for u in range(1, 4):
            land(u)
        oacross(near)
        oacross(far)
        across(0)

    def late_across(u):
        pl.when(no(org))(lambda: across(u))

    for k_ in range(3):
        for h in range(2):
            pl.when(up_ok(k_))(lambda k_=k_, h=h: tok_up(k_, h).wait_send())
            pl.when(down_ok(k_))(lambda k_=k_, h=h: tok_down(k_, h).wait_send())
    for src in range(2):
        for qi in range(2):
            mine_too = (c == src) & (z == 2 * c + qi)

            @pl.when(no(mine_too))
            def _(src=src, qi=qi):
                slot = att_slot(src, qi)
                remote(slot, slot, at_s.at[0], at_r.at[src, qi], (core, z)).wait_recv()

    for qi in range(2):
        for w, where in enumerate((chip_b, chip_d)):
            ref = opiece(qi, where)
            remote(ref, ref, ob_s.at[qi], ob_r.at[w, qi], (core, z)).wait_recv()

    def out_proj(rows):
        return sum(
            jnp.dot(attn2[rows, qi * 256 : (qi + 1) * 256], Wo[qi], preferred_element_type=F32) for qi in range(2)
        )

    acc[...] = out_proj(other)
    y_copy = remote(acc, yr, y_s, y_r, (core, z))
    y_copy.start()
    late_across(1)
    X1[...] = tok[...].astype(F32) + out_proj(own)
    y_copy.wait()

    def chunk(r):
        return pl.ds(pl.multiple_of(r * 32, 32), 32)

    def own_chunk(r):
        return pl.ds(pl.multiple_of(c * 256 + r * 32, 32), 32)

    def block_chunk(r):
        return pl.ds(pl.multiple_of((2 * zq + c) * 256 + r * 32, 32), 32)

    @pl.loop(0, 8)
    def _(r):
        x1 = X1[chunk(r), :] + yr[chunk(r), :]
        X1[chunk(r), :] = x1
        xhat, _r = norm_rows(x1)
        h2a[block_chunk(r), :] = (xhat * gain2).astype(BF)

    h_copy = (
        remote(h2a.at[ob], h2a.at[ob], n_s.at[0], n_r.at[0], (core, z)),
        remote(h2a.at[ob], h2a.at[ob], n_s.at[1], n_r.at[1], (dp, zp)),
        remote(h2a.at[zb], h2a.at[zb], n_s.at[2], n_r.at[2], (core, z)),
    )
    h_copy[1].start()
    h_copy[0].start()
    late_across(2)
    late_across(3)
    remote(cot, cot4.at[zb], cx_s.at[1], cx_r.at[1], (dp, zp)).wait_recv()
    cot_copy[2].start()
    remote(cot, cot4.at[cb], cx_s.at[0], cx_r.at[0], (core, z)).wait_recv()
    remote(cot, cot4.at[db], cx_s.at[2], cx_r.at[2], (core, z)).wait_recv()
    for u in range(4):
        for w, where in enumerate((chip_b, chip_d)):
            ref = piece(u, where)
            remote(ref, ref, pb_s.at[u], pb_r.at[w, u], (core, z)).wait_recv()
    remote(h2a.at[zb], h2a.at[zb], n_s.at[1], n_r.at[1], (dp, zp)).wait_recv()
    h_copy[2].start()
    remote(h2a.at[cb], h2a.at[cb], n_s.at[0], n_r.at[0], (core, z)).wait_recv()

    def tile(r0, n, tokens):
        h2 = h2a[tokens, :]
        act = lax.dot_general(G[r0 : r0 + n, :], h2, NT, preferred_element_type=F32)
        up = lax.dot_general(G[HID + r0 : HID + r0 + n, :], h2, NT, preferred_element_type=F32)
        dh = lax.dot_general(
            G[2 * HID + r0 : 2 * HID + r0 + n, :], cot4[tokens, :], NT, preferred_element_type=F32
        )
        Phi = 0.5 + 0.5 * lax.erf(act * INV_SQRT2)
        phi = jnp.exp(-0.5 * act * act) * INV_SQRT_2PI
        gel = act * Phi
        rr = slice(r0, r0 + n)
        hidT[rr, tokens] = (gel * up).astype(BF)
        daT[rr, tokens] = (dh * up * (Phi + act * phi)).astype(BF)
        duT[rr, tokens] = (dh * gel).astype(BF)

    @pl.loop(0, 2)
    def _(t):
        there = lax.rem(zq + t, 2)

        @pl.when(t == 1)
        def _():
            remote(h2a.at[db], h2a.at[db], n_s.at[2], n_r.at[2], (core, z)).wait_recv()

        for r0, n in ((0, 224), (224, 224), (448, 208)):
            tile(r0, n, cols(there * 512, 512))

    def tn(lhs, rhs):
        return lax.dot_general(lhs, rhs, TN, preferred_element_type=F32)

    def f_rows(m):
        return pl.ds(FROWS[m][0], HID)

    def d_norm(rows, hc):
        return tn(daT[:, rows], G[f_rows(0), hc]) + tn(duT[:, rows], G[f_rows(1), hc])

    def mlp_out(rows, hc):
        return tn(hidT[:, rows], G[f_rows(2), hc])

    def quad(term, sb, got, zs, zgot, ss, rs):
        halves = (slice(0, 512), slice(512, 1024))
        copies = (
            remote(sb.at[0], got.at[0], ss.at[0], rs.at[0], (core, z)),
            remote(sb.at[1], got.at[1], ss.at[1], rs.at[1], (core, z)),
            remote(zs, zgot, ss.at[2], rs.at[2], (dp, zp)),
        )
        for j, rows in enumerate((db, cb)):
            for hc in halves:
                sb[j, :, hc] = term(rows, hc).astype(BF)
            copies[j].start()
        copies[0].wait_recv()
        for hc in halves:
            zs[:, hc] = (term(zb, hc) + got[0, :, hc].astype(F32)).astype(BF)
        copies[2].start()
        return copies

    def keep(term, dst, plus=None):
        for hc in (slice(0, 512), slice(512, 1024)):
            r = term(ob, hc)
            dst[:, hc] = r if plus is None else r + plus[:, hc]

    def grads(m):
        lhs, rhs = ((daT, h2a), (duT, h2a), (hidT, cot4))[m]

        @pl.loop(0, 4)
        def _(t):
            tc = cols(t * 256, 256)
            G[f_rows(m), tc] = jnp.dot(lhs[...], rhs[:, tc], preferred_element_type=F32).astype(BF)

    def rows_of(e):
        m, o, n = HALVES[e]
        return pl.ds(FROWS[m][0] + o, n)

    def part(e, where):
        if e < NF:
            return G.at[rows_of(e), cols(where * 256, 256)]
        return opiece(e - NF, where)

    def from_b(e, slot):
        return Rb.at[slot, rows_of(e)] if e < NF else Rbo.at[slot, e - NF]

    def from_a(e):
        return Ra.at[rows_of(e)] if e < NF else Rao.at[e - NF]

    def unit_b(e, slot):
        src = part(e, chip_b if slot == 0 else chip_d)
        return remote(src, from_b(e, slot), b_s.at[slot, e], b_r.at[slot, e], (b, z))

    def unit_a(e):
        return remote(part(e, chip_a), from_a(e), a_s.at[e], a_r.at[e], (a, z))

    def send_b(e):
        unit_b(e, 1).start()
        unit_b(e, 0).start()

    def stage1(e):
        unit_b(e, 1).wait_recv()
        ref = part(e, chip_a)
        ref[...] = (ref[...].astype(F32) + from_b(e, 1)[...].astype(F32)).astype(BF)
        unit_a(e).start()

    def unit_z(e):
        return remote(part(e, chip), Z.at[rows_of(e)], zu_s.at[e], z_r.at[0, e], (dp, z2))

    def unit_o(e):
        t = 2 * c + e - NF
        slot = lax.rem(z - t + 4, 4) - 1
        return remote(part(e, chip), Zo.at[slot], zu_s.at[e], z_r.at[slot, e], (dp, t))

    def stage2(e):
        unit_b(e, 0).wait_recv()
        unit_a(e).wait_recv()
        ref = part(e, chip)
        ref[...] = (
            ref[...].astype(F32) + from_b(e, 0)[...].astype(F32) + from_a(e)[...].astype(F32)
        ).astype(BF)
        if e < NF:
            pl.when(no(org))(lambda: unit_z(e).start())
        else:
            pl.when(z != 2 * c + e - NF)(lambda: unit_o(e).start())

    def line_wait(e, slot):
        remote(Zo.at[slot], Zo.at[slot], zu_s.at[e], z_r.at[slot, e], (core, z)).wait_recv()

    def final(e):
        if e < NF:
            m, o, n = HALVES[e]
            return e, give.at[rows_of(e)], dw4[m].at[pl.ds(o, n)]
        return NF, give.at[FF3 : FF3 + 256], dwout_o

    def stage4(e):
        here = org if e < NF else z == 2 * c + e - NF

        @pl.when(here)
        def _():
            slot, gift, dst = final(e)
            if e < NF:
                unit_z(e).wait_recv()
            for who, ref in ((c, dst), (1 - c, gift)):
                ref[...] = part(e, chip)[:, cols(who * 128, 128)].astype(F32)

            def take(got):
                for who, ref in ((c, dst), (1 - c, gift)):
                    ref[...] = ref[...] + got[:, cols(who * 128, 128)].astype(F32)

            def line_take(where):
                line_wait(e, where)
                take(Zo.at[where])

            if e < NF:
                take(Z.at[rows_of(e)])
            else:
                for slot_ in range(3):
                    line_take(slot_)
            remote(gift, dst, fin_s.at[slot], fin_r.at[slot], (core, z)).start()

    def tick(t):
        for lag, step in ((0, stage1), (1, stage2), (4, stage4)):
            if 0 <= t - lag < NU:
                step(t - lag)

    d_copies = quad(d_norm, dsb, dr, dzs, dzr, d_s, d_r)
    keep(d_norm, dX1)
    u_copies = quad(mlp_out, usb, ur, uzs, uzr, u_s, u_r)
    keep(mlp_out, dtok_o, X1)
    for u in range(4):
        plane_a(u).wait_send()
        plane_b(u).wait_send()
        plane_f(u).wait_send()
        pl.when(org)(lambda u=u: leap(u).wait_send())

    def ff_grads(m):
        grads(m)
        for e in range(NF):
            if HALVES[e][0] == m:
                send_b(e)

    ff_grads(2)
    ff_grads(0)
    ff_grads(1)
    d_copies[1].wait_recv()
    d_copies[2].wait_recv()

    @pl.loop(0, 8)
    def _(r):
        dh2 = dX1[chunk(r), :] + dr[1, chunk(r), :].astype(F32) + dzr[chunk(r), :].astype(F32)
        xhat, rstd = norm_rows(X1[chunk(r), :])
        e2 = dh2 * gain2
        m1 = jnp.mean(e2, axis=-1, keepdims=True)
        m2 = jnp.mean(e2 * xhat, axis=-1, keepdims=True)
        dx = cot4[block_chunk(r), :].astype(F32) + rstd * (e2 - m1 - xhat * m2)
        dX1[chunk(r), :] = dx
        dya[own_chunk(r), :] = dx.astype(BF)

    e_copy = remote(dya.at[own], dya.at[own], e_s, e_r, (core, z))
    e_copy.start()
    tick(0)
    e_copy.wait()
    for qi in range(2):
        dsend[qi] = lax.dot_general(dya[...], Wo[qi], NT, preferred_element_type=F32).astype(BF)

    def att_back(c0, qi):
        dst = datt.at[cols(z * 256, 256)]
        return remote(
            dsend.at[qi, pl.ds(c0 * 256, 256)], dst, t_s.at[c0, qi], t_r.at[z], (2 * chip + c0, 2 * c + qi)
        )

    def is_self(c0, qi):
        return (c == c0) & (z == 2 * c + qi)

    for c0 in range(2):
        for qi in range(2):
            pl.when(no(is_self(c0, qi)))(lambda c0=c0, qi=qi: att_back(c0, qi).start())

            @pl.when(is_self(c0, qi))
            def _(c0=c0, qi=qi):
                datt[cols(z * 256, 256), :] = dsend[qi, c0 * 256 : (c0 + 1) * 256, :]

    for n in range(1, 4):
        pl.when(org)(lambda n=n: ofar(n).wait_send())
    for qi in range(2):
        for cp in oplane(qi):
            cp.wait_send()

        @pl.loop(0, 4)
        def _(t, qi=qi):
            tc = cols(t * 256, 256)
            Wo[qi, :, tc] = tn(attn2[:, qi * 256 : (qi + 1) * 256], dya[:, tc]).astype(BF)

        send_b(NF + qi)
    tick(1)
    tick(2)
    for cp in h_copy:
        cp.wait_send()
    dq[...] = jnp.zeros_like(dq)
    dk[...] = jnp.zeros_like(dk)
    dv[...] = jnp.zeros_like(dv)
    for i in range(4):

        @pl.when(no(org & (z == i)))
        def _(i=i):
            ref = datt.at[pl.ds(i * 256, 256)]
            remote(ref, ref, t_s.at[0, 0], t_r.at[i], (core, z)).wait_recv()

    @pl.loop(0, 4)
    def _(i):
        rows = pl.ds(pl.multiple_of(i * 256, 256), 256)
        t = (datt[rows, :].astype(F32) * att[rows, :].astype(F32)).T
        for h in range(4):
            s = jnp.sum(t[h * 64 : (h + 1) * 64, :], axis=0, keepdims=True)
            delta[h, i] = jnp.broadcast_to(s, (8, 256))

    def block_order(l):
        inner = lax.div(z * (3 - z), 2)
        base = inner * jnp.minimum(l, 1) * (lax.rem(l + 1, 3) + 1) + (1 - inner) * l
        return (1 - home) * (3 - base) + home * base

    def pair(i, j):
        ri = pl.ds(pl.multiple_of(i * 256, 256), 256)
        rj = pl.ds(pl.multiple_of(j * 256, 256), 256)

        kj, vj, qi_, dai = k[rj, :], v[rj, :], q[ri, :], datt[ri, :]
        seg_k = segc[rj, :]
        same = jnp.concatenate([seg_k, seg_k], axis=1) == segr[0:1, ri]
        none = jnp.zeros((), BF)
        dvs, dks, dqs = [], [], []
        for h in range(4):
            mine = head_of == h
            qh, dah = jnp.where(mine, qi_, none), jnp.where(mine, dai, none)
            s = lax.dot_general(kj, qh, NT, preferred_element_type=F32)
            p = jnp.exp(jnp.where(same, s, masked_fill) - lse[h, i, 0:1, :])
            dp_ = lax.dot_general(vj, dah, NT, preferred_element_type=F32)
            dsc = (p * (dp_ - delta[h, i, 0:1, :])).astype(BF)
            dvs.append(jnp.dot(p.astype(BF), dah, preferred_element_type=F32))
            dks.append(jnp.dot(dsc, qh, preferred_element_type=F32))
            dqs.append(tn(dsc, jnp.where(mine, kj, none)))
        dv[rj, :] = dv[rj, :] + (dvs[0] + dvs[1] + dvs[2] + dvs[3])
        dk[rj, :] = dk[rj, :] + (dks[0] + dks[1] + dks[2] + dks[3])
        dq[ri, :] = dq[ri, :] + (dqs[0] + dqs[1] + dqs[2] + dqs[3])

    def quarter(t):
        return pl.ds(pl.multiple_of(t * 64, 64), 64)

    def h_up(i, t, last):
        if last:
            return remote(Hs.at[i, quarter(t)], Hx.at[quarter(t)], hu_s.at[i, t], hx_r.at[t], (dp, z + 1))
        return remote(Hs.at[i, quarter(t)], Hi.at[i, quarter(t)], hu_s.at[i, t], hi_r.at[i, t], (dp, z + 1))

    def h_down(i, t):
        return remote(Hs.at[i, quarter(t)], Hi.at[i, quarter(t)], hd_s.at[i, t], hi_r.at[i, t], (dp, z - 1))

    def h_inward(i, t, act):
        pl.when(z > i)(lambda: act(h_down(i, t)))
        pl.when(z + 1 == i)(lambda: act(h_up(i, t, True)))
        pl.when(z + 1 < i)(lambda: act(h_up(i, t, False)))

    def h_wait(i, t):
        ref = Hi.at[i, quarter(t)]
        remote(ref, ref, hd_s.at[i, t], hi_r.at[i, t], (core, z)).wait_recv()

    def h_mid(i, depth):
        mid = ((z > i) & (z == 3 - depth)) | ((z < i) & (z == depth))

        @pl.when(mid)
        def _():
            @pl.loop(0, 4)
            def _(t):
                h_wait(i, t)
                Hs[i, quarter(t), :] = (
                    Hs[i, quarter(t), :].astype(F32) + Hi[i, quarter(t), :].astype(F32)
                ).astype(BF)
                h_inward(i, t, begin)

    def finish(i):
        rows = pl.ds(pl.multiple_of(i * 256, 256), 256)
        cb, sb = cs[rows, :], -sn[rows, :]
        low = (
            turn(dq[rows, :] * (HEAD_DIM**-0.5), cb, sb).astype(BF),
            turn(dk[rows, :], cb, sb).astype(BF),
            dv[rows, :].astype(BF),
        )
        for p in range(3):
            dqkvT[p * 256 : (p + 1) * 256, rows] = low[p].T
        for half in range(2):
            hc = slice(half * 512, half * 512 + 512)
            dh = sum(
                lax.dot_general(low[p], wq[p, hc, :], NT, preferred_element_type=F32) for p in range(3)
            )
            Hs[i, :, hc] = dh.astype(BF)

            @pl.when(z == i)
            def _(dh=dh, hc=hc):
                acc[:, hc] = dh

        @pl.when(((z == 3) & (z > i)) | ((z == 0) & (z < i)))
        def _():
            for t in range(4):
                h_inward(i, t, begin)


    slots = {0: [3], 2: [4], 5: [5], 8: [6], 11: [7], 14: [8]}
    h_slots = {12: [(0, 1), (3, 1)]}

    @pl.loop(0, 16)
    def _(n):
        def past(v):
            return lax.div(n + 16 - v, 16)

        ph = past(7) + past(12) + past(15)
        t = n - 7 * past(7) - 5 * past(12) - 3 * past(15)
        left = 4 - ph
        over = lax.div(t, left)
        li = ph + over * (t - left + 1)
        lj = ph + (1 - over) * t
        pair(block_order(li), block_order(lj))
        pl.when((n == 6) | (n == 11) | (n == 14) | (n == 15))(lambda: finish(block_order(ph)))
        for s in range(16):
            todo = [lambda t=t: tick(t) for t in slots.get(s, ())]
            todo += [lambda i=i, d=d: h_mid(i, d) for i, d in h_slots.get(s, ())]

            @pl.when(n == s)
            def _(todo=todo):
                for op in todo:
                    op()

    @pl.loop(0, 4)
    def _(t):
        tc = cols(t * 256, 256)
        Wp[:, tc] = jnp.dot(dqkvT[...], h1[:, tc], preferred_element_type=F32).astype(BF)

    def core_copy(w):
        return remote(
            Wp.at[:, cols(w * 256 + (1 - c) * 128, 128)], Wc.at[w], wc_s.at[w], wc_r.at[w], (core, z)
        )

    for w in range(4):
        core_copy(w).start()
    h_mid(3, 2)
    h_mid(0, 2)
    u_copies[1].wait_recv()
    u_copies[2].wait_recv()
    out_o[...] = (dtok_o[...] + ur[1].astype(F32) + uzr[...].astype(F32)).astype(BF)

    def both(w):
        Wc[w] = (Wc[w].astype(F32) + Wp[:, cols(w * 256 + c * 128, 128)].astype(F32)).astype(BF)

    for w in range(4):
        core_copy(w).wait_recv()
    both(chip_d)
    both(chip_b)
    wb_copy = [
        remote(Wc.at[where], Wb.at[slot], wb_s.at[slot], wb_r.at[slot], (b, z))
        for slot, where in ((0, chip_b), (1, chip_d))
    ]
    wb_copy[1].start()
    wb_copy[0].start()
    both(chip_a)
    both(chip)
    wa_copy = remote(Wc.at[chip_a], Wa, wa_s, wa_r, (a, z))
    h_mid(2, 1)
    h_mid(1, 1)
    tick(9)
    wb_copy[1].wait_recv()
    Wc[chip_a] = (Wc[chip_a].astype(F32) + Wb[1].astype(F32)).astype(BF)
    wa_copy.start()

    for t in range(4):
        ref = Hx.at[quarter(t)]
        pl.when(z < 3)(lambda t=t: h_wait(z, t))
        pl.when(z > 0)(lambda t=t, ref=ref: remote(ref, ref, hu_s.at[0, t], hx_r.at[t], (core, z)).wait_recv())
    has_above, has_below = z < 3, z > 0

    @pl.when(has_above)
    def _():
        acc[...] = acc[...] + Hi[z].astype(F32)

    @pl.when(has_below)
    def _():
        acc[...] = acc[...] + Hx[...].astype(F32)

    @pl.loop(0, 8)
    def _(r):
        xhat, rstd = norm_rows(tok[chunk(r), :].astype(F32))
        e1 = acc[chunk(r), :] * gain1
        m1 = jnp.mean(e1, axis=-1, keepdims=True)
        m2 = jnp.mean(e1 * xhat, axis=-1, keepdims=True)
        dtok_o[chunk(r), :] = dX1[chunk(r), :] + rstd * (e1 - m1 - xhat * m2)

    wb_copy[0].wait_recv()
    wa_copy.wait_recv()
    total = Wc[chip].astype(F32) + Wb[0].astype(F32) + Wa[...].astype(F32)
    dot_one = jnp.zeros((1, 128), F32)
    for p in range(3):
        piece = total[p * 256 : (p + 1) * 256, :]
        dwq_o[p] = piece.T
        dot_one = dot_one + jnp.sum(piece * wqkv[p].T.astype(F32), axis=0, keepdims=True)
    for t in range(10, NU + 4):
        tick(t)
    for e in range(NF + 1):

        @pl.when(no(org))
        def _(e=e):
            slot, _, ref = final(e)
            remote(ref, ref, fin_s.at[slot], fin_r.at[slot], (core, z)).wait_recv()

    part_two = jnp.sum(dwin_o[...] * w3[0 : 2 * HID, :].astype(F32), axis=0, keepdims=True)
    gz[z, 0:1, :] = dot_one / gains[dp, 0:1, :]
    gz[z, 1:2, :] = part_two / gains[dp, 1:2, :]
    gz[z, 2:8, :] = jnp.zeros((6, 128), F32)
    gain_copy = [
        remote(gz.at[z], gz.at[z], gz_s.at[n], gz_r.at[z], (dp, lax.rem(z + n, 4))) for n in range(1, 4)
    ]
    for cp in gain_copy:
        cp.start()
    for n in range(1, 4):
        o = lax.rem(z + n, 4)
        remote(gz.at[o], gz.at[o], gz_s.at[n], gz_r.at[o], (core, z)).wait_recv()
    dg_o[...] = gz[0] + gz[1] + gz[2] + gz[3]

    for cp in gain_copy:
        cp.wait_send()
    for w in range(4):
        core_copy(w).wait_send()
    wb_copy[0].wait_send()
    wb_copy[1].wait_send()
    wa_copy.wait_send()
    for i in range(4):
        for t in range(4):
            h_inward(i, t, done)
    for c0 in range(2):
        for qi in range(2):
            pl.when(no(is_self(c0, qi)))(lambda c0=c0, qi=qi: att_back(c0, qi).wait_send())
    for cp in d_copies + u_copies:
        cp.wait_send()
    for e in range(NU):
        unit_b(e, 0).wait_send()
        unit_b(e, 1).wait_send()
        unit_a(e).wait_send()
        if e < NF:
            pl.when(no(org))(lambda e=e: unit_z(e).wait_send())
        else:
            pl.when(z != 2 * c + e - NF)(lambda e=e: unit_o(e).wait_send())

        @pl.when(org if e < NF else z == 2 * c + e - NF)
        def _(e=e):
            slot, gift, dst = final(e)
            remote(gift, dst, fin_s.at[slot], fin_r.at[slot], (core, z)).wait_send()

    for d in range(1, 8):
        remote(gains_in, gains.at[dp], g_s.at[d], g_r.at[d], (core, z)).wait_send()
    for j in range(3):
        remote(wqkv, wq.at[:, own_rows], wr_s.at[j], wr_r.at[j], (core, z)).wait_send()
    for j in range(4):
        remote(wqkv, wq.at[:, own_rows], wx_s.at[j], wx_r.at[j], (core, z)).wait_send()
    for cp in hop:
        pl.when(no(org))(lambda cp=cp: cp.wait_send())
    for cp in cot_copy:
        cp.wait_send()
    for n in range(3):
        att_copy(n, lax.rem(z + 1 + n, 4)).wait_send()
    pl.when(no(org))(lambda: att_copy(3, z).wait_send())


def run_layer(*args):
    V = pl.BlockSpec(memory_space=pltpu.VMEM)
    S = pl.BlockSpec(memory_space=pltpu.SMEM)
    dma = pltpu.SemaphoreType.DMA
    s = jax.ShapeDtypeStruct
    vm = pltpu.VMEM
    return pl.pallas_call(
        layer_kernel,
        out_shape=(
            s((256, 1024), BF), s((256, 1024), F32), s((3, 128, 256), F32), s((2 * HID, 128), F32),
            s((HID, 128), F32), s((256, 128), F32), s((8, 128), F32),
        ),
        in_specs=[S, S] + [V] * 6 + [pl.BlockSpec(memory_space=pl.ANY)],
        out_specs=[V] * 7,
        scratch_shapes=[
            vm((8, 8, 128), F32), vm((FF3, 128), BF), vm((1024, 128), F32), vm((1024, 128), F32),
            vm((1024, 128), F32), vm((8, 1024), F32), vm((1024, 256), BF), vm((1024, 256), BF),
            vm((1024, 256), BF), vm((4, 4, 8, 256), F32), vm((1024, 256), BF), vm((512, 512), BF),
            vm((1024, 1024), BF), vm((3, 1024, 256), BF), vm((1024, 1024), BF),
            vm((FF3, 1024), BF), vm((2, 256, 1024), BF), vm((256, 1024), F32), vm((1024, 1024), BF), vm((512, 1024), BF),
            vm((256, 1024), F32), vm((256, 1024), F32), vm((HID, 1024), BF), vm((HID, 1024), BF),
            vm((HID, 1024), BF), vm((256, 1024), F32),
            vm((2, 256, 1024), BF), vm((2, 256, 1024), BF), vm((256, 1024), BF), vm((256, 1024), BF),
            vm((2, 256, 1024), BF), vm((2, 256, 1024), BF), vm((256, 1024), BF), vm((256, 1024), BF),
            vm((2, 512, 256), BF), vm((1024, 256), BF), vm((4, 4, 8, 256), F32),
            vm((1024, 256), F32), vm((1024, 256), F32), vm((1024, 256), F32),
            vm((4, 256, 1024), BF), vm((4, 256, 1024), BF), vm((256, 1024), BF),
            vm((2, FF3, 256), BF), vm((FF3, 256), BF), vm((FF3, 256), BF),
            vm((2, 2, 256, 256), BF), vm((2, 256, 256), BF), vm((3, 256, 256), BF), vm((FF3 + 256, 128), F32),
            vm((768, 1024), BF), vm((4, 768, 128), BF), vm((2, 768, 128), BF), vm((768, 128), BF), vm((4, 8, 128), F32),
            dma((4, 2)), dma((4, 2)), dma((4, 2)), dma((4, 2)),
            dma((3,)), dma((3,)), dma((4,)), dma((4,)), dma((8,)), dma((8,)), dma((3,)), dma((3,)), dma((2,)), dma((2,)),
            dma((4,)), dma((2,)), dma((2,)), dma((2,)), dma((2,)), dma((2,)), dma((2, 2)),
            dma((4,)), dma((4,)), dma((4,)), dma((4,)), dma((4,)), dma((4,)), dma((2, 4)), dma((4,)), dma((2, 2)),
            dma, dma, dma((3,)), dma((3,)), dma((3,)), dma((3,)), dma((3,)), dma((3,)), dma, dma, dma((2, 2)), dma((4,)),
            dma((2, NU)), dma((2, NU)), dma((NU,)), dma((NU,)), dma((NU,)), dma((3, NU)),
            dma((NF + 1,)), dma((NF + 1,)), dma((4, 4)), dma((4, 4)), dma((4, 4)), dma((4,)),
            dma((4,)), dma((4,)), dma((2,)), dma((2,)), dma, dma, dma((4,)), dma((4,)), dma,
        ],
        compiler_params=pltpu.CompilerParams(
            collective_id=1, has_side_effects=True, vmem_limit_bytes=63 << 20
        ),
        name="layer",
    )(*args)


def local_fast(
    tokens, lengths, seq_order, gain_attn, w_qkv, w_attn_out, gain_mlp, w_in, w_mlp_out, cotangent
):
    half = HEAD_DIM // 2
    frequency = jnp.tile(rope_base ** (-2.0 * jnp.arange(half, dtype=F32) / HEAD_DIM), 4)
    sign = jnp.tile(jnp.repeat(jnp.array([-1.0, 1.0], F32), half), 2)
    rows = (gain_attn.astype(F32), gain_mlp.astype(F32), frequency, sign)
    gains = jnp.concatenate([r[None, :] for r in rows] + [jnp.zeros((4, 128), F32)], axis=0)
    out, d_tok, d_qkv, d_in, d_down, d_out, d_gain = run_layer(
        lengths, seq_order, tokens, w_qkv, w_in.transpose(1, 2, 0).reshape(2 * HID, 128), w_mlp_out, w_attn_out, gains, cotangent
    )
    return (out, d_tok, d_gain[0], d_qkv, d_out, d_gain[1], d_in.reshape(2, HID, 128).transpose(2, 0, 1), d_down)


def layer_norm(field_in, norm_gain):
    row_mean = jnp.mean(field_in, axis=-1, keepdims=True)
    centered = field_in - row_mean
    variance = jnp.mean(centered * centered, axis=-1, keepdims=True)
    return centered * lax.rsqrt(variance + norm_eps) * norm_gain


def rotate(field_in, position):
    half_size = field_in.shape[-1] // 2
    index_range = jnp.arange(half_size, dtype=jnp.float32)
    frequency = rope_base ** (-2.0 * index_range / field_in.shape[-1])
    angles = position[:, None] * frequency[None, :]
    cosine = jnp.cos(angles)[:, None, :]
    sine_part = jnp.sin(angles)[:, None, :]
    first_half = field_in[..., :half_size]
    second_half = field_in[..., half_size:]
    return jnp.concatenate(
        [
            first_half * cosine - second_half * sine_part,
            second_half * cosine + first_half * sine_part,
        ],
        axis=-1,
    )


def geglu(act_part, up_part):
    return jax.nn.gelu(act_part, approximate=False) * up_part


def layout(lengths, seq_order, group_rows):
    seq_total = seq_order.shape[0]
    first_seq = lax.axis_index("dp") * SEQ_GRP
    chosen = lax.dynamic_slice_in_dim(seq_order, first_seq, SEQ_GRP)
    matched = chosen[:, None] == jnp.arange(seq_total, dtype=jnp.int32)[None, :]
    dealt_lengths = jnp.sum(jnp.where(matched, lengths[None, :], 0), axis=1)
    seq_ends = jnp.cumsum(dealt_lengths)
    row_index = jnp.arange(group_rows, dtype=jnp.int32)
    passed = row_index[:, None] >= seq_ends[None, :]
    segment = jnp.sum(passed.astype(jnp.int32), axis=1)
    row_start = jnp.sum(jnp.where(passed, dealt_lengths[None, :], 0), axis=1)
    return (segment, (row_index - row_start).astype(jnp.float32))


def item_layout(array_in, block_rows):
    group_rows, head_count, head_size = array_in.shape
    block_count = group_rows // block_rows
    shaped = array_in.reshape(block_count, block_rows, head_count, head_size)
    return shaped.transpose(2, 0, 1, 3).reshape(head_count * block_count, block_rows, head_size)


def from_items(items, group_rows):
    item_count, block_rows, head_size = items.shape
    block_count = group_rows // block_rows
    head_count = item_count // block_count
    shaped = items.reshape(head_count, block_count, block_rows, head_size)
    return shaped.transpose(1, 2, 0, 3).reshape(group_rows, head_count, head_size)


def masked_scores(query_block, key_head, segment_block, segment):
    score_scale = query_block.shape[-1] ** (-0.5)
    raw_scores = lax.dot_general(
        query_block, key_head, (((1,), (1,)), ((), ())), preferred_element_type=jnp.float32
    )
    allowed = segment_block[:, None] == segment[None, :]
    return jnp.where(allowed, raw_scores * score_scale, masked_fill)


def attend_forward(query_rot, key_rot, value_low, segment, block_rows):
    group_rows, head_count, head_size = query_rot.shape
    block_count = group_rows // block_rows
    query_items = item_layout(query_rot, block_rows)
    key_heads = key_rot.transpose(1, 0, 2)
    value_heads = value_low.transpose(1, 0, 2)
    segment_blocks = segment.reshape(block_count, block_rows)

    def one_item(item_index):
        head_index = item_index // block_count
        block_index = item_index % block_count
        query_block = lax.dynamic_index_in_dim(query_items, item_index, 0, False)
        key_head = lax.dynamic_index_in_dim(key_heads, head_index, 0, False)
        value_head = lax.dynamic_index_in_dim(value_heads, head_index, 0, False)
        segment_block = lax.dynamic_index_in_dim(segment_blocks, block_index, 0, False)
        scores = masked_scores(query_block, key_head, segment_block, segment)
        row_top = jnp.max(scores, axis=1, keepdims=True)
        weights = jnp.exp(scores - row_top)
        row_total = jnp.sum(weights, axis=1, keepdims=True)
        probs_low = (weights / row_total).astype(jnp.bfloat16)
        result = jnp.dot(probs_low, value_head, preferred_element_type=jnp.float32)
        return (result, row_top[:, 0] + jnp.log(row_total[:, 0]))

    results, log_totals = lax.map(one_item, jnp.arange(head_count * block_count, dtype=jnp.int32))
    return (from_items(results, group_rows), log_totals)


def attend_backward(query_rot, key_rot, value_low, grad_out, log_totals, segment, block_rows):
    group_rows, head_count, head_size = query_rot.shape
    block_count = group_rows // block_rows
    score_scale = head_size ** (-0.5)
    query_items = item_layout(query_rot, block_rows)
    grad_items = item_layout(grad_out, block_rows)
    key_heads = key_rot.transpose(1, 0, 2)
    value_heads = value_low.transpose(1, 0, 2)
    segment_blocks = segment.reshape(block_count, block_rows)

    def one_item(carried, item_index):
        key_grads, value_grads = carried
        head_index = item_index // block_count
        block_index = item_index % block_count
        query_block = lax.dynamic_index_in_dim(query_items, item_index, 0, False)
        grad_block = lax.dynamic_index_in_dim(grad_items, item_index, 0, False)
        log_row = lax.dynamic_index_in_dim(log_totals, item_index, 0, False)
        key_head = lax.dynamic_index_in_dim(key_heads, head_index, 0, False)
        value_head = lax.dynamic_index_in_dim(value_heads, head_index, 0, False)
        segment_block = lax.dynamic_index_in_dim(segment_blocks, block_index, 0, False)
        scores = masked_scores(query_block, key_head, segment_block, segment)
        prob_full = jnp.exp(scores - log_row[:, None])
        probs_low = prob_full.astype(jnp.bfloat16)
        grad_probs = lax.dot_general(
            grad_block, value_head, (((1,), (1,)), ((), ())), preferred_element_type=jnp.float32
        )
        row_delta = jnp.sum(prob_full * grad_probs, axis=1, keepdims=True)
        grad_scores = (prob_full * (grad_probs - row_delta)).astype(jnp.bfloat16)
        grad_query = (
            jnp.dot(grad_scores, key_head, preferred_element_type=jnp.float32) * score_scale
        )
        grad_key = (
            lax.dot_general(
                grad_scores,
                query_block,
                (((0,), (0,)), ((), ())),
                preferred_element_type=jnp.float32,
            )
            * score_scale
        )
        grad_value = lax.dot_general(
            probs_low, grad_block, (((0,), (0,)), ((), ())), preferred_element_type=jnp.float32
        )
        key_grads = lax.dynamic_update_index_in_dim(
            key_grads,
            lax.dynamic_index_in_dim(key_grads, head_index, 0, False) + grad_key,
            head_index,
            0,
        )
        value_grads = lax.dynamic_update_index_in_dim(
            value_grads,
            lax.dynamic_index_in_dim(value_grads, head_index, 0, False) + grad_value,
            head_index,
            0,
        )
        return ((key_grads, value_grads), grad_query)

    zero_heads = jnp.zeros((head_count, group_rows, head_size), jnp.float32)
    (key_grads, value_grads), query_grads = lax.scan(
        one_item, (zero_heads, zero_heads), jnp.arange(head_count * block_count, dtype=jnp.int32)
    )
    return (
        from_items(query_grads, group_rows),
        key_grads.transpose(1, 0, 2),
        value_grads.transpose(1, 0, 2),
    )


def spread_rows(local_rows):
    return lax.all_gather(local_rows, "tensor", axis=0, tiled=True)


def spread_grads(local_grads):
    return lax.all_gather(local_grads, "tensor", axis=0, tiled=True)


def sum_heads(activations, weight_part, row_count):

    def row_term(first_row, row_number):
        return jnp.dot(activations, weight_part, preferred_element_type=jnp.float32)

    return lax.psum_scatter(
        row_term(jnp.int32(0), row_count * lax.axis_size("tensor")),
        "tensor",
        scatter_dimension=0,
        tiled=True,
    )


def sum_grads(grads_low, weight_full, einsum_form, row_count):

    def row_term(first_row, row_number):
        return jnp.einsum(einsum_form, grads_low, weight_full, preferred_element_type=jnp.float32)

    return lax.psum_scatter(
        row_term(jnp.int32(0), row_count * lax.axis_size("tensor")),
        "tensor",
        scatter_dimension=0,
        tiled=True,
    )


def local_plain(
    tokens, lengths, seq_order, gain_attn, w_qkv, w_attn_out, gain_mlp, w_in, w_mlp_out, cotangent
):
    row_count = tokens.shape[0]
    group_rows = row_count * lax.axis_size("tensor")
    block_rows = min(512, group_rows)
    segment, position = layout(lengths, seq_order, group_rows)
    gain_low_one, qkv_weight, out_weight, gain_low_two, in_weight, down_weight = (
        lax.all_gather(gain_attn, "dp", axis=0, tiled=True),
        lax.all_gather(w_qkv, "dp", axis=1, tiled=True),
        lax.all_gather(w_attn_out, "dp", axis=1, tiled=True),
        lax.all_gather(gain_mlp, "dp", axis=0, tiled=True),
        lax.all_gather(w_in, "dp", axis=0, tiled=True),
        lax.all_gather(w_mlp_out, "dp", axis=1, tiled=True),
    )
    gain_one = gain_low_one.astype(jnp.float32)
    gain_two = gain_low_two.astype(jnp.float32)
    residual = tokens.astype(jnp.float32)
    normed_one = spread_rows(layer_norm(residual, gain_one).astype(jnp.bfloat16))
    qkv = jnp.einsum("rd,pdc->rpc", normed_one, qkv_weight, preferred_element_type=jnp.float32)
    head_count = qkv.shape[2] // HEAD_DIM
    head_shape = (group_rows, head_count, HEAD_DIM)
    query_rot = rotate(qkv[:, 0].reshape(head_shape), position).astype(jnp.bfloat16)
    key_rot = rotate(qkv[:, 1].reshape(head_shape), position).astype(jnp.bfloat16)
    value_low = qkv[:, 2].reshape(head_shape).astype(jnp.bfloat16)
    attended, log_totals = attend_forward(query_rot, key_rot, value_low, segment, block_rows)
    attn_low = attended.reshape(group_rows, head_count * HEAD_DIM).astype(jnp.bfloat16)
    resid_mid = residual + sum_heads(attn_low, out_weight, row_count)
    normed_two = spread_rows(layer_norm(resid_mid, gain_two).astype(jnp.bfloat16))
    gate_up = jnp.einsum("rd,dpc->rpc", normed_two, in_weight, preferred_element_type=jnp.float32)
    hidden = geglu(gate_up[:, 0], gate_up[:, 1]).astype(jnp.bfloat16)
    output = (resid_mid + sum_heads(hidden, down_weight, row_count)).astype(jnp.bfloat16)
    grad_two = spread_grads(cotangent)
    d_hidden = lax.dot_general(
        grad_two, down_weight, (((1,), (1,)), ((), ())), preferred_element_type=jnp.float32
    )
    d_down = lax.dot_general(
        hidden, grad_two, (((0,), (0,)), ((), ())), preferred_element_type=jnp.float32
    )
    geglu_pull = jax.vjp(geglu, gate_up[:, 0], gate_up[:, 1])[1]
    d_act, d_up = geglu_pull(d_hidden)
    d_gate_up = jnp.stack([d_act, d_up], axis=1).astype(jnp.bfloat16)
    d_in = jnp.einsum("rd,rpc->dpc", normed_two, d_gate_up, preferred_element_type=jnp.float32)
    d_normed_two = sum_grads(d_gate_up, in_weight, "rpc,dpc->rd", row_count)
    norm_pull_two = jax.vjp(layer_norm, resid_mid, gain_two)[1]
    d_mid_norm, d_gain_two = norm_pull_two(d_normed_two)
    d_mid = cotangent.astype(jnp.float32) + d_mid_norm
    grad_one = spread_grads(d_mid.astype(jnp.bfloat16))
    d_out = lax.dot_general(
        attn_low, grad_one, (((0,), (0,)), ((), ())), preferred_element_type=jnp.float32
    )
    d_att = lax.dot_general(
        grad_one, out_weight, (((1,), (1,)), ((), ())), preferred_element_type=jnp.float32
    ).astype(jnp.bfloat16)
    d_query_rot, d_key_rot, d_value = attend_backward(
        query_rot, key_rot, value_low, d_att.reshape(head_shape), log_totals, segment, block_rows
    )
    rotate_pull = jax.vjp(lambda field_in: rotate(field_in, position), d_query_rot)[1]
    d_query = rotate_pull(d_query_rot)[0]
    d_key = rotate_pull(d_key_rot)[0]
    flat_shape = (group_rows, head_count * HEAD_DIM)
    d_qkv = jnp.stack(
        [d_query.reshape(flat_shape), d_key.reshape(flat_shape), d_value.reshape(flat_shape)],
        axis=1,
    ).astype(jnp.bfloat16)
    d_qkv_weight = jnp.einsum("rd,rpc->pdc", normed_one, d_qkv, preferred_element_type=jnp.float32)
    d_normed_one = sum_grads(d_qkv, qkv_weight, "rpc,pdc->rd", row_count)
    norm_pull_one = jax.vjp(layer_norm, residual, gain_one)[1]
    d_first, d_gain_one = norm_pull_one(d_normed_one)
    d_tokens = d_mid + d_first
    gain_sums = lax.psum((d_gain_one, d_gain_two), "tensor")
    shares = (
        lax.psum_scatter(gain_sums[0], "dp", scatter_dimension=0, tiled=True),
        lax.psum_scatter(d_qkv_weight, "dp", scatter_dimension=1, tiled=True),
        lax.psum_scatter(d_out, "dp", scatter_dimension=1, tiled=True),
        lax.psum_scatter(gain_sums[1], "dp", scatter_dimension=0, tiled=True),
        lax.psum_scatter(d_in, "dp", scatter_dimension=0, tiled=True),
        lax.psum_scatter(d_down, "dp", scatter_dimension=1, tiled=True),
    )
    return (output, d_tokens, shares[0], shares[1], shares[2], shares[3], shares[4], shares[5])


def solution(mesh):
    fast = mesh.shape["dp"] == 8 and mesh.shape["tensor"] == 4
    return jax.shard_map(
        local_fast if fast else local_plain,
        mesh=mesh,
        in_specs=(
            P(("dp", "tensor"), None),
            P(),
            P(),
            P("dp"),
            P(None, "dp", "tensor"),
            P("tensor", "dp"),
            P("dp"),
            P("dp", None, "tensor"),
            P("tensor", "dp"),
            P(("dp", "tensor"), None),
        ),
        out_specs=(
            P(("dp", "tensor"), None),
            P(("dp", "tensor"), None),
            P("dp"),
            P(None, "dp", "tensor"),
            P("tensor", "dp"),
            P("dp"),
            P("dp", None, "tensor"),
            P("tensor", "dp"),
        ),
        check_vma=False,
    )
```

```python
import functools

import jax
import jax.numpy as jnp
from jax import lax
from jax.experimental import pallas as pl
from jax.experimental.pallas import tpu as pltpu
from jax.sharding import PartitionSpec as P

HEAD_DIM = 64
SEQ_GRP = 4
rope_base = 160000.0
norm_eps = 1e-05
masked_fill = -1e30
MESH = pl.DeviceIdType.MESH
BF = jnp.bfloat16
F32 = jnp.float32

NT = (((1,), (1,)), ((), ()))
TN = (((0,), (0,)), ((), ()))


def place():
    dp = lax.axis_index("dp")
    z = lax.axis_index("tensor")
    c = lax.rem(dp, 2)
    x = lax.rem(lax.div(dp, 2), 2)
    y = lax.div(dp, 4)
    return dp, z, c, x, y


def flip(dp, bits, distance):
    out = dp
    for b, bit in enumerate(bits):
        if (distance >> b) & 1:
            out = out + (1 << b) - (2 << b) * bit
    return out


def remote(src, dst, send, recv, dev):
    return pltpu.make_async_remote_copy(
        src_ref=src, dst_ref=dst, send_sem=send, recv_sem=recv, device_id=dev, device_id_type=MESH
    )


def cols(start, size):
    return pl.ds(pl.multiple_of(start, size), size)


def greet(dp, z, bits):
    c = bits[0]
    barrier = pltpu.get_barrier_semaphore()
    peers = [(flip(dp, bits, d), z) for d in range(1, 8)]
    core = flip(dp, bits, 1)
    for k in range(1, 4):
        peers.append((dp, lax.rem(z + k, 4)))
        peers.append((core, lax.rem(z + k, 4)))
    for p in peers:
        pl.semaphore_signal(barrier, inc=1, device_id=p, device_id_type=MESH)
    pl.semaphore_wait(barrier, len(peers))


def norm_rows(v):
    mean = jnp.mean(v, axis=-1, keepdims=True)
    centered = v - mean
    var = jnp.mean(centered * centered, axis=-1, keepdims=True)
    rstd = lax.rsqrt(var + norm_eps)
    return centered * rstd, rstd


def turn(v, cs, sn):
    lane = lax.broadcasted_iota(jnp.int32, cs.shape, 1)
    low_half = lax.rem(lane, HEAD_DIM) < HEAD_DIM // 2
    parts = []
    for t in range(v.shape[1] // 128):
        piece = v[:, t * 128 : (t + 1) * 128]
        swapped = jnp.where(low_half, pltpu.roll(piece, 96, 1), pltpu.roll(piece, 32, 1))
        parts.append(piece * cs + swapped * sn)
    return jnp.concatenate(parts, axis=1)


def gain_row(gains, row):
    return jnp.concatenate([gains[p, row : row + 1, :] for p in range(8)], axis=1)


HID = 656
FF3 = 3 * HID
FROWS = ((0, HID), (HID, HID), (2 * HID, HID))
CUTS = ((0, 496), (496, 496), (992, 496), (1488, 480))
HALVES = tuple((m, o, n) for m in (2, 0, 1) for o, n in ((0, 336), (336, 320)))
NF = len(HALVES)
NU = NF + 2
INV_SQRT2 = 0.7071067811865476
INV_SQRT_2PI = 0.3989422804014327


def layer_kernel(
    lengths, seq_order, tok, wqkv, win, wmlp, wout, gains_in, cot,
    out_o, dtok_o, dwq_o, dwin_o, dwmlp_o, dwout_o, dg_o,
    gains, w3, cs, sn, segc, segr, q, k, v, lse, att, attn2, h1, wq, cot4,
    G, Wo, X1, h2a, dya, yr, acc, hidT, daT, duT, dX1, dsb, dr, dzs, dzr, usb, ur, uzs, uzr, dsend, datt, delta,
    dq, dk, dv, Hs, Hi, Hx, Rb, Ra, Z, Rbo, Rao, Zo, give, Wp, Wc, Wb, Wa, gz,
    us, ds, rb, ra, wr_s, wr_r, wx_s, wx_r, g_s, g_r, cx_s, cx_r, hop_s, hop_r,
    ou_s, o_r, oa_s, ob_s, of_s, oa_r, ob_r,
    fz_s, fz_r, pa_s, pb_s, pf_s, pa_r, pb_r, at_s, at_r,
    y_s, y_r, n_s, n_r, d_s, d_r, u_s, u_r, e_s, e_r, t_s, t_r,
    b_s, b_r, a_s, a_r, zu_s, z_r, fin_s, fin_r,
    hu_s, hd_s, hi_r, hx_r, wc_s, wc_r, wb_s, wb_r, wa_s, wa_r, gz_s, gz_r, lc,
):
    dp, z, c, x, y = place()
    bits = (c, x, y)
    core = flip(dp, bits, 1)
    px, py = flip(dp, bits, 2), flip(dp, bits, 4)
    a = (1 - c) * px + c * py
    b = (1 - c) * py + c * px
    chip, chip_a, chip_b = lax.div(dp, 2), lax.div(a, 2), lax.div(b, 2)
    chip_d = 3 - chip
    home = lax.div(z, 2)
    org = c == home
    zq = lax.rem(z, 2)
    zp = z + 1 - 2 * zq
    z2 = z + 2 - 4 * home
    end = (z == 0) | (z == 3)
    own = cols(c * 256, 256)
    other = cols((1 - c) * 256, 256)

    def block(core_bit, line_bit):
        return cols((2 * line_bit + core_bit) * 256, 256)

    ob, cb, zb, db = block(c, zq), block(1 - c, zq), block(c, 1 - zq), block(1 - c, 1 - zq)
    tall, vT, kT, oT, dqkvT = Hs, Hx, dzs, acc.at[:, 0:256], h2a.at[0:768]
    dw4 = (dwin_o.at[0:HID], dwin_o.at[HID : 2 * HID], dwmlp_o)
    greet(dp, z, bits)

    def no(cond):
        return jnp.logical_not(cond)

    def tok_up(k_, h):
        ref = tall.at[z - k_, pl.ds(h * 128, 128)]
        src = tok.at[pl.ds(h * 128, 128)] if k_ == 0 else ref
        return remote(src, ref, us.at[k_, h], rb.at[k_ + 1, h], (dp, z + 1))

    def tok_down(k_, h):
        ref = tall.at[z + k_, pl.ds(h * 128, 128)]
        src = tok.at[pl.ds(h * 128, 128)] if k_ == 0 else ref
        return remote(src, ref, ds.at[k_, h], ra.at[k_ + 1, h], (dp, z - 1))

    def up_ok(k_):
        return (z >= k_) & (z < 3)

    def down_ok(k_):
        return (z + k_ <= 3) & (z > 0)

    for h in range(2):
        pl.when(up_ok(0))(lambda h=h: tok_up(0, h).start())
        pl.when(down_ok(0))(lambda h=h: tok_down(0, h).start())

    for d in range(1, 8):
        remote(gains_in, gains.at[dp], g_s.at[d], g_r.at[d], (flip(dp, bits, d), z)).start()
    own_rows = cols(dp * 128, 128)
    for j, d in enumerate((2, 4, 6)):
        remote(wqkv, wq.at[:, own_rows], wr_s.at[j], wr_r.at[j], (flip(dp, bits, d), z)).start()
    remote(wqkv, wq.at[:, own_rows], wx_s.at[3], wx_r.at[3], (core, z)).start()
    cot_copy = (
        remote(cot, cot4.at[ob], cx_s.at[0], cx_r.at[0], (core, z)),
        remote(cot, cot4.at[ob], cx_s.at[1], cx_r.at[1], (dp, zp)),
        remote(cot4.at[zb], cot4.at[zb], cx_s.at[2], cx_r.at[2], (core, z)),
    )
    cot_copy[0].start()
    cot_local = pltpu.make_async_copy(cot, cot4.at[ob], lc)
    cot_local.start()

    w3[0 : 2 * HID, :] = win[...]
    w3[2 * HID : FF3, :] = wmlp[...]
    lanes = cols(dp * 128, 128)
    hop = (
        remote(w3, G.at[:, lanes], hop_s.at[0], hop_r.at[0], (core, z)),
        remote(wout, Wo.at[zq, :, lanes], hop_s.at[1], hop_r.at[1], (core, z)),
    )

    @pl.when(no(org))
    def _():
        hop[1].start()
        hop[0].start()

    @pl.when(org)
    def _():
        G[:, lanes] = w3[...]
        Wo[zq, :, lanes] = wout[...]

    gains[dp] = gains_in[...]
    wq[:, own_rows, :] = wqkv[...]
    tall[z] = tok[...]
    cot_local.wait()

    def begin(cp):
        cp.start()

    def done(cp):
        cp.wait_send()

    def piece(u, where):
        r0, n = CUTS[u]
        return G.at[pl.ds(r0, n), cols(where * 256, 256)]

    def way(u):
        s = lax.rem(c + u, 2)
        one = (1 - s) * px + s * py
        two = (1 - s) * py + s * px
        return one, two, lax.div(one, 2), lax.div(two, 2)

    def plane_a(u):
        return remote(piece(u, chip), piece(u, chip), pa_s.at[u], pa_r.at[u], (way(u)[0], z))

    def plane_b(u):
        return remote(piece(u, chip), piece(u, chip), pb_s.at[u], pb_r.at[0, u], (way(u)[1], z))

    def plane_f(u):
        ref = piece(u, way(u)[2])
        return remote(ref, ref, pf_s.at[u], pb_r.at[1, u], (way(u)[1], z))

    def leap(u):
        return remote(piece(u, chip), piece(u, chip), fz_s.at[u], fz_r.at[u], (dp, z2))

    def spread(u):
        plane_a(u).start()
        plane_b(u).start()

    def across(u):
        ref = piece(u, way(u)[2])
        remote(ref, ref, pa_s.at[u], pa_r.at[u], (way(u)[0], z)).wait_recv()
        plane_f(u).start()

    def land(u):
        leap(u).wait_recv()
        spread(u)

    near = (1 - c) * lax.div(z + 2, 3) + c * lax.div(z, 3)
    far = 1 - near

    def opiece(qi, where):
        return Wo.at[qi, :, cols(where * 256, 256)]

    def ofar(k_):
        ref = opiece(zq, chip)
        return remote(ref, ref, ou_s.at[k_], o_r.at[zq], (dp, lax.rem(z + k_, 4)))

    def oplane(qi):
        ref, ref_a = opiece(qi, chip), opiece(qi, chip_a)
        return (
            remote(ref, ref, oa_s.at[qi], oa_r.at[qi], (a, z)),
            remote(ref, ref, ob_s.at[qi], ob_r.at[0, qi], (b, z)),
            remote(ref_a, ref_a, of_s.at[qi], ob_r.at[1, qi], (b, z)),
        )

    def ospread(qi):
        cps = oplane(qi)
        cps[0].start()
        cps[1].start()

    def oland(qi):
        ref = opiece(qi, chip)
        remote(ref, ref, ou_s.at[1], o_r.at[qi], (core, z)).wait_recv()
        ospread(qi)

    def oacross(qi):
        ref = opiece(qi, chip_a)
        remote(ref, ref, oa_s.at[qi], oa_r.at[qi], (a, z)).wait_recv()
        oplane(qi)[2].start()

    ends, starts, total = [], [], 0
    for j in range(SEQ_GRP):
        ends.append(total)
        total = total + lengths[seq_order[dp * SEQ_GRP + j]]
    for dst, shape, axis in ((segc, (1024, 128), 0), (segr, (8, 1024), 1)):
        row = lax.broadcasted_iota(jnp.int32, shape, axis)
        seg = jnp.zeros(shape, F32)
        start = jnp.zeros(shape, jnp.int32)
        for j in range(1, SEQ_GRP):
            passed = row >= ends[j]
            seg = jnp.where(passed, float(j), seg)
            start = jnp.where(passed, ends[j], start)
        dst[...] = seg
        if axis == 0:
            angle = (row - start).astype(F32) * gains_in[2:3, :]
            cs[...] = jnp.cos(angle)
            sn[...] = jnp.sin(angle) * gains_in[3:4, :]

    for d in range(1, 8):
        p = flip(dp, bits, d)
        remote(gains_in, gains.at[p], g_s.at[d], g_r.at[d], (p, z)).wait_recv()

    @pl.when(org)
    def _():
        remote(wout, Wo.at[zq, :, cols(core * 128, 128)], hop_s.at[1], hop_r.at[1], (core, z)).wait_recv()
        ospread(near)
        remote(w3, G.at[:, cols(core * 128, 128)], hop_s.at[0], hop_r.at[0], (core, z)).wait_recv()
        for u in range(4):
            spread(u)

    for j, d in enumerate((2, 4, 6)):
        p = flip(dp, bits, d)
        rows = wq.at[:, cols(p * 128, 128)]
        remote(wqkv, rows, wr_s.at[j], wr_r.at[j], (p, z)).wait_recv()
        remote(rows, rows, wx_s.at[j], wx_r.at[j], (core, z)).start()
    for j, d in enumerate((3, 5, 7, 1)):
        p = flip(dp, bits, d)
        remote(wqkv, wq.at[:, cols(p * 128, 128)], wx_s.at[j], wx_r.at[j], (core, z)).wait_recv()

    gain1, gain2 = gain_row(gains, 0), gain_row(gains, 1)

    def project(s):
        base = s * 256

        @pl.loop(0, 8)
        def _(r):
            xhat, _r = norm_rows(tall[s, pl.ds(pl.multiple_of(r * 32, 32), 32), :].astype(F32))
            h1[pl.ds(pl.multiple_of(base + r * 32, 32), 32), :] = (xhat * gain1).astype(BF)

        rows = pl.ds(pl.multiple_of(base, 256), 256)
        hb = h1[rows, :]
        cb, sb = cs[rows, :], sn[rows, :]
        for p, dst in enumerate((q, k, v)):
            r = jnp.dot(hb, wq[p], preferred_element_type=F32)
            if p < 2:
                r = turn(r, cb, sb)
            if p == 0:
                r = r * (HEAD_DIM**-0.5)
            dst[rows, :] = r.astype(BF)

    for k_ in range(4):
        if k_ > 0:
            below, above = z - k_ >= 0, z + k_ <= 3
            for h in range(2):

                @pl.when(below)
                def _(k_=k_, h=h):
                    ref = tall.at[z - k_, pl.ds(h * 128, 128)]
                    remote(ref, ref, us.at[k_, h], rb.at[k_, h], (core, z)).wait_recv()
                    if k_ < 3:
                        pl.when(up_ok(k_))(lambda: tok_up(k_, h).start())

                @pl.when(above)
                def _(k_=k_, h=h):
                    ref = tall.at[z + k_, pl.ds(h * 128, 128)]
                    remote(ref, ref, ds.at[k_, h], ra.at[k_, h], (core, z)).wait_recv()
                    if k_ < 3:
                        pl.when(down_ok(k_))(lambda: tok_down(k_, h).start())

        if k_ == 1:

            @pl.when(org)
            def _():
                for n in range(1, 4):
                    ofar(n).start()

        @pl.loop(0, 2)
        def _(t, k_=k_):
            s = z - k_ + 2 * k_ * t
            pl.when((s >= 0) & (s <= 3) & ((k_ > 0) | (t == 0)))(lambda: project(s))

        if k_ == 1:

            @pl.when(org)
            def _():
                oacross(near)
                for u in range(4):
                    across(u)

        if k_ == 2:

            @pl.when(org & end)
            def _():
                for u in range(4):
                    leap(u).start()

    for s in range(4):
        vT[:, s * 256 : (s + 1) * 256] = v[s * 256 : (s + 1) * 256, :].T
    head_of = lax.div(lax.broadcasted_iota(jnp.int32, (256, 256), 1), HEAD_DIM)

    def attend(i):
        rows = pl.ds(pl.multiple_of(i * 256, 256), 256)
        qb = q[rows, :]
        seg_q = segr[0:1, rows]
        heads = range(4)
        qh = [jnp.where(head_of == h, qb, jnp.zeros((), BF)) for h in heads]
        chunks = [slice(kc * 256, kc * 256 + 256) for kc in range(4)]
        for h in heads:
            hr = slice(h * HEAD_DIM, (h + 1) * HEAD_DIM)
            scores, tops = [], []
            for keys in chunks:
                seg_k = segc[keys, :]
                same = jnp.concatenate([seg_k, seg_k], axis=1) == seg_q
                s = lax.dot_general(k[keys, :], qh[h], NT, preferred_element_type=F32)
                s = jnp.where(same, s, masked_fill)
                scores.append(s)
                tops.append(jnp.max(s, axis=0, keepdims=True))
            top = jnp.maximum(jnp.maximum(tops[0], tops[1]), jnp.maximum(tops[2], tops[3]))
            tot, out = 0.0, 0.0
            for keys, s in zip(chunks, scores):
                p = jnp.exp(s - top)
                tot = tot + jnp.sum(p, axis=0, keepdims=True)
                out = out + jnp.dot(vT[hr, keys], p.astype(BF), preferred_element_type=F32)
            oT[hr, :] = out * (1.0 / tot)
            lse[h, i] = jnp.broadcast_to(top + jnp.log(tot), (8, 256))
        att[rows, :] = oT[...].T.astype(BF)

    def att_slot(src_core, q):
        return attn2.at[cols(src_core * 256, 256), cols(q * 256, 256)]

    def att_copy(n, i):
        rows = pl.ds(pl.multiple_of(i * 256, 256), 256)
        return remote(
            att.at[rows, :], att_slot(c, zq), at_s.at[n], at_r.at[c, zq], (2 * chip + home, i)
        )

    @pl.loop(0, 4)
    def _(n):
        i = lax.rem(z + 1 + n, 4)
        attend(i)
        for m in range(4):

            @pl.when((n == m) & ((m < 3) | no(org)))
            def _(m=m):
                att_copy(m, i).start()

        @pl.when((n == 3) & org)
        def _():
            attn2[own, cols(zq * 256, 256)] = att[pl.ds(pl.multiple_of(z * 256, 256), 256), :]

        @pl.when((n == 1) & org & no(end))
        def _():
            for u in range(4):
                leap(u).start()

        pl.when(n == 3)(lambda: cot_copy[1].start())

        @pl.when((n == 1) & end)
        def _():
            oland(far)
            pl.when(no(org))(lambda: oland(near))

        @pl.when((n == 3) & end)
        def _():
            oacross(far)
            pl.when(no(org))(lambda: oacross(near))

    @pl.when(no(end))
    def _():
        oland(far)
        pl.when(no(org))(lambda: oland(near))

    @pl.when(no(end))
    def _():
        oacross(far)
        pl.when(no(org))(lambda: oacross(near))

    def late(*ops):
        @pl.when(no(org))
        def _():
            for op, u in ops:
                op(u)

    pl.when(no(end))(lambda: late((land, 0), (land, 1), (land, 2), (land, 3), (across, 0), (across, 1)))
    pl.when(end)(lambda: late((land, 0)))

    for k_ in range(3):
        for h in range(2):
            pl.when(up_ok(k_))(lambda k_=k_, h=h: tok_up(k_, h).wait_send())
            pl.when(down_ok(k_))(lambda k_=k_, h=h: tok_down(k_, h).wait_send())
    for src in range(2):
        for qi in range(2):
            mine_too = (c == src) & (z == 2 * c + qi)

            @pl.when(no(mine_too))
            def _(src=src, qi=qi):
                slot = att_slot(src, qi)
                remote(slot, slot, at_s.at[0], at_r.at[src, qi], (core, z)).wait_recv()

    pl.when(end)(lambda: late((land, 1)))
    for qi in range(2):
        for w, where in enumerate((chip_b, chip_d)):
            ref = opiece(qi, where)
            remote(ref, ref, ob_s.at[qi], ob_r.at[w, qi], (core, z)).wait_recv()

    def out_proj(rows):
        return sum(
            jnp.dot(attn2[rows, qi * 256 : (qi + 1) * 256], Wo[qi], preferred_element_type=F32) for qi in range(2)
        )

    acc[...] = out_proj(other)
    y_copy = remote(acc, yr, y_s, y_r, (core, z))
    y_copy.start()
    pl.when(end)(lambda: late((land, 2)))
    X1[...] = tok[...].astype(F32) + out_proj(own)
    y_copy.wait()
    pl.when(end)(lambda: late((land, 3)))

    def chunk(r):
        return pl.ds(pl.multiple_of(r * 32, 32), 32)

    def own_chunk(r):
        return pl.ds(pl.multiple_of(c * 256 + r * 32, 32), 32)

    def block_chunk(r):
        return pl.ds(pl.multiple_of((2 * zq + c) * 256 + r * 32, 32), 32)

    @pl.loop(0, 8)
    def _(r):
        x1 = X1[chunk(r), :] + yr[chunk(r), :]
        X1[chunk(r), :] = x1
        xhat, _r = norm_rows(x1)
        h2a[block_chunk(r), :] = (xhat * gain2).astype(BF)

    h_copy = (
        remote(h2a.at[ob], h2a.at[ob], n_s.at[0], n_r.at[0], (core, z)),
        remote(h2a.at[ob], h2a.at[ob], n_s.at[1], n_r.at[1], (dp, zp)),
        remote(h2a.at[zb], h2a.at[zb], n_s.at[2], n_r.at[2], (core, z)),
    )
    h_copy[1].start()
    h_copy[0].start()
    pl.when(end)(lambda: late((across, 0), (across, 1)))
    late((across, 2), (across, 3))
    remote(cot, cot4.at[zb], cx_s.at[1], cx_r.at[1], (dp, zp)).wait_recv()
    cot_copy[2].start()
    remote(cot, cot4.at[cb], cx_s.at[0], cx_r.at[0], (core, z)).wait_recv()
    remote(cot, cot4.at[db], cx_s.at[2], cx_r.at[2], (core, z)).wait_recv()
    for u in range(4):
        for w, where in enumerate((way(u)[3], chip_d)):
            ref = piece(u, where)
            remote(ref, ref, pb_s.at[u], pb_r.at[w, u], (core, z)).wait_recv()
    remote(h2a.at[cb], h2a.at[cb], n_s.at[0], n_r.at[0], (core, z)).wait_recv()

    def tile(r0, n, tokens):
        h2 = h2a[tokens, :]
        act = lax.dot_general(G[r0 : r0 + n, :], h2, NT, preferred_element_type=F32)
        up = lax.dot_general(G[HID + r0 : HID + r0 + n, :], h2, NT, preferred_element_type=F32)
        dh = lax.dot_general(
            G[2 * HID + r0 : 2 * HID + r0 + n, :], cot4[tokens, :], NT, preferred_element_type=F32
        )
        Phi = 0.5 + 0.5 * lax.erf(act * INV_SQRT2)
        phi = jnp.exp(-0.5 * act * act) * INV_SQRT_2PI
        gel = act * Phi
        rr = slice(r0, r0 + n)
        hidT[rr, tokens] = (gel * up).astype(BF)
        daT[rr, tokens] = (dh * up * (Phi + act * phi)).astype(BF)
        duT[rr, tokens] = (dh * gel).astype(BF)

    @pl.loop(0, 2)
    def _(t):
        there = lax.rem(zq + t, 2)

        @pl.when(t == 1)
        def _():
            remote(h2a.at[zb], h2a.at[zb], n_s.at[1], n_r.at[1], (dp, zp)).wait_recv()
            h_copy[2].start()
            remote(h2a.at[db], h2a.at[db], n_s.at[2], n_r.at[2], (core, z)).wait_recv()

        for r0, n in ((0, 224), (224, 224), (448, 208)):
            tile(r0, n, cols(there * 512, 512))

    def tn(lhs, rhs):
        return lax.dot_general(lhs, rhs, TN, preferred_element_type=F32)

    def f_rows(m):
        return pl.ds(FROWS[m][0], HID)

    def d_norm(rows, hc):
        return tn(daT[:, rows], G[f_rows(0), hc]) + tn(duT[:, rows], G[f_rows(1), hc])

    def mlp_out(rows, hc):
        return tn(hidT[:, rows], G[f_rows(2), hc])

    def quad(term, sb, got, zs, zgot, ss, rs, hold=False):
        halves = (slice(0, 512), slice(512, 1024))
        copies = (
            remote(sb.at[0], got.at[0], ss.at[0], rs.at[0], (core, z)),
            remote(sb.at[1], got.at[1], ss.at[1], rs.at[1], (core, z)),
            remote(zs, zgot, ss.at[2], rs.at[2], (dp, zp)),
        )
        for j, rows in enumerate((db, cb)):
            for hc in halves:
                sb[j, :, hc] = term(rows, hc).astype(BF)
            copies[j].start()
        copies[0].wait_recv()
        for hc in halves:
            zs[:, hc] = (term(zb, hc) + got[0, :, hc].astype(F32)).astype(BF)
        if not hold:
            copies[2].start()
        return copies

    def keep(term, dst, plus=None):
        for hc in (slice(0, 512), slice(512, 1024)):
            r = term(ob, hc)
            dst[:, hc] = r if plus is None else r + plus[:, hc]

    def grads(m):
        lhs, rhs = ((daT, h2a), (duT, h2a), (hidT, cot4))[m]

        @pl.loop(0, 4)
        def _(t):
            tc = cols(t * 256, 256)
            G[f_rows(m), tc] = jnp.dot(lhs[...], rhs[:, tc], preferred_element_type=F32).astype(BF)

    def rows_of(e):
        m, o, n = HALVES[e]
        return pl.ds(FROWS[m][0] + o, n)

    def part(e, where):
        if e < NF:
            return G.at[rows_of(e), cols(where * 256, 256)]
        return opiece(e - NF, where)

    def from_b(e, slot):
        return Rb.at[slot, rows_of(e)] if e < NF else Rbo.at[slot, e - NF]

    def from_a(e):
        return Ra.at[rows_of(e)] if e < NF else Rao.at[e - NF]

    def unit_b(e, slot):
        src = part(e, chip_b if slot == 0 else chip_d)
        return remote(src, from_b(e, slot), b_s.at[slot, e], b_r.at[slot, e], (b, z))

    def unit_a(e):
        return remote(part(e, chip_a), from_a(e), a_s.at[e], a_r.at[e], (a, z))

    def send_b(e):
        unit_b(e, 1).start()
        unit_b(e, 0).start()

    def stage1(e):
        unit_b(e, 1).wait_recv()
        ref = part(e, chip_a)
        ref[...] = (ref[...].astype(F32) + from_b(e, 1)[...].astype(F32)).astype(BF)
        unit_a(e).start()

    def unit_z(e):
        return remote(part(e, chip), Z.at[rows_of(e)], zu_s.at[e], z_r.at[0, e], (dp, z2))

    def unit_o(e):
        t = 2 * c + e - NF
        slot = lax.rem(z - t + 4, 4) - 1
        return remote(part(e, chip), Zo.at[slot], zu_s.at[e], z_r.at[slot, e], (dp, t))

    def stage2(e):
        unit_b(e, 0).wait_recv()
        unit_a(e).wait_recv()
        ref = part(e, chip)
        ref[...] = (
            ref[...].astype(F32) + from_b(e, 0)[...].astype(F32) + from_a(e)[...].astype(F32)
        ).astype(BF)
        if e < NF:
            pl.when(no(org))(lambda: unit_z(e).start())
        else:
            pl.when(z != 2 * c + e - NF)(lambda: unit_o(e).start())

    def line_wait(e, slot):
        remote(Zo.at[slot], Zo.at[slot], zu_s.at[e], z_r.at[slot, e], (core, z)).wait_recv()

    def final(e):
        if e < NF:
            m, o, n = HALVES[e]
            return e, give.at[rows_of(e)], dw4[m].at[pl.ds(o, n)]
        return NF, give.at[FF3 : FF3 + 256], dwout_o

    def stage4(e):
        here = org if e < NF else z == 2 * c + e - NF

        @pl.when(here)
        def _():
            slot, gift, dst = final(e)
            if e < NF:
                unit_z(e).wait_recv()
            for who, ref in ((c, dst), (1 - c, gift)):
                ref[...] = part(e, chip)[:, cols(who * 128, 128)].astype(F32)

            def take(got):
                for who, ref in ((c, dst), (1 - c, gift)):
                    ref[...] = ref[...] + got[:, cols(who * 128, 128)].astype(F32)

            def line_take(where):
                line_wait(e, where)
                take(Zo.at[where])

            if e < NF:
                take(Z.at[rows_of(e)])
            else:
                for slot_ in range(3):
                    line_take(slot_)
            remote(gift, dst, fin_s.at[slot], fin_r.at[slot], (core, z)).start()

    def tick(t):
        for lag, step in ((0, stage1), (1, stage2), (4, stage4)):
            if 0 <= t - lag < NU:
                step(t - lag)

    d_copies = quad(d_norm, dsb, dr, dzs, dzr, d_s, d_r)
    keep(d_norm, dX1)
    u_copies = quad(mlp_out, usb, ur, uzs, uzr, u_s, u_r, hold=True)
    keep(mlp_out, dtok_o, X1)
    for u in range(4):
        plane_a(u).wait_send()
        plane_b(u).wait_send()
        plane_f(u).wait_send()
        pl.when(org)(lambda u=u: leap(u).wait_send())

    def ff_grads(m):
        grads(m)
        for e in range(NF):
            if HALVES[e][0] == m:
                send_b(e)

    ff_grads(2)
    ff_grads(0)
    ff_grads(1)
    d_copies[1].wait_recv()
    d_copies[2].wait_recv()

    @pl.loop(0, 8)
    def _(r):
        dh2 = dX1[chunk(r), :] + dr[1, chunk(r), :].astype(F32) + dzr[chunk(r), :].astype(F32)
        xhat, rstd = norm_rows(X1[chunk(r), :])
        e2 = dh2 * gain2
        m1 = jnp.mean(e2, axis=-1, keepdims=True)
        m2 = jnp.mean(e2 * xhat, axis=-1, keepdims=True)
        dx = cot4[block_chunk(r), :].astype(F32) + rstd * (e2 - m1 - xhat * m2)
        dX1[chunk(r), :] = dx
        dya[own_chunk(r), :] = dx.astype(BF)

    e_copy = remote(dya.at[own], dya.at[own], e_s, e_r, (core, z))
    e_copy.start()
    tick(0)
    e_copy.wait()
    for qi in range(2):
        dsend[qi] = lax.dot_general(dya[...], Wo[qi], NT, preferred_element_type=F32).astype(BF)

    def att_back(c0, qi):
        dst = datt.at[cols(z * 256, 256)]
        return remote(
            dsend.at[qi, pl.ds(c0 * 256, 256)], dst, t_s.at[c0, qi], t_r.at[z], (2 * chip + c0, 2 * c + qi)
        )

    def is_self(c0, qi):
        return (c == c0) & (z == 2 * c + qi)

    for c0 in range(2):
        for qi in range(2):
            pl.when(no(is_self(c0, qi)))(lambda c0=c0, qi=qi: att_back(c0, qi).start())

            @pl.when(is_self(c0, qi))
            def _(c0=c0, qi=qi):
                datt[cols(z * 256, 256), :] = dsend[qi, c0 * 256 : (c0 + 1) * 256, :]

    u_copies[2].start()
    for n in range(1, 4):
        pl.when(org)(lambda n=n: ofar(n).wait_send())
    for qi in range(2):
        for cp in oplane(qi):
            cp.wait_send()

        @pl.loop(0, 4)
        def _(t, qi=qi):
            tc = cols(t * 256, 256)
            Wo[qi, :, tc] = tn(attn2[:, qi * 256 : (qi + 1) * 256], dya[:, tc]).astype(BF)

        send_b(NF + qi)
    tick(1)
    tick(2)
    for cp in h_copy:
        cp.wait_send()
    d_copies[2].wait_send()
    for s in range(4):
        kT[:, s * 256 : (s + 1) * 256] = k[s * 256 : (s + 1) * 256, :].T
    dq[...] = jnp.zeros_like(dq)
    dk[...] = jnp.zeros_like(dk)
    dv[...] = jnp.zeros_like(dv)
    for i in range(4):

        @pl.when(no(org & (z == i)))
        def _(i=i):
            ref = datt.at[pl.ds(i * 256, 256)]
            remote(ref, ref, t_s.at[0, 0], t_r.at[i], (core, z)).wait_recv()

    @pl.loop(0, 4)
    def _(i):
        rows = pl.ds(pl.multiple_of(i * 256, 256), 256)
        t = (datt[rows, :].astype(F32) * att[rows, :].astype(F32)).T
        for h in range(4):
            s = jnp.sum(t[h * 64 : (h + 1) * 64, :], axis=0, keepdims=True)
            delta[h, i] = jnp.broadcast_to(s, (8, 256))

    def block_order(l):
        inner = lax.div(z * (3 - z), 2)
        base = inner * jnp.minimum(l, 1) * (lax.rem(l + 1, 3) + 1) + (1 - inner) * l
        return (1 - home) * (3 - base) + home * base

    def pair(i, j):
        ri = pl.ds(pl.multiple_of(i * 256, 256), 256)
        rj = pl.ds(pl.multiple_of(j * 256, 256), 256)

        kj, vj, qi_, dai = k[rj, :], v[rj, :], q[ri, :], datt[ri, :]
        seg_k = segc[rj, :]
        same = jnp.concatenate([seg_k, seg_k], axis=1) == segr[0:1, ri]
        none = jnp.zeros((), BF)
        dvs, dks, dqs = [], [], []
        for h in range(4):
            mine = head_of == h
            qh, dah = jnp.where(mine, qi_, none), jnp.where(mine, dai, none)
            s = lax.dot_general(kj, qh, NT, preferred_element_type=F32)
            p = jnp.exp(jnp.where(same, s, masked_fill) - lse[h, i, 0:1, :])
            dp_ = lax.dot_general(vj, dah, NT, preferred_element_type=F32)
            dsc = (p * (dp_ - delta[h, i, 0:1, :])).astype(BF)
            dvs.append(jnp.dot(p.astype(BF), dah, preferred_element_type=F32))
            dks.append(jnp.dot(dsc, qh, preferred_element_type=F32))
            hr = slice(h * HEAD_DIM, (h + 1) * HEAD_DIM)
            dqs.append(jnp.dot(kT[hr, rj], dsc, preferred_element_type=F32))
        dv[rj, :] = dv[rj, :] + (dvs[0] + dvs[1] + dvs[2] + dvs[3])
        dk[rj, :] = dk[rj, :] + (dks[0] + dks[1] + dks[2] + dks[3])
        for h in range(4):
            hr = slice(h * HEAD_DIM, (h + 1) * HEAD_DIM)
            dq[hr, ri] = dq[hr, ri] + dqs[h]

    def quarter(t):
        return pl.ds(pl.multiple_of(t * 64, 64), 64)

    def h_up(i, t, last):
        if last:
            return remote(Hs.at[i, quarter(t)], Hx.at[quarter(t)], hu_s.at[i, t], hx_r.at[t], (dp, z + 1))
        return remote(Hs.at[i, quarter(t)], Hi.at[i, quarter(t)], hu_s.at[i, t], hi_r.at[i, t], (dp, z + 1))

    def h_down(i, t):
        return remote(Hs.at[i, quarter(t)], Hi.at[i, quarter(t)], hd_s.at[i, t], hi_r.at[i, t], (dp, z - 1))

    def h_inward(i, t, act):
        pl.when(z > i)(lambda: act(h_down(i, t)))
        pl.when(z + 1 == i)(lambda: act(h_up(i, t, True)))
        pl.when(z + 1 < i)(lambda: act(h_up(i, t, False)))

    def h_wait(i, t):
        ref = Hi.at[i, quarter(t)]
        remote(ref, ref, hd_s.at[i, t], hi_r.at[i, t], (core, z)).wait_recv()

    def h_mid(i, depth):
        mid = ((z > i) & (z == 3 - depth)) | ((z < i) & (z == depth))

        @pl.when(mid)
        def _():
            @pl.loop(0, 4)
            def _(t):
                h_wait(i, t)
                Hs[i, quarter(t), :] = (
                    Hs[i, quarter(t), :].astype(F32) + Hi[i, quarter(t), :].astype(F32)
                ).astype(BF)
                h_inward(i, t, begin)

    def finish(i):
        rows = pl.ds(pl.multiple_of(i * 256, 256), 256)
        cb, sb = cs[rows, :], -sn[rows, :]
        low = (
            turn(dq[:, rows].T * (HEAD_DIM**-0.5), cb, sb).astype(BF),
            turn(dk[rows, :], cb, sb).astype(BF),
            dv[rows, :].astype(BF),
        )
        for p in range(3):
            dqkvT[p * 256 : (p + 1) * 256, rows] = low[p].T
        for half in range(2):
            hc = slice(half * 512, half * 512 + 512)
            dh = sum(
                lax.dot_general(low[p], wq[p, hc, :], NT, preferred_element_type=F32) for p in range(3)
            )
            Hs[i, :, hc] = dh.astype(BF)

            @pl.when(z == i)
            def _(dh=dh, hc=hc):
                acc[:, hc] = dh

        @pl.when(((z == 3) & (z > i)) | ((z == 0) & (z < i)))
        def _():
            for t in range(4):
                h_inward(i, t, begin)


    slots = {0: [3], 2: [4], 5: [5], 8: [6], 11: [7], 14: [8]}
    h_slots = {14: [(0, 1), (3, 1)]}

    @pl.loop(0, 16)
    def _(n):
        def past(v):
            return lax.div(n + 16 - v, 16)

        ph = past(7) + past(12) + past(15)
        t = n - 7 * past(7) - 5 * past(12) - 3 * past(15)
        left = 4 - ph
        over = lax.div(t, left)
        li = ph + over * (t - left + 1)
        lj = ph + (1 - over) * t
        pair(block_order(li), block_order(lj))
        pl.when((n == 6) | (n == 11) | (n == 14) | (n == 15))(lambda: finish(block_order(ph)))
        for s in range(16):
            todo = [lambda t=t: tick(t) for t in slots.get(s, ())]
            todo += [lambda i=i, d=d: h_mid(i, d) for i, d in h_slots.get(s, ())]

            @pl.when(n == s)
            def _(todo=todo):
                for op in todo:
                    op()

    @pl.loop(0, 4)
    def _(t):
        tc = cols(t * 256, 256)
        Wp[:, tc] = jnp.dot(dqkvT[...], h1[:, tc], preferred_element_type=F32).astype(BF)

    def core_copy(w):
        return remote(
            Wp.at[:, cols(w * 256 + (1 - c) * 128, 128)], Wc.at[w], wc_s.at[w], wc_r.at[w], (core, z)
        )

    for w in range(4):
        core_copy(w).start()
    tick(9)

    def both(w):
        Wc[w] = (Wc[w].astype(F32) + Wp[:, cols(w * 256 + c * 128, 128)].astype(F32)).astype(BF)

    for w in range(4):
        core_copy(w).wait_recv()
    both(chip_d)
    both(chip_b)
    wb_copy = [
        remote(Wc.at[where], Wb.at[slot], wb_s.at[slot], wb_r.at[slot], (b, z))
        for slot, where in ((0, chip_b), (1, chip_d))
    ]
    wb_copy[1].start()
    wb_copy[0].start()
    both(chip_a)
    both(chip)
    wa_copy = remote(Wc.at[chip_a], Wa, wa_s, wa_r, (a, z))
    h_mid(3, 2)
    h_mid(0, 2)
    wb_copy[1].wait_recv()
    Wc[chip_a] = (Wc[chip_a].astype(F32) + Wb[1].astype(F32)).astype(BF)
    wa_copy.start()
    h_mid(2, 1)
    h_mid(1, 1)
    u_copies[1].wait_recv()
    u_copies[2].wait_recv()
    out_o[...] = (dtok_o[...] + ur[1].astype(F32) + uzr[...].astype(F32)).astype(BF)

    for t in range(4):
        ref = Hx.at[quarter(t)]
        pl.when(z < 3)(lambda t=t: h_wait(z, t))
        pl.when(z > 0)(lambda t=t, ref=ref: remote(ref, ref, hu_s.at[0, t], hx_r.at[t], (core, z)).wait_recv())
    has_above, has_below = z < 3, z > 0

    @pl.when(has_above)
    def _():
        acc[...] = acc[...] + Hi[z].astype(F32)

    @pl.when(has_below)
    def _():
        acc[...] = acc[...] + Hx[...].astype(F32)

    @pl.loop(0, 8)
    def _(r):
        xhat, rstd = norm_rows(tok[chunk(r), :].astype(F32))
        e1 = acc[chunk(r), :] * gain1
        m1 = jnp.mean(e1, axis=-1, keepdims=True)
        m2 = jnp.mean(e1 * xhat, axis=-1, keepdims=True)
        dtok_o[chunk(r), :] = dX1[chunk(r), :] + rstd * (e1 - m1 - xhat * m2)

    wb_copy[0].wait_recv()
    wa_copy.wait_recv()
    total = Wc[chip].astype(F32) + Wb[0].astype(F32) + Wa[...].astype(F32)
    dot_one = jnp.zeros((1, 128), F32)
    for p in range(3):
        piece = total[p * 256 : (p + 1) * 256, :]
        dwq_o[p] = piece.T
        dot_one = dot_one + jnp.sum(piece * wqkv[p].T.astype(F32), axis=0, keepdims=True)
    tick(10)
    tick(11)
    for e in range(NF + 1):

        @pl.when(no(org))
        def _(e=e):
            slot, _, ref = final(e)
            remote(ref, ref, fin_s.at[slot], fin_r.at[slot], (core, z)).wait_recv()

    part_two = jnp.sum(dwin_o[...] * w3[0 : 2 * HID, :].astype(F32), axis=0, keepdims=True)
    gz[z, 0:1, :] = dot_one / gains[dp, 0:1, :]
    gz[z, 1:2, :] = part_two / gains[dp, 1:2, :]
    gz[z, 2:8, :] = jnp.zeros((6, 128), F32)
    gain_copy = [
        remote(gz.at[z], gz.at[z], gz_s.at[n], gz_r.at[z], (dp, lax.rem(z + n, 4))) for n in range(1, 4)
    ]
    for cp in gain_copy:
        cp.start()
    for n in range(1, 4):
        o = lax.rem(z + n, 4)
        remote(gz.at[o], gz.at[o], gz_s.at[n], gz_r.at[o], (core, z)).wait_recv()
    dg_o[...] = gz[0] + gz[1] + gz[2] + gz[3]

    for cp in gain_copy:
        cp.wait_send()
    for w in range(4):
        core_copy(w).wait_send()
    wb_copy[0].wait_send()
    wb_copy[1].wait_send()
    wa_copy.wait_send()
    for i in range(4):
        for t in range(4):
            h_inward(i, t, done)
    for c0 in range(2):
        for qi in range(2):
            pl.when(no(is_self(c0, qi)))(lambda c0=c0, qi=qi: att_back(c0, qi).wait_send())
    for cp in d_copies[:2] + u_copies:
        cp.wait_send()
    for e in range(NU):
        unit_b(e, 0).wait_send()
        unit_b(e, 1).wait_send()
        unit_a(e).wait_send()
        if e < NF:
            pl.when(no(org))(lambda e=e: unit_z(e).wait_send())
        else:
            pl.when(z != 2 * c + e - NF)(lambda e=e: unit_o(e).wait_send())

        @pl.when(org if e < NF else z == 2 * c + e - NF)
        def _(e=e):
            slot, gift, dst = final(e)
            remote(gift, dst, fin_s.at[slot], fin_r.at[slot], (core, z)).wait_send()

    for d in range(1, 8):
        remote(gains_in, gains.at[dp], g_s.at[d], g_r.at[d], (core, z)).wait_send()
    for j in range(3):
        remote(wqkv, wq.at[:, own_rows], wr_s.at[j], wr_r.at[j], (core, z)).wait_send()
    for j in range(4):
        remote(wqkv, wq.at[:, own_rows], wx_s.at[j], wx_r.at[j], (core, z)).wait_send()
    for cp in hop:
        pl.when(no(org))(lambda cp=cp: cp.wait_send())
    for cp in cot_copy:
        cp.wait_send()
    for n in range(3):
        att_copy(n, lax.rem(z + 1 + n, 4)).wait_send()
    pl.when(no(org))(lambda: att_copy(3, z).wait_send())


def run_layer(*args):
    V = pl.BlockSpec(memory_space=pltpu.VMEM)
    S = pl.BlockSpec(memory_space=pltpu.SMEM)
    dma = pltpu.SemaphoreType.DMA
    s = jax.ShapeDtypeStruct
    vm = pltpu.VMEM
    return pl.pallas_call(
        layer_kernel,
        out_shape=(
            s((256, 1024), BF), s((256, 1024), F32), s((3, 128, 256), F32), s((2 * HID, 128), F32),
            s((HID, 128), F32), s((256, 128), F32), s((8, 128), F32),
        ),
        in_specs=[S, S] + [V] * 6 + [pl.BlockSpec(memory_space=pl.ANY)],
        out_specs=[V] * 7,
        scratch_shapes=[
            vm((8, 8, 128), F32), vm((FF3, 128), BF), vm((1024, 128), F32), vm((1024, 128), F32),
            vm((1024, 128), F32), vm((8, 1024), F32), vm((1024, 256), BF), vm((1024, 256), BF),
            vm((1024, 256), BF), vm((4, 4, 8, 256), F32), vm((1024, 256), BF), vm((512, 512), BF),
            vm((1024, 1024), BF), vm((3, 1024, 256), BF), vm((1024, 1024), BF),
            vm((FF3, 1024), BF), vm((2, 256, 1024), BF), vm((256, 1024), F32), vm((1024, 1024), BF), vm((512, 1024), BF),
            vm((256, 1024), F32), vm((256, 1024), F32), vm((HID, 1024), BF), vm((HID, 1024), BF),
            vm((HID, 1024), BF), vm((256, 1024), F32),
            vm((2, 256, 1024), BF), vm((2, 256, 1024), BF), vm((256, 1024), BF), vm((256, 1024), BF),
            vm((2, 256, 1024), BF), vm((2, 256, 1024), BF), vm((256, 1024), BF), vm((256, 1024), BF),
            vm((2, 512, 256), BF), vm((1024, 256), BF), vm((4, 4, 8, 256), F32),
            vm((256, 1024), F32), vm((1024, 256), F32), vm((1024, 256), F32),
            vm((4, 256, 1024), BF), vm((4, 256, 1024), BF), vm((256, 1024), BF),
            vm((2, FF3, 256), BF), vm((FF3, 256), BF), vm((FF3, 256), BF),
            vm((2, 2, 256, 256), BF), vm((2, 256, 256), BF), vm((3, 256, 256), BF), vm((FF3 + 256, 128), F32),
            vm((768, 1024), BF), vm((4, 768, 128), BF), vm((2, 768, 128), BF), vm((768, 128), BF), vm((4, 8, 128), F32),
            dma((4, 2)), dma((4, 2)), dma((4, 2)), dma((4, 2)),
            dma((3,)), dma((3,)), dma((4,)), dma((4,)), dma((8,)), dma((8,)), dma((3,)), dma((3,)), dma((2,)), dma((2,)),
            dma((4,)), dma((2,)), dma((2,)), dma((2,)), dma((2,)), dma((2,)), dma((2, 2)),
            dma((4,)), dma((4,)), dma((4,)), dma((4,)), dma((4,)), dma((4,)), dma((2, 4)), dma((4,)), dma((2, 2)),
            dma, dma, dma((3,)), dma((3,)), dma((3,)), dma((3,)), dma((3,)), dma((3,)), dma, dma, dma((2, 2)), dma((4,)),
            dma((2, NU)), dma((2, NU)), dma((NU,)), dma((NU,)), dma((NU,)), dma((3, NU)),
            dma((NF + 1,)), dma((NF + 1,)), dma((4, 4)), dma((4, 4)), dma((4, 4)), dma((4,)),
            dma((4,)), dma((4,)), dma((2,)), dma((2,)), dma, dma, dma((4,)), dma((4,)), dma,
        ],
        compiler_params=pltpu.CompilerParams(
            collective_id=1, has_side_effects=True, vmem_limit_bytes=63 << 20
        ),
        name="layer",
    )(*args)


def local_fast(
    tokens, lengths, seq_order, gain_attn, w_qkv, w_attn_out, gain_mlp, w_in, w_mlp_out, cotangent
):
    half = HEAD_DIM // 2
    frequency = jnp.tile(rope_base ** (-2.0 * jnp.arange(half, dtype=F32) / HEAD_DIM), 4)
    sign = jnp.tile(jnp.repeat(jnp.array([-1.0, 1.0], F32), half), 2)
    rows = (gain_attn.astype(F32), gain_mlp.astype(F32), frequency, sign)
    gains = jnp.concatenate([r[None, :] for r in rows] + [jnp.zeros((4, 128), F32)], axis=0)
    out, d_tok, d_qkv, d_in, d_down, d_out, d_gain = run_layer(
        lengths, seq_order, tokens, w_qkv, w_in.transpose(1, 2, 0).reshape(2 * HID, 128), w_mlp_out, w_attn_out, gains, cotangent
    )
    return (out, d_tok, d_gain[0], d_qkv, d_out, d_gain[1], d_in.reshape(2, HID, 128).transpose(2, 0, 1), d_down)


def layer_norm(field_in, norm_gain):
    row_mean = jnp.mean(field_in, axis=-1, keepdims=True)
    centered = field_in - row_mean
    variance = jnp.mean(centered * centered, axis=-1, keepdims=True)
    return centered * lax.rsqrt(variance + norm_eps) * norm_gain


def rotate(field_in, position):
    half_size = field_in.shape[-1] // 2
    index_range = jnp.arange(half_size, dtype=jnp.float32)
    frequency = rope_base ** (-2.0 * index_range / field_in.shape[-1])
    angles = position[:, None] * frequency[None, :]
    cosine = jnp.cos(angles)[:, None, :]
    sine_part = jnp.sin(angles)[:, None, :]
    first_half = field_in[..., :half_size]
    second_half = field_in[..., half_size:]
    return jnp.concatenate(
        [
            first_half * cosine - second_half * sine_part,
            second_half * cosine + first_half * sine_part,
        ],
        axis=-1,
    )


def geglu(act_part, up_part):
    return jax.nn.gelu(act_part, approximate=False) * up_part


def layout(lengths, seq_order, group_rows):
    seq_total = seq_order.shape[0]
    first_seq = lax.axis_index("dp") * SEQ_GRP
    chosen = lax.dynamic_slice_in_dim(seq_order, first_seq, SEQ_GRP)
    matched = chosen[:, None] == jnp.arange(seq_total, dtype=jnp.int32)[None, :]
    dealt_lengths = jnp.sum(jnp.where(matched, lengths[None, :], 0), axis=1)
    seq_ends = jnp.cumsum(dealt_lengths)
    row_index = jnp.arange(group_rows, dtype=jnp.int32)
    passed = row_index[:, None] >= seq_ends[None, :]
    segment = jnp.sum(passed.astype(jnp.int32), axis=1)
    row_start = jnp.sum(jnp.where(passed, dealt_lengths[None, :], 0), axis=1)
    return (segment, (row_index - row_start).astype(jnp.float32))


def item_layout(array_in, block_rows):
    group_rows, head_count, head_size = array_in.shape
    block_count = group_rows // block_rows
    shaped = array_in.reshape(block_count, block_rows, head_count, head_size)
    return shaped.transpose(2, 0, 1, 3).reshape(head_count * block_count, block_rows, head_size)


def from_items(items, group_rows):
    item_count, block_rows, head_size = items.shape
    block_count = group_rows // block_rows
    head_count = item_count // block_count
    shaped = items.reshape(head_count, block_count, block_rows, head_size)
    return shaped.transpose(1, 2, 0, 3).reshape(group_rows, head_count, head_size)


def masked_scores(query_block, key_head, segment_block, segment):
    score_scale = query_block.shape[-1] ** (-0.5)
    raw_scores = lax.dot_general(
        query_block, key_head, (((1,), (1,)), ((), ())), preferred_element_type=jnp.float32
    )
    allowed = segment_block[:, None] == segment[None, :]
    return jnp.where(allowed, raw_scores * score_scale, masked_fill)


def attend_forward(query_rot, key_rot, value_low, segment, block_rows):
    group_rows, head_count, head_size = query_rot.shape
    block_count = group_rows // block_rows
    query_items = item_layout(query_rot, block_rows)
    key_heads = key_rot.transpose(1, 0, 2)
    value_heads = value_low.transpose(1, 0, 2)
    segment_blocks = segment.reshape(block_count, block_rows)

    def one_item(item_index):
        head_index = item_index // block_count
        block_index = item_index % block_count
        query_block = lax.dynamic_index_in_dim(query_items, item_index, 0, False)
        key_head = lax.dynamic_index_in_dim(key_heads, head_index, 0, False)
        value_head = lax.dynamic_index_in_dim(value_heads, head_index, 0, False)
        segment_block = lax.dynamic_index_in_dim(segment_blocks, block_index, 0, False)
        scores = masked_scores(query_block, key_head, segment_block, segment)
        row_top = jnp.max(scores, axis=1, keepdims=True)
        weights = jnp.exp(scores - row_top)
        row_total = jnp.sum(weights, axis=1, keepdims=True)
        probs_low = (weights / row_total).astype(jnp.bfloat16)
        result = jnp.dot(probs_low, value_head, preferred_element_type=jnp.float32)
        return (result, row_top[:, 0] + jnp.log(row_total[:, 0]))

    results, log_totals = lax.map(one_item, jnp.arange(head_count * block_count, dtype=jnp.int32))
    return (from_items(results, group_rows), log_totals)


def attend_backward(query_rot, key_rot, value_low, grad_out, log_totals, segment, block_rows):
    group_rows, head_count, head_size = query_rot.shape
    block_count = group_rows // block_rows
    score_scale = head_size ** (-0.5)
    query_items = item_layout(query_rot, block_rows)
    grad_items = item_layout(grad_out, block_rows)
    key_heads = key_rot.transpose(1, 0, 2)
    value_heads = value_low.transpose(1, 0, 2)
    segment_blocks = segment.reshape(block_count, block_rows)

    def one_item(carried, item_index):
        key_grads, value_grads = carried
        head_index = item_index // block_count
        block_index = item_index % block_count
        query_block = lax.dynamic_index_in_dim(query_items, item_index, 0, False)
        grad_block = lax.dynamic_index_in_dim(grad_items, item_index, 0, False)
        log_row = lax.dynamic_index_in_dim(log_totals, item_index, 0, False)
        key_head = lax.dynamic_index_in_dim(key_heads, head_index, 0, False)
        value_head = lax.dynamic_index_in_dim(value_heads, head_index, 0, False)
        segment_block = lax.dynamic_index_in_dim(segment_blocks, block_index, 0, False)
        scores = masked_scores(query_block, key_head, segment_block, segment)
        prob_full = jnp.exp(scores - log_row[:, None])
        probs_low = prob_full.astype(jnp.bfloat16)
        grad_probs = lax.dot_general(
            grad_block, value_head, (((1,), (1,)), ((), ())), preferred_element_type=jnp.float32
        )
        row_delta = jnp.sum(prob_full * grad_probs, axis=1, keepdims=True)
        grad_scores = (prob_full * (grad_probs - row_delta)).astype(jnp.bfloat16)
        grad_query = (
            jnp.dot(grad_scores, key_head, preferred_element_type=jnp.float32) * score_scale
        )
        grad_key = (
            lax.dot_general(
                grad_scores,
                query_block,
                (((0,), (0,)), ((), ())),
                preferred_element_type=jnp.float32,
            )
            * score_scale
        )
        grad_value = lax.dot_general(
            probs_low, grad_block, (((0,), (0,)), ((), ())), preferred_element_type=jnp.float32
        )
        key_grads = lax.dynamic_update_index_in_dim(
            key_grads,
            lax.dynamic_index_in_dim(key_grads, head_index, 0, False) + grad_key,
            head_index,
            0,
        )
        value_grads = lax.dynamic_update_index_in_dim(
            value_grads,
            lax.dynamic_index_in_dim(value_grads, head_index, 0, False) + grad_value,
            head_index,
            0,
        )
        return ((key_grads, value_grads), grad_query)

    zero_heads = jnp.zeros((head_count, group_rows, head_size), jnp.float32)
    (key_grads, value_grads), query_grads = lax.scan(
        one_item, (zero_heads, zero_heads), jnp.arange(head_count * block_count, dtype=jnp.int32)
    )
    return (
        from_items(query_grads, group_rows),
        key_grads.transpose(1, 0, 2),
        value_grads.transpose(1, 0, 2),
    )


def spread_rows(local_rows):
    return lax.all_gather(local_rows, "tensor", axis=0, tiled=True)


def spread_grads(local_grads):
    return lax.all_gather(local_grads, "tensor", axis=0, tiled=True)


def sum_heads(activations, weight_part, row_count):

    def row_term(first_row, row_number):
        return jnp.dot(activations, weight_part, preferred_element_type=jnp.float32)

    return lax.psum_scatter(
        row_term(jnp.int32(0), row_count * lax.axis_size("tensor")),
        "tensor",
        scatter_dimension=0,
        tiled=True,
    )


def sum_grads(grads_low, weight_full, einsum_form, row_count):

    def row_term(first_row, row_number):
        return jnp.einsum(einsum_form, grads_low, weight_full, preferred_element_type=jnp.float32)

    return lax.psum_scatter(
        row_term(jnp.int32(0), row_count * lax.axis_size("tensor")),
        "tensor",
        scatter_dimension=0,
        tiled=True,
    )


def local_plain(
    tokens, lengths, seq_order, gain_attn, w_qkv, w_attn_out, gain_mlp, w_in, w_mlp_out, cotangent
):
    row_count = tokens.shape[0]
    group_rows = row_count * lax.axis_size("tensor")
    block_rows = min(512, group_rows)
    segment, position = layout(lengths, seq_order, group_rows)
    gain_low_one, qkv_weight, out_weight, gain_low_two, in_weight, down_weight = (
        lax.all_gather(gain_attn, "dp", axis=0, tiled=True),
        lax.all_gather(w_qkv, "dp", axis=1, tiled=True),
        lax.all_gather(w_attn_out, "dp", axis=1, tiled=True),
        lax.all_gather(gain_mlp, "dp", axis=0, tiled=True),
        lax.all_gather(w_in, "dp", axis=0, tiled=True),
        lax.all_gather(w_mlp_out, "dp", axis=1, tiled=True),
    )
    gain_one = gain_low_one.astype(jnp.float32)
    gain_two = gain_low_two.astype(jnp.float32)
    residual = tokens.astype(jnp.float32)
    normed_one = spread_rows(layer_norm(residual, gain_one).astype(jnp.bfloat16))
    qkv = jnp.einsum("rd,pdc->rpc", normed_one, qkv_weight, preferred_element_type=jnp.float32)
    head_count = qkv.shape[2] // HEAD_DIM
    head_shape = (group_rows, head_count, HEAD_DIM)
    query_rot = rotate(qkv[:, 0].reshape(head_shape), position).astype(jnp.bfloat16)
    key_rot = rotate(qkv[:, 1].reshape(head_shape), position).astype(jnp.bfloat16)
    value_low = qkv[:, 2].reshape(head_shape).astype(jnp.bfloat16)
    attended, log_totals = attend_forward(query_rot, key_rot, value_low, segment, block_rows)
    attn_low = attended.reshape(group_rows, head_count * HEAD_DIM).astype(jnp.bfloat16)
    resid_mid = residual + sum_heads(attn_low, out_weight, row_count)
    normed_two = spread_rows(layer_norm(resid_mid, gain_two).astype(jnp.bfloat16))
    gate_up = jnp.einsum("rd,dpc->rpc", normed_two, in_weight, preferred_element_type=jnp.float32)
    hidden = geglu(gate_up[:, 0], gate_up[:, 1]).astype(jnp.bfloat16)
    output = (resid_mid + sum_heads(hidden, down_weight, row_count)).astype(jnp.bfloat16)
    grad_two = spread_grads(cotangent)
    d_hidden = lax.dot_general(
        grad_two, down_weight, (((1,), (1,)), ((), ())), preferred_element_type=jnp.float32
    )
    d_down = lax.dot_general(
        hidden, grad_two, (((0,), (0,)), ((), ())), preferred_element_type=jnp.float32
    )
    geglu_pull = jax.vjp(geglu, gate_up[:, 0], gate_up[:, 1])[1]
    d_act, d_up = geglu_pull(d_hidden)
    d_gate_up = jnp.stack([d_act, d_up], axis=1).astype(jnp.bfloat16)
    d_in = jnp.einsum("rd,rpc->dpc", normed_two, d_gate_up, preferred_element_type=jnp.float32)
    d_normed_two = sum_grads(d_gate_up, in_weight, "rpc,dpc->rd", row_count)
    norm_pull_two = jax.vjp(layer_norm, resid_mid, gain_two)[1]
    d_mid_norm, d_gain_two = norm_pull_two(d_normed_two)
    d_mid = cotangent.astype(jnp.float32) + d_mid_norm
    grad_one = spread_grads(d_mid.astype(jnp.bfloat16))
    d_out = lax.dot_general(
        attn_low, grad_one, (((0,), (0,)), ((), ())), preferred_element_type=jnp.float32
    )
    d_att = lax.dot_general(
        grad_one, out_weight, (((1,), (1,)), ((), ())), preferred_element_type=jnp.float32
    ).astype(jnp.bfloat16)
    d_query_rot, d_key_rot, d_value = attend_backward(
        query_rot, key_rot, value_low, d_att.reshape(head_shape), log_totals, segment, block_rows
    )
    rotate_pull = jax.vjp(lambda field_in: rotate(field_in, position), d_query_rot)[1]
    d_query = rotate_pull(d_query_rot)[0]
    d_key = rotate_pull(d_key_rot)[0]
    flat_shape = (group_rows, head_count * HEAD_DIM)
    d_qkv = jnp.stack(
        [d_query.reshape(flat_shape), d_key.reshape(flat_shape), d_value.reshape(flat_shape)],
        axis=1,
    ).astype(jnp.bfloat16)
    d_qkv_weight = jnp.einsum("rd,rpc->pdc", normed_one, d_qkv, preferred_element_type=jnp.float32)
    d_normed_one = sum_grads(d_qkv, qkv_weight, "rpc,pdc->rd", row_count)
    norm_pull_one = jax.vjp(layer_norm, residual, gain_one)[1]
    d_first, d_gain_one = norm_pull_one(d_normed_one)
    d_tokens = d_mid + d_first
    gain_sums = lax.psum((d_gain_one, d_gain_two), "tensor")
    shares = (
        lax.psum_scatter(gain_sums[0], "dp", scatter_dimension=0, tiled=True),
        lax.psum_scatter(d_qkv_weight, "dp", scatter_dimension=1, tiled=True),
        lax.psum_scatter(d_out, "dp", scatter_dimension=1, tiled=True),
        lax.psum_scatter(gain_sums[1], "dp", scatter_dimension=0, tiled=True),
        lax.psum_scatter(d_in, "dp", scatter_dimension=0, tiled=True),
        lax.psum_scatter(d_down, "dp", scatter_dimension=1, tiled=True),
    )
    return (output, d_tokens, shares[0], shares[1], shares[2], shares[3], shares[4], shares[5])


def solution(mesh):
    fast = mesh.shape["dp"] == 8 and mesh.shape["tensor"] == 4
    return jax.shard_map(
        local_fast if fast else local_plain,
        mesh=mesh,
        in_specs=(
            P(("dp", "tensor"), None),
            P(),
            P(),
            P("dp"),
            P(None, "dp", "tensor"),
            P("tensor", "dp"),
            P("dp"),
            P("dp", None, "tensor"),
            P("tensor", "dp"),
            P(("dp", "tensor"), None),
        ),
        out_specs=(
            P(("dp", "tensor"), None),
            P(("dp", "tensor"), None),
            P("dp"),
            P(None, "dp", "tensor"),
            P("tensor", "dp"),
            P("dp"),
            P("dp", None, "tensor"),
            P("tensor", "dp"),
        ),
        check_vma=False,
    )
```

```python
import functools

import jax
import jax.numpy as jnp
from jax import lax
from jax.experimental import pallas as pl
from jax.experimental.pallas import tpu as pltpu
from jax.sharding import PartitionSpec as P

HEAD_DIM = 64
SEQ_GRP = 4
rope_base = 160000.0
norm_eps = 1e-05
masked_fill = -1e30
MESH = pl.DeviceIdType.MESH
BF = jnp.bfloat16
F32 = jnp.float32

NT = (((1,), (1,)), ((), ()))
TN = (((0,), (0,)), ((), ()))


def place():
    dp = lax.axis_index("dp")
    z = lax.axis_index("tensor")
    c = lax.rem(dp, 2)
    x = lax.rem(lax.div(dp, 2), 2)
    y = lax.div(dp, 4)
    return dp, z, c, x, y


def flip(dp, bits, distance):
    out = dp
    for b, bit in enumerate(bits):
        if (distance >> b) & 1:
            out = out + (1 << b) - (2 << b) * bit
    return out


def remote(src, dst, send, recv, dev):
    return pltpu.make_async_remote_copy(
        src_ref=src, dst_ref=dst, send_sem=send, recv_sem=recv, device_id=dev, device_id_type=MESH
    )


def cols(start, size):
    return pl.ds(pl.multiple_of(start, size), size)


def greet(dp, z, bits):
    c = bits[0]
    barrier = pltpu.get_barrier_semaphore()
    peers = [(flip(dp, bits, d), z) for d in range(1, 8)]
    core = flip(dp, bits, 1)
    for k in range(1, 4):
        peers.append((dp, lax.rem(z + k, 4)))
        peers.append((core, lax.rem(z + k, 4)))
    for p in peers:
        pl.semaphore_signal(barrier, inc=1, device_id=p, device_id_type=MESH)
    pl.semaphore_wait(barrier, len(peers))


def norm_rows(v):
    mean = jnp.mean(v, axis=-1, keepdims=True)
    centered = v - mean
    var = jnp.mean(centered * centered, axis=-1, keepdims=True)
    rstd = lax.rsqrt(var + norm_eps)
    return centered * rstd, rstd


def turn(v, cs, sn):
    lane = lax.broadcasted_iota(jnp.int32, cs.shape, 1)
    low_half = lax.rem(lane, HEAD_DIM) < HEAD_DIM // 2
    parts = []
    for t in range(v.shape[1] // 128):
        piece = v[:, t * 128 : (t + 1) * 128]
        swapped = jnp.where(low_half, pltpu.roll(piece, 96, 1), pltpu.roll(piece, 32, 1))
        parts.append(piece * cs + swapped * sn)
    return jnp.concatenate(parts, axis=1)


def gain_row(gains, row):
    return jnp.concatenate([gains[p, row : row + 1, :] for p in range(8)], axis=1)


HID = 656
FF3 = 3 * HID
FROWS = ((0, HID), (HID, HID), (2 * HID, HID))
CUTS = ((0, 496), (496, 496), (992, 496), (1488, 480))
HALVES = tuple((m, o, n) for m in (2, 0, 1) for o, n in ((0, 336), (336, 320)))
NF = len(HALVES)
NU = NF + 2
INV_SQRT2 = 0.7071067811865476
INV_SQRT_2PI = 0.3989422804014327


def layer_kernel(
    lengths, seq_order, tok, wqkv, win, wmlp, wout, gains_in, cot,
    out_o, dtok_o, dwq_o, dwin_o, dwmlp_o, dwout_o, dg_o,
    gains, w3, cs, sn, segc, segr, q, k, v, lse, att, attn2, h1, wq, cot4,
    G, Wo, X1, h2a, dya, yr, acc, hidT, daT, duT, dX1, dsb, dr, dzs, dzr, usb, ur, uzs, uzr, dsend, datt, delta,
    dq, dk, dv, Hs, Hi, Hx, Rb, Ra, Z, Rbo, Rao, Zo, give, Wp, Wc, Wb, Wa, gz,
    us, ds, rb, ra, wr_s, wr_r, wx_s, wx_r, g_s, g_r, cx_s, cx_r, hop_s, hop_r,
    ou_s, o_r, oa_s, ob_s, of_s, oa_r, ob_r,
    fz_s, fz_r, pa_s, pb_s, pf_s, pa_r, pb_r, at_s, at_r,
    y_s, y_r, n_s, n_r, d_s, d_r, u_s, u_r, e_s, e_r, t_s, t_r,
    b_s, b_r, a_s, a_r, zu_s, z_r, fin_s, fin_r,
    hu_s, hd_s, hi_r, hx_r, wc_s, wc_r, wb_s, wb_r, wa_s, wa_r, gz_s, gz_r, lc,
):
    dp, z, c, x, y = place()
    bits = (c, x, y)
    core = flip(dp, bits, 1)
    px, py = flip(dp, bits, 2), flip(dp, bits, 4)
    a = (1 - c) * px + c * py
    b = (1 - c) * py + c * px
    chip, chip_a, chip_b = lax.div(dp, 2), lax.div(a, 2), lax.div(b, 2)
    chip_d = 3 - chip
    home = lax.div(z, 2)
    org = c == home
    zq = lax.rem(z, 2)
    zp = z + 1 - 2 * zq
    z2 = z + 2 - 4 * home
    end = (z == 0) | (z == 3)
    own = cols(c * 256, 256)
    other = cols((1 - c) * 256, 256)

    def block(core_bit, line_bit):
        return cols((2 * line_bit + core_bit) * 256, 256)

    ob, cb, zb, db = block(c, zq), block(1 - c, zq), block(c, 1 - zq), block(1 - c, 1 - zq)
    tall, vT, kT, oT, dqkvT = Hs, Hx, dzs, acc.at[:, 0:256], h2a.at[0:768]
    dw4 = (dwin_o.at[0:HID], dwin_o.at[HID : 2 * HID], dwmlp_o)
    greet(dp, z, bits)

    def no(cond):
        return jnp.logical_not(cond)

    def tok_up(k_, h):
        ref = tall.at[z - k_, pl.ds(h * 128, 128)]
        src = tok.at[pl.ds(h * 128, 128)] if k_ == 0 else ref
        return remote(src, ref, us.at[k_, h], rb.at[k_ + 1, h], (dp, z + 1))

    def tok_down(k_, h):
        ref = tall.at[z + k_, pl.ds(h * 128, 128)]
        src = tok.at[pl.ds(h * 128, 128)] if k_ == 0 else ref
        return remote(src, ref, ds.at[k_, h], ra.at[k_ + 1, h], (dp, z - 1))

    def up_ok(k_):
        return (z >= k_) & (z < 3)

    def down_ok(k_):
        return (z + k_ <= 3) & (z > 0)

    for h in range(2):
        pl.when(up_ok(0))(lambda h=h: tok_up(0, h).start())
        pl.when(down_ok(0))(lambda h=h: tok_down(0, h).start())

    for d in range(1, 8):
        remote(gains_in, gains.at[dp], g_s.at[d], g_r.at[d], (flip(dp, bits, d), z)).start()
    own_rows = cols(dp * 128, 128)
    for j, d in enumerate((2, 4, 6)):
        remote(wqkv, wq.at[:, own_rows], wr_s.at[j], wr_r.at[j], (flip(dp, bits, d), z)).start()
    remote(wqkv, wq.at[:, own_rows], wx_s.at[3], wx_r.at[3], (core, z)).start()
    cot_copy = (
        remote(cot, cot4.at[ob], cx_s.at[0], cx_r.at[0], (core, z)),
        remote(cot, cot4.at[ob], cx_s.at[1], cx_r.at[1], (dp, zp)),
        remote(cot4.at[zb], cot4.at[zb], cx_s.at[2], cx_r.at[2], (core, z)),
    )
    cot_copy[0].start()
    cot_local = pltpu.make_async_copy(cot, cot4.at[ob], lc)
    cot_local.start()

    w3[0 : 2 * HID, :] = win[...]
    w3[2 * HID : FF3, :] = wmlp[...]
    lanes = cols(dp * 128, 128)
    hop = (
        remote(w3, G.at[:, lanes], hop_s.at[0], hop_r.at[0], (core, z)),
        remote(wout, Wo.at[zq, :, lanes], hop_s.at[1], hop_r.at[1], (core, z)),
    )

    @pl.when(no(org))
    def _():
        hop[1].start()
        hop[0].start()

    @pl.when(org)
    def _():
        G[:, lanes] = w3[...]
        Wo[zq, :, lanes] = wout[...]

    gains[dp] = gains_in[...]
    wq[:, own_rows, :] = wqkv[...]
    tall[z] = tok[...]
    cot_local.wait()

    def begin(cp):
        cp.start()

    def done(cp):
        cp.wait_send()

    def piece(u, where):
        r0, n = CUTS[u]
        return G.at[pl.ds(r0, n), cols(where * 256, 256)]

    def way(u):
        s = lax.rem(c + u, 2)
        one = (1 - s) * px + s * py
        two = (1 - s) * py + s * px
        return one, two, lax.div(one, 2), lax.div(two, 2)

    def plane_a(u):
        return remote(piece(u, chip), piece(u, chip), pa_s.at[u], pa_r.at[u], (way(u)[0], z))

    def plane_b(u):
        return remote(piece(u, chip), piece(u, chip), pb_s.at[u], pb_r.at[0, u], (way(u)[1], z))

    def plane_f(u):
        ref = piece(u, way(u)[2])
        return remote(ref, ref, pf_s.at[u], pb_r.at[1, u], (way(u)[1], z))

    def leap(u):
        return remote(piece(u, chip), piece(u, chip), fz_s.at[u], fz_r.at[u], (dp, z2))

    def spread(u):
        plane_a(u).start()
        plane_b(u).start()

    def across(u):
        ref = piece(u, way(u)[2])
        remote(ref, ref, pa_s.at[u], pa_r.at[u], (way(u)[0], z)).wait_recv()
        plane_f(u).start()

    def land(u):
        leap(u).wait_recv()
        spread(u)

    near = (1 - c) * lax.div(z + 2, 3) + c * lax.div(z, 3)
    far = 1 - near

    def opiece(qi, where):
        return Wo.at[qi, :, cols(where * 256, 256)]

    def ofar(k_):
        ref = opiece(zq, chip)
        return remote(ref, ref, ou_s.at[k_], o_r.at[zq], (dp, lax.rem(z + k_, 4)))

    def oplane(qi):
        ref, ref_a = opiece(qi, chip), opiece(qi, chip_a)
        return (
            remote(ref, ref, oa_s.at[qi], oa_r.at[qi], (a, z)),
            remote(ref, ref, ob_s.at[qi], ob_r.at[0, qi], (b, z)),
            remote(ref_a, ref_a, of_s.at[qi], ob_r.at[1, qi], (b, z)),
        )

    def ospread(qi):
        cps = oplane(qi)
        cps[0].start()
        cps[1].start()

    def oland(qi):
        ref = opiece(qi, chip)
        remote(ref, ref, ou_s.at[1], o_r.at[qi], (core, z)).wait_recv()
        ospread(qi)

    def oacross(qi):
        ref = opiece(qi, chip_a)
        remote(ref, ref, oa_s.at[qi], oa_r.at[qi], (a, z)).wait_recv()
        oplane(qi)[2].start()

    ends, starts, total = [], [], 0
    for j in range(SEQ_GRP):
        ends.append(total)
        total = total + lengths[seq_order[dp * SEQ_GRP + j]]
    for dst, shape, axis in ((segc, (1024, 128), 0), (segr, (8, 1024), 1)):
        row = lax.broadcasted_iota(jnp.int32, shape, axis)
        seg = jnp.zeros(shape, F32)
        start = jnp.zeros(shape, jnp.int32)
        for j in range(1, SEQ_GRP):
            passed = row >= ends[j]
            seg = jnp.where(passed, float(j), seg)
            start = jnp.where(passed, ends[j], start)
        dst[...] = seg
        if axis == 0:
            angle = (row - start).astype(F32) * gains_in[2:3, :]
            cs[...] = jnp.cos(angle)
            sn[...] = jnp.sin(angle) * gains_in[3:4, :]

    for d in range(1, 8):
        p = flip(dp, bits, d)
        remote(gains_in, gains.at[p], g_s.at[d], g_r.at[d], (p, z)).wait_recv()

    @pl.when(org)
    def _():
        remote(wout, Wo.at[zq, :, cols(core * 128, 128)], hop_s.at[1], hop_r.at[1], (core, z)).wait_recv()
        ospread(near)
        remote(w3, G.at[:, cols(core * 128, 128)], hop_s.at[0], hop_r.at[0], (core, z)).wait_recv()
        for u in range(4):
            spread(u)

    for j, d in enumerate((2, 4, 6)):
        p = flip(dp, bits, d)
        rows = wq.at[:, cols(p * 128, 128)]
        remote(wqkv, rows, wr_s.at[j], wr_r.at[j], (p, z)).wait_recv()
        remote(rows, rows, wx_s.at[j], wx_r.at[j], (core, z)).start()
    for j, d in enumerate((3, 5, 7, 1)):
        p = flip(dp, bits, d)
        remote(wqkv, wq.at[:, cols(p * 128, 128)], wx_s.at[j], wx_r.at[j], (core, z)).wait_recv()

    gain1, gain2 = gain_row(gains, 0), gain_row(gains, 1)

    def project(s):
        base = s * 256

        @pl.loop(0, 8)
        def _(r):
            xhat, _r = norm_rows(tall[s, pl.ds(pl.multiple_of(r * 32, 32), 32), :].astype(F32))
            h1[pl.ds(pl.multiple_of(base + r * 32, 32), 32), :] = (xhat * gain1).astype(BF)

        rows = pl.ds(pl.multiple_of(base, 256), 256)
        hb = h1[rows, :]
        cb, sb = cs[rows, :], sn[rows, :]
        for p, dst in enumerate((q, k, v)):
            r = jnp.dot(hb, wq[p], preferred_element_type=F32)
            if p < 2:
                r = turn(r, cb, sb)
            if p == 0:
                r = r * (HEAD_DIM**-0.5)
            dst[rows, :] = r.astype(BF)

    for k_ in range(4):
        if k_ > 0:
            below, above = z - k_ >= 0, z + k_ <= 3
            for h in range(2):

                @pl.when(below)
                def _(k_=k_, h=h):
                    ref = tall.at[z - k_, pl.ds(h * 128, 128)]
                    remote(ref, ref, us.at[k_, h], rb.at[k_, h], (core, z)).wait_recv()
                    if k_ < 3:
                        pl.when(up_ok(k_))(lambda: tok_up(k_, h).start())

                @pl.when(above)
                def _(k_=k_, h=h):
                    ref = tall.at[z + k_, pl.ds(h * 128, 128)]
                    remote(ref, ref, ds.at[k_, h], ra.at[k_, h], (core, z)).wait_recv()
                    if k_ < 3:
                        pl.when(down_ok(k_))(lambda: tok_down(k_, h).start())

        if k_ == 1:

            @pl.when(org)
            def _():
                for n in range(1, 4):
                    ofar(n).start()

        @pl.loop(0, 2)
        def _(t, k_=k_):
            s = z - k_ + 2 * k_ * t
            pl.when((s >= 0) & (s <= 3) & ((k_ > 0) | (t == 0)))(lambda: project(s))

        if k_ == 1:

            @pl.when(org)
            def _():
                oacross(near)
                for u in range(4):
                    across(u)

        if k_ == 2:

            @pl.when(org & end)
            def _():
                for u in range(4):
                    leap(u).start()

    for s in range(4):
        vT[:, s * 256 : (s + 1) * 256] = v[s * 256 : (s + 1) * 256, :].T
    head_of = lax.div(lax.broadcasted_iota(jnp.int32, (256, 256), 1), HEAD_DIM)

    def attend(i):
        rows = pl.ds(pl.multiple_of(i * 256, 256), 256)
        qb = q[rows, :]
        seg_q = segr[0:1, rows]
        heads = range(4)
        qh = [jnp.where(head_of == h, qb, jnp.zeros((), BF)) for h in heads]
        chunks = [slice(kc * 256, kc * 256 + 256) for kc in range(4)]
        for h in heads:
            hr = slice(h * HEAD_DIM, (h + 1) * HEAD_DIM)
            scores, tops = [], []
            for keys in chunks:
                seg_k = segc[keys, :]
                same = jnp.concatenate([seg_k, seg_k], axis=1) == seg_q
                s = lax.dot_general(k[keys, :], qh[h], NT, preferred_element_type=F32)
                s = jnp.where(same, s, masked_fill)
                scores.append(s)
                tops.append(jnp.max(s, axis=0, keepdims=True))
            top = jnp.maximum(jnp.maximum(tops[0], tops[1]), jnp.maximum(tops[2], tops[3]))
            tot, out = 0.0, 0.0
            for keys, s in zip(chunks, scores):
                p = jnp.exp(s - top)
                tot = tot + jnp.sum(p, axis=0, keepdims=True)
                out = out + jnp.dot(vT[hr, keys], p.astype(BF), preferred_element_type=F32)
            oT[hr, :] = out * (1.0 / tot)
            lse[h, i] = jnp.broadcast_to(top + jnp.log(tot), (8, 256))
        att[rows, :] = oT[...].T.astype(BF)

    def att_slot(src_core, q):
        return attn2.at[cols(src_core * 256, 256), cols(q * 256, 256)]

    def att_copy(n, i):
        rows = pl.ds(pl.multiple_of(i * 256, 256), 256)
        return remote(
            att.at[rows, :], att_slot(c, zq), at_s.at[n], at_r.at[c, zq], (2 * chip + home, i)
        )

    @pl.loop(0, 4)
    def _(n):
        i = lax.rem(z + 1 + n, 4)
        attend(i)
        for m in range(4):

            @pl.when((n == m) & ((m < 3) | no(org)))
            def _(m=m):
                att_copy(m, i).start()

        @pl.when((n == 3) & org)
        def _():
            attn2[own, cols(zq * 256, 256)] = att[pl.ds(pl.multiple_of(z * 256, 256), 256), :]

        @pl.when((n == 1) & org & no(end))
        def _():
            for u in range(4):
                leap(u).start()

        pl.when(n == 3)(lambda: cot_copy[1].start())

        @pl.when((n == 1) & end)
        def _():
            oland(far)
            pl.when(no(org))(lambda: oland(near))

        @pl.when((n == 3) & end)
        def _():
            oacross(far)
            pl.when(no(org))(lambda: oacross(near))

    @pl.when(no(end))
    def _():
        oland(far)
        pl.when(no(org))(lambda: oland(near))

    @pl.when(no(end))
    def _():
        oacross(far)
        pl.when(no(org))(lambda: oacross(near))

    def late(*ops):
        @pl.when(no(org))
        def _():
            for op, u in ops:
                op(u)

    pl.when(no(end))(lambda: late((land, 0), (land, 1), (land, 2), (land, 3), (across, 0), (across, 1)))
    pl.when(end)(lambda: late((land, 0)))

    for k_ in range(3):
        for h in range(2):
            pl.when(up_ok(k_))(lambda k_=k_, h=h: tok_up(k_, h).wait_send())
            pl.when(down_ok(k_))(lambda k_=k_, h=h: tok_down(k_, h).wait_send())
    for src in range(2):
        for qi in range(2):
            mine_too = (c == src) & (z == 2 * c + qi)

            @pl.when(no(mine_too))
            def _(src=src, qi=qi):
                slot = att_slot(src, qi)
                remote(slot, slot, at_s.at[0], at_r.at[src, qi], (core, z)).wait_recv()

    pl.when(end)(lambda: late((land, 1)))
    for qi in range(2):
        for w, where in enumerate((chip_b, chip_d)):
            ref = opiece(qi, where)
            remote(ref, ref, ob_s.at[qi], ob_r.at[w, qi], (core, z)).wait_recv()

    def out_proj(rows):
        return sum(
            jnp.dot(attn2[rows, qi * 256 : (qi + 1) * 256], Wo[qi], preferred_element_type=F32) for qi in range(2)
        )

    acc[...] = out_proj(other)
    y_copy = remote(acc, yr, y_s, y_r, (core, z))
    y_copy.start()
    pl.when(end)(lambda: late((land, 2)))
    X1[...] = tok[...].astype(F32) + out_proj(own)
    y_copy.wait()
    pl.when(end)(lambda: late((land, 3)))

    def chunk(r):
        return pl.ds(pl.multiple_of(r * 32, 32), 32)

    def own_chunk(r):
        return pl.ds(pl.multiple_of(c * 256 + r * 32, 32), 32)

    def block_chunk(r):
        return pl.ds(pl.multiple_of((2 * zq + c) * 256 + r * 32, 32), 32)

    @pl.loop(0, 8)
    def _(r):
        x1 = X1[chunk(r), :] + yr[chunk(r), :]
        X1[chunk(r), :] = x1
        xhat, _r = norm_rows(x1)
        h2a[block_chunk(r), :] = (xhat * gain2).astype(BF)

    h_copy = (
        remote(h2a.at[ob], h2a.at[ob], n_s.at[0], n_r.at[0], (core, z)),
        remote(h2a.at[ob], h2a.at[ob], n_s.at[1], n_r.at[1], (dp, zp)),
        remote(h2a.at[zb], h2a.at[zb], n_s.at[2], n_r.at[2], (core, z)),
    )
    h_copy[1].start()
    h_copy[0].start()
    pl.when(end)(lambda: late((across, 0), (across, 1)))
    late((across, 2), (across, 3))
    remote(cot, cot4.at[zb], cx_s.at[1], cx_r.at[1], (dp, zp)).wait_recv()
    cot_copy[2].start()
    remote(cot, cot4.at[cb], cx_s.at[0], cx_r.at[0], (core, z)).wait_recv()
    remote(cot, cot4.at[db], cx_s.at[2], cx_r.at[2], (core, z)).wait_recv()
    for u in range(4):
        for w, where in enumerate((way(u)[3], chip_d)):
            ref = piece(u, where)
            remote(ref, ref, pb_s.at[u], pb_r.at[w, u], (core, z)).wait_recv()
    remote(h2a.at[cb], h2a.at[cb], n_s.at[0], n_r.at[0], (core, z)).wait_recv()

    def tile(r0, n, tokens):
        h2 = h2a[tokens, :]
        act = lax.dot_general(G[r0 : r0 + n, :], h2, NT, preferred_element_type=F32)
        up = lax.dot_general(G[HID + r0 : HID + r0 + n, :], h2, NT, preferred_element_type=F32)
        dh = lax.dot_general(
            G[2 * HID + r0 : 2 * HID + r0 + n, :], cot4[tokens, :], NT, preferred_element_type=F32
        )
        Phi = 0.5 + 0.5 * lax.erf(act * INV_SQRT2)
        phi = jnp.exp(-0.5 * act * act) * INV_SQRT_2PI
        gel = act * Phi
        rr = slice(r0, r0 + n)
        hidT[rr, tokens] = (gel * up).astype(BF)
        daT[rr, tokens] = (dh * up * (Phi + act * phi)).astype(BF)
        duT[rr, tokens] = (dh * gel).astype(BF)

    @pl.loop(0, 2)
    def _(t):
        there = lax.rem(zq + t, 2)

        @pl.when(t == 1)
        def _():
            remote(h2a.at[zb], h2a.at[zb], n_s.at[1], n_r.at[1], (dp, zp)).wait_recv()
            h_copy[2].start()
            remote(h2a.at[db], h2a.at[db], n_s.at[2], n_r.at[2], (core, z)).wait_recv()

        for r0, n in ((0, 224), (224, 224), (448, 208)):
            tile(r0, n, cols(there * 512, 512))

    def tn(lhs, rhs):
        return lax.dot_general(lhs, rhs, TN, preferred_element_type=F32)

    def f_rows(m):
        return pl.ds(FROWS[m][0], HID)

    def d_norm(rows, hc):
        return tn(daT[:, rows], G[f_rows(0), hc]) + tn(duT[:, rows], G[f_rows(1), hc])

    def mlp_out(rows, hc):
        return tn(hidT[:, rows], G[f_rows(2), hc])

    def quad(term, sb, got, zs, zgot, ss, rs, hold=False):
        halves = (slice(0, 512), slice(512, 1024))
        copies = (
            remote(sb.at[0], got.at[0], ss.at[0], rs.at[0], (core, z)),
            remote(sb.at[1], got.at[1], ss.at[1], rs.at[1], (core, z)),
            remote(zs, zgot, ss.at[2], rs.at[2], (dp, zp)),
        )
        for j, rows in enumerate((db, cb)):
            for hc in halves:
                sb[j, :, hc] = term(rows, hc).astype(BF)
            copies[j].start()
        copies[0].wait_recv()
        for hc in halves:
            zs[:, hc] = (term(zb, hc) + got[0, :, hc].astype(F32)).astype(BF)
        if not hold:
            copies[2].start()
        return copies

    def keep(term, dst, plus=None):
        for hc in (slice(0, 512), slice(512, 1024)):
            r = term(ob, hc)
            dst[:, hc] = r if plus is None else r + plus[:, hc]

    def grads(m):
        lhs, rhs = ((daT, h2a), (duT, h2a), (hidT, cot4))[m]

        @pl.loop(0, 4)
        def _(t):
            tc = cols(t * 256, 256)
            G[f_rows(m), tc] = jnp.dot(lhs[...], rhs[:, tc], preferred_element_type=F32).astype(BF)

    def rows_of(e):
        m, o, n = HALVES[e]
        return pl.ds(FROWS[m][0] + o, n)

    def part(e, where):
        if e < NF:
            return G.at[rows_of(e), cols(where * 256, 256)]
        return opiece(e - NF, where)

    def from_b(e, slot):
        return Rb.at[slot, rows_of(e)] if e < NF else Rbo.at[slot, e - NF]

    def from_a(e):
        return Ra.at[rows_of(e)] if e < NF else Rao.at[e - NF]

    def unit_b(e, slot):
        src = part(e, chip_b if slot == 0 else chip_d)
        return remote(src, from_b(e, slot), b_s.at[slot, e], b_r.at[slot, e], (b, z))

    def unit_a(e):
        return remote(part(e, chip_a), from_a(e), a_s.at[e], a_r.at[e], (a, z))

    def send_b(e):
        unit_b(e, 1).start()
        unit_b(e, 0).start()

    def stage1(e):
        unit_b(e, 1).wait_recv()
        ref = part(e, chip_a)
        ref[...] = (ref[...].astype(F32) + from_b(e, 1)[...].astype(F32)).astype(BF)
        unit_a(e).start()

    def unit_z(e):
        return remote(part(e, chip), Z.at[rows_of(e)], zu_s.at[e], z_r.at[0, e], (dp, z2))

    def unit_o(e):
        t = 2 * c + e - NF
        slot = lax.rem(z - t + 4, 4) - 1
        return remote(part(e, chip), Zo.at[slot], zu_s.at[e], z_r.at[slot, e], (dp, t))

    def stage2(e):
        unit_b(e, 0).wait_recv()
        unit_a(e).wait_recv()
        ref = part(e, chip)
        ref[...] = (
            ref[...].astype(F32) + from_b(e, 0)[...].astype(F32) + from_a(e)[...].astype(F32)
        ).astype(BF)
        if e < NF:
            pl.when(no(org))(lambda: unit_z(e).start())
        else:
            pl.when(z != 2 * c + e - NF)(lambda: unit_o(e).start())

    def line_wait(e, slot):
        remote(Zo.at[slot], Zo.at[slot], zu_s.at[e], z_r.at[slot, e], (core, z)).wait_recv()

    def final(e):
        if e < NF:
            m, o, n = HALVES[e]
            return e, give.at[rows_of(e)], dw4[m].at[pl.ds(o, n)]
        return NF, give.at[FF3 : FF3 + 256], dwout_o

    def stage4(e):
        here = org if e < NF else z == 2 * c + e - NF

        @pl.when(here)
        def _():
            slot, gift, dst = final(e)
            if e < NF:
                unit_z(e).wait_recv()
            for who, ref in ((c, dst), (1 - c, gift)):
                ref[...] = part(e, chip)[:, cols(who * 128, 128)].astype(F32)

            def take(got):
                for who, ref in ((c, dst), (1 - c, gift)):
                    ref[...] = ref[...] + got[:, cols(who * 128, 128)].astype(F32)

            def line_take(where):
                line_wait(e, where)
                take(Zo.at[where])

            if e < NF:
                take(Z.at[rows_of(e)])
            else:
                for slot_ in range(3):
                    line_take(slot_)
            remote(gift, dst, fin_s.at[slot], fin_r.at[slot], (core, z)).start()

    def tick(t):
        for lag, step in ((0, stage1), (1, stage2), (4, stage4)):
            if 0 <= t - lag < NU:
                step(t - lag)

    d_copies = quad(d_norm, dsb, dr, dzs, dzr, d_s, d_r)
    keep(d_norm, dX1)
    u_copies = quad(mlp_out, usb, ur, uzs, uzr, u_s, u_r, hold=True)
    keep(mlp_out, dtok_o, X1)
    for u in range(4):
        plane_a(u).wait_send()
        plane_b(u).wait_send()
        plane_f(u).wait_send()
        pl.when(org)(lambda u=u: leap(u).wait_send())

    def ff_grads(m):
        grads(m)
        for e in range(NF):
            if HALVES[e][0] == m:
                send_b(e)

    ff_grads(2)
    ff_grads(0)
    ff_grads(1)
    d_copies[1].wait_recv()
    d_copies[2].wait_recv()

    @pl.loop(0, 8)
    def _(r):
        dh2 = dX1[chunk(r), :] + dr[1, chunk(r), :].astype(F32) + dzr[chunk(r), :].astype(F32)
        xhat, rstd = norm_rows(X1[chunk(r), :])
        e2 = dh2 * gain2
        m1 = jnp.mean(e2, axis=-1, keepdims=True)
        m2 = jnp.mean(e2 * xhat, axis=-1, keepdims=True)
        dx = cot4[block_chunk(r), :].astype(F32) + rstd * (e2 - m1 - xhat * m2)
        dX1[chunk(r), :] = dx
        dya[own_chunk(r), :] = dx.astype(BF)

    e_copy = remote(dya.at[own], dya.at[own], e_s, e_r, (core, z))
    e_copy.start()
    tick(0)
    e_copy.wait()
    for qi in range(2):
        dsend[qi] = lax.dot_general(dya[...], Wo[qi], NT, preferred_element_type=F32).astype(BF)

    def att_back(c0, qi):
        dst = datt.at[cols(z * 256, 256)]
        return remote(
            dsend.at[qi, pl.ds(c0 * 256, 256)], dst, t_s.at[c0, qi], t_r.at[z], (2 * chip + c0, 2 * c + qi)
        )

    def is_self(c0, qi):
        return (c == c0) & (z == 2 * c + qi)

    for c0 in range(2):
        for qi in range(2):
            pl.when(no(is_self(c0, qi)))(lambda c0=c0, qi=qi: att_back(c0, qi).start())

            @pl.when(is_self(c0, qi))
            def _(c0=c0, qi=qi):
                datt[cols(z * 256, 256), :] = dsend[qi, c0 * 256 : (c0 + 1) * 256, :]

    u_copies[2].start()
    for n in range(1, 4):
        pl.when(org)(lambda n=n: ofar(n).wait_send())
    for qi in range(2):
        for cp in oplane(qi):
            cp.wait_send()

        @pl.loop(0, 4)
        def _(t, qi=qi):
            tc = cols(t * 256, 256)
            Wo[qi, :, tc] = tn(attn2[:, qi * 256 : (qi + 1) * 256], dya[:, tc]).astype(BF)

        send_b(NF + qi)
    tick(1)
    tick(2)
    for cp in h_copy:
        cp.wait_send()
    d_copies[2].wait_send()
    for s in range(4):
        kT[:, s * 256 : (s + 1) * 256] = k[s * 256 : (s + 1) * 256, :].T
    dq[...] = jnp.zeros_like(dq)
    dk[...] = jnp.zeros_like(dk)
    dv[...] = jnp.zeros_like(dv)
    for i in range(4):

        @pl.when(no(org & (z == i)))
        def _(i=i):
            ref = datt.at[pl.ds(i * 256, 256)]
            remote(ref, ref, t_s.at[0, 0], t_r.at[i], (core, z)).wait_recv()

    @pl.loop(0, 4)
    def _(i):
        rows = pl.ds(pl.multiple_of(i * 256, 256), 256)
        t = (datt[rows, :].astype(F32) * att[rows, :].astype(F32)).T
        for h in range(4):
            s = jnp.sum(t[h * 64 : (h + 1) * 64, :], axis=0, keepdims=True)
            delta[h, i] = jnp.broadcast_to(s, (8, 256))

    def block_order(l):
        inner = lax.div(z * (3 - z), 2)
        base = inner * jnp.minimum(l, 1) * (lax.rem(l + 1, 3) + 1) + (1 - inner) * l
        return (1 - home) * (3 - base) + home * base

    def pair(i, j):
        ri = pl.ds(pl.multiple_of(i * 256, 256), 256)
        rj = pl.ds(pl.multiple_of(j * 256, 256), 256)

        kj, vj, qi_, dai = k[rj, :], v[rj, :], q[ri, :], datt[ri, :]
        seg_k = segc[rj, :]
        same = jnp.concatenate([seg_k, seg_k], axis=1) == segr[0:1, ri]
        none = jnp.zeros((), BF)
        heads = range(4)
        qh = [jnp.where(head_of == h, qi_, none) for h in heads]
        dah = [jnp.where(head_of == h, dai, none) for h in heads]
        ss = [lax.dot_general(kj, qh[h], NT, preferred_element_type=F32) for h in heads]
        dps = [lax.dot_general(vj, dah[h], NT, preferred_element_type=F32) for h in heads]
        ps = [jnp.exp(jnp.where(same, ss[h], masked_fill) - lse[h, i, 0:1, :]) for h in heads]
        dss = [(ps[h] * (dps[h] - delta[h, i, 0:1, :])).astype(BF) for h in heads]
        dvs = [jnp.dot(ps[h].astype(BF), dah[h], preferred_element_type=F32) for h in heads]
        dks = [jnp.dot(dss[h], qh[h], preferred_element_type=F32) for h in heads]
        dqs = [
            jnp.dot(kT[h * HEAD_DIM : (h + 1) * HEAD_DIM, rj], dss[h], preferred_element_type=F32) for h in heads
        ]
        dv[rj, :] = dv[rj, :] + (dvs[0] + dvs[1] + dvs[2] + dvs[3])
        dk[rj, :] = dk[rj, :] + (dks[0] + dks[1] + dks[2] + dks[3])
        for h in range(4):
            hr = slice(h * HEAD_DIM, (h + 1) * HEAD_DIM)
            dq[hr, ri] = dq[hr, ri] + dqs[h]

    def quarter(t):
        return pl.ds(pl.multiple_of(t * 64, 64), 64)

    def h_up(i, t, last):
        if last:
            return remote(Hs.at[i, quarter(t)], Hx.at[quarter(t)], hu_s.at[i, t], hx_r.at[t], (dp, z + 1))
        return remote(Hs.at[i, quarter(t)], Hi.at[i, quarter(t)], hu_s.at[i, t], hi_r.at[i, t], (dp, z + 1))

    def h_down(i, t):
        return remote(Hs.at[i, quarter(t)], Hi.at[i, quarter(t)], hd_s.at[i, t], hi_r.at[i, t], (dp, z - 1))

    def h_inward(i, t, act):
        pl.when(z > i)(lambda: act(h_down(i, t)))
        pl.when(z + 1 == i)(lambda: act(h_up(i, t, True)))
        pl.when(z + 1 < i)(lambda: act(h_up(i, t, False)))

    def h_wait(i, t):
        ref = Hi.at[i, quarter(t)]
        remote(ref, ref, hd_s.at[i, t], hi_r.at[i, t], (core, z)).wait_recv()

    def h_mid(i, depth):
        mid = ((z > i) & (z == 3 - depth)) | ((z < i) & (z == depth))

        @pl.when(mid)
        def _():
            @pl.loop(0, 4)
            def _(t):
                h_wait(i, t)
                Hs[i, quarter(t), :] = (
                    Hs[i, quarter(t), :].astype(F32) + Hi[i, quarter(t), :].astype(F32)
                ).astype(BF)
                h_inward(i, t, begin)

    def finish(i):
        rows = pl.ds(pl.multiple_of(i * 256, 256), 256)
        cb, sb = cs[rows, :], -sn[rows, :]
        low = (
            turn(dq[:, rows].T * (HEAD_DIM**-0.5), cb, sb).astype(BF),
            turn(dk[rows, :], cb, sb).astype(BF),
            dv[rows, :].astype(BF),
        )
        for p in range(3):
            dqkvT[p * 256 : (p + 1) * 256, rows] = low[p].T
        for half in range(2):
            hc = slice(half * 512, half * 512 + 512)
            dh = sum(
                lax.dot_general(low[p], wq[p, hc, :], NT, preferred_element_type=F32) for p in range(3)
            )
            Hs[i, :, hc] = dh.astype(BF)

            @pl.when(z == i)
            def _(dh=dh, hc=hc):
                acc[:, hc] = dh

        @pl.when(((z == 3) & (z > i)) | ((z == 0) & (z < i)))
        def _():
            for t in range(4):
                h_inward(i, t, begin)


    slots = {0: [3], 2: [4], 5: [5], 8: [6], 11: [7], 14: [8]}
    h_slots = {14: [(0, 1), (3, 1)]}

    @pl.loop(0, 16)
    def _(n):
        def past(v):
            return lax.div(n + 16 - v, 16)

        ph = past(7) + past(12) + past(15)
        t = n - 7 * past(7) - 5 * past(12) - 3 * past(15)
        left = 4 - ph
        over = lax.div(t, left)
        li = ph + over * (t - left + 1)
        lj = ph + (1 - over) * t
        pair(block_order(li), block_order(lj))
        pl.when((n == 6) | (n == 11) | (n == 14) | (n == 15))(lambda: finish(block_order(ph)))
        for s in range(16):
            todo = [lambda t=t: tick(t) for t in slots.get(s, ())]
            todo += [lambda i=i, d=d: h_mid(i, d) for i, d in h_slots.get(s, ())]

            @pl.when(n == s)
            def _(todo=todo):
                for op in todo:
                    op()

    @pl.loop(0, 4)
    def _(t):
        tc = cols(t * 256, 256)
        Wp[:, tc] = jnp.dot(dqkvT[...], h1[:, tc], preferred_element_type=F32).astype(BF)

    def core_copy(w):
        return remote(
            Wp.at[:, cols(w * 256 + (1 - c) * 128, 128)], Wc.at[w], wc_s.at[w], wc_r.at[w], (core, z)
        )

    for w in range(4):
        core_copy(w).start()
    tick(9)

    def both(w):
        Wc[w] = (Wc[w].astype(F32) + Wp[:, cols(w * 256 + c * 128, 128)].astype(F32)).astype(BF)

    for w in range(4):
        core_copy(w).wait_recv()
    both(chip_d)
    both(chip_b)
    wb_copy = [
        remote(Wc.at[where], Wb.at[slot], wb_s.at[slot], wb_r.at[slot], (b, z))
        for slot, where in ((0, chip_b), (1, chip_d))
    ]
    wb_copy[1].start()
    wb_copy[0].start()
    both(chip_a)
    both(chip)
    wa_copy = remote(Wc.at[chip_a], Wa, wa_s, wa_r, (a, z))
    h_mid(3, 2)
    h_mid(0, 2)
    wb_copy[1].wait_recv()
    Wc[chip_a] = (Wc[chip_a].astype(F32) + Wb[1].astype(F32)).astype(BF)
    wa_copy.start()
    h_mid(2, 1)
    h_mid(1, 1)
    u_copies[1].wait_recv()
    u_copies[2].wait_recv()
    out_o[...] = (dtok_o[...] + ur[1].astype(F32) + uzr[...].astype(F32)).astype(BF)

    wb_copy[0].wait_recv()
    wa_copy.wait_recv()
    total = Wc[chip].astype(F32) + Wb[0].astype(F32) + Wa[...].astype(F32)
    dot_one = jnp.zeros((1, 128), F32)
    for p in range(3):
        piece = total[p * 256 : (p + 1) * 256, :]
        dwq_o[p] = piece.T
        dot_one = dot_one + jnp.sum(piece * wqkv[p].T.astype(F32), axis=0, keepdims=True)
    def finals(slots_):
        for e in slots_:

            @pl.when(no(org))
            def _(e=e):
                slot, _, ref = final(e)
                remote(ref, ref, fin_s.at[slot], fin_r.at[slot], (core, z)).wait_recv()

    finals(range(NF))
    part_two = jnp.sum(dwin_o[...] * w3[0 : 2 * HID, :].astype(F32), axis=0, keepdims=True)
    gz[z, 0:1, :] = dot_one / gains[dp, 0:1, :]
    gz[z, 1:2, :] = part_two / gains[dp, 1:2, :]
    gz[z, 2:8, :] = jnp.zeros((6, 128), F32)
    gain_copy = [
        remote(gz.at[z], gz.at[z], gz_s.at[n], gz_r.at[z], (dp, lax.rem(z + n, 4))) for n in range(1, 4)
    ]
    for cp in gain_copy:
        cp.start()
    for t in range(4):
        ref = Hx.at[quarter(t)]
        pl.when(z < 3)(lambda t=t: h_wait(z, t))
        pl.when(z > 0)(lambda t=t, ref=ref: remote(ref, ref, hu_s.at[0, t], hx_r.at[t], (core, z)).wait_recv())
    has_above, has_below = z < 3, z > 0

    @pl.when(has_above)
    def _():
        acc[...] = acc[...] + Hi[z].astype(F32)

    @pl.when(has_below)
    def _():
        acc[...] = acc[...] + Hx[...].astype(F32)

    @pl.loop(0, 8)
    def _(r):
        xhat, rstd = norm_rows(tok[chunk(r), :].astype(F32))
        e1 = acc[chunk(r), :] * gain1
        m1 = jnp.mean(e1, axis=-1, keepdims=True)
        m2 = jnp.mean(e1 * xhat, axis=-1, keepdims=True)
        dtok_o[chunk(r), :] = dX1[chunk(r), :] + rstd * (e1 - m1 - xhat * m2)

    tick(10)
    tick(11)
    finals((NF,))
    for n in range(1, 4):
        o = lax.rem(z + n, 4)
        remote(gz.at[o], gz.at[o], gz_s.at[n], gz_r.at[o], (core, z)).wait_recv()
    dg_o[...] = gz[0] + gz[1] + gz[2] + gz[3]

    for cp in gain_copy:
        cp.wait_send()
    for w in range(4):
        core_copy(w).wait_send()
    wb_copy[0].wait_send()
    wb_copy[1].wait_send()
    wa_copy.wait_send()
    for i in range(4):
        for t in range(4):
            h_inward(i, t, done)
    for c0 in range(2):
        for qi in range(2):
            pl.when(no(is_self(c0, qi)))(lambda c0=c0, qi=qi: att_back(c0, qi).wait_send())
    for cp in d_copies[:2] + u_copies:
        cp.wait_send()
    for e in range(NU):
        unit_b(e, 0).wait_send()
        unit_b(e, 1).wait_send()
        unit_a(e).wait_send()
        if e < NF:
            pl.when(no(org))(lambda e=e: unit_z(e).wait_send())
        else:
            pl.when(z != 2 * c + e - NF)(lambda e=e: unit_o(e).wait_send())

        @pl.when(org if e < NF else z == 2 * c + e - NF)
        def _(e=e):
            slot, gift, dst = final(e)
            remote(gift, dst, fin_s.at[slot], fin_r.at[slot], (core, z)).wait_send()

    for d in range(1, 8):
        remote(gains_in, gains.at[dp], g_s.at[d], g_r.at[d], (core, z)).wait_send()
    for j in range(3):
        remote(wqkv, wq.at[:, own_rows], wr_s.at[j], wr_r.at[j], (core, z)).wait_send()
    for j in range(4):
        remote(wqkv, wq.at[:, own_rows], wx_s.at[j], wx_r.at[j], (core, z)).wait_send()
    for cp in hop:
        pl.when(no(org))(lambda cp=cp: cp.wait_send())
    for cp in cot_copy:
        cp.wait_send()
    for n in range(3):
        att_copy(n, lax.rem(z + 1 + n, 4)).wait_send()
    pl.when(no(org))(lambda: att_copy(3, z).wait_send())


def run_layer(*args):
    V = pl.BlockSpec(memory_space=pltpu.VMEM)
    S = pl.BlockSpec(memory_space=pltpu.SMEM)
    dma = pltpu.SemaphoreType.DMA
    s = jax.ShapeDtypeStruct
    vm = pltpu.VMEM
    return pl.pallas_call(
        layer_kernel,
        out_shape=(
            s((256, 1024), BF), s((256, 1024), F32), s((3, 128, 256), F32), s((2 * HID, 128), F32),
            s((HID, 128), F32), s((256, 128), F32), s((8, 128), F32),
        ),
        in_specs=[S, S] + [V] * 6 + [pl.BlockSpec(memory_space=pl.ANY)],
        out_specs=[V] * 7,
        scratch_shapes=[
            vm((8, 8, 128), F32), vm((FF3, 128), BF), vm((1024, 128), F32), vm((1024, 128), F32),
            vm((1024, 128), F32), vm((8, 1024), F32), vm((1024, 256), BF), vm((1024, 256), BF),
            vm((1024, 256), BF), vm((4, 4, 8, 256), F32), vm((1024, 256), BF), vm((512, 512), BF),
            vm((1024, 1024), BF), vm((3, 1024, 256), BF), vm((1024, 1024), BF),
            vm((FF3, 1024), BF), vm((2, 256, 1024), BF), vm((256, 1024), F32), vm((1024, 1024), BF), vm((512, 1024), BF),
            vm((256, 1024), F32), vm((256, 1024), F32), vm((HID, 1024), BF), vm((HID, 1024), BF),
            vm((HID, 1024), BF), vm((256, 1024), F32),
            vm((2, 256, 1024), BF), vm((2, 256, 1024), BF), vm((256, 1024), BF), vm((256, 1024), BF),
            vm((2, 256, 1024), BF), vm((2, 256, 1024), BF), vm((256, 1024), BF), vm((256, 1024), BF),
            vm((2, 512, 256), BF), vm((1024, 256), BF), vm((4, 4, 8, 256), F32),
            vm((256, 1024), F32), vm((1024, 256), F32), vm((1024, 256), F32),
            vm((4, 256, 1024), BF), vm((4, 256, 1024), BF), vm((256, 1024), BF),
            vm((2, FF3, 256), BF), vm((FF3, 256), BF), vm((FF3, 256), BF),
            vm((2, 2, 256, 256), BF), vm((2, 256, 256), BF), vm((3, 256, 256), BF), vm((FF3 + 256, 128), F32),
            vm((768, 1024), BF), vm((4, 768, 128), BF), vm((2, 768, 128), BF), vm((768, 128), BF), vm((4, 8, 128), F32),
            dma((4, 2)), dma((4, 2)), dma((4, 2)), dma((4, 2)),
            dma((3,)), dma((3,)), dma((4,)), dma((4,)), dma((8,)), dma((8,)), dma((3,)), dma((3,)), dma((2,)), dma((2,)),
            dma((4,)), dma((2,)), dma((2,)), dma((2,)), dma((2,)), dma((2,)), dma((2, 2)),
            dma((4,)), dma((4,)), dma((4,)), dma((4,)), dma((4,)), dma((4,)), dma((2, 4)), dma((4,)), dma((2, 2)),
            dma, dma, dma((3,)), dma((3,)), dma((3,)), dma((3,)), dma((3,)), dma((3,)), dma, dma, dma((2, 2)), dma((4,)),
            dma((2, NU)), dma((2, NU)), dma((NU,)), dma((NU,)), dma((NU,)), dma((3, NU)),
            dma((NF + 1,)), dma((NF + 1,)), dma((4, 4)), dma((4, 4)), dma((4, 4)), dma((4,)),
            dma((4,)), dma((4,)), dma((2,)), dma((2,)), dma, dma, dma((4,)), dma((4,)), dma,
        ],
        compiler_params=pltpu.CompilerParams(
            collective_id=1, has_side_effects=True, vmem_limit_bytes=63 << 20
        ),
        name="layer",
    )(*args)


def local_fast(
    tokens, lengths, seq_order, gain_attn, w_qkv, w_attn_out, gain_mlp, w_in, w_mlp_out, cotangent
):
    half = HEAD_DIM // 2
    frequency = jnp.tile(rope_base ** (-2.0 * jnp.arange(half, dtype=F32) / HEAD_DIM), 4)
    sign = jnp.tile(jnp.repeat(jnp.array([-1.0, 1.0], F32), half), 2)
    rows = (gain_attn.astype(F32), gain_mlp.astype(F32), frequency, sign)
    gains = jnp.concatenate([r[None, :] for r in rows] + [jnp.zeros((4, 128), F32)], axis=0)
    out, d_tok, d_qkv, d_in, d_down, d_out, d_gain = run_layer(
        lengths, seq_order, tokens, w_qkv, w_in.transpose(1, 2, 0).reshape(2 * HID, 128), w_mlp_out, w_attn_out, gains, cotangent
    )
    return (out, d_tok, d_gain[0], d_qkv, d_out, d_gain[1], d_in.reshape(2, HID, 128).transpose(2, 0, 1), d_down)


def layer_norm(field_in, norm_gain):
    row_mean = jnp.mean(field_in, axis=-1, keepdims=True)
    centered = field_in - row_mean
    variance = jnp.mean(centered * centered, axis=-1, keepdims=True)
    return centered * lax.rsqrt(variance + norm_eps) * norm_gain


def rotate(field_in, position):
    half_size = field_in.shape[-1] // 2
    index_range = jnp.arange(half_size, dtype=jnp.float32)
    frequency = rope_base ** (-2.0 * index_range / field_in.shape[-1])
    angles = position[:, None] * frequency[None, :]
    cosine = jnp.cos(angles)[:, None, :]
    sine_part = jnp.sin(angles)[:, None, :]
    first_half = field_in[..., :half_size]
    second_half = field_in[..., half_size:]
    return jnp.concatenate(
        [
            first_half * cosine - second_half * sine_part,
            second_half * cosine + first_half * sine_part,
        ],
        axis=-1,
    )


def geglu(act_part, up_part):
    return jax.nn.gelu(act_part, approximate=False) * up_part


def layout(lengths, seq_order, group_rows):
    seq_total = seq_order.shape[0]
    first_seq = lax.axis_index("dp") * SEQ_GRP
    chosen = lax.dynamic_slice_in_dim(seq_order, first_seq, SEQ_GRP)
    matched = chosen[:, None] == jnp.arange(seq_total, dtype=jnp.int32)[None, :]
    dealt_lengths = jnp.sum(jnp.where(matched, lengths[None, :], 0), axis=1)
    seq_ends = jnp.cumsum(dealt_lengths)
    row_index = jnp.arange(group_rows, dtype=jnp.int32)
    passed = row_index[:, None] >= seq_ends[None, :]
    segment = jnp.sum(passed.astype(jnp.int32), axis=1)
    row_start = jnp.sum(jnp.where(passed, dealt_lengths[None, :], 0), axis=1)
    return (segment, (row_index - row_start).astype(jnp.float32))


def item_layout(array_in, block_rows):
    group_rows, head_count, head_size = array_in.shape
    block_count = group_rows // block_rows
    shaped = array_in.reshape(block_count, block_rows, head_count, head_size)
    return shaped.transpose(2, 0, 1, 3).reshape(head_count * block_count, block_rows, head_size)


def from_items(items, group_rows):
    item_count, block_rows, head_size = items.shape
    block_count = group_rows // block_rows
    head_count = item_count // block_count
    shaped = items.reshape(head_count, block_count, block_rows, head_size)
    return shaped.transpose(1, 2, 0, 3).reshape(group_rows, head_count, head_size)


def masked_scores(query_block, key_head, segment_block, segment):
    score_scale = query_block.shape[-1] ** (-0.5)
    raw_scores = lax.dot_general(
        query_block, key_head, (((1,), (1,)), ((), ())), preferred_element_type=jnp.float32
    )
    allowed = segment_block[:, None] == segment[None, :]
    return jnp.where(allowed, raw_scores * score_scale, masked_fill)


def attend_forward(query_rot, key_rot, value_low, segment, block_rows):
    group_rows, head_count, head_size = query_rot.shape
    block_count = group_rows // block_rows
    query_items = item_layout(query_rot, block_rows)
    key_heads = key_rot.transpose(1, 0, 2)
    value_heads = value_low.transpose(1, 0, 2)
    segment_blocks = segment.reshape(block_count, block_rows)

    def one_item(item_index):
        head_index = item_index // block_count
        block_index = item_index % block_count
        query_block = lax.dynamic_index_in_dim(query_items, item_index, 0, False)
        key_head = lax.dynamic_index_in_dim(key_heads, head_index, 0, False)
        value_head = lax.dynamic_index_in_dim(value_heads, head_index, 0, False)
        segment_block = lax.dynamic_index_in_dim(segment_blocks, block_index, 0, False)
        scores = masked_scores(query_block, key_head, segment_block, segment)
        row_top = jnp.max(scores, axis=1, keepdims=True)
        weights = jnp.exp(scores - row_top)
        row_total = jnp.sum(weights, axis=1, keepdims=True)
        probs_low = (weights / row_total).astype(jnp.bfloat16)
        result = jnp.dot(probs_low, value_head, preferred_element_type=jnp.float32)
        return (result, row_top[:, 0] + jnp.log(row_total[:, 0]))

    results, log_totals = lax.map(one_item, jnp.arange(head_count * block_count, dtype=jnp.int32))
    return (from_items(results, group_rows), log_totals)


def attend_backward(query_rot, key_rot, value_low, grad_out, log_totals, segment, block_rows):
    group_rows, head_count, head_size = query_rot.shape
    block_count = group_rows // block_rows
    score_scale = head_size ** (-0.5)
    query_items = item_layout(query_rot, block_rows)
    grad_items = item_layout(grad_out, block_rows)
    key_heads = key_rot.transpose(1, 0, 2)
    value_heads = value_low.transpose(1, 0, 2)
    segment_blocks = segment.reshape(block_count, block_rows)

    def one_item(carried, item_index):
        key_grads, value_grads = carried
        head_index = item_index // block_count
        block_index = item_index % block_count
        query_block = lax.dynamic_index_in_dim(query_items, item_index, 0, False)
        grad_block = lax.dynamic_index_in_dim(grad_items, item_index, 0, False)
        log_row = lax.dynamic_index_in_dim(log_totals, item_index, 0, False)
        key_head = lax.dynamic_index_in_dim(key_heads, head_index, 0, False)
        value_head = lax.dynamic_index_in_dim(value_heads, head_index, 0, False)
        segment_block = lax.dynamic_index_in_dim(segment_blocks, block_index, 0, False)
        scores = masked_scores(query_block, key_head, segment_block, segment)
        prob_full = jnp.exp(scores - log_row[:, None])
        probs_low = prob_full.astype(jnp.bfloat16)
        grad_probs = lax.dot_general(
            grad_block, value_head, (((1,), (1,)), ((), ())), preferred_element_type=jnp.float32
        )
        row_delta = jnp.sum(prob_full * grad_probs, axis=1, keepdims=True)
        grad_scores = (prob_full * (grad_probs - row_delta)).astype(jnp.bfloat16)
        grad_query = (
            jnp.dot(grad_scores, key_head, preferred_element_type=jnp.float32) * score_scale
        )
        grad_key = (
            lax.dot_general(
                grad_scores,
                query_block,
                (((0,), (0,)), ((), ())),
                preferred_element_type=jnp.float32,
            )
            * score_scale
        )
        grad_value = lax.dot_general(
            probs_low, grad_block, (((0,), (0,)), ((), ())), preferred_element_type=jnp.float32
        )
        key_grads = lax.dynamic_update_index_in_dim(
            key_grads,
            lax.dynamic_index_in_dim(key_grads, head_index, 0, False) + grad_key,
            head_index,
            0,
        )
        value_grads = lax.dynamic_update_index_in_dim(
            value_grads,
            lax.dynamic_index_in_dim(value_grads, head_index, 0, False) + grad_value,
            head_index,
            0,
        )
        return ((key_grads, value_grads), grad_query)

    zero_heads = jnp.zeros((head_count, group_rows, head_size), jnp.float32)
    (key_grads, value_grads), query_grads = lax.scan(
        one_item, (zero_heads, zero_heads), jnp.arange(head_count * block_count, dtype=jnp.int32)
    )
    return (
        from_items(query_grads, group_rows),
        key_grads.transpose(1, 0, 2),
        value_grads.transpose(1, 0, 2),
    )


def spread_rows(local_rows):
    return lax.all_gather(local_rows, "tensor", axis=0, tiled=True)


def spread_grads(local_grads):
    return lax.all_gather(local_grads, "tensor", axis=0, tiled=True)


def sum_heads(activations, weight_part, row_count):

    def row_term(first_row, row_number):
        return jnp.dot(activations, weight_part, preferred_element_type=jnp.float32)

    return lax.psum_scatter(
        row_term(jnp.int32(0), row_count * lax.axis_size("tensor")),
        "tensor",
        scatter_dimension=0,
        tiled=True,
    )


def sum_grads(grads_low, weight_full, einsum_form, row_count):

    def row_term(first_row, row_number):
        return jnp.einsum(einsum_form, grads_low, weight_full, preferred_element_type=jnp.float32)

    return lax.psum_scatter(
        row_term(jnp.int32(0), row_count * lax.axis_size("tensor")),
        "tensor",
        scatter_dimension=0,
        tiled=True,
    )


def local_plain(
    tokens, lengths, seq_order, gain_attn, w_qkv, w_attn_out, gain_mlp, w_in, w_mlp_out, cotangent
):
    row_count = tokens.shape[0]
    group_rows = row_count * lax.axis_size("tensor")
    block_rows = min(512, group_rows)
    segment, position = layout(lengths, seq_order, group_rows)
    gain_low_one, qkv_weight, out_weight, gain_low_two, in_weight, down_weight = (
        lax.all_gather(gain_attn, "dp", axis=0, tiled=True),
        lax.all_gather(w_qkv, "dp", axis=1, tiled=True),
        lax.all_gather(w_attn_out, "dp", axis=1, tiled=True),
        lax.all_gather(gain_mlp, "dp", axis=0, tiled=True),
        lax.all_gather(w_in, "dp", axis=0, tiled=True),
        lax.all_gather(w_mlp_out, "dp", axis=1, tiled=True),
    )
    gain_one = gain_low_one.astype(jnp.float32)
    gain_two = gain_low_two.astype(jnp.float32)
    residual = tokens.astype(jnp.float32)
    normed_one = spread_rows(layer_norm(residual, gain_one).astype(jnp.bfloat16))
    qkv = jnp.einsum("rd,pdc->rpc", normed_one, qkv_weight, preferred_element_type=jnp.float32)
    head_count = qkv.shape[2] // HEAD_DIM
    head_shape = (group_rows, head_count, HEAD_DIM)
    query_rot = rotate(qkv[:, 0].reshape(head_shape), position).astype(jnp.bfloat16)
    key_rot = rotate(qkv[:, 1].reshape(head_shape), position).astype(jnp.bfloat16)
    value_low = qkv[:, 2].reshape(head_shape).astype(jnp.bfloat16)
    attended, log_totals = attend_forward(query_rot, key_rot, value_low, segment, block_rows)
    attn_low = attended.reshape(group_rows, head_count * HEAD_DIM).astype(jnp.bfloat16)
    resid_mid = residual + sum_heads(attn_low, out_weight, row_count)
    normed_two = spread_rows(layer_norm(resid_mid, gain_two).astype(jnp.bfloat16))
    gate_up = jnp.einsum("rd,dpc->rpc", normed_two, in_weight, preferred_element_type=jnp.float32)
    hidden = geglu(gate_up[:, 0], gate_up[:, 1]).astype(jnp.bfloat16)
    output = (resid_mid + sum_heads(hidden, down_weight, row_count)).astype(jnp.bfloat16)
    grad_two = spread_grads(cotangent)
    d_hidden = lax.dot_general(
        grad_two, down_weight, (((1,), (1,)), ((), ())), preferred_element_type=jnp.float32
    )
    d_down = lax.dot_general(
        hidden, grad_two, (((0,), (0,)), ((), ())), preferred_element_type=jnp.float32
    )
    geglu_pull = jax.vjp(geglu, gate_up[:, 0], gate_up[:, 1])[1]
    d_act, d_up = geglu_pull(d_hidden)
    d_gate_up = jnp.stack([d_act, d_up], axis=1).astype(jnp.bfloat16)
    d_in = jnp.einsum("rd,rpc->dpc", normed_two, d_gate_up, preferred_element_type=jnp.float32)
    d_normed_two = sum_grads(d_gate_up, in_weight, "rpc,dpc->rd", row_count)
    norm_pull_two = jax.vjp(layer_norm, resid_mid, gain_two)[1]
    d_mid_norm, d_gain_two = norm_pull_two(d_normed_two)
    d_mid = cotangent.astype(jnp.float32) + d_mid_norm
    grad_one = spread_grads(d_mid.astype(jnp.bfloat16))
    d_out = lax.dot_general(
        attn_low, grad_one, (((0,), (0,)), ((), ())), preferred_element_type=jnp.float32
    )
    d_att = lax.dot_general(
        grad_one, out_weight, (((1,), (1,)), ((), ())), preferred_element_type=jnp.float32
    ).astype(jnp.bfloat16)
    d_query_rot, d_key_rot, d_value = attend_backward(
        query_rot, key_rot, value_low, d_att.reshape(head_shape), log_totals, segment, block_rows
    )
    rotate_pull = jax.vjp(lambda field_in: rotate(field_in, position), d_query_rot)[1]
    d_query = rotate_pull(d_query_rot)[0]
    d_key = rotate_pull(d_key_rot)[0]
    flat_shape = (group_rows, head_count * HEAD_DIM)
    d_qkv = jnp.stack(
        [d_query.reshape(flat_shape), d_key.reshape(flat_shape), d_value.reshape(flat_shape)],
        axis=1,
    ).astype(jnp.bfloat16)
    d_qkv_weight = jnp.einsum("rd,rpc->pdc", normed_one, d_qkv, preferred_element_type=jnp.float32)
    d_normed_one = sum_grads(d_qkv, qkv_weight, "rpc,pdc->rd", row_count)
    norm_pull_one = jax.vjp(layer_norm, residual, gain_one)[1]
    d_first, d_gain_one = norm_pull_one(d_normed_one)
    d_tokens = d_mid + d_first
    gain_sums = lax.psum((d_gain_one, d_gain_two), "tensor")
    shares = (
        lax.psum_scatter(gain_sums[0], "dp", scatter_dimension=0, tiled=True),
        lax.psum_scatter(d_qkv_weight, "dp", scatter_dimension=1, tiled=True),
        lax.psum_scatter(d_out, "dp", scatter_dimension=1, tiled=True),
        lax.psum_scatter(gain_sums[1], "dp", scatter_dimension=0, tiled=True),
        lax.psum_scatter(d_in, "dp", scatter_dimension=0, tiled=True),
        lax.psum_scatter(d_down, "dp", scatter_dimension=1, tiled=True),
    )
    return (output, d_tokens, shares[0], shares[1], shares[2], shares[3], shares[4], shares[5])


def solution(mesh):
    fast = mesh.shape["dp"] == 8 and mesh.shape["tensor"] == 4
    return jax.shard_map(
        local_fast if fast else local_plain,
        mesh=mesh,
        in_specs=(
            P(("dp", "tensor"), None),
            P(),
            P(),
            P("dp"),
            P(None, "dp", "tensor"),
            P("tensor", "dp"),
            P("dp"),
            P("dp", None, "tensor"),
            P("tensor", "dp"),
            P(("dp", "tensor"), None),
        ),
        out_specs=(
            P(("dp", "tensor"), None),
            P(("dp", "tensor"), None),
            P("dp"),
            P(None, "dp", "tensor"),
            P("tensor", "dp"),
            P("dp"),
            P("dp", None, "tensor"),
            P("tensor", "dp"),
        ),
        check_vma=False,
    )
```

```python
import functools

import jax
import jax.numpy as jnp
from jax import lax
from jax.experimental import pallas as pl
from jax.experimental.pallas import tpu as pltpu
from jax.sharding import PartitionSpec as P

HEAD_DIM = 64
SEQ_GRP = 4
rope_base = 160000.0
norm_eps = 1e-05
masked_fill = -1e30
MESH = pl.DeviceIdType.MESH
BF = jnp.bfloat16
F32 = jnp.float32

NT = (((1,), (1,)), ((), ()))
TN = (((0,), (0,)), ((), ()))


def place():
    dp = lax.axis_index("dp")
    z = lax.axis_index("tensor")
    c = lax.rem(dp, 2)
    x = lax.rem(lax.div(dp, 2), 2)
    y = lax.div(dp, 4)
    return dp, z, c, x, y


def flip(dp, bits, distance):
    out = dp
    for b, bit in enumerate(bits):
        if (distance >> b) & 1:
            out = out + (1 << b) - (2 << b) * bit
    return out


def remote(src, dst, send, recv, dev):
    return pltpu.make_async_remote_copy(
        src_ref=src, dst_ref=dst, send_sem=send, recv_sem=recv, device_id=dev, device_id_type=MESH
    )


def cols(start, size):
    return pl.ds(pl.multiple_of(start, size), size)


def greet(dp, z, bits):
    c = bits[0]
    barrier = pltpu.get_barrier_semaphore()
    peers = [(flip(dp, bits, d), z) for d in range(1, 8)]
    core = flip(dp, bits, 1)
    for k in range(1, 4):
        peers.append((dp, lax.rem(z + k, 4)))
        peers.append((core, lax.rem(z + k, 4)))
    for p in peers:
        pl.semaphore_signal(barrier, inc=1, device_id=p, device_id_type=MESH)
    pl.semaphore_wait(barrier, len(peers))


def norm_rows(v):
    mean = jnp.mean(v, axis=-1, keepdims=True)
    centered = v - mean
    var = jnp.mean(centered * centered, axis=-1, keepdims=True)
    rstd = lax.rsqrt(var + norm_eps)
    return centered * rstd, rstd


def turn(v, cs, sn):
    lane = lax.broadcasted_iota(jnp.int32, cs.shape, 1)
    low_half = lax.rem(lane, HEAD_DIM) < HEAD_DIM // 2
    parts = []
    for t in range(v.shape[1] // 128):
        piece = v[:, t * 128 : (t + 1) * 128]
        swapped = jnp.where(low_half, pltpu.roll(piece, 96, 1), pltpu.roll(piece, 32, 1))
        parts.append(piece * cs + swapped * sn)
    return jnp.concatenate(parts, axis=1)


def gain_row(gains, row):
    return jnp.concatenate([gains[p, row : row + 1, :] for p in range(8)], axis=1)


HID = 656
FF3 = 3 * HID
FROWS = ((0, HID), (HID, HID), (2 * HID, HID))
CUTS = ((0, 496), (496, 496), (992, 496), (1488, 480))
HALVES = tuple((m, o, n) for m in (2, 0, 1) for o, n in ((0, 336), (336, 320)))
NF = len(HALVES)
NU = NF + 2
INV_SQRT2 = 0.7071067811865476
INV_SQRT_2PI = 0.3989422804014327


def layer_kernel(
    lengths, seq_order, tok, wqkv, win, wmlp, wout, gains_in, cot,
    out_o, dtok_o, dwq_o, dwin_o, dwmlp_o, dwout_o, dg_o,
    gains, w3, cs, sn, segc, segr, q, k, v, lse, att, attn2, h1, wq, cot4,
    G, Wo, X1, h2a, dya, yr, acc, hidT, daT, duT, dX1, dsb, dr, dzs, dzr, usb, ur, uzs, uzr, dsend, datt, delta,
    dq, dk, dv, Hs, Hi, Hx, Rb, Ra, Z, Rbo, Rao, Zo, give, Wp, Wc, Wb, Wa, gz,
    us, ds, rb, ra, wr_s, wr_r, wx_s, wx_r, g_s, g_r, cx_s, cx_r, hop_s, hop_r,
    ou_s, o_r, oa_s, ob_s, of_s, oa_r, ob_r,
    fz_s, fz_r, pa_s, pb_s, pf_s, pa_r, pb_r, at_s, at_r,
    y_s, y_r, n_s, n_r, d_s, d_r, u_s, u_r, e_s, e_r, t_s, t_r,
    b_s, b_r, a_s, a_r, zu_s, z_r, fin_s, fin_r,
    hu_s, hd_s, hi_r, hx_r, wc_s, wc_r, wb_s, wb_r, wa_s, wa_r, gz_s, gz_r, lc,
):
    dp, z, c, x, y = place()
    bits = (c, x, y)
    core = flip(dp, bits, 1)
    px, py = flip(dp, bits, 2), flip(dp, bits, 4)
    a = (1 - c) * px + c * py
    b = (1 - c) * py + c * px
    chip, chip_a, chip_b = lax.div(dp, 2), lax.div(a, 2), lax.div(b, 2)
    chip_d = 3 - chip
    home = lax.div(z, 2)
    org = c == home
    zq = lax.rem(z, 2)
    zp = z + 1 - 2 * zq
    z2 = z + 2 - 4 * home
    end = (z == 0) | (z == 3)
    own = cols(c * 256, 256)
    other = cols((1 - c) * 256, 256)

    def block(core_bit, line_bit):
        return cols((2 * line_bit + core_bit) * 256, 256)

    ob, cb, zb, db = block(c, zq), block(1 - c, zq), block(c, 1 - zq), block(1 - c, 1 - zq)
    tall, vT, kT, oT, dqkvT = Hs, Hx, dzs, acc.at[:, 0:256], h2a.at[0:768]
    dw4 = (dwin_o.at[0:HID], dwin_o.at[HID : 2 * HID], dwmlp_o)
    greet(dp, z, bits)

    def no(cond):
        return jnp.logical_not(cond)

    def tok_up(k_, h):
        ref = tall.at[z - k_, pl.ds(h * 128, 128)]
        src = tok.at[pl.ds(h * 128, 128)] if k_ == 0 else ref
        return remote(src, ref, us.at[k_, h], rb.at[k_ + 1, h], (dp, z + 1))

    def tok_down(k_, h):
        ref = tall.at[z + k_, pl.ds(h * 128, 128)]
        src = tok.at[pl.ds(h * 128, 128)] if k_ == 0 else ref
        return remote(src, ref, ds.at[k_, h], ra.at[k_ + 1, h], (dp, z - 1))

    def up_ok(k_):
        return (z >= k_) & (z < 3)

    def down_ok(k_):
        return (z + k_ <= 3) & (z > 0)

    for h in range(2):
        pl.when(up_ok(0))(lambda h=h: tok_up(0, h).start())
        pl.when(down_ok(0))(lambda h=h: tok_down(0, h).start())

    for d in range(1, 8):
        remote(gains_in, gains.at[dp], g_s.at[d], g_r.at[d], (flip(dp, bits, d), z)).start()
    own_rows = cols(dp * 128, 128)
    for j, d in enumerate((2, 4, 6)):
        remote(wqkv, wq.at[:, own_rows], wr_s.at[j], wr_r.at[j], (flip(dp, bits, d), z)).start()
    remote(wqkv, wq.at[:, own_rows], wx_s.at[3], wx_r.at[3], (core, z)).start()
    cot_copy = (
        remote(cot, cot4.at[ob], cx_s.at[0], cx_r.at[0], (core, z)),
        remote(cot, cot4.at[ob], cx_s.at[1], cx_r.at[1], (dp, zp)),
        remote(cot4.at[zb], cot4.at[zb], cx_s.at[2], cx_r.at[2], (core, z)),
    )
    cot_copy[0].start()
    cot_local = pltpu.make_async_copy(cot, cot4.at[ob], lc)
    cot_local.start()

    w3[0 : 2 * HID, :] = win[...]
    w3[2 * HID : FF3, :] = wmlp[...]
    lanes = cols(dp * 128, 128)
    hop = (
        remote(w3, G.at[:, lanes], hop_s.at[0], hop_r.at[0], (core, z)),
        remote(wout, Wo.at[zq, :, lanes], hop_s.at[1], hop_r.at[1], (core, z)),
    )

    @pl.when(no(org))
    def _():
        hop[1].start()
        hop[0].start()

    @pl.when(org)
    def _():
        G[:, lanes] = w3[...]
        Wo[zq, :, lanes] = wout[...]

    gains[dp] = gains_in[...]
    wq[:, own_rows, :] = wqkv[...]
    tall[z] = tok[...]
    cot_local.wait()

    def begin(cp):
        cp.start()

    def done(cp):
        cp.wait_send()

    def piece(u, where):
        r0, n = CUTS[u]
        return G.at[pl.ds(r0, n), cols(where * 256, 256)]

    def way(u):
        s = lax.rem(c + u, 2)
        one = (1 - s) * px + s * py
        two = (1 - s) * py + s * px
        return one, two, lax.div(one, 2), lax.div(two, 2)

    def plane_a(u):
        return remote(piece(u, chip), piece(u, chip), pa_s.at[u], pa_r.at[u], (way(u)[0], z))

    def plane_b(u):
        return remote(piece(u, chip), piece(u, chip), pb_s.at[u], pb_r.at[0, u], (way(u)[1], z))

    def plane_f(u):
        ref = piece(u, way(u)[2])
        return remote(ref, ref, pf_s.at[u], pb_r.at[1, u], (way(u)[1], z))

    def leap(u):
        return remote(piece(u, chip), piece(u, chip), fz_s.at[u], fz_r.at[u], (dp, z2))

    def spread(u):
        plane_a(u).start()
        plane_b(u).start()

    def across(u):
        ref = piece(u, way(u)[2])
        remote(ref, ref, pa_s.at[u], pa_r.at[u], (way(u)[0], z)).wait_recv()
        plane_f(u).start()

    def land(u):
        leap(u).wait_recv()
        spread(u)

    near = (1 - c) * lax.div(z + 2, 3) + c * lax.div(z, 3)
    far = 1 - near

    def opiece(qi, where):
        return Wo.at[qi, :, cols(where * 256, 256)]

    def ofar(k_):
        ref = opiece(zq, chip)
        return remote(ref, ref, ou_s.at[k_], o_r.at[zq], (dp, lax.rem(z + k_, 4)))

    def oplane(qi):
        ref, ref_a = opiece(qi, chip), opiece(qi, chip_a)
        return (
            remote(ref, ref, oa_s.at[qi], oa_r.at[qi], (a, z)),
            remote(ref, ref, ob_s.at[qi], ob_r.at[0, qi], (b, z)),
            remote(ref_a, ref_a, of_s.at[qi], ob_r.at[1, qi], (b, z)),
        )

    def ospread(qi):
        cps = oplane(qi)
        cps[0].start()
        cps[1].start()

    def oland(qi):
        ref = opiece(qi, chip)
        remote(ref, ref, ou_s.at[1], o_r.at[qi], (core, z)).wait_recv()
        ospread(qi)

    def oacross(qi):
        ref = opiece(qi, chip_a)
        remote(ref, ref, oa_s.at[qi], oa_r.at[qi], (a, z)).wait_recv()
        oplane(qi)[2].start()

    ends, starts, total = [], [], 0
    for j in range(SEQ_GRP):
        ends.append(total)
        total = total + lengths[seq_order[dp * SEQ_GRP + j]]
    for dst, shape, axis in ((segc, (1024, 128), 0), (segr, (8, 1024), 1)):
        row = lax.broadcasted_iota(jnp.int32, shape, axis)
        seg = jnp.zeros(shape, F32)
        start = jnp.zeros(shape, jnp.int32)
        for j in range(1, SEQ_GRP):
            passed = row >= ends[j]
            seg = jnp.where(passed, float(j), seg)
            start = jnp.where(passed, ends[j], start)
        dst[...] = seg
        if axis == 0:
            angle = (row - start).astype(F32) * gains_in[2:3, :]
            cs[...] = jnp.cos(angle)
            sn[...] = jnp.sin(angle) * gains_in[3:4, :]

    for d in range(1, 8):
        p = flip(dp, bits, d)
        remote(gains_in, gains.at[p], g_s.at[d], g_r.at[d], (p, z)).wait_recv()

    @pl.when(org)
    def _():
        remote(wout, Wo.at[zq, :, cols(core * 128, 128)], hop_s.at[1], hop_r.at[1], (core, z)).wait_recv()
        ospread(near)
        remote(w3, G.at[:, cols(core * 128, 128)], hop_s.at[0], hop_r.at[0], (core, z)).wait_recv()
        for u in range(4):
            spread(u)

    for j, d in enumerate((2, 4, 6)):
        p = flip(dp, bits, d)
        rows = wq.at[:, cols(p * 128, 128)]
        remote(wqkv, rows, wr_s.at[j], wr_r.at[j], (p, z)).wait_recv()
        remote(rows, rows, wx_s.at[j], wx_r.at[j], (core, z)).start()
    for j, d in enumerate((3, 5, 7, 1)):
        p = flip(dp, bits, d)
        remote(wqkv, wq.at[:, cols(p * 128, 128)], wx_s.at[j], wx_r.at[j], (core, z)).wait_recv()

    gain1, gain2 = gain_row(gains, 0), gain_row(gains, 1)

    def project(s):
        base = s * 256

        @pl.loop(0, 8)
        def _(r):
            xhat, _r = norm_rows(tall[s, pl.ds(pl.multiple_of(r * 32, 32), 32), :].astype(F32))
            h1[pl.ds(pl.multiple_of(base + r * 32, 32), 32), :] = (xhat * gain1).astype(BF)

        rows = pl.ds(pl.multiple_of(base, 256), 256)
        hb = h1[rows, :]
        cb, sb = cs[rows, :], sn[rows, :]
        for p, dst in enumerate((q, k, v)):
            r = jnp.dot(hb, wq[p], preferred_element_type=F32)
            if p < 2:
                r = turn(r, cb, sb)
            if p == 0:
                r = r * (HEAD_DIM**-0.5)
            dst[rows, :] = r.astype(BF)

    def receive(k_):
        below, above = z - k_ >= 0, z + k_ <= 3
        for h in range(2):

            @pl.when(below)
            def _(k_=k_, h=h):
                ref = tall.at[z - k_, pl.ds(h * 128, 128)]
                remote(ref, ref, us.at[k_, h], rb.at[k_, h], (core, z)).wait_recv()
                if k_ < 3:
                    pl.when(up_ok(k_))(lambda: tok_up(k_, h).start())

            @pl.when(above)
            def _(k_=k_, h=h):
                ref = tall.at[z + k_, pl.ds(h * 128, 128)]
                remote(ref, ref, ds.at[k_, h], ra.at[k_, h], (core, z)).wait_recv()
                if k_ < 3:
                    pl.when(down_ok(k_))(lambda: tok_down(k_, h).start())

    for k_ in range(4):
        if k_ != 1:
            receive(max(k_, 1))

        if k_ == 1:

            @pl.when(org)
            def _():
                for n in range(1, 4):
                    ofar(n).start()

        @pl.loop(0, 2)
        def _(t, k_=k_):
            s = z - k_ + 2 * k_ * t
            pl.when((s >= 0) & (s <= 3) & ((k_ > 0) | (t == 0)))(lambda: project(s))

        if k_ == 1:

            @pl.when(org)
            def _():
                oacross(near)
                for u in range(4):
                    across(u)

        if k_ == 2:

            @pl.when(org & end)
            def _():
                for u in range(4):
                    leap(u).start()

    for s in range(4):
        vT[:, s * 256 : (s + 1) * 256] = v[s * 256 : (s + 1) * 256, :].T
    head_of = lax.div(lax.broadcasted_iota(jnp.int32, (256, 256), 1), HEAD_DIM)

    def attend(i):
        rows = pl.ds(pl.multiple_of(i * 256, 256), 256)
        qb = q[rows, :]
        seg_q = segr[0:1, rows]
        heads = range(4)
        qh = [jnp.where(head_of == h, qb, jnp.zeros((), BF)) for h in heads]
        chunks = [slice(kc * 256, kc * 256 + 256) for kc in range(4)]
        for h in heads:
            hr = slice(h * HEAD_DIM, (h + 1) * HEAD_DIM)
            scores, tops = [], []
            for keys in chunks:
                seg_k = segc[keys, :]
                same = jnp.concatenate([seg_k, seg_k], axis=1) == seg_q
                s = lax.dot_general(k[keys, :], qh[h], NT, preferred_element_type=F32)
                s = jnp.where(same, s, masked_fill)
                scores.append(s)
                tops.append(jnp.max(s, axis=0, keepdims=True))
            top = jnp.maximum(jnp.maximum(tops[0], tops[1]), jnp.maximum(tops[2], tops[3]))
            tot, out = 0.0, 0.0
            for keys, s in zip(chunks, scores):
                p = jnp.exp(s - top)
                tot = tot + jnp.sum(p, axis=0, keepdims=True)
                out = out + jnp.dot(vT[hr, keys], p.astype(BF), preferred_element_type=F32)
            oT[hr, :] = out * (1.0 / tot)
            lse[h, i] = jnp.broadcast_to(top + jnp.log(tot), (8, 256))
        att[rows, :] = oT[...].T.astype(BF)

    def att_slot(src_core, q):
        return attn2.at[cols(src_core * 256, 256), cols(q * 256, 256)]

    def att_copy(n, i):
        rows = pl.ds(pl.multiple_of(i * 256, 256), 256)
        return remote(
            att.at[rows, :], att_slot(c, zq), at_s.at[n], at_r.at[c, zq], (2 * chip + home, i)
        )

    @pl.loop(0, 4)
    def _(n):
        i = lax.rem(z + 1 + n, 4)
        attend(i)
        for m in range(4):

            @pl.when((n == m) & ((m < 3) | no(org)))
            def _(m=m):
                att_copy(m, i).start()

        @pl.when((n == 3) & org)
        def _():
            attn2[own, cols(zq * 256, 256)] = att[pl.ds(pl.multiple_of(z * 256, 256), 256), :]

        @pl.when((n == 1) & org & no(end))
        def _():
            for u in range(4):
                leap(u).start()

        pl.when(n == 3)(lambda: cot_copy[1].start())

        @pl.when((n == 1) & end)
        def _():
            oland(far)
            pl.when(no(org))(lambda: oland(near))

        @pl.when((n == 3) & end)
        def _():
            oacross(far)
            pl.when(no(org))(lambda: oacross(near))

    @pl.when(no(end))
    def _():
        oland(far)
        pl.when(no(org))(lambda: oland(near))

    @pl.when(no(end))
    def _():
        oacross(far)
        pl.when(no(org))(lambda: oacross(near))

    def late(*ops):
        @pl.when(no(org))
        def _():
            for op, u in ops:
                op(u)

    pl.when(no(end))(lambda: late((land, 0), (land, 1), (land, 2), (land, 3), (across, 0), (across, 1)))
    pl.when(end)(lambda: late((land, 0)))

    for k_ in range(3):
        for h in range(2):
            pl.when(up_ok(k_))(lambda k_=k_, h=h: tok_up(k_, h).wait_send())
            pl.when(down_ok(k_))(lambda k_=k_, h=h: tok_down(k_, h).wait_send())
    for src in range(2):
        for qi in range(2):
            mine_too = (c == src) & (z == 2 * c + qi)

            @pl.when(no(mine_too))
            def _(src=src, qi=qi):
                slot = att_slot(src, qi)
                remote(slot, slot, at_s.at[0], at_r.at[src, qi], (core, z)).wait_recv()

    pl.when(end)(lambda: late((land, 1)))
    for qi in range(2):
        for w, where in enumerate((chip_b, chip_d)):
            ref = opiece(qi, where)
            remote(ref, ref, ob_s.at[qi], ob_r.at[w, qi], (core, z)).wait_recv()

    def out_proj(rows):
        return sum(
            jnp.dot(attn2[rows, qi * 256 : (qi + 1) * 256], Wo[qi], preferred_element_type=F32) for qi in range(2)
        )

    acc[...] = out_proj(other)
    y_copy = remote(acc, yr, y_s, y_r, (core, z))
    y_copy.start()
    pl.when(end)(lambda: late((land, 2)))
    X1[...] = tok[...].astype(F32) + out_proj(own)
    y_copy.wait()
    pl.when(end)(lambda: late((land, 3)))

    def chunk(r):
        return pl.ds(pl.multiple_of(r * 32, 32), 32)

    def own_chunk(r):
        return pl.ds(pl.multiple_of(c * 256 + r * 32, 32), 32)

    def block_chunk(r):
        return pl.ds(pl.multiple_of((2 * zq + c) * 256 + r * 32, 32), 32)

    @pl.loop(0, 8)
    def _(r):
        x1 = X1[chunk(r), :] + yr[chunk(r), :]
        X1[chunk(r), :] = x1
        xhat, _r = norm_rows(x1)
        h2a[block_chunk(r), :] = (xhat * gain2).astype(BF)

    h_copy = (
        remote(h2a.at[ob], h2a.at[ob], n_s.at[0], n_r.at[0], (core, z)),
        remote(h2a.at[ob], h2a.at[ob], n_s.at[1], n_r.at[1], (dp, zp)),
        remote(h2a.at[zb], h2a.at[zb], n_s.at[2], n_r.at[2], (core, z)),
    )
    h_copy[1].start()
    h_copy[0].start()
    pl.when(end)(lambda: late((across, 0), (across, 1)))
    late((across, 2), (across, 3))
    remote(cot, cot4.at[zb], cx_s.at[1], cx_r.at[1], (dp, zp)).wait_recv()
    cot_copy[2].start()
    remote(cot, cot4.at[cb], cx_s.at[0], cx_r.at[0], (core, z)).wait_recv()
    remote(cot, cot4.at[db], cx_s.at[2], cx_r.at[2], (core, z)).wait_recv()
    for u in range(4):
        for w, where in enumerate((way(u)[3], chip_d)):
            ref = piece(u, where)
            remote(ref, ref, pb_s.at[u], pb_r.at[w, u], (core, z)).wait_recv()
    remote(h2a.at[cb], h2a.at[cb], n_s.at[0], n_r.at[0], (core, z)).wait_recv()

    def tile(r0, n, tokens):
        h2 = h2a[tokens, :]
        act = lax.dot_general(G[r0 : r0 + n, :], h2, NT, preferred_element_type=F32)
        up = lax.dot_general(G[HID + r0 : HID + r0 + n, :], h2, NT, preferred_element_type=F32)
        dh = lax.dot_general(
            G[2 * HID + r0 : 2 * HID + r0 + n, :], cot4[tokens, :], NT, preferred_element_type=F32
        )
        Phi = 0.5 + 0.5 * lax.erf(act * INV_SQRT2)
        phi = jnp.exp(-0.5 * act * act) * INV_SQRT_2PI
        gel = act * Phi
        rr = slice(r0, r0 + n)
        hidT[rr, tokens] = (gel * up).astype(BF)
        daT[rr, tokens] = (dh * up * (Phi + act * phi)).astype(BF)
        duT[rr, tokens] = (dh * gel).astype(BF)

    @pl.loop(0, 2)
    def _(t):
        there = lax.rem(zq + t, 2)

        @pl.when(t == 1)
        def _():
            remote(h2a.at[zb], h2a.at[zb], n_s.at[1], n_r.at[1], (dp, zp)).wait_recv()
            h_copy[2].start()
            remote(h2a.at[db], h2a.at[db], n_s.at[2], n_r.at[2], (core, z)).wait_recv()

        for r0, n in ((0, 224), (224, 224), (448, 208)):
            tile(r0, n, cols(there * 512, 512))

    def tn(lhs, rhs):
        return lax.dot_general(lhs, rhs, TN, preferred_element_type=F32)

    def f_rows(m):
        return pl.ds(FROWS[m][0], HID)

    def d_norm(rows, hc):
        return tn(daT[:, rows], G[f_rows(0), hc]) + tn(duT[:, rows], G[f_rows(1), hc])

    def mlp_out(rows, hc):
        return tn(hidT[:, rows], G[f_rows(2), hc])

    def quad(term, sb, got, zs, zgot, ss, rs, hold=False):
        halves = (slice(0, 512), slice(512, 1024))
        copies = (
            remote(sb.at[0], got.at[0], ss.at[0], rs.at[0], (core, z)),
            remote(sb.at[1], got.at[1], ss.at[1], rs.at[1], (core, z)),
            remote(zs, zgot, ss.at[2], rs.at[2], (dp, zp)),
        )
        for j, rows in enumerate((db, cb)):
            for hc in halves:
                sb[j, :, hc] = term(rows, hc).astype(BF)
            copies[j].start()
        copies[0].wait_recv()
        for hc in halves:
            zs[:, hc] = (term(zb, hc) + got[0, :, hc].astype(F32)).astype(BF)
        if not hold:
            copies[2].start()
        return copies

    def keep(term, dst, plus=None):
        for hc in (slice(0, 512), slice(512, 1024)):
            r = term(ob, hc)
            dst[:, hc] = r if plus is None else r + plus[:, hc]

    def grads(m):
        lhs, rhs = ((daT, h2a), (duT, h2a), (hidT, cot4))[m]

        @pl.loop(0, 4)
        def _(t):
            tc = cols(t * 256, 256)
            G[f_rows(m), tc] = jnp.dot(lhs[...], rhs[:, tc], preferred_element_type=F32).astype(BF)

    def rows_of(e):
        m, o, n = HALVES[e]
        return pl.ds(FROWS[m][0] + o, n)

    def part(e, where):
        if e < NF:
            return G.at[rows_of(e), cols(where * 256, 256)]
        return opiece(e - NF, where)

    def from_b(e, slot):
        return Rb.at[slot, rows_of(e)] if e < NF else Rbo.at[slot, e - NF]

    def from_a(e):
        return Ra.at[rows_of(e)] if e < NF else Rao.at[e - NF]

    def unit_b(e, slot):
        src = part(e, chip_b if slot == 0 else chip_d)
        return remote(src, from_b(e, slot), b_s.at[slot, e], b_r.at[slot, e], (b, z))

    def unit_a(e):
        return remote(part(e, chip_a), from_a(e), a_s.at[e], a_r.at[e], (a, z))

    def send_b(e):
        unit_b(e, 1).start()
        unit_b(e, 0).start()

    def stage1(e):
        unit_b(e, 1).wait_recv()
        ref = part(e, chip_a)
        ref[...] = (ref[...].astype(F32) + from_b(e, 1)[...].astype(F32)).astype(BF)
        unit_a(e).start()

    def unit_z(e):
        return remote(part(e, chip), Z.at[rows_of(e)], zu_s.at[e], z_r.at[0, e], (dp, z2))

    def unit_o(e):
        t = 2 * c + e - NF
        slot = lax.rem(z - t + 4, 4) - 1
        return remote(part(e, chip), Zo.at[slot], zu_s.at[e], z_r.at[slot, e], (dp, t))

    def stage2(e):
        unit_b(e, 0).wait_recv()
        unit_a(e).wait_recv()
        ref = part(e, chip)
        ref[...] = (
            ref[...].astype(F32) + from_b(e, 0)[...].astype(F32) + from_a(e)[...].astype(F32)
        ).astype(BF)
        if e < NF:
            pl.when(no(org))(lambda: unit_z(e).start())
        else:
            pl.when(z != 2 * c + e - NF)(lambda: unit_o(e).start())

    def line_wait(e, slot):
        remote(Zo.at[slot], Zo.at[slot], zu_s.at[e], z_r.at[slot, e], (core, z)).wait_recv()

    def final(e):
        if e < NF:
            m, o, n = HALVES[e]
            return e, give.at[rows_of(e)], dw4[m].at[pl.ds(o, n)]
        return NF, give.at[FF3 : FF3 + 256], dwout_o

    def stage4(e):
        here = org if e < NF else z == 2 * c + e - NF

        @pl.when(here)
        def _():
            slot, gift, dst = final(e)
            if e < NF:
                unit_z(e).wait_recv()
            for who, ref in ((c, dst), (1 - c, gift)):
                ref[...] = part(e, chip)[:, cols(who * 128, 128)].astype(F32)

            def take(got):
                for who, ref in ((c, dst), (1 - c, gift)):
                    ref[...] = ref[...] + got[:, cols(who * 128, 128)].astype(F32)

            def line_take(where):
                line_wait(e, where)
                take(Zo.at[where])

            if e < NF:
                take(Z.at[rows_of(e)])
            else:
                for slot_ in range(3):
                    line_take(slot_)
            remote(gift, dst, fin_s.at[slot], fin_r.at[slot], (core, z)).start()

    def tick(t):
        for lag, step in ((0, stage1), (1, stage2), (4, stage4)):
            if 0 <= t - lag < NU:
                step(t - lag)

    d_copies = quad(d_norm, dsb, dr, dzs, dzr, d_s, d_r)
    keep(d_norm, dX1)
    u_copies = quad(mlp_out, usb, ur, uzs, uzr, u_s, u_r, hold=True)
    keep(mlp_out, dtok_o, X1)
    for u in range(4):
        plane_a(u).wait_send()
        plane_b(u).wait_send()
        plane_f(u).wait_send()
        pl.when(org)(lambda u=u: leap(u).wait_send())

    def ff_grads(m):
        grads(m)
        for e in range(NF):
            if HALVES[e][0] == m:
                send_b(e)

    ff_grads(2)
    ff_grads(0)
    ff_grads(1)
    d_copies[1].wait_recv()
    d_copies[2].wait_recv()

    @pl.loop(0, 8)
    def _(r):
        dh2 = dX1[chunk(r), :] + dr[1, chunk(r), :].astype(F32) + dzr[chunk(r), :].astype(F32)
        xhat, rstd = norm_rows(X1[chunk(r), :])
        e2 = dh2 * gain2
        m1 = jnp.mean(e2, axis=-1, keepdims=True)
        m2 = jnp.mean(e2 * xhat, axis=-1, keepdims=True)
        dx = cot4[block_chunk(r), :].astype(F32) + rstd * (e2 - m1 - xhat * m2)
        dX1[chunk(r), :] = dx
        dya[own_chunk(r), :] = dx.astype(BF)

    e_copy = remote(dya.at[own], dya.at[own], e_s, e_r, (core, z))
    e_copy.start()
    tick(0)
    e_copy.wait()
    for qi in range(2):
        dsend[qi] = lax.dot_general(dya[...], Wo[qi], NT, preferred_element_type=F32).astype(BF)

    def att_back(c0, qi):
        dst = datt.at[cols(z * 256, 256)]
        return remote(
            dsend.at[qi, pl.ds(c0 * 256, 256)], dst, t_s.at[c0, qi], t_r.at[z], (2 * chip + c0, 2 * c + qi)
        )

    def is_self(c0, qi):
        return (c == c0) & (z == 2 * c + qi)

    for c0 in range(2):
        for qi in range(2):
            pl.when(no(is_self(c0, qi)))(lambda c0=c0, qi=qi: att_back(c0, qi).start())

            @pl.when(is_self(c0, qi))
            def _(c0=c0, qi=qi):
                datt[cols(z * 256, 256), :] = dsend[qi, c0 * 256 : (c0 + 1) * 256, :]

    u_copies[2].start()
    for n in range(1, 4):
        pl.when(org)(lambda n=n: ofar(n).wait_send())
    for qi in range(2):
        for cp in oplane(qi):
            cp.wait_send()

        @pl.loop(0, 4)
        def _(t, qi=qi):
            tc = cols(t * 256, 256)
            Wo[qi, :, tc] = tn(attn2[:, qi * 256 : (qi + 1) * 256], dya[:, tc]).astype(BF)

        send_b(NF + qi)
    tick(1)
    tick(2)
    for cp in h_copy:
        cp.wait_send()
    d_copies[2].wait_send()
    for s in range(4):
        kT[:, s * 256 : (s + 1) * 256] = k[s * 256 : (s + 1) * 256, :].T
    dq[...] = jnp.zeros_like(dq)
    dk[...] = jnp.zeros_like(dk)
    dv[...] = jnp.zeros_like(dv)
    for i in range(4):

        @pl.when(no(org & (z == i)))
        def _(i=i):
            ref = datt.at[pl.ds(i * 256, 256)]
            remote(ref, ref, t_s.at[0, 0], t_r.at[i], (core, z)).wait_recv()

    @pl.loop(0, 4)
    def _(i):
        rows = pl.ds(pl.multiple_of(i * 256, 256), 256)
        t = (datt[rows, :].astype(F32) * att[rows, :].astype(F32)).T
        for h in range(4):
            s = jnp.sum(t[h * 64 : (h + 1) * 64, :], axis=0, keepdims=True)
            delta[h, i] = jnp.broadcast_to(s, (8, 256))

    def block_order(l):
        inner = lax.div(z * (3 - z), 2)
        base = inner * jnp.minimum(l, 1) * (lax.rem(l + 1, 3) + 1) + (1 - inner) * l
        return (1 - home) * (3 - base) + home * base

    def pair(i, j):
        ri = pl.ds(pl.multiple_of(i * 256, 256), 256)
        rj = pl.ds(pl.multiple_of(j * 256, 256), 256)

        kj, vj, qi_, dai = k[rj, :], v[rj, :], q[ri, :], datt[ri, :]
        seg_k = segc[rj, :]
        same = jnp.concatenate([seg_k, seg_k], axis=1) == segr[0:1, ri]
        none = jnp.zeros((), BF)
        heads = range(4)
        qh = [jnp.where(head_of == h, qi_, none) for h in heads]
        dah = [jnp.where(head_of == h, dai, none) for h in heads]
        ss = [lax.dot_general(kj, qh[h], NT, preferred_element_type=F32) for h in heads]
        dps = [lax.dot_general(vj, dah[h], NT, preferred_element_type=F32) for h in heads]
        ps = [jnp.exp(jnp.where(same, ss[h], masked_fill) - lse[h, i, 0:1, :]) for h in heads]
        dss = [(ps[h] * (dps[h] - delta[h, i, 0:1, :])).astype(BF) for h in heads]
        dvs = [jnp.dot(ps[h].astype(BF), dah[h], preferred_element_type=F32) for h in heads]
        dks = [jnp.dot(dss[h], qh[h], preferred_element_type=F32) for h in heads]
        dqs = [
            jnp.dot(kT[h * HEAD_DIM : (h + 1) * HEAD_DIM, rj], dss[h], preferred_element_type=F32) for h in heads
        ]
        dv[rj, :] = dv[rj, :] + (dvs[0] + dvs[1] + dvs[2] + dvs[3])
        dk[rj, :] = dk[rj, :] + (dks[0] + dks[1] + dks[2] + dks[3])
        for h in range(4):
            hr = slice(h * HEAD_DIM, (h + 1) * HEAD_DIM)
            dq[hr, ri] = dq[hr, ri] + dqs[h]

    def quarter(t):
        return pl.ds(pl.multiple_of(t * 64, 64), 64)

    def h_up(i, t, last):
        if last:
            return remote(Hs.at[i, quarter(t)], Hx.at[quarter(t)], hu_s.at[i, t], hx_r.at[t], (dp, z + 1))
        return remote(Hs.at[i, quarter(t)], Hi.at[i, quarter(t)], hu_s.at[i, t], hi_r.at[i, t], (dp, z + 1))

    def h_down(i, t):
        return remote(Hs.at[i, quarter(t)], Hi.at[i, quarter(t)], hd_s.at[i, t], hi_r.at[i, t], (dp, z - 1))

    def h_inward(i, t, act):
        pl.when(z > i)(lambda: act(h_down(i, t)))
        pl.when(z + 1 == i)(lambda: act(h_up(i, t, True)))
        pl.when(z + 1 < i)(lambda: act(h_up(i, t, False)))

    def h_wait(i, t):
        ref = Hi.at[i, quarter(t)]
        remote(ref, ref, hd_s.at[i, t], hi_r.at[i, t], (core, z)).wait_recv()

    def h_mid(i, depth):
        mid = ((z > i) & (z == 3 - depth)) | ((z < i) & (z == depth))

        @pl.when(mid)
        def _():
            @pl.loop(0, 4)
            def _(t):
                h_wait(i, t)
                Hs[i, quarter(t), :] = (
                    Hs[i, quarter(t), :].astype(F32) + Hi[i, quarter(t), :].astype(F32)
                ).astype(BF)
                h_inward(i, t, begin)

    def finish(i):
        rows = pl.ds(pl.multiple_of(i * 256, 256), 256)
        cb, sb = cs[rows, :], -sn[rows, :]
        low = (
            turn(dq[:, rows].T * (HEAD_DIM**-0.5), cb, sb).astype(BF),
            turn(dk[rows, :], cb, sb).astype(BF),
            dv[rows, :].astype(BF),
        )
        for p in range(3):
            dqkvT[p * 256 : (p + 1) * 256, rows] = low[p].T
        for half in range(2):
            hc = slice(half * 512, half * 512 + 512)
            dh = sum(
                lax.dot_general(low[p], wq[p, hc, :], NT, preferred_element_type=F32) for p in range(3)
            )
            Hs[i, :, hc] = dh.astype(BF)

            @pl.when(z == i)
            def _(dh=dh, hc=hc):
                acc[:, hc] = dh

        @pl.when(((z == 3) & (z > i)) | ((z == 0) & (z < i)))
        def _():
            for t in range(4):
                h_inward(i, t, begin)


    slots = {0: [3], 2: [4], 5: [5], 8: [6], 11: [7], 14: [8]}
    h_slots = {14: [(0, 1), (3, 1)]}

    @pl.loop(0, 16)
    def _(n):
        def past(v):
            return lax.div(n + 16 - v, 16)

        ph = past(7) + past(12) + past(15)
        t = n - 7 * past(7) - 5 * past(12) - 3 * past(15)
        left = 4 - ph
        over = lax.div(t, left)
        li = ph + over * (t - left + 1)
        lj = ph + (1 - over) * t
        pair(block_order(li), block_order(lj))
        pl.when((n == 6) | (n == 11) | (n == 14) | (n == 15))(lambda: finish(block_order(ph)))
        for s in range(16):
            todo = [lambda t=t: tick(t) for t in slots.get(s, ())]
            todo += [lambda i=i, d=d: h_mid(i, d) for i, d in h_slots.get(s, ())]

            @pl.when(n == s)
            def _(todo=todo):
                for op in todo:
                    op()

    @pl.loop(0, 4)
    def _(t):
        tc = cols(t * 256, 256)
        Wp[:, tc] = jnp.dot(dqkvT[...], h1[:, tc], preferred_element_type=F32).astype(BF)

    def core_copy(w):
        return remote(
            Wp.at[:, cols(w * 256 + (1 - c) * 128, 128)], Wc.at[w], wc_s.at[w], wc_r.at[w], (core, z)
        )

    for w in range(4):
        core_copy(w).start()
    tick(9)

    def both(w):
        Wc[w] = (Wc[w].astype(F32) + Wp[:, cols(w * 256 + c * 128, 128)].astype(F32)).astype(BF)

    for w in range(4):
        core_copy(w).wait_recv()
    both(chip_d)
    both(chip_b)
    wb_copy = [
        remote(Wc.at[where], Wb.at[slot], wb_s.at[slot], wb_r.at[slot], (b, z))
        for slot, where in ((0, chip_b), (1, chip_d))
    ]
    wb_copy[1].start()
    wb_copy[0].start()
    both(chip_a)
    both(chip)
    wa_copy = remote(Wc.at[chip_a], Wa, wa_s, wa_r, (a, z))
    h_mid(3, 2)
    h_mid(0, 2)
    wb_copy[1].wait_recv()
    Wc[chip_a] = (Wc[chip_a].astype(F32) + Wb[1].astype(F32)).astype(BF)
    wa_copy.start()
    h_mid(2, 1)
    h_mid(1, 1)
    u_copies[1].wait_recv()
    u_copies[2].wait_recv()
    out_o[...] = (dtok_o[...] + ur[1].astype(F32) + uzr[...].astype(F32)).astype(BF)

    wb_copy[0].wait_recv()
    wa_copy.wait_recv()
    total = Wc[chip].astype(F32) + Wb[0].astype(F32) + Wa[...].astype(F32)
    dot_one = jnp.zeros((1, 128), F32)
    for p in range(3):
        piece = total[p * 256 : (p + 1) * 256, :]
        dwq_o[p] = piece.T
        dot_one = dot_one + jnp.sum(piece * wqkv[p].T.astype(F32), axis=0, keepdims=True)
    def finals(slots_):
        for e in slots_:

            @pl.when(no(org))
            def _(e=e):
                slot, _, ref = final(e)
                remote(ref, ref, fin_s.at[slot], fin_r.at[slot], (core, z)).wait_recv()

    finals(range(NF))
    part_two = jnp.sum(dwin_o[...] * w3[0 : 2 * HID, :].astype(F32), axis=0, keepdims=True)
    gz[z, 0:1, :] = dot_one / gains[dp, 0:1, :]
    gz[z, 1:2, :] = part_two / gains[dp, 1:2, :]
    gz[z, 2:8, :] = jnp.zeros((6, 128), F32)
    gain_copy = [
        remote(gz.at[z], gz.at[z], gz_s.at[n], gz_r.at[z], (dp, lax.rem(z + n, 4))) for n in range(1, 4)
    ]
    for cp in gain_copy:
        cp.start()
    for t in range(4):
        ref = Hx.at[quarter(t)]
        pl.when(z < 3)(lambda t=t: h_wait(z, t))
        pl.when(z > 0)(lambda t=t, ref=ref: remote(ref, ref, hu_s.at[0, t], hx_r.at[t], (core, z)).wait_recv())
    has_above, has_below = z < 3, z > 0

    @pl.when(has_above)
    def _():
        acc[...] = acc[...] + Hi[z].astype(F32)

    @pl.when(has_below)
    def _():
        acc[...] = acc[...] + Hx[...].astype(F32)

    @pl.loop(0, 8)
    def _(r):
        xhat, rstd = norm_rows(tok[chunk(r), :].astype(F32))
        e1 = acc[chunk(r), :] * gain1
        m1 = jnp.mean(e1, axis=-1, keepdims=True)
        m2 = jnp.mean(e1 * xhat, axis=-1, keepdims=True)
        dtok_o[chunk(r), :] = dX1[chunk(r), :] + rstd * (e1 - m1 - xhat * m2)

    tick(10)
    tick(11)
    finals((NF,))
    for n in range(1, 4):
        o = lax.rem(z + n, 4)
        remote(gz.at[o], gz.at[o], gz_s.at[n], gz_r.at[o], (core, z)).wait_recv()
    dg_o[...] = gz[0] + gz[1] + gz[2] + gz[3]

    for cp in gain_copy:
        cp.wait_send()
    for w in range(4):
        core_copy(w).wait_send()
    wb_copy[0].wait_send()
    wb_copy[1].wait_send()
    wa_copy.wait_send()
    for i in range(4):
        for t in range(4):
            h_inward(i, t, done)
    for c0 in range(2):
        for qi in range(2):
            pl.when(no(is_self(c0, qi)))(lambda c0=c0, qi=qi: att_back(c0, qi).wait_send())
    for cp in d_copies[:2] + u_copies:
        cp.wait_send()
    for e in range(NU):
        unit_b(e, 0).wait_send()
        unit_b(e, 1).wait_send()
        unit_a(e).wait_send()
        if e < NF:
            pl.when(no(org))(lambda e=e: unit_z(e).wait_send())
        else:
            pl.when(z != 2 * c + e - NF)(lambda e=e: unit_o(e).wait_send())

        @pl.when(org if e < NF else z == 2 * c + e - NF)
        def _(e=e):
            slot, gift, dst = final(e)
            remote(gift, dst, fin_s.at[slot], fin_r.at[slot], (core, z)).wait_send()

    for d in range(1, 8):
        remote(gains_in, gains.at[dp], g_s.at[d], g_r.at[d], (core, z)).wait_send()
    for j in range(3):
        remote(wqkv, wq.at[:, own_rows], wr_s.at[j], wr_r.at[j], (core, z)).wait_send()
    for j in range(4):
        remote(wqkv, wq.at[:, own_rows], wx_s.at[j], wx_r.at[j], (core, z)).wait_send()
    for cp in hop:
        pl.when(no(org))(lambda cp=cp: cp.wait_send())
    for cp in cot_copy:
        cp.wait_send()
    for n in range(3):
        att_copy(n, lax.rem(z + 1 + n, 4)).wait_send()
    pl.when(no(org))(lambda: att_copy(3, z).wait_send())


def run_layer(*args):
    V = pl.BlockSpec(memory_space=pltpu.VMEM)
    S = pl.BlockSpec(memory_space=pltpu.SMEM)
    dma = pltpu.SemaphoreType.DMA
    s = jax.ShapeDtypeStruct
    vm = pltpu.VMEM
    return pl.pallas_call(
        layer_kernel,
        out_shape=(
            s((256, 1024), BF), s((256, 1024), F32), s((3, 128, 256), F32), s((2 * HID, 128), F32),
            s((HID, 128), F32), s((256, 128), F32), s((8, 128), F32),
        ),
        in_specs=[S, S] + [V] * 6 + [pl.BlockSpec(memory_space=pl.ANY)],
        out_specs=[V] * 7,
        scratch_shapes=[
            vm((8, 8, 128), F32), vm((FF3, 128), BF), vm((1024, 128), F32), vm((1024, 128), F32),
            vm((1024, 128), F32), vm((8, 1024), F32), vm((1024, 256), BF), vm((1024, 256), BF),
            vm((1024, 256), BF), vm((4, 4, 8, 256), F32), vm((1024, 256), BF), vm((512, 512), BF),
            vm((1024, 1024), BF), vm((3, 1024, 256), BF), vm((1024, 1024), BF),
            vm((FF3, 1024), BF), vm((2, 256, 1024), BF), vm((256, 1024), F32), vm((1024, 1024), BF), vm((512, 1024), BF),
            vm((256, 1024), F32), vm((256, 1024), F32), vm((HID, 1024), BF), vm((HID, 1024), BF),
            vm((HID, 1024), BF), vm((256, 1024), F32),
            vm((2, 256, 1024), BF), vm((2, 256, 1024), BF), vm((256, 1024), BF), vm((256, 1024), BF),
            vm((2, 256, 1024), BF), vm((2, 256, 1024), BF), vm((256, 1024), BF), vm((256, 1024), BF),
            vm((2, 512, 256), BF), vm((1024, 256), BF), vm((4, 4, 8, 256), F32),
            vm((256, 1024), F32), vm((1024, 256), F32), vm((1024, 256), F32),
            vm((4, 256, 1024), BF), vm((4, 256, 1024), BF), vm((256, 1024), BF),
            vm((2, FF3, 256), BF), vm((FF3, 256), BF), vm((FF3, 256), BF),
            vm((2, 2, 256, 256), BF), vm((2, 256, 256), BF), vm((3, 256, 256), BF), vm((FF3 + 256, 128), F32),
            vm((768, 1024), BF), vm((4, 768, 128), BF), vm((2, 768, 128), BF), vm((768, 128), BF), vm((4, 8, 128), F32),
            dma((4, 2)), dma((4, 2)), dma((4, 2)), dma((4, 2)),
            dma((3,)), dma((3,)), dma((4,)), dma((4,)), dma((8,)), dma((8,)), dma((3,)), dma((3,)), dma((2,)), dma((2,)),
            dma((4,)), dma((2,)), dma((2,)), dma((2,)), dma((2,)), dma((2,)), dma((2, 2)),
            dma((4,)), dma((4,)), dma((4,)), dma((4,)), dma((4,)), dma((4,)), dma((2, 4)), dma((4,)), dma((2, 2)),
            dma, dma, dma((3,)), dma((3,)), dma((3,)), dma((3,)), dma((3,)), dma((3,)), dma, dma, dma((2, 2)), dma((4,)),
            dma((2, NU)), dma((2, NU)), dma((NU,)), dma((NU,)), dma((NU,)), dma((3, NU)),
            dma((NF + 1,)), dma((NF + 1,)), dma((4, 4)), dma((4, 4)), dma((4, 4)), dma((4,)),
            dma((4,)), dma((4,)), dma((2,)), dma((2,)), dma, dma, dma((4,)), dma((4,)), dma,
        ],
        compiler_params=pltpu.CompilerParams(
            collective_id=1, has_side_effects=True, vmem_limit_bytes=63 << 20
        ),
        name="layer",
    )(*args)


def local_fast(
    tokens, lengths, seq_order, gain_attn, w_qkv, w_attn_out, gain_mlp, w_in, w_mlp_out, cotangent
):
    half = HEAD_DIM // 2
    frequency = jnp.tile(rope_base ** (-2.0 * jnp.arange(half, dtype=F32) / HEAD_DIM), 4)
    sign = jnp.tile(jnp.repeat(jnp.array([-1.0, 1.0], F32), half), 2)
    rows = (gain_attn.astype(F32), gain_mlp.astype(F32), frequency, sign)
    gains = jnp.concatenate([r[None, :] for r in rows] + [jnp.zeros((4, 128), F32)], axis=0)
    out, d_tok, d_qkv, d_in, d_down, d_out, d_gain = run_layer(
        lengths, seq_order, tokens, w_qkv, w_in.transpose(1, 2, 0).reshape(2 * HID, 128), w_mlp_out, w_attn_out, gains, cotangent
    )
    return (out, d_tok, d_gain[0], d_qkv, d_out, d_gain[1], d_in.reshape(2, HID, 128).transpose(2, 0, 1), d_down)


def layer_norm(field_in, norm_gain):
    row_mean = jnp.mean(field_in, axis=-1, keepdims=True)
    centered = field_in - row_mean
    variance = jnp.mean(centered * centered, axis=-1, keepdims=True)
    return centered * lax.rsqrt(variance + norm_eps) * norm_gain


def rotate(field_in, position):
    half_size = field_in.shape[-1] // 2
    index_range = jnp.arange(half_size, dtype=jnp.float32)
    frequency = rope_base ** (-2.0 * index_range / field_in.shape[-1])
    angles = position[:, None] * frequency[None, :]
    cosine = jnp.cos(angles)[:, None, :]
    sine_part = jnp.sin(angles)[:, None, :]
    first_half = field_in[..., :half_size]
    second_half = field_in[..., half_size:]
    return jnp.concatenate(
        [
            first_half * cosine - second_half * sine_part,
            second_half * cosine + first_half * sine_part,
        ],
        axis=-1,
    )


def geglu(act_part, up_part):
    return jax.nn.gelu(act_part, approximate=False) * up_part


def layout(lengths, seq_order, group_rows):
    seq_total = seq_order.shape[0]
    first_seq = lax.axis_index("dp") * SEQ_GRP
    chosen = lax.dynamic_slice_in_dim(seq_order, first_seq, SEQ_GRP)
    matched = chosen[:, None] == jnp.arange(seq_total, dtype=jnp.int32)[None, :]
    dealt_lengths = jnp.sum(jnp.where(matched, lengths[None, :], 0), axis=1)
    seq_ends = jnp.cumsum(dealt_lengths)
    row_index = jnp.arange(group_rows, dtype=jnp.int32)
    passed = row_index[:, None] >= seq_ends[None, :]
    segment = jnp.sum(passed.astype(jnp.int32), axis=1)
    row_start = jnp.sum(jnp.where(passed, dealt_lengths[None, :], 0), axis=1)
    return (segment, (row_index - row_start).astype(jnp.float32))


def item_layout(array_in, block_rows):
    group_rows, head_count, head_size = array_in.shape
    block_count = group_rows // block_rows
    shaped = array_in.reshape(block_count, block_rows, head_count, head_size)
    return shaped.transpose(2, 0, 1, 3).reshape(head_count * block_count, block_rows, head_size)


def from_items(items, group_rows):
    item_count, block_rows, head_size = items.shape
    block_count = group_rows // block_rows
    head_count = item_count // block_count
    shaped = items.reshape(head_count, block_count, block_rows, head_size)
    return shaped.transpose(1, 2, 0, 3).reshape(group_rows, head_count, head_size)


def masked_scores(query_block, key_head, segment_block, segment):
    score_scale = query_block.shape[-1] ** (-0.5)
    raw_scores = lax.dot_general(
        query_block, key_head, (((1,), (1,)), ((), ())), preferred_element_type=jnp.float32
    )
    allowed = segment_block[:, None] == segment[None, :]
    return jnp.where(allowed, raw_scores * score_scale, masked_fill)


def attend_forward(query_rot, key_rot, value_low, segment, block_rows):
    group_rows, head_count, head_size = query_rot.shape
    block_count = group_rows // block_rows
    query_items = item_layout(query_rot, block_rows)
    key_heads = key_rot.transpose(1, 0, 2)
    value_heads = value_low.transpose(1, 0, 2)
    segment_blocks = segment.reshape(block_count, block_rows)

    def one_item(item_index):
        head_index = item_index // block_count
        block_index = item_index % block_count
        query_block = lax.dynamic_index_in_dim(query_items, item_index, 0, False)
        key_head = lax.dynamic_index_in_dim(key_heads, head_index, 0, False)
        value_head = lax.dynamic_index_in_dim(value_heads, head_index, 0, False)
        segment_block = lax.dynamic_index_in_dim(segment_blocks, block_index, 0, False)
        scores = masked_scores(query_block, key_head, segment_block, segment)
        row_top = jnp.max(scores, axis=1, keepdims=True)
        weights = jnp.exp(scores - row_top)
        row_total = jnp.sum(weights, axis=1, keepdims=True)
        probs_low = (weights / row_total).astype(jnp.bfloat16)
        result = jnp.dot(probs_low, value_head, preferred_element_type=jnp.float32)
        return (result, row_top[:, 0] + jnp.log(row_total[:, 0]))

    results, log_totals = lax.map(one_item, jnp.arange(head_count * block_count, dtype=jnp.int32))
    return (from_items(results, group_rows), log_totals)


def attend_backward(query_rot, key_rot, value_low, grad_out, log_totals, segment, block_rows):
    group_rows, head_count, head_size = query_rot.shape
    block_count = group_rows // block_rows
    score_scale = head_size ** (-0.5)
    query_items = item_layout(query_rot, block_rows)
    grad_items = item_layout(grad_out, block_rows)
    key_heads = key_rot.transpose(1, 0, 2)
    value_heads = value_low.transpose(1, 0, 2)
    segment_blocks = segment.reshape(block_count, block_rows)

    def one_item(carried, item_index):
        key_grads, value_grads = carried
        head_index = item_index // block_count
        block_index = item_index % block_count
        query_block = lax.dynamic_index_in_dim(query_items, item_index, 0, False)
        grad_block = lax.dynamic_index_in_dim(grad_items, item_index, 0, False)
        log_row = lax.dynamic_index_in_dim(log_totals, item_index, 0, False)
        key_head = lax.dynamic_index_in_dim(key_heads, head_index, 0, False)
        value_head = lax.dynamic_index_in_dim(value_heads, head_index, 0, False)
        segment_block = lax.dynamic_index_in_dim(segment_blocks, block_index, 0, False)
        scores = masked_scores(query_block, key_head, segment_block, segment)
        prob_full = jnp.exp(scores - log_row[:, None])
        probs_low = prob_full.astype(jnp.bfloat16)
        grad_probs = lax.dot_general(
            grad_block, value_head, (((1,), (1,)), ((), ())), preferred_element_type=jnp.float32
        )
        row_delta = jnp.sum(prob_full * grad_probs, axis=1, keepdims=True)
        grad_scores = (prob_full * (grad_probs - row_delta)).astype(jnp.bfloat16)
        grad_query = (
            jnp.dot(grad_scores, key_head, preferred_element_type=jnp.float32) * score_scale
        )
        grad_key = (
            lax.dot_general(
                grad_scores,
                query_block,
                (((0,), (0,)), ((), ())),
                preferred_element_type=jnp.float32,
            )
            * score_scale
        )
        grad_value = lax.dot_general(
            probs_low, grad_block, (((0,), (0,)), ((), ())), preferred_element_type=jnp.float32
        )
        key_grads = lax.dynamic_update_index_in_dim(
            key_grads,
            lax.dynamic_index_in_dim(key_grads, head_index, 0, False) + grad_key,
            head_index,
            0,
        )
        value_grads = lax.dynamic_update_index_in_dim(
            value_grads,
            lax.dynamic_index_in_dim(value_grads, head_index, 0, False) + grad_value,
            head_index,
            0,
        )
        return ((key_grads, value_grads), grad_query)

    zero_heads = jnp.zeros((head_count, group_rows, head_size), jnp.float32)
    (key_grads, value_grads), query_grads = lax.scan(
        one_item, (zero_heads, zero_heads), jnp.arange(head_count * block_count, dtype=jnp.int32)
    )
    return (
        from_items(query_grads, group_rows),
        key_grads.transpose(1, 0, 2),
        value_grads.transpose(1, 0, 2),
    )


def spread_rows(local_rows):
    return lax.all_gather(local_rows, "tensor", axis=0, tiled=True)


def spread_grads(local_grads):
    return lax.all_gather(local_grads, "tensor", axis=0, tiled=True)


def sum_heads(activations, weight_part, row_count):

    def row_term(first_row, row_number):
        return jnp.dot(activations, weight_part, preferred_element_type=jnp.float32)

    return lax.psum_scatter(
        row_term(jnp.int32(0), row_count * lax.axis_size("tensor")),
        "tensor",
        scatter_dimension=0,
        tiled=True,
    )


def sum_grads(grads_low, weight_full, einsum_form, row_count):

    def row_term(first_row, row_number):
        return jnp.einsum(einsum_form, grads_low, weight_full, preferred_element_type=jnp.float32)

    return lax.psum_scatter(
        row_term(jnp.int32(0), row_count * lax.axis_size("tensor")),
        "tensor",
        scatter_dimension=0,
        tiled=True,
    )


def local_plain(
    tokens, lengths, seq_order, gain_attn, w_qkv, w_attn_out, gain_mlp, w_in, w_mlp_out, cotangent
):
    row_count = tokens.shape[0]
    group_rows = row_count * lax.axis_size("tensor")
    block_rows = min(512, group_rows)
    segment, position = layout(lengths, seq_order, group_rows)
    gain_low_one, qkv_weight, out_weight, gain_low_two, in_weight, down_weight = (
        lax.all_gather(gain_attn, "dp", axis=0, tiled=True),
        lax.all_gather(w_qkv, "dp", axis=1, tiled=True),
        lax.all_gather(w_attn_out, "dp", axis=1, tiled=True),
        lax.all_gather(gain_mlp, "dp", axis=0, tiled=True),
        lax.all_gather(w_in, "dp", axis=0, tiled=True),
        lax.all_gather(w_mlp_out, "dp", axis=1, tiled=True),
    )
    gain_one = gain_low_one.astype(jnp.float32)
    gain_two = gain_low_two.astype(jnp.float32)
    residual = tokens.astype(jnp.float32)
    normed_one = spread_rows(layer_norm(residual, gain_one).astype(jnp.bfloat16))
    qkv = jnp.einsum("rd,pdc->rpc", normed_one, qkv_weight, preferred_element_type=jnp.float32)
    head_count = qkv.shape[2] // HEAD_DIM
    head_shape = (group_rows, head_count, HEAD_DIM)
    query_rot = rotate(qkv[:, 0].reshape(head_shape), position).astype(jnp.bfloat16)
    key_rot = rotate(qkv[:, 1].reshape(head_shape), position).astype(jnp.bfloat16)
    value_low = qkv[:, 2].reshape(head_shape).astype(jnp.bfloat16)
    attended, log_totals = attend_forward(query_rot, key_rot, value_low, segment, block_rows)
    attn_low = attended.reshape(group_rows, head_count * HEAD_DIM).astype(jnp.bfloat16)
    resid_mid = residual + sum_heads(attn_low, out_weight, row_count)
    normed_two = spread_rows(layer_norm(resid_mid, gain_two).astype(jnp.bfloat16))
    gate_up = jnp.einsum("rd,dpc->rpc", normed_two, in_weight, preferred_element_type=jnp.float32)
    hidden = geglu(gate_up[:, 0], gate_up[:, 1]).astype(jnp.bfloat16)
    output = (resid_mid + sum_heads(hidden, down_weight, row_count)).astype(jnp.bfloat16)
    grad_two = spread_grads(cotangent)
    d_hidden = lax.dot_general(
        grad_two, down_weight, (((1,), (1,)), ((), ())), preferred_element_type=jnp.float32
    )
    d_down = lax.dot_general(
        hidden, grad_two, (((0,), (0,)), ((), ())), preferred_element_type=jnp.float32
    )
    geglu_pull = jax.vjp(geglu, gate_up[:, 0], gate_up[:, 1])[1]
    d_act, d_up = geglu_pull(d_hidden)
    d_gate_up = jnp.stack([d_act, d_up], axis=1).astype(jnp.bfloat16)
    d_in = jnp.einsum("rd,rpc->dpc", normed_two, d_gate_up, preferred_element_type=jnp.float32)
    d_normed_two = sum_grads(d_gate_up, in_weight, "rpc,dpc->rd", row_count)
    norm_pull_two = jax.vjp(layer_norm, resid_mid, gain_two)[1]
    d_mid_norm, d_gain_two = norm_pull_two(d_normed_two)
    d_mid = cotangent.astype(jnp.float32) + d_mid_norm
    grad_one = spread_grads(d_mid.astype(jnp.bfloat16))
    d_out = lax.dot_general(
        attn_low, grad_one, (((0,), (0,)), ((), ())), preferred_element_type=jnp.float32
    )
    d_att = lax.dot_general(
        grad_one, out_weight, (((1,), (1,)), ((), ())), preferred_element_type=jnp.float32
    ).astype(jnp.bfloat16)
    d_query_rot, d_key_rot, d_value = attend_backward(
        query_rot, key_rot, value_low, d_att.reshape(head_shape), log_totals, segment, block_rows
    )
    rotate_pull = jax.vjp(lambda field_in: rotate(field_in, position), d_query_rot)[1]
    d_query = rotate_pull(d_query_rot)[0]
    d_key = rotate_pull(d_key_rot)[0]
    flat_shape = (group_rows, head_count * HEAD_DIM)
    d_qkv = jnp.stack(
        [d_query.reshape(flat_shape), d_key.reshape(flat_shape), d_value.reshape(flat_shape)],
        axis=1,
    ).astype(jnp.bfloat16)
    d_qkv_weight = jnp.einsum("rd,rpc->pdc", normed_one, d_qkv, preferred_element_type=jnp.float32)
    d_normed_one = sum_grads(d_qkv, qkv_weight, "rpc,pdc->rd", row_count)
    norm_pull_one = jax.vjp(layer_norm, residual, gain_one)[1]
    d_first, d_gain_one = norm_pull_one(d_normed_one)
    d_tokens = d_mid + d_first
    gain_sums = lax.psum((d_gain_one, d_gain_two), "tensor")
    shares = (
        lax.psum_scatter(gain_sums[0], "dp", scatter_dimension=0, tiled=True),
        lax.psum_scatter(d_qkv_weight, "dp", scatter_dimension=1, tiled=True),
        lax.psum_scatter(d_out, "dp", scatter_dimension=1, tiled=True),
        lax.psum_scatter(gain_sums[1], "dp", scatter_dimension=0, tiled=True),
        lax.psum_scatter(d_in, "dp", scatter_dimension=0, tiled=True),
        lax.psum_scatter(d_down, "dp", scatter_dimension=1, tiled=True),
    )
    return (output, d_tokens, shares[0], shares[1], shares[2], shares[3], shares[4], shares[5])


def solution(mesh):
    fast = mesh.shape["dp"] == 8 and mesh.shape["tensor"] == 4
    return jax.shard_map(
        local_fast if fast else local_plain,
        mesh=mesh,
        in_specs=(
            P(("dp", "tensor"), None),
            P(),
            P(),
            P("dp"),
            P(None, "dp", "tensor"),
            P("tensor", "dp"),
            P("dp"),
            P("dp", None, "tensor"),
            P("tensor", "dp"),
            P(("dp", "tensor"), None),
        ),
        out_specs=(
            P(("dp", "tensor"), None),
            P(("dp", "tensor"), None),
            P("dp"),
            P(None, "dp", "tensor"),
            P("tensor", "dp"),
            P("dp"),
            P("dp", None, "tensor"),
            P("tensor", "dp"),
        ),
        check_vma=False,
    )
```

```python
import functools

import jax
import jax.numpy as jnp
from jax import lax
from jax.experimental import pallas as pl
from jax.experimental.pallas import tpu as pltpu
from jax.sharding import PartitionSpec as P

HEAD_DIM = 64
SEQ_GRP = 4
rope_base = 160000.0
norm_eps = 1e-05
masked_fill = -1e30
MESH = pl.DeviceIdType.MESH
BF = jnp.bfloat16
F32 = jnp.float32

NT = (((1,), (1,)), ((), ()))
TN = (((0,), (0,)), ((), ()))


def place():
    dp = lax.axis_index("dp")
    z = lax.axis_index("tensor")
    c = lax.rem(dp, 2)
    x = lax.rem(lax.div(dp, 2), 2)
    y = lax.div(dp, 4)
    return dp, z, c, x, y


def flip(dp, bits, distance):
    out = dp
    for b, bit in enumerate(bits):
        if (distance >> b) & 1:
            out = out + (1 << b) - (2 << b) * bit
    return out


def remote(src, dst, send, recv, dev):
    return pltpu.make_async_remote_copy(
        src_ref=src, dst_ref=dst, send_sem=send, recv_sem=recv, device_id=dev, device_id_type=MESH
    )


def cols(start, size):
    return pl.ds(pl.multiple_of(start, size), size)


def greet(dp, z, bits):
    c = bits[0]
    barrier = pltpu.get_barrier_semaphore()
    peers = [(flip(dp, bits, d), z) for d in range(1, 8)]
    core = flip(dp, bits, 1)
    for k in range(1, 4):
        peers.append((dp, lax.rem(z + k, 4)))
        peers.append((core, lax.rem(z + k, 4)))
    for p in peers:
        pl.semaphore_signal(barrier, inc=1, device_id=p, device_id_type=MESH)
    pl.semaphore_wait(barrier, len(peers))


def norm_rows(v):
    mean = jnp.mean(v, axis=-1, keepdims=True)
    centered = v - mean
    var = jnp.mean(centered * centered, axis=-1, keepdims=True)
    rstd = lax.rsqrt(var + norm_eps)
    return centered * rstd, rstd


def turn(v, cs, sn):
    lane = lax.broadcasted_iota(jnp.int32, cs.shape, 1)
    low_half = lax.rem(lane, HEAD_DIM) < HEAD_DIM // 2
    parts = []
    for t in range(v.shape[1] // 128):
        piece = v[:, t * 128 : (t + 1) * 128]
        swapped = jnp.where(low_half, pltpu.roll(piece, 96, 1), pltpu.roll(piece, 32, 1))
        parts.append(piece * cs + swapped * sn)
    return jnp.concatenate(parts, axis=1)


def gain_row(gains, row):
    return jnp.concatenate([gains[p, row : row + 1, :] for p in range(8)], axis=1)


HID = 656
FF3 = 3 * HID
FROWS = ((0, HID), (HID, HID), (2 * HID, HID))
CUTS = ((0, 496), (496, 496), (992, 496), (1488, 480))
HALVES = tuple((m, o, n) for m in (2, 0, 1) for o, n in ((0, 336), (336, 320)))
NF = len(HALVES)
NU = NF + 2
INV_SQRT2 = 0.7071067811865476
INV_SQRT_2PI = 0.3989422804014327


def layer_kernel(
    lengths, seq_order, tok, wqkv, win, wmlp, wout, gains_in, cot,
    out_o, dtok_o, dwq_o, dwin_o, dwmlp_o, dwout_o, dg_o,
    gains, w3, cs, sn, segc, segr, q, k, v, lse, att, attn2, h1, wq, cot4,
    G, Wo, X1, h2a, dya, yr, acc, hidT, daT, duT, dX1, dsb, dr, dzs, dzr, usb, ur, uzs, uzr, dsend, datt, delta,
    dq, dk, dv, Hs, Hi, Hx, Rb, Ra, Z, Rbo, Rao, Zo, give, Wp, Wc, Wb, Wa, gz,
    us, ds, rb, ra, wr_s, wr_r, wx_s, wx_r, g_s, g_r, cx_s, cx_r, hop_s, hop_r,
    ou_s, o_r, oa_s, ob_s, of_s, oa_r, ob_r,
    fz_s, fz_r, pa_s, pb_s, pf_s, pa_r, pb_r, at_s, at_r,
    y_s, y_r, n_s, n_r, d_s, d_r, u_s, u_r, e_s, e_r, t_s, t_r,
    b_s, b_r, a_s, a_r, zu_s, z_r, fin_s, fin_r,
    hu_s, hd_s, hi_r, hx_r, wc_s, wc_r, wb_s, wb_r, wa_s, wa_r, gz_s, gz_r, lc,
):
    dp, z, c, x, y = place()
    bits = (c, x, y)
    core = flip(dp, bits, 1)
    px, py = flip(dp, bits, 2), flip(dp, bits, 4)
    a = (1 - c) * px + c * py
    b = (1 - c) * py + c * px
    chip, chip_a, chip_b = lax.div(dp, 2), lax.div(a, 2), lax.div(b, 2)
    chip_d = 3 - chip
    home = lax.div(z, 2)
    org = c == home
    zq = lax.rem(z, 2)
    zp = z + 1 - 2 * zq
    z2 = z + 2 - 4 * home
    end = (z == 0) | (z == 3)
    own = cols(c * 256, 256)
    other = cols((1 - c) * 256, 256)

    def block(core_bit, line_bit):
        return cols((2 * line_bit + core_bit) * 256, 256)

    ob, cb, zb, db = block(c, zq), block(1 - c, zq), block(c, 1 - zq), block(1 - c, 1 - zq)
    tall, vT, kT, oT, dqkvT = Hs, Hx, dzs, acc.at[:, 0:256], h2a.at[0:768]
    dw4 = (dwin_o.at[0:HID], dwin_o.at[HID : 2 * HID], dwmlp_o)
    greet(dp, z, bits)

    def no(cond):
        return jnp.logical_not(cond)

    def tok_up(k_, h):
        ref = tall.at[z - k_, pl.ds(h * 128, 128)]
        src = tok.at[pl.ds(h * 128, 128)] if k_ == 0 else ref
        return remote(src, ref, us.at[k_, h], rb.at[k_ + 1, h], (dp, z + 1))

    def tok_down(k_, h):
        ref = tall.at[z + k_, pl.ds(h * 128, 128)]
        src = tok.at[pl.ds(h * 128, 128)] if k_ == 0 else ref
        return remote(src, ref, ds.at[k_, h], ra.at[k_ + 1, h], (dp, z - 1))

    def up_ok(k_):
        return (z >= k_) & (z < 3)

    def down_ok(k_):
        return (z + k_ <= 3) & (z > 0)

    for h in range(2):
        pl.when(up_ok(0))(lambda h=h: tok_up(0, h).start())
        pl.when(down_ok(0))(lambda h=h: tok_down(0, h).start())

    for d in range(1, 8):
        remote(gains_in, gains.at[dp], g_s.at[d], g_r.at[d], (flip(dp, bits, d), z)).start()
    own_rows = cols(dp * 128, 128)
    for j, d in enumerate((2, 4, 6)):
        remote(wqkv, wq.at[:, own_rows], wr_s.at[j], wr_r.at[j], (flip(dp, bits, d), z)).start()
    remote(wqkv, wq.at[:, own_rows], wx_s.at[3], wx_r.at[3], (core, z)).start()
    cot_copy = (
        remote(cot, cot4.at[ob], cx_s.at[0], cx_r.at[0], (core, z)),
        remote(cot, cot4.at[ob], cx_s.at[1], cx_r.at[1], (dp, zp)),
        remote(cot4.at[zb], cot4.at[zb], cx_s.at[2], cx_r.at[2], (core, z)),
    )
    cot_copy[0].start()
    cot_local = pltpu.make_async_copy(cot, cot4.at[ob], lc)
    cot_local.start()

    w3[0 : 2 * HID, :] = win[...]
    w3[2 * HID : FF3, :] = wmlp[...]
    lanes = cols(dp * 128, 128)
    hop = (
        remote(w3, G.at[:, lanes], hop_s.at[0], hop_r.at[0], (core, z)),
        remote(wout, Wo.at[zq, :, lanes], hop_s.at[1], hop_r.at[1], (core, z)),
    )

    @pl.when(no(org))
    def _():
        hop[1].start()
        hop[0].start()

    @pl.when(org)
    def _():
        G[:, lanes] = w3[...]
        Wo[zq, :, lanes] = wout[...]

    gains[dp] = gains_in[...]
    wq[:, own_rows, :] = wqkv[...]
    tall[z] = tok[...]
    cot_local.wait()

    def begin(cp):
        cp.start()

    def done(cp):
        cp.wait_send()

    def piece(u, where):
        r0, n = CUTS[u]
        return G.at[pl.ds(r0, n), cols(where * 256, 256)]

    def way(u):
        s = lax.rem(c + u, 2)
        one = (1 - s) * px + s * py
        two = (1 - s) * py + s * px
        return one, two, lax.div(one, 2), lax.div(two, 2)

    def plane_a(u):
        return remote(piece(u, chip), piece(u, chip), pa_s.at[u], pa_r.at[u], (way(u)[0], z))

    def plane_b(u):
        return remote(piece(u, chip), piece(u, chip), pb_s.at[u], pb_r.at[0, u], (way(u)[1], z))

    def plane_f(u):
        ref = piece(u, way(u)[2])
        return remote(ref, ref, pf_s.at[u], pb_r.at[1, u], (way(u)[1], z))

    def leap(u):
        return remote(piece(u, chip), piece(u, chip), fz_s.at[u], fz_r.at[u], (dp, z2))

    def spread(u):
        plane_a(u).start()
        plane_b(u).start()

    def across(u):
        ref = piece(u, way(u)[2])
        remote(ref, ref, pa_s.at[u], pa_r.at[u], (way(u)[0], z)).wait_recv()
        plane_f(u).start()

    def land(u):
        leap(u).wait_recv()
        spread(u)

    near = (1 - c) * lax.div(z + 2, 3) + c * lax.div(z, 3)
    far = 1 - near

    def opiece(qi, where):
        return Wo.at[qi, :, cols(where * 256, 256)]

    def ofar(k_):
        ref = opiece(zq, chip)
        return remote(ref, ref, ou_s.at[k_], o_r.at[zq], (dp, lax.rem(z + k_, 4)))

    def oplane(qi):
        ref, ref_a = opiece(qi, chip), opiece(qi, chip_a)
        return (
            remote(ref, ref, oa_s.at[qi], oa_r.at[qi], (a, z)),
            remote(ref, ref, ob_s.at[qi], ob_r.at[0, qi], (b, z)),
            remote(ref_a, ref_a, of_s.at[qi], ob_r.at[1, qi], (b, z)),
        )

    def ospread(qi):
        cps = oplane(qi)
        cps[0].start()
        cps[1].start()

    def oland(qi):
        ref = opiece(qi, chip)
        remote(ref, ref, ou_s.at[1], o_r.at[qi], (core, z)).wait_recv()
        ospread(qi)

    def oacross(qi):
        ref = opiece(qi, chip_a)
        remote(ref, ref, oa_s.at[qi], oa_r.at[qi], (a, z)).wait_recv()
        oplane(qi)[2].start()

    ends, starts, total = [], [], 0
    for j in range(SEQ_GRP):
        ends.append(total)
        total = total + lengths[seq_order[dp * SEQ_GRP + j]]
    for dst, shape, axis in ((segc, (1024, 128), 0), (segr, (8, 1024), 1)):
        row = lax.broadcasted_iota(jnp.int32, shape, axis)
        seg = jnp.zeros(shape, F32)
        start = jnp.zeros(shape, jnp.int32)
        for j in range(1, SEQ_GRP):
            passed = row >= ends[j]
            seg = jnp.where(passed, float(j), seg)
            start = jnp.where(passed, ends[j], start)
        dst[...] = seg
        if axis == 0:
            angle = (row - start).astype(F32) * gains_in[2:3, :]
            cs[...] = jnp.cos(angle)
            sn[...] = jnp.sin(angle) * gains_in[3:4, :]

    for d in range(1, 8):
        p = flip(dp, bits, d)
        remote(gains_in, gains.at[p], g_s.at[d], g_r.at[d], (p, z)).wait_recv()

    @pl.when(org)
    def _():
        remote(wout, Wo.at[zq, :, cols(core * 128, 128)], hop_s.at[1], hop_r.at[1], (core, z)).wait_recv()
        ospread(near)
        remote(w3, G.at[:, cols(core * 128, 128)], hop_s.at[0], hop_r.at[0], (core, z)).wait_recv()
        for u in range(4):
            spread(u)

    for j, d in enumerate((2, 4, 6)):
        p = flip(dp, bits, d)
        rows = wq.at[:, cols(p * 128, 128)]
        remote(wqkv, rows, wr_s.at[j], wr_r.at[j], (p, z)).wait_recv()
        remote(rows, rows, wx_s.at[j], wx_r.at[j], (core, z)).start()
    for j, d in enumerate((3, 5, 7, 1)):
        p = flip(dp, bits, d)
        remote(wqkv, wq.at[:, cols(p * 128, 128)], wx_s.at[j], wx_r.at[j], (core, z)).wait_recv()

    gain1, gain2 = gain_row(gains, 0), gain_row(gains, 1)

    def project(s):
        base = s * 256

        @pl.loop(0, 8)
        def _(r):
            xhat, _r = norm_rows(tall[s, pl.ds(pl.multiple_of(r * 32, 32), 32), :].astype(F32))
            h1[pl.ds(pl.multiple_of(base + r * 32, 32), 32), :] = (xhat * gain1).astype(BF)

        rows = pl.ds(pl.multiple_of(base, 256), 256)
        hb = h1[rows, :]
        cb, sb = cs[rows, :], sn[rows, :]
        for p, dst in enumerate((q, k, v)):
            r = jnp.dot(hb, wq[p], preferred_element_type=F32)
            if p < 2:
                r = turn(r, cb, sb)
            if p == 0:
                r = r * (HEAD_DIM**-0.5)
            dst[rows, :] = r.astype(BF)

    def receive(k_):
        below, above = z - k_ >= 0, z + k_ <= 3
        for h in range(2):

            @pl.when(below)
            def _(k_=k_, h=h):
                ref = tall.at[z - k_, pl.ds(h * 128, 128)]
                remote(ref, ref, us.at[k_, h], rb.at[k_, h], (core, z)).wait_recv()
                if k_ < 3:
                    pl.when(up_ok(k_))(lambda: tok_up(k_, h).start())

            @pl.when(above)
            def _(k_=k_, h=h):
                ref = tall.at[z + k_, pl.ds(h * 128, 128)]
                remote(ref, ref, ds.at[k_, h], ra.at[k_, h], (core, z)).wait_recv()
                if k_ < 3:
                    pl.when(down_ok(k_))(lambda: tok_down(k_, h).start())

    for k_ in range(4):
        if k_ != 1:
            receive(max(k_, 1))

        if k_ == 1:

            @pl.when(org)
            def _():
                for n in range(1, 4):
                    ofar(n).start()

        @pl.loop(0, 2)
        def _(t, k_=k_):
            s = z - k_ + 2 * k_ * t
            pl.when((s >= 0) & (s <= 3) & ((k_ > 0) | (t == 0)))(lambda: project(s))

        if k_ == 1:

            @pl.when(org)
            def _():
                oacross(near)
                for u in range(4):
                    across(u)

        if k_ == 2:

            @pl.when(org & end)
            def _():
                for u in range(4):
                    leap(u).start()

    for s in range(4):
        vT[:, s * 256 : (s + 1) * 256] = v[s * 256 : (s + 1) * 256, :].T
    head_of = lax.div(lax.broadcasted_iota(jnp.int32, (256, 256), 1), HEAD_DIM)

    def attend(i):
        rows = pl.ds(pl.multiple_of(i * 256, 256), 256)
        qb = q[rows, :]
        seg_q = segr[0:1, rows]
        heads = range(4)
        qh = [jnp.where(head_of == h, qb, jnp.zeros((), BF)) for h in heads]
        chunks = [slice(kc * 256, kc * 256 + 256) for kc in range(4)]
        for h in heads:
            hr = slice(h * HEAD_DIM, (h + 1) * HEAD_DIM)
            scores, tops = [], []
            for keys in chunks:
                seg_k = segc[keys, :]
                same = jnp.concatenate([seg_k, seg_k], axis=1) == seg_q
                s = lax.dot_general(k[keys, :], qh[h], NT, preferred_element_type=F32)
                s = jnp.where(same, s, masked_fill)
                scores.append(s)
                tops.append(jnp.max(s, axis=0, keepdims=True))
            top = jnp.maximum(jnp.maximum(tops[0], tops[1]), jnp.maximum(tops[2], tops[3]))
            tot, out = 0.0, 0.0
            for keys, s in zip(chunks, scores):
                p = jnp.exp(s - top)
                tot = tot + jnp.sum(p, axis=0, keepdims=True)
                out = out + jnp.dot(vT[hr, keys], p.astype(BF), preferred_element_type=F32)
            oT[hr, :] = out * (1.0 / tot)
            lse[h, i] = jnp.broadcast_to(top + jnp.log(tot), (8, 256))
        att[rows, :] = oT[...].T.astype(BF)

    def att_slot(src_core, q):
        return attn2.at[cols(src_core * 256, 256), cols(q * 256, 256)]

    def att_copy(n, i):
        rows = pl.ds(pl.multiple_of(i * 256, 256), 256)
        return remote(
            att.at[rows, :], att_slot(c, zq), at_s.at[n], at_r.at[c, zq], (2 * chip + home, i)
        )

    @pl.loop(0, 4)
    def _(n):
        i = lax.rem(z + 1 + n, 4)
        attend(i)
        for m in range(4):

            @pl.when((n == m) & ((m < 3) | no(org)))
            def _(m=m):
                att_copy(m, i).start()

        @pl.when((n == 3) & org)
        def _():
            attn2[own, cols(zq * 256, 256)] = att[pl.ds(pl.multiple_of(z * 256, 256), 256), :]

        @pl.when((n == 1) & org & no(end))
        def _():
            for u in range(4):
                leap(u).start()

        pl.when(n == 3)(lambda: cot_copy[1].start())

        @pl.when((n == 1) & end)
        def _():
            oland(far)
            pl.when(no(org))(lambda: oland(near))

        @pl.when((n == 3) & end)
        def _():
            oacross(far)
            pl.when(no(org))(lambda: oacross(near))

    @pl.when(no(end))
    def _():
        oland(far)
        pl.when(no(org))(lambda: oland(near))

    @pl.when(no(end))
    def _():
        oacross(far)
        pl.when(no(org))(lambda: oacross(near))

    def late(*ops):
        @pl.when(no(org))
        def _():
            for op, u in ops:
                op(u)

    pl.when(no(end))(lambda: late((land, 0), (land, 1), (land, 2), (land, 3), (across, 0), (across, 1)))
    pl.when(end)(lambda: late((land, 0)))

    for k_ in range(3):
        for h in range(2):
            pl.when(up_ok(k_))(lambda k_=k_, h=h: tok_up(k_, h).wait_send())
            pl.when(down_ok(k_))(lambda k_=k_, h=h: tok_down(k_, h).wait_send())
    for src in range(2):
        for qi in range(2):
            mine_too = (c == src) & (z == 2 * c + qi)

            @pl.when(no(mine_too))
            def _(src=src, qi=qi):
                slot = att_slot(src, qi)
                remote(slot, slot, at_s.at[0], at_r.at[src, qi], (core, z)).wait_recv()

    pl.when(end)(lambda: late((land, 1)))
    for qi in range(2):
        for w, where in enumerate((chip_b, chip_d)):
            ref = opiece(qi, where)
            remote(ref, ref, ob_s.at[qi], ob_r.at[w, qi], (core, z)).wait_recv()

    def out_proj(rows):
        return sum(
            jnp.dot(attn2[rows, qi * 256 : (qi + 1) * 256], Wo[qi], preferred_element_type=F32) for qi in range(2)
        )

    acc[...] = out_proj(other)
    y_copy = remote(acc, yr, y_s, y_r, (core, z))
    y_copy.start()
    pl.when(end)(lambda: late((land, 2)))
    X1[...] = tok[...].astype(F32) + out_proj(own)
    y_copy.wait()
    pl.when(end)(lambda: late((land, 3)))

    def chunk(r):
        return pl.ds(pl.multiple_of(r * 32, 32), 32)

    def own_chunk(r):
        return pl.ds(pl.multiple_of(c * 256 + r * 32, 32), 32)

    def block_chunk(r):
        return pl.ds(pl.multiple_of((2 * zq + c) * 256 + r * 32, 32), 32)

    @pl.loop(0, 8)
    def _(r):
        x1 = X1[chunk(r), :] + yr[chunk(r), :]
        X1[chunk(r), :] = x1
        xhat, _r = norm_rows(x1)
        h2a[block_chunk(r), :] = (xhat * gain2).astype(BF)

    h_copy = (
        remote(h2a.at[ob], h2a.at[ob], n_s.at[0], n_r.at[0], (core, z)),
        remote(h2a.at[ob], h2a.at[ob], n_s.at[1], n_r.at[1], (dp, zp)),
        remote(h2a.at[zb], h2a.at[zb], n_s.at[2], n_r.at[2], (core, z)),
    )
    h_copy[1].start()
    h_copy[0].start()
    pl.when(end)(lambda: late((across, 0), (across, 1)))
    late((across, 2), (across, 3))
    remote(cot, cot4.at[zb], cx_s.at[1], cx_r.at[1], (dp, zp)).wait_recv()
    cot_copy[2].start()
    remote(cot, cot4.at[cb], cx_s.at[0], cx_r.at[0], (core, z)).wait_recv()
    remote(cot, cot4.at[db], cx_s.at[2], cx_r.at[2], (core, z)).wait_recv()
    for u in range(4):
        for w, where in enumerate((way(u)[3], chip_d)):
            ref = piece(u, where)
            remote(ref, ref, pb_s.at[u], pb_r.at[w, u], (core, z)).wait_recv()
    remote(h2a.at[cb], h2a.at[cb], n_s.at[0], n_r.at[0], (core, z)).wait_recv()

    def tile(r0, n, tokens):
        h2 = h2a[tokens, :]
        act = lax.dot_general(G[r0 : r0 + n, :], h2, NT, preferred_element_type=F32)
        up = lax.dot_general(G[HID + r0 : HID + r0 + n, :], h2, NT, preferred_element_type=F32)
        dh = lax.dot_general(
            G[2 * HID + r0 : 2 * HID + r0 + n, :], cot4[tokens, :], NT, preferred_element_type=F32
        )
        Phi = 0.5 + 0.5 * lax.erf(act * INV_SQRT2)
        phi = jnp.exp(-0.5 * act * act) * INV_SQRT_2PI
        gel = act * Phi
        rr = slice(r0, r0 + n)
        hidT[rr, tokens] = (gel * up).astype(BF)
        daT[rr, tokens] = (dh * up * (Phi + act * phi)).astype(BF)
        duT[rr, tokens] = (dh * gel).astype(BF)

    @pl.loop(0, 2)
    def _(t):
        there = lax.rem(zq + t, 2)

        @pl.when(t == 1)
        def _():
            remote(h2a.at[zb], h2a.at[zb], n_s.at[1], n_r.at[1], (dp, zp)).wait_recv()
            h_copy[2].start()
            remote(h2a.at[db], h2a.at[db], n_s.at[2], n_r.at[2], (core, z)).wait_recv()

        for r0, n in ((0, 336), (336, 320)):
            tile(r0, n, cols(there * 512, 512))

    def tn(lhs, rhs):
        return lax.dot_general(lhs, rhs, TN, preferred_element_type=F32)

    def f_rows(m):
        return pl.ds(FROWS[m][0], HID)

    def d_norm(rows, hc):
        return tn(daT[:, rows], G[f_rows(0), hc]) + tn(duT[:, rows], G[f_rows(1), hc])

    def mlp_out(rows, hc):
        return tn(hidT[:, rows], G[f_rows(2), hc])

    def quad(term, sb, got, zs, zgot, ss, rs, hold=False):
        halves = (slice(0, 512), slice(512, 1024))
        copies = (
            remote(sb.at[0], got.at[0], ss.at[0], rs.at[0], (core, z)),
            remote(sb.at[1], got.at[1], ss.at[1], rs.at[1], (core, z)),
            remote(zs, zgot, ss.at[2], rs.at[2], (dp, zp)),
        )
        for j, rows in enumerate((db, cb)):
            for hc in halves:
                sb[j, :, hc] = term(rows, hc).astype(BF)
            copies[j].start()
        copies[0].wait_recv()
        for hc in halves:
            zs[:, hc] = (term(zb, hc) + got[0, :, hc].astype(F32)).astype(BF)
        if not hold:
            copies[2].start()
        return copies

    def keep(term, dst, plus=None):
        for hc in (slice(0, 512), slice(512, 1024)):
            r = term(ob, hc)
            dst[:, hc] = r if plus is None else r + plus[:, hc]

    def grads(m):
        lhs, rhs = ((daT, h2a), (duT, h2a), (hidT, cot4))[m]

        @pl.loop(0, 4)
        def _(t):
            tc = cols(t * 256, 256)
            G[f_rows(m), tc] = jnp.dot(lhs[...], rhs[:, tc], preferred_element_type=F32).astype(BF)

    def rows_of(e):
        m, o, n = HALVES[e]
        return pl.ds(FROWS[m][0] + o, n)

    def part(e, where):
        if e < NF:
            return G.at[rows_of(e), cols(where * 256, 256)]
        return opiece(e - NF, where)

    def from_b(e, slot):
        return Rb.at[slot, rows_of(e)] if e < NF else Rbo.at[slot, e - NF]

    def from_a(e):
        return Ra.at[rows_of(e)] if e < NF else Rao.at[e - NF]

    def unit_b(e, slot):
        src = part(e, chip_b if slot == 0 else chip_d)
        return remote(src, from_b(e, slot), b_s.at[slot, e], b_r.at[slot, e], (b, z))

    def unit_a(e):
        return remote(part(e, chip_a), from_a(e), a_s.at[e], a_r.at[e], (a, z))

    def send_b(e):
        unit_b(e, 1).start()
        unit_b(e, 0).start()

    def stage1(e):
        unit_b(e, 1).wait_recv()
        ref = part(e, chip_a)
        ref[...] = (ref[...].astype(F32) + from_b(e, 1)[...].astype(F32)).astype(BF)
        unit_a(e).start()

    def unit_z(e):
        return remote(part(e, chip), Z.at[rows_of(e)], zu_s.at[e], z_r.at[0, e], (dp, z2))

    def unit_o(e):
        t = 2 * c + e - NF
        slot = lax.rem(z - t + 4, 4) - 1
        return remote(part(e, chip), Zo.at[slot], zu_s.at[e], z_r.at[slot, e], (dp, t))

    def stage2(e):
        unit_b(e, 0).wait_recv()
        unit_a(e).wait_recv()
        ref = part(e, chip)
        ref[...] = (
            ref[...].astype(F32) + from_b(e, 0)[...].astype(F32) + from_a(e)[...].astype(F32)
        ).astype(BF)
        if e < NF:
            pl.when(no(org))(lambda: unit_z(e).start())
        else:
            pl.when(z != 2 * c + e - NF)(lambda: unit_o(e).start())

    def line_wait(e, slot):
        remote(Zo.at[slot], Zo.at[slot], zu_s.at[e], z_r.at[slot, e], (core, z)).wait_recv()

    def final(e):
        if e < NF:
            m, o, n = HALVES[e]
            return e, give.at[rows_of(e)], dw4[m].at[pl.ds(o, n)]
        return NF, give.at[FF3 : FF3 + 256], dwout_o

    def stage4(e):
        here = org if e < NF else z == 2 * c + e - NF

        @pl.when(here)
        def _():
            slot, gift, dst = final(e)
            if e < NF:
                unit_z(e).wait_recv()
            for who, ref in ((c, dst), (1 - c, gift)):
                ref[...] = part(e, chip)[:, cols(who * 128, 128)].astype(F32)

            def take(got):
                for who, ref in ((c, dst), (1 - c, gift)):
                    ref[...] = ref[...] + got[:, cols(who * 128, 128)].astype(F32)

            def line_take(where):
                line_wait(e, where)
                take(Zo.at[where])

            if e < NF:
                take(Z.at[rows_of(e)])
            else:
                for slot_ in range(3):
                    line_take(slot_)
            remote(gift, dst, fin_s.at[slot], fin_r.at[slot], (core, z)).start()

    def tick(t):
        for lag, step in ((0, stage1), (1, stage2), (4, stage4)):
            if 0 <= t - lag < NU:
                step(t - lag)

    d_copies = quad(d_norm, dsb, dr, dzs, dzr, d_s, d_r)
    keep(d_norm, dX1)
    u_copies = quad(mlp_out, usb, ur, uzs, uzr, u_s, u_r, hold=True)
    keep(mlp_out, dtok_o, X1)
    for u in range(4):
        plane_a(u).wait_send()
        plane_b(u).wait_send()
        plane_f(u).wait_send()
        pl.when(org)(lambda u=u: leap(u).wait_send())

    def ff_grads(m):
        grads(m)
        for e in range(NF):
            if HALVES[e][0] == m:
                send_b(e)

    ff_grads(2)
    ff_grads(0)
    ff_grads(1)
    d_copies[1].wait_recv()
    d_copies[2].wait_recv()

    @pl.loop(0, 8)
    def _(r):
        dh2 = dX1[chunk(r), :] + dr[1, chunk(r), :].astype(F32) + dzr[chunk(r), :].astype(F32)
        xhat, rstd = norm_rows(X1[chunk(r), :])
        e2 = dh2 * gain2
        m1 = jnp.mean(e2, axis=-1, keepdims=True)
        m2 = jnp.mean(e2 * xhat, axis=-1, keepdims=True)
        dx = cot4[block_chunk(r), :].astype(F32) + rstd * (e2 - m1 - xhat * m2)
        dX1[chunk(r), :] = dx
        dya[own_chunk(r), :] = dx.astype(BF)

    e_copy = remote(dya.at[own], dya.at[own], e_s, e_r, (core, z))
    e_copy.start()
    tick(0)
    e_copy.wait()
    for qi in range(2):
        dsend[qi] = lax.dot_general(dya[...], Wo[qi], NT, preferred_element_type=F32).astype(BF)

    def att_back(c0, qi):
        dst = datt.at[cols(z * 256, 256)]
        return remote(
            dsend.at[qi, pl.ds(c0 * 256, 256)], dst, t_s.at[c0, qi], t_r.at[z], (2 * chip + c0, 2 * c + qi)
        )

    def is_self(c0, qi):
        return (c == c0) & (z == 2 * c + qi)

    for c0 in range(2):
        for qi in range(2):
            pl.when(no(is_self(c0, qi)))(lambda c0=c0, qi=qi: att_back(c0, qi).start())

            @pl.when(is_self(c0, qi))
            def _(c0=c0, qi=qi):
                datt[cols(z * 256, 256), :] = dsend[qi, c0 * 256 : (c0 + 1) * 256, :]

    u_copies[2].start()
    for n in range(1, 4):
        pl.when(org)(lambda n=n: ofar(n).wait_send())
    for qi in range(2):
        for cp in oplane(qi):
            cp.wait_send()

        @pl.loop(0, 4)
        def _(t, qi=qi):
            tc = cols(t * 256, 256)
            Wo[qi, :, tc] = tn(attn2[:, qi * 256 : (qi + 1) * 256], dya[:, tc]).astype(BF)

        send_b(NF + qi)
    tick(1)
    tick(2)
    for cp in h_copy:
        cp.wait_send()
    d_copies[2].wait_send()
    for s in range(4):
        kT[:, s * 256 : (s + 1) * 256] = k[s * 256 : (s + 1) * 256, :].T
    dq[...] = jnp.zeros_like(dq)
    dk[...] = jnp.zeros_like(dk)
    dv[...] = jnp.zeros_like(dv)
    for i in range(4):

        @pl.when(no(org & (z == i)))
        def _(i=i):
            ref = datt.at[pl.ds(i * 256, 256)]
            remote(ref, ref, t_s.at[0, 0], t_r.at[i], (core, z)).wait_recv()

    @pl.loop(0, 4)
    def _(i):
        rows = pl.ds(pl.multiple_of(i * 256, 256), 256)
        t = (datt[rows, :].astype(F32) * att[rows, :].astype(F32)).T
        for h in range(4):
            s = jnp.sum(t[h * 64 : (h + 1) * 64, :], axis=0, keepdims=True)
            delta[h, i] = jnp.broadcast_to(s, (8, 256))

    def block_order(l):
        inner = lax.div(z * (3 - z), 2)
        base = inner * jnp.minimum(l, 1) * (lax.rem(l + 1, 3) + 1) + (1 - inner) * l
        return (1 - home) * (3 - base) + home * base

    def pair(i, j):
        ri = pl.ds(pl.multiple_of(i * 256, 256), 256)
        rj = pl.ds(pl.multiple_of(j * 256, 256), 256)

        kj, vj, qi_, dai = k[rj, :], v[rj, :], q[ri, :], datt[ri, :]
        seg_k = segc[rj, :]
        same = jnp.concatenate([seg_k, seg_k], axis=1) == segr[0:1, ri]
        none = jnp.zeros((), BF)
        heads = range(4)
        qh = [jnp.where(head_of == h, qi_, none) for h in heads]
        dah = [jnp.where(head_of == h, dai, none) for h in heads]
        ss = [lax.dot_general(kj, qh[h], NT, preferred_element_type=F32) for h in heads]
        dps = [lax.dot_general(vj, dah[h], NT, preferred_element_type=F32) for h in heads]
        ps = [jnp.exp(jnp.where(same, ss[h], masked_fill) - lse[h, i, 0:1, :]) for h in heads]
        dss = [(ps[h] * (dps[h] - delta[h, i, 0:1, :])).astype(BF) for h in heads]
        dvs = [jnp.dot(ps[h].astype(BF), dah[h], preferred_element_type=F32) for h in heads]
        dks = [jnp.dot(dss[h], qh[h], preferred_element_type=F32) for h in heads]
        dqs = [
            jnp.dot(kT[h * HEAD_DIM : (h + 1) * HEAD_DIM, rj], dss[h], preferred_element_type=F32) for h in heads
        ]
        dv[rj, :] = dv[rj, :] + (dvs[0] + dvs[1] + dvs[2] + dvs[3])
        dk[rj, :] = dk[rj, :] + (dks[0] + dks[1] + dks[2] + dks[3])
        for h in range(4):
            hr = slice(h * HEAD_DIM, (h + 1) * HEAD_DIM)
            dq[hr, ri] = dq[hr, ri] + dqs[h]

    def quarter(t):
        return pl.ds(pl.multiple_of(t * 64, 64), 64)

    def h_up(i, t, last):
        if last:
            return remote(Hs.at[i, quarter(t)], Hx.at[quarter(t)], hu_s.at[i, t], hx_r.at[t], (dp, z + 1))
        return remote(Hs.at[i, quarter(t)], Hi.at[i, quarter(t)], hu_s.at[i, t], hi_r.at[i, t], (dp, z + 1))

    def h_down(i, t):
        return remote(Hs.at[i, quarter(t)], Hi.at[i, quarter(t)], hd_s.at[i, t], hi_r.at[i, t], (dp, z - 1))

    def h_inward(i, t, act):
        pl.when(z > i)(lambda: act(h_down(i, t)))
        pl.when(z + 1 == i)(lambda: act(h_up(i, t, True)))
        pl.when(z + 1 < i)(lambda: act(h_up(i, t, False)))

    def h_wait(i, t):
        ref = Hi.at[i, quarter(t)]
        remote(ref, ref, hd_s.at[i, t], hi_r.at[i, t], (core, z)).wait_recv()

    def h_mid(i, depth):
        mid = ((z > i) & (z == 3 - depth)) | ((z < i) & (z == depth))

        @pl.when(mid)
        def _():
            @pl.loop(0, 4)
            def _(t):
                h_wait(i, t)
                Hs[i, quarter(t), :] = (
                    Hs[i, quarter(t), :].astype(F32) + Hi[i, quarter(t), :].astype(F32)
                ).astype(BF)
                h_inward(i, t, begin)

    def finish(i):
        rows = pl.ds(pl.multiple_of(i * 256, 256), 256)
        cb, sb = cs[rows, :], -sn[rows, :]
        low = (
            turn(dq[:, rows].T * (HEAD_DIM**-0.5), cb, sb).astype(BF),
            turn(dk[rows, :], cb, sb).astype(BF),
            dv[rows, :].astype(BF),
        )
        for p in range(3):
            dqkvT[p * 256 : (p + 1) * 256, rows] = low[p].T
        for half in range(2):
            hc = slice(half * 512, half * 512 + 512)
            dh = sum(
                lax.dot_general(low[p], wq[p, hc, :], NT, preferred_element_type=F32) for p in range(3)
            )
            Hs[i, :, hc] = dh.astype(BF)

            @pl.when(z == i)
            def _(dh=dh, hc=hc):
                acc[:, hc] = dh

        @pl.when(((z == 3) & (z > i)) | ((z == 0) & (z < i)))
        def _():
            for t in range(4):
                h_inward(i, t, begin)


    slots = {0: [3], 2: [4], 5: [5], 8: [6], 11: [7], 14: [8]}
    h_slots = {14: [(0, 1), (3, 1)]}

    @pl.loop(0, 16)
    def _(n):
        def past(v):
            return lax.div(n + 16 - v, 16)

        ph = past(7) + past(12) + past(15)
        t = n - 7 * past(7) - 5 * past(12) - 3 * past(15)
        left = 4 - ph
        over = lax.div(t, left)
        li = ph + over * (t - left + 1)
        lj = ph + (1 - over) * t
        pair(block_order(li), block_order(lj))
        pl.when((n == 6) | (n == 11) | (n == 14) | (n == 15))(lambda: finish(block_order(ph)))
        for s in range(16):
            todo = [lambda t=t: tick(t) for t in slots.get(s, ())]
            todo += [lambda i=i, d=d: h_mid(i, d) for i, d in h_slots.get(s, ())]

            @pl.when(n == s)
            def _(todo=todo):
                for op in todo:
                    op()

    @pl.loop(0, 4)
    def _(t):
        tc = cols(t * 256, 256)
        Wp[:, tc] = jnp.dot(dqkvT[...], h1[:, tc], preferred_element_type=F32).astype(BF)

    def core_copy(w):
        return remote(
            Wp.at[:, cols(w * 256 + (1 - c) * 128, 128)], Wc.at[w], wc_s.at[w], wc_r.at[w], (core, z)
        )

    for w in range(4):
        core_copy(w).start()
    tick(9)

    def both(w):
        Wc[w] = (Wc[w].astype(F32) + Wp[:, cols(w * 256 + c * 128, 128)].astype(F32)).astype(BF)

    for w in range(4):
        core_copy(w).wait_recv()
    both(chip_d)
    both(chip_b)
    wb_copy = [
        remote(Wc.at[where], Wb.at[slot], wb_s.at[slot], wb_r.at[slot], (b, z))
        for slot, where in ((0, chip_b), (1, chip_d))
    ]
    wb_copy[1].start()
    wb_copy[0].start()
    both(chip_a)
    both(chip)
    wa_copy = remote(Wc.at[chip_a], Wa, wa_s, wa_r, (a, z))
    h_mid(3, 2)
    h_mid(0, 2)
    wb_copy[1].wait_recv()
    Wc[chip_a] = (Wc[chip_a].astype(F32) + Wb[1].astype(F32)).astype(BF)
    wa_copy.start()
    h_mid(2, 1)
    h_mid(1, 1)
    u_copies[1].wait_recv()
    u_copies[2].wait_recv()
    out_o[...] = (dtok_o[...] + ur[1].astype(F32) + uzr[...].astype(F32)).astype(BF)

    wb_copy[0].wait_recv()
    wa_copy.wait_recv()
    total = Wc[chip].astype(F32) + Wb[0].astype(F32) + Wa[...].astype(F32)
    dot_one = jnp.zeros((1, 128), F32)
    for p in range(3):
        piece = total[p * 256 : (p + 1) * 256, :]
        dwq_o[p] = piece.T
        dot_one = dot_one + jnp.sum(piece * wqkv[p].T.astype(F32), axis=0, keepdims=True)
    def finals(slots_):
        for e in slots_:

            @pl.when(no(org))
            def _(e=e):
                slot, _, ref = final(e)
                remote(ref, ref, fin_s.at[slot], fin_r.at[slot], (core, z)).wait_recv()

    finals(range(NF))
    part_two = jnp.sum(dwin_o[...] * w3[0 : 2 * HID, :].astype(F32), axis=0, keepdims=True)
    gz[z, 0:1, :] = dot_one / gains[dp, 0:1, :]
    gz[z, 1:2, :] = part_two / gains[dp, 1:2, :]
    gz[z, 2:8, :] = jnp.zeros((6, 128), F32)
    gain_copy = [
        remote(gz.at[z], gz.at[z], gz_s.at[n], gz_r.at[z], (dp, lax.rem(z + n, 4))) for n in range(1, 4)
    ]
    for cp in gain_copy:
        cp.start()
    for t in range(4):
        ref = Hx.at[quarter(t)]
        pl.when(z < 3)(lambda t=t: h_wait(z, t))
        pl.when(z > 0)(lambda t=t, ref=ref: remote(ref, ref, hu_s.at[0, t], hx_r.at[t], (core, z)).wait_recv())
    has_above, has_below = z < 3, z > 0

    @pl.when(has_above)
    def _():
        acc[...] = acc[...] + Hi[z].astype(F32)

    @pl.when(has_below)
    def _():
        acc[...] = acc[...] + Hx[...].astype(F32)

    @pl.loop(0, 8)
    def _(r):
        xhat, rstd = norm_rows(tok[chunk(r), :].astype(F32))
        e1 = acc[chunk(r), :] * gain1
        m1 = jnp.mean(e1, axis=-1, keepdims=True)
        m2 = jnp.mean(e1 * xhat, axis=-1, keepdims=True)
        dtok_o[chunk(r), :] = dX1[chunk(r), :] + rstd * (e1 - m1 - xhat * m2)

    tick(10)
    tick(11)
    finals((NF,))
    for n in range(1, 4):
        o = lax.rem(z + n, 4)
        remote(gz.at[o], gz.at[o], gz_s.at[n], gz_r.at[o], (core, z)).wait_recv()
    dg_o[...] = gz[0] + gz[1] + gz[2] + gz[3]

    for cp in gain_copy:
        cp.wait_send()
    for w in range(4):
        core_copy(w).wait_send()
    wb_copy[0].wait_send()
    wb_copy[1].wait_send()
    wa_copy.wait_send()
    for i in range(4):
        for t in range(4):
            h_inward(i, t, done)
    for c0 in range(2):
        for qi in range(2):
            pl.when(no(is_self(c0, qi)))(lambda c0=c0, qi=qi: att_back(c0, qi).wait_send())
    for cp in d_copies[:2] + u_copies:
        cp.wait_send()
    for e in range(NU):
        unit_b(e, 0).wait_send()
        unit_b(e, 1).wait_send()
        unit_a(e).wait_send()
        if e < NF:
            pl.when(no(org))(lambda e=e: unit_z(e).wait_send())
        else:
            pl.when(z != 2 * c + e - NF)(lambda e=e: unit_o(e).wait_send())

        @pl.when(org if e < NF else z == 2 * c + e - NF)
        def _(e=e):
            slot, gift, dst = final(e)
            remote(gift, dst, fin_s.at[slot], fin_r.at[slot], (core, z)).wait_send()

    for d in range(1, 8):
        remote(gains_in, gains.at[dp], g_s.at[d], g_r.at[d], (core, z)).wait_send()
    for j in range(3):
        remote(wqkv, wq.at[:, own_rows], wr_s.at[j], wr_r.at[j], (core, z)).wait_send()
    for j in range(4):
        remote(wqkv, wq.at[:, own_rows], wx_s.at[j], wx_r.at[j], (core, z)).wait_send()
    for cp in hop:
        pl.when(no(org))(lambda cp=cp: cp.wait_send())
    for cp in cot_copy:
        cp.wait_send()
    for n in range(3):
        att_copy(n, lax.rem(z + 1 + n, 4)).wait_send()
    pl.when(no(org))(lambda: att_copy(3, z).wait_send())


def run_layer(*args):
    V = pl.BlockSpec(memory_space=pltpu.VMEM)
    S = pl.BlockSpec(memory_space=pltpu.SMEM)
    dma = pltpu.SemaphoreType.DMA
    s = jax.ShapeDtypeStruct
    vm = pltpu.VMEM
    return pl.pallas_call(
        layer_kernel,
        out_shape=(
            s((256, 1024), BF), s((256, 1024), F32), s((3, 128, 256), F32), s((2 * HID, 128), F32),
            s((HID, 128), F32), s((256, 128), F32), s((8, 128), F32),
        ),
        in_specs=[S, S] + [V] * 6 + [pl.BlockSpec(memory_space=pl.ANY)],
        out_specs=[V] * 7,
        scratch_shapes=[
            vm((8, 8, 128), F32), vm((FF3, 128), BF), vm((1024, 128), F32), vm((1024, 128), F32),
            vm((1024, 128), F32), vm((8, 1024), F32), vm((1024, 256), BF), vm((1024, 256), BF),
            vm((1024, 256), BF), vm((4, 4, 8, 256), F32), vm((1024, 256), BF), vm((512, 512), BF),
            vm((1024, 1024), BF), vm((3, 1024, 256), BF), vm((1024, 1024), BF),
            vm((FF3, 1024), BF), vm((2, 256, 1024), BF), vm((256, 1024), F32), vm((1024, 1024), BF), vm((512, 1024), BF),
            vm((256, 1024), F32), vm((256, 1024), F32), vm((HID, 1024), BF), vm((HID, 1024), BF),
            vm((HID, 1024), BF), vm((256, 1024), F32),
            vm((2, 256, 1024), BF), vm((2, 256, 1024), BF), vm((256, 1024), BF), vm((256, 1024), BF),
            vm((2, 256, 1024), BF), vm((2, 256, 1024), BF), vm((256, 1024), BF), vm((256, 1024), BF),
            vm((2, 512, 256), BF), vm((1024, 256), BF), vm((4, 4, 8, 256), F32),
            vm((256, 1024), F32), vm((1024, 256), F32), vm((1024, 256), F32),
            vm((4, 256, 1024), BF), vm((4, 256, 1024), BF), vm((256, 1024), BF),
            vm((2, FF3, 256), BF), vm((FF3, 256), BF), vm((FF3, 256), BF),
            vm((2, 2, 256, 256), BF), vm((2, 256, 256), BF), vm((3, 256, 256), BF), vm((FF3 + 256, 128), F32),
            vm((768, 1024), BF), vm((4, 768, 128), BF), vm((2, 768, 128), BF), vm((768, 128), BF), vm((4, 8, 128), F32),
            dma((4, 2)), dma((4, 2)), dma((4, 2)), dma((4, 2)),
            dma((3,)), dma((3,)), dma((4,)), dma((4,)), dma((8,)), dma((8,)), dma((3,)), dma((3,)), dma((2,)), dma((2,)),
            dma((4,)), dma((2,)), dma((2,)), dma((2,)), dma((2,)), dma((2,)), dma((2, 2)),
            dma((4,)), dma((4,)), dma((4,)), dma((4,)), dma((4,)), dma((4,)), dma((2, 4)), dma((4,)), dma((2, 2)),
            dma, dma, dma((3,)), dma((3,)), dma((3,)), dma((3,)), dma((3,)), dma((3,)), dma, dma, dma((2, 2)), dma((4,)),
            dma((2, NU)), dma((2, NU)), dma((NU,)), dma((NU,)), dma((NU,)), dma((3, NU)),
            dma((NF + 1,)), dma((NF + 1,)), dma((4, 4)), dma((4, 4)), dma((4, 4)), dma((4,)),
            dma((4,)), dma((4,)), dma((2,)), dma((2,)), dma, dma, dma((4,)), dma((4,)), dma,
        ],
        compiler_params=pltpu.CompilerParams(
            collective_id=1, has_side_effects=True, vmem_limit_bytes=63 << 20
        ),
        name="layer",
    )(*args)


def local_fast(
    tokens, lengths, seq_order, gain_attn, w_qkv, w_attn_out, gain_mlp, w_in, w_mlp_out, cotangent
):
    half = HEAD_DIM // 2
    frequency = jnp.tile(rope_base ** (-2.0 * jnp.arange(half, dtype=F32) / HEAD_DIM), 4)
    sign = jnp.tile(jnp.repeat(jnp.array([-1.0, 1.0], F32), half), 2)
    rows = (gain_attn.astype(F32), gain_mlp.astype(F32), frequency, sign)
    gains = jnp.concatenate([r[None, :] for r in rows] + [jnp.zeros((4, 128), F32)], axis=0)
    out, d_tok, d_qkv, d_in, d_down, d_out, d_gain = run_layer(
        lengths, seq_order, tokens, w_qkv, w_in.transpose(1, 2, 0).reshape(2 * HID, 128), w_mlp_out, w_attn_out, gains, cotangent
    )
    return (out, d_tok, d_gain[0], d_qkv, d_out, d_gain[1], d_in.reshape(2, HID, 128).transpose(2, 0, 1), d_down)


def layer_norm(field_in, norm_gain):
    row_mean = jnp.mean(field_in, axis=-1, keepdims=True)
    centered = field_in - row_mean
    variance = jnp.mean(centered * centered, axis=-1, keepdims=True)
    return centered * lax.rsqrt(variance + norm_eps) * norm_gain


def rotate(field_in, position):
    half_size = field_in.shape[-1] // 2
    index_range = jnp.arange(half_size, dtype=jnp.float32)
    frequency = rope_base ** (-2.0 * index_range / field_in.shape[-1])
    angles = position[:, None] * frequency[None, :]
    cosine = jnp.cos(angles)[:, None, :]
    sine_part = jnp.sin(angles)[:, None, :]
    first_half = field_in[..., :half_size]
    second_half = field_in[..., half_size:]
    return jnp.concatenate(
        [
            first_half * cosine - second_half * sine_part,
            second_half * cosine + first_half * sine_part,
        ],
        axis=-1,
    )


def geglu(act_part, up_part):
    return jax.nn.gelu(act_part, approximate=False) * up_part


def layout(lengths, seq_order, group_rows):
    seq_total = seq_order.shape[0]
    first_seq = lax.axis_index("dp") * SEQ_GRP
    chosen = lax.dynamic_slice_in_dim(seq_order, first_seq, SEQ_GRP)
    matched = chosen[:, None] == jnp.arange(seq_total, dtype=jnp.int32)[None, :]
    dealt_lengths = jnp.sum(jnp.where(matched, lengths[None, :], 0), axis=1)
    seq_ends = jnp.cumsum(dealt_lengths)
    row_index = jnp.arange(group_rows, dtype=jnp.int32)
    passed = row_index[:, None] >= seq_ends[None, :]
    segment = jnp.sum(passed.astype(jnp.int32), axis=1)
    row_start = jnp.sum(jnp.where(passed, dealt_lengths[None, :], 0), axis=1)
    return (segment, (row_index - row_start).astype(jnp.float32))


def item_layout(array_in, block_rows):
    group_rows, head_count, head_size = array_in.shape
    block_count = group_rows // block_rows
    shaped = array_in.reshape(block_count, block_rows, head_count, head_size)
    return shaped.transpose(2, 0, 1, 3).reshape(head_count * block_count, block_rows, head_size)


def from_items(items, group_rows):
    item_count, block_rows, head_size = items.shape
    block_count = group_rows // block_rows
    head_count = item_count // block_count
    shaped = items.reshape(head_count, block_count, block_rows, head_size)
    return shaped.transpose(1, 2, 0, 3).reshape(group_rows, head_count, head_size)


def masked_scores(query_block, key_head, segment_block, segment):
    score_scale = query_block.shape[-1] ** (-0.5)
    raw_scores = lax.dot_general(
        query_block, key_head, (((1,), (1,)), ((), ())), preferred_element_type=jnp.float32
    )
    allowed = segment_block[:, None] == segment[None, :]
    return jnp.where(allowed, raw_scores * score_scale, masked_fill)


def attend_forward(query_rot, key_rot, value_low, segment, block_rows):
    group_rows, head_count, head_size = query_rot.shape
    block_count = group_rows // block_rows
    query_items = item_layout(query_rot, block_rows)
    key_heads = key_rot.transpose(1, 0, 2)
    value_heads = value_low.transpose(1, 0, 2)
    segment_blocks = segment.reshape(block_count, block_rows)

    def one_item(item_index):
        head_index = item_index // block_count
        block_index = item_index % block_count
        query_block = lax.dynamic_index_in_dim(query_items, item_index, 0, False)
        key_head = lax.dynamic_index_in_dim(key_heads, head_index, 0, False)
        value_head = lax.dynamic_index_in_dim(value_heads, head_index, 0, False)
        segment_block = lax.dynamic_index_in_dim(segment_blocks, block_index, 0, False)
        scores = masked_scores(query_block, key_head, segment_block, segment)
        row_top = jnp.max(scores, axis=1, keepdims=True)
        weights = jnp.exp(scores - row_top)
        row_total = jnp.sum(weights, axis=1, keepdims=True)
        probs_low = (weights / row_total).astype(jnp.bfloat16)
        result = jnp.dot(probs_low, value_head, preferred_element_type=jnp.float32)
        return (result, row_top[:, 0] + jnp.log(row_total[:, 0]))

    results, log_totals = lax.map(one_item, jnp.arange(head_count * block_count, dtype=jnp.int32))
    return (from_items(results, group_rows), log_totals)


def attend_backward(query_rot, key_rot, value_low, grad_out, log_totals, segment, block_rows):
    group_rows, head_count, head_size = query_rot.shape
    block_count = group_rows // block_rows
    score_scale = head_size ** (-0.5)
    query_items = item_layout(query_rot, block_rows)
    grad_items = item_layout(grad_out, block_rows)
    key_heads = key_rot.transpose(1, 0, 2)
    value_heads = value_low.transpose(1, 0, 2)
    segment_blocks = segment.reshape(block_count, block_rows)

    def one_item(carried, item_index):
        key_grads, value_grads = carried
        head_index = item_index // block_count
        block_index = item_index % block_count
        query_block = lax.dynamic_index_in_dim(query_items, item_index, 0, False)
        grad_block = lax.dynamic_index_in_dim(grad_items, item_index, 0, False)
        log_row = lax.dynamic_index_in_dim(log_totals, item_index, 0, False)
        key_head = lax.dynamic_index_in_dim(key_heads, head_index, 0, False)
        value_head = lax.dynamic_index_in_dim(value_heads, head_index, 0, False)
        segment_block = lax.dynamic_index_in_dim(segment_blocks, block_index, 0, False)
        scores = masked_scores(query_block, key_head, segment_block, segment)
        prob_full = jnp.exp(scores - log_row[:, None])
        probs_low = prob_full.astype(jnp.bfloat16)
        grad_probs = lax.dot_general(
            grad_block, value_head, (((1,), (1,)), ((), ())), preferred_element_type=jnp.float32
        )
        row_delta = jnp.sum(prob_full * grad_probs, axis=1, keepdims=True)
        grad_scores = (prob_full * (grad_probs - row_delta)).astype(jnp.bfloat16)
        grad_query = (
            jnp.dot(grad_scores, key_head, preferred_element_type=jnp.float32) * score_scale
        )
        grad_key = (
            lax.dot_general(
                grad_scores,
                query_block,
                (((0,), (0,)), ((), ())),
                preferred_element_type=jnp.float32,
            )
            * score_scale
        )
        grad_value = lax.dot_general(
            probs_low, grad_block, (((0,), (0,)), ((), ())), preferred_element_type=jnp.float32
        )
        key_grads = lax.dynamic_update_index_in_dim(
            key_grads,
            lax.dynamic_index_in_dim(key_grads, head_index, 0, False) + grad_key,
            head_index,
            0,
        )
        value_grads = lax.dynamic_update_index_in_dim(
            value_grads,
            lax.dynamic_index_in_dim(value_grads, head_index, 0, False) + grad_value,
            head_index,
            0,
        )
        return ((key_grads, value_grads), grad_query)

    zero_heads = jnp.zeros((head_count, group_rows, head_size), jnp.float32)
    (key_grads, value_grads), query_grads = lax.scan(
        one_item, (zero_heads, zero_heads), jnp.arange(head_count * block_count, dtype=jnp.int32)
    )
    return (
        from_items(query_grads, group_rows),
        key_grads.transpose(1, 0, 2),
        value_grads.transpose(1, 0, 2),
    )


def spread_rows(local_rows):
    return lax.all_gather(local_rows, "tensor", axis=0, tiled=True)


def spread_grads(local_grads):
    return lax.all_gather(local_grads, "tensor", axis=0, tiled=True)


def sum_heads(activations, weight_part, row_count):

    def row_term(first_row, row_number):
        return jnp.dot(activations, weight_part, preferred_element_type=jnp.float32)

    return lax.psum_scatter(
        row_term(jnp.int32(0), row_count * lax.axis_size("tensor")),
        "tensor",
        scatter_dimension=0,
        tiled=True,
    )


def sum_grads(grads_low, weight_full, einsum_form, row_count):

    def row_term(first_row, row_number):
        return jnp.einsum(einsum_form, grads_low, weight_full, preferred_element_type=jnp.float32)

    return lax.psum_scatter(
        row_term(jnp.int32(0), row_count * lax.axis_size("tensor")),
        "tensor",
        scatter_dimension=0,
        tiled=True,
    )


def local_plain(
    tokens, lengths, seq_order, gain_attn, w_qkv, w_attn_out, gain_mlp, w_in, w_mlp_out, cotangent
):
    row_count = tokens.shape[0]
    group_rows = row_count * lax.axis_size("tensor")
    block_rows = min(512, group_rows)
    segment, position = layout(lengths, seq_order, group_rows)
    gain_low_one, qkv_weight, out_weight, gain_low_two, in_weight, down_weight = (
        lax.all_gather(gain_attn, "dp", axis=0, tiled=True),
        lax.all_gather(w_qkv, "dp", axis=1, tiled=True),
        lax.all_gather(w_attn_out, "dp", axis=1, tiled=True),
        lax.all_gather(gain_mlp, "dp", axis=0, tiled=True),
        lax.all_gather(w_in, "dp", axis=0, tiled=True),
        lax.all_gather(w_mlp_out, "dp", axis=1, tiled=True),
    )
    gain_one = gain_low_one.astype(jnp.float32)
    gain_two = gain_low_two.astype(jnp.float32)
    residual = tokens.astype(jnp.float32)
    normed_one = spread_rows(layer_norm(residual, gain_one).astype(jnp.bfloat16))
    qkv = jnp.einsum("rd,pdc->rpc", normed_one, qkv_weight, preferred_element_type=jnp.float32)
    head_count = qkv.shape[2] // HEAD_DIM
    head_shape = (group_rows, head_count, HEAD_DIM)
    query_rot = rotate(qkv[:, 0].reshape(head_shape), position).astype(jnp.bfloat16)
    key_rot = rotate(qkv[:, 1].reshape(head_shape), position).astype(jnp.bfloat16)
    value_low = qkv[:, 2].reshape(head_shape).astype(jnp.bfloat16)
    attended, log_totals = attend_forward(query_rot, key_rot, value_low, segment, block_rows)
    attn_low = attended.reshape(group_rows, head_count * HEAD_DIM).astype(jnp.bfloat16)
    resid_mid = residual + sum_heads(attn_low, out_weight, row_count)
    normed_two = spread_rows(layer_norm(resid_mid, gain_two).astype(jnp.bfloat16))
    gate_up = jnp.einsum("rd,dpc->rpc", normed_two, in_weight, preferred_element_type=jnp.float32)
    hidden = geglu(gate_up[:, 0], gate_up[:, 1]).astype(jnp.bfloat16)
    output = (resid_mid + sum_heads(hidden, down_weight, row_count)).astype(jnp.bfloat16)
    grad_two = spread_grads(cotangent)
    d_hidden = lax.dot_general(
        grad_two, down_weight, (((1,), (1,)), ((), ())), preferred_element_type=jnp.float32
    )
    d_down = lax.dot_general(
        hidden, grad_two, (((0,), (0,)), ((), ())), preferred_element_type=jnp.float32
    )
    geglu_pull = jax.vjp(geglu, gate_up[:, 0], gate_up[:, 1])[1]
    d_act, d_up = geglu_pull(d_hidden)
    d_gate_up = jnp.stack([d_act, d_up], axis=1).astype(jnp.bfloat16)
    d_in = jnp.einsum("rd,rpc->dpc", normed_two, d_gate_up, preferred_element_type=jnp.float32)
    d_normed_two = sum_grads(d_gate_up, in_weight, "rpc,dpc->rd", row_count)
    norm_pull_two = jax.vjp(layer_norm, resid_mid, gain_two)[1]
    d_mid_norm, d_gain_two = norm_pull_two(d_normed_two)
    d_mid = cotangent.astype(jnp.float32) + d_mid_norm
    grad_one = spread_grads(d_mid.astype(jnp.bfloat16))
    d_out = lax.dot_general(
        attn_low, grad_one, (((0,), (0,)), ((), ())), preferred_element_type=jnp.float32
    )
    d_att = lax.dot_general(
        grad_one, out_weight, (((1,), (1,)), ((), ())), preferred_element_type=jnp.float32
    ).astype(jnp.bfloat16)
    d_query_rot, d_key_rot, d_value = attend_backward(
        query_rot, key_rot, value_low, d_att.reshape(head_shape), log_totals, segment, block_rows
    )
    rotate_pull = jax.vjp(lambda field_in: rotate(field_in, position), d_query_rot)[1]
    d_query = rotate_pull(d_query_rot)[0]
    d_key = rotate_pull(d_key_rot)[0]
    flat_shape = (group_rows, head_count * HEAD_DIM)
    d_qkv = jnp.stack(
        [d_query.reshape(flat_shape), d_key.reshape(flat_shape), d_value.reshape(flat_shape)],
        axis=1,
    ).astype(jnp.bfloat16)
    d_qkv_weight = jnp.einsum("rd,rpc->pdc", normed_one, d_qkv, preferred_element_type=jnp.float32)
    d_normed_one = sum_grads(d_qkv, qkv_weight, "rpc,pdc->rd", row_count)
    norm_pull_one = jax.vjp(layer_norm, residual, gain_one)[1]
    d_first, d_gain_one = norm_pull_one(d_normed_one)
    d_tokens = d_mid + d_first
    gain_sums = lax.psum((d_gain_one, d_gain_two), "tensor")
    shares = (
        lax.psum_scatter(gain_sums[0], "dp", scatter_dimension=0, tiled=True),
        lax.psum_scatter(d_qkv_weight, "dp", scatter_dimension=1, tiled=True),
        lax.psum_scatter(d_out, "dp", scatter_dimension=1, tiled=True),
        lax.psum_scatter(gain_sums[1], "dp", scatter_dimension=0, tiled=True),
        lax.psum_scatter(d_in, "dp", scatter_dimension=0, tiled=True),
        lax.psum_scatter(d_down, "dp", scatter_dimension=1, tiled=True),
    )
    return (output, d_tokens, shares[0], shares[1], shares[2], shares[3], shares[4], shares[5])


def solution(mesh):
    fast = mesh.shape["dp"] == 8 and mesh.shape["tensor"] == 4
    return jax.shard_map(
        local_fast if fast else local_plain,
        mesh=mesh,
        in_specs=(
            P(("dp", "tensor"), None),
            P(),
            P(),
            P("dp"),
            P(None, "dp", "tensor"),
            P("tensor", "dp"),
            P("dp"),
            P("dp", None, "tensor"),
            P("tensor", "dp"),
            P(("dp", "tensor"), None),
        ),
        out_specs=(
            P(("dp", "tensor"), None),
            P(("dp", "tensor"), None),
            P("dp"),
            P(None, "dp", "tensor"),
            P("tensor", "dp"),
            P("dp"),
            P("dp", None, "tensor"),
            P("tensor", "dp"),
        ),
        check_vma=False,
    )
```
